32 devices in a mesh: replica: 4 (over x, core), fsdp: 8 (over z, y).
Axes of the slice: x: 2, y: 2, z: 4, core: 2. Of those that a mesh axis runs over, the one named last changes fastest.
Arguments:
- tokens: bfloat16 [8192, 768], P(('replica', 'fsdp')), may hold values from -6 to 6
- cotangent: bfloat16 [8192, 768], P(('replica', 'fsdp')), may hold values from -6 to 6
- lengths: int32 [64], P(('replica', 'fsdp')), may hold values from 32 to 128, as said below
- routes: int32 [8192, 2], P(('replica', 'fsdp')), may hold values from 0 to 3, as said below
- slots: int32 [8192, 2], P(('replica', 'fsdp')), may hold values from 0 to 63, as said below
- gain_attn: bfloat16 [768], P('fsdp'), may hold values from 0.5 to 1.5
- w_qkv: bfloat16 [768, 2304], P('fsdp'), may hold values from -0.21875 to 0.21875
- w_proj: bfloat16 [768, 768], P('fsdp'), may hold values from -0.875 to 0.875
- rel_table: bfloat16 [128, 12], P('fsdp'), may hold values from -4 to 4
- gain_moe: bfloat16 [768], P('fsdp'), may hold values from 0.5 to 1.5
- w_router: bfloat16 [768, 4], P('fsdp'), may hold values from -0.21875 to 0.21875
- w_up: bfloat16 [8, 768, 1536], P('fsdp'), may hold values from -0.21875 to 0.21875
- w_down: bfloat16 [8, 1536, 768], P('fsdp'), may hold values from -0.109375 to 0.109375
Outputs:
- mixed: bfloat16 [8192, 768], P(('replica', 'fsdp'))
- grad_tokens: float32 [8192, 768], P(('replica', 'fsdp'))
- grad_gain_attn: float32 [768], P('fsdp')
- grad_w_qkv: float32 [768, 2304], P('fsdp')
- grad_w_proj: float32 [768, 768], P('fsdp')
- grad_rel_table: float32 [128, 12], P('fsdp')
- grad_gain_moe: float32 [768], P('fsdp')
- grad_w_router: float32 [768, 4], P('fsdp')
- grad_w_up: float32 [8, 768, 1536], P('fsdp')
- grad_w_down: float32 [8, 1536, 768], P('fsdp')
The draws below stay inside these ranges and needn't reach their ends.
Inputs may be any that keep to these rules, and one draw needn't show every extreme that they name: `lengths`: each sequence's live slots come first; one sequence has all 128 slots live. Each slot names two different experts. Within one sequence's 128 slots, padded ones included, every expert is named by exactly 64 routes. Routes of slots that are not live are ignored. Within one sequence, the routes to one expert have distinct slots; a first route's slot is below 32, a second route's slot is 32 or more.
All inputs are finite; a program needn't handle non-finite values.
Results may differ from the reference program's by a relative error of at most 0.012.
Values may be sent and summed in bfloat16 or wider, within the bound.
A program may use at most 192 MiB of HBM per device.

```python
import math
import jax
import jax.numpy as jnp
from jax import lax

D = 768
HEADS = 12
HEAD = 64
FF = 3072
SEQ = 128
EXPERTS = 4
CAP = 64
SEQUENCES = 64
TOKENS = 8192
N_FSDP = 8


def draw_lengths(key, part):
    spread = jax.random.randint(jax.random.fold_in(key, 3), (SEQUENCES,), SEQ // 4, SEQ + 1, dtype=jnp.int32)
    longest = jax.random.randint(jax.random.fold_in(key, 4), (), 0, SEQUENCES, dtype=jnp.int32)
    return jnp.where(jnp.arange(SEQUENCES, dtype=jnp.int32) == longest, SEQ, spread).astype(jnp.int32)


def follow_cycle(cycle, current):
    ranks = jnp.argsort(cycle, axis=1, stable=True).astype(jnp.int32)
    where_now = jnp.take_along_axis(ranks, current, axis=1)
    return jnp.take_along_axis(cycle, (where_now + 1) % EXPERTS, axis=1)


def route_tables(key):
    base = jax.random.fold_in(key, 11)
    order_keys = jax.random.split(jax.random.fold_in(base, 1), SEQUENCES)
    order = jax.vmap(lambda item: jax.random.permutation(item, SEQ))(order_keys).astype(jnp.int32)
    even_keys = jax.random.split(jax.random.fold_in(base, 2), SEQUENCES)
    odd_keys = jax.random.split(jax.random.fold_in(base, 3), SEQUENCES)
    cycle_even = jax.vmap(lambda item: jax.random.permutation(item, EXPERTS))(even_keys).astype(jnp.int32)
    cycle_odd = jax.vmap(lambda item: jax.random.permutation(item, EXPERTS))(odd_keys).astype(jnp.int32)
    half_cap = SEQ // EXPERTS
    first = order // half_cap
    first_slot = order % half_cap
    second = jnp.where(first_slot % 2 == 0, follow_cycle(cycle_even, first), follow_cycle(cycle_odd, first))
    route_pairs = jnp.stack([first, second], axis=-1).reshape(TOKENS, 2).astype(jnp.int32)
    slot_pairs = jnp.stack([first_slot, first_slot + half_cap], axis=-1).reshape(TOKENS, 2).astype(jnp.int32)
    return (route_pairs, slot_pairs)


def draw_routes(key, part):
    return route_tables(key)[0]


def draw_slots(key, part):
    return route_tables(key)[1]


def level_of(stream_key, shape, shards, least, high):
    def one(axis_at, shards_of):
        heights = jax.random.uniform(jax.random.fold_in(jax.random.fold_in(stream_key, 6), axis_at), (shards_of,), jnp.float32, least / len(shards), high / len(shards))
        return jnp.repeat(jnp.exp(heights), shape[axis_at] // shards_of).reshape((-1,) + (1,) * (len(shape) - axis_at - 1))

    level = one(*shards[0])
    for cut in shards[1:]:
        level = level * one(*cut)
    return level


def gaussian(rng, dims, deviation, bound, cuts=(), held_as=jnp.bfloat16):
    entries = jax.random.normal(rng, dims, jnp.float32) * deviation
    if len(cuts) > 0:
        entries = level_of(rng, dims, cuts, -0.22, 0.18) * entries
    return jnp.clip(entries, min=-bound, max=bound).astype(held_as)


def setup_inputs(seed: int = 0) -> dict:
    splits = jax.random.split(jax.random.key(seed), 14)
    tokens = gaussian(splits[0], (TOKENS, D), 1.0, 6.0, ((0, 32),))
    cotangent = gaussian(splits[1], (TOKENS, D), 1.0, 6.0, ((0, 32),))
    lengths = draw_lengths(jax.random.fold_in(splits[13], 71), 0)
    routes = draw_routes(jax.random.fold_in(splits[13], 71), 0)
    slots = draw_slots(jax.random.fold_in(splits[13], 71), 0)
    gain_attn = jnp.clip(1.0 + 0.1 * jax.random.normal(splits[5], (D,), jnp.float32), 0.5, 1.5).astype(jnp.bfloat16)
    w_qkv = gaussian(splits[6], (D, 3 * D), D ** -0.5, 0.21875, ((0, 8),))
    w_proj = gaussian(splits[7], (D, D), (D // 16) ** -0.5, 0.875, ((0, 8),))
    rel_table = gaussian(splits[8], (SEQ, HEADS), 1.0, 4.0, ((0, 8),))
    gain_moe = jnp.clip(1.0 + 0.1 * jax.random.normal(splits[9], (D,), jnp.float32), 0.5, 1.5).astype(jnp.bfloat16)
    w_router = gaussian(splits[10], (D, EXPERTS), D ** -0.5, 0.21875, ((0, 8),))
    w_up = gaussian(splits[11], (N_FSDP, D, FF // 2), D ** -0.5, 0.21875, ((0, 8),))
    w_down = gaussian(splits[12], (N_FSDP, FF // 2, D), FF ** -0.5, 0.109375, ((0, 8),))
    return {"tokens": tokens, "cotangent": cotangent, "lengths": lengths, "routes": routes, "slots": slots, "gain_attn": gain_attn, "w_qkv": w_qkv, "w_proj": w_proj, "rel_table": rel_table, "gain_moe": gain_moe, "w_router": w_router, "w_up": w_up, "w_down": w_down}


@jax.custom_vjp
def low(v):
    return lax.optimization_barrier(v.astype(jnp.bfloat16)).astype(jnp.float32)

@jax.custom_vjp
def low_back(v):
    return v

def low_keep(v):
    return (low(v), None)

def low_pass(kept, grad):
    return (grad,)

def back_keep(v):
    return (v, None)

def back_low(kept, grad):
    return (low(grad),)
low.defvjp(low_keep, low_pass)
low_back.defvjp(back_keep, back_low)
epsilon = 1e-06
exact_precision = lax.Precision.HIGHEST

def rms_norm(values, gain):
    factor = lax.rsqrt(lax.optimization_barrier(jnp.mean(values * values, axis=-1, keepdims=True)) + epsilon)
    return values * factor * gain

def bias_matrix(table):
    places = jnp.arange(SEQ, dtype=jnp.int32)
    distance = jnp.clip(places[:, None] - places[None, :], 0, SEQ - 1)
    return jnp.transpose(table[distance], (2, 0, 1))

def expert_half(rows, up_half, down_half):
    rows = low_back(rows)
    before = low_back(jnp.dot(rows, up_half, precision=exact_precision))
    active = low(jax.nn.gelu(before, approximate=False))
    return low(jnp.dot(active, down_half, precision=exact_precision))

def reference(tokens, cotangent, lengths, routes, slots, gain_attn, w_qkv, w_proj, rel_table, gain_moe, w_router, w_up, w_down):
    token_ids = jnp.arange(TOKENS, dtype=jnp.int32)
    seq_of = token_ids // SEQ
    place = token_ids % SEQ
    live_mask = place < lengths[seq_of]
    slot_place = (seq_of[:, None] * EXPERTS + routes) * CAP + slots
    target = jnp.where(live_mask[:, None], slot_place, 2 * TOKENS).astype(jnp.int32)
    owners = jnp.full((2 * TOKENS,), TOKENS, jnp.int32)
    owners = owners.at[target.reshape(-1)].set(jnp.repeat(token_ids, 2), mode='drop')
    gather_rows = owners.reshape(SEQUENCES, EXPERTS, CAP).transpose(1, 0, 2).reshape(EXPERTS, SEQUENCES * CAP)
    flat_slot = (routes * (SEQUENCES * CAP) + seq_of[:, None] * CAP + slots).astype(jnp.int32)
    places = jnp.arange(SEQ, dtype=jnp.int32)
    causal = places[:, None] >= places[None, :]
    per_group = math.gcd(SEQUENCES, max(1, 4096 // SEQ))

    def layer(x_float, gain_a, qkv_w, proj_w, table, gain_m, router_w, up_w, down_w):
        live_float = live_mask.astype(x_float.dtype)

        def attend(x_group, live_group):
            count = x_group.shape[0]
            normed = low(rms_norm(x_group, gain_a))
            qkv_rows = low_back(low(jnp.einsum('gsd,de->gse', normed, qkv_w, precision=exact_precision)))
            qkv_rows = qkv_rows.reshape(count, SEQ, 3, HEADS, HEAD)
            raw = jnp.einsum('gqhd,gkhd->ghqk', qkv_rows[:, :, 0], qkv_rows[:, :, 1], precision=exact_precision)
            scores = low_back(raw * HEAD ** (-0.5) + bias_matrix(table)[None])
            allowed = causal[None, None] & (live_group[:, None, None, :] > 0.5)
            probs = low(jax.nn.softmax(jnp.where(allowed, scores, -1e+30), axis=-1))
            attended = jnp.einsum('ghqk,gkhd->gqhd', probs, qkv_rows[:, :, 2], precision=exact_precision)
            attended = low_back(low(attended.reshape(count, SEQ, D)))
            branch = low_back(jnp.einsum('gsd,de->gse', attended, proj_w, precision=exact_precision))
            return x_group + live_group[..., None] * branch

        def attend_items(items):
            return attend(items[0], items[1])
        grouped = x_float.reshape(SEQUENCES // per_group, per_group, SEQ, D)
        live_grouped = live_float.reshape(SEQUENCES // per_group, per_group, SEQ)
        hidden = lax.map(jax.checkpoint(attend_items), (grouped, live_grouped))
        hidden = hidden.reshape(TOKENS, D)
        normed2 = low(rms_norm(hidden, gain_m))
        logits = jnp.dot(normed2, router_w, precision=exact_precision)
        picked = jnp.take_along_axis(logits, routes, axis=1)
        gate_first = jax.nn.sigmoid(picked[:, 0] - picked[:, 1])
        padded = jnp.concatenate([normed2, jnp.zeros((1, D), normed2.dtype)], axis=0)

        def expert_rows(items):
            row_ids, up_a, up_b, down_a, down_b = items
            rows = padded[row_ids]
            return low_back(expert_half(rows, up_a, down_a) + expert_half(rows, up_b, down_b))
        outputs = lax.map(jax.checkpoint(expert_rows), (gather_rows, up_w[0::2], up_w[1::2], down_w[0::2], down_w[1::2]))
        flat = outputs.reshape(EXPERTS * SEQUENCES * CAP, D)
        first_out = flat[flat_slot[:, 0]]
        second_out = flat[flat_slot[:, 1]]
        moe = live_float[:, None] * (gate_first[:, None] * first_out + (1.0 - gate_first)[:, None] * second_out)
        return hidden + moe
    result, pullback = jax.vjp(layer, tokens.astype(jnp.float32), gain_attn.astype(jnp.float32), w_qkv.astype(jnp.float32), w_proj.astype(jnp.float32), rel_table.astype(jnp.float32), gain_moe.astype(jnp.float32), w_router.astype(jnp.float32), w_up.astype(jnp.float32), w_down.astype(jnp.float32))
    grads = pullback(cotangent.astype(jnp.float32))
    return (result.astype(jnp.bfloat16), grads[0], grads[1], grads[2], grads[3], grads[4], grads[5], grads[6], grads[7], grads[8])
```

```python
import jax
import jax.numpy as jnp
from jax import lax
from jax.sharding import PartitionSpec as P

D = 768
HEADS = 12
HEAD = 64
FF = 3072
SEQ = 128
MB = 2


epsilon = 1e-06
exact_precision = lax.Precision.HIGHEST


def rms_norm(values, gain):
    factor = lax.rsqrt(jnp.mean(values * values, axis=-1, keepdims=True) + epsilon)
    return values * factor * gain


def distance_hot():
    places = jnp.arange(SEQ, dtype=jnp.int32)
    distance = jnp.clip(places[:, None] - places[None, :], 0, SEQ - 1).reshape(1, SEQ * SEQ)
    return (distance == places[:, None]).astype(jnp.bfloat16)


def bias_matrix(table, hot):
    flat = jnp.einsum("dh,dp->hp", table, hot, preferred_element_type=jnp.float32)
    return flat.reshape(table.shape[1], SEQ, SEQ)


def exact_gelu(values):
    return jax.nn.gelu(values, approximate=False)


def masked_scores(qkv_rows, bias, allowed, factor):
    raw = jnp.einsum(
        "qhd,khd->hqk", qkv_rows[:, 0], qkv_rows[:, 1], preferred_element_type=jnp.float32
    )
    return jnp.where(allowed[None], raw * factor + bias, -1e30)


def fetch_weights(gain_attn, w_qkv, w_proj, rel_table, gain_moe, w_router):
    rows, experts = w_router.shape
    spread = rel_table.shape[0]
    packed = jnp.concatenate(
        [gain_attn, gain_moe, w_router.reshape(-1), rel_table.reshape(-1)]
    )
    small = lax.all_gather(packed, "fsdp", axis=0, tiled=False)
    groups = small.shape[0]
    edge = 2 * rows + rows * experts
    return (
        small[:, :rows].reshape(-1),
        lax.all_gather(w_qkv, "fsdp", axis=0, tiled=True),
        lax.all_gather(w_proj, "fsdp", axis=0, tiled=True),
        small[:, edge:].reshape(groups * spread, HEADS),
        small[:, rows : 2 * rows].reshape(-1),
        small[:, 2 * rows : edge].reshape(groups * rows, experts),
    )


def body(
    tokens,
    cotangent,
    lengths,
    routes,
    slots,
    gain_attn,
    w_qkv,
    w_proj,
    rel_table,
    gain_moe,
    w_router,
    w_up,
    w_down,
):
    groups = lax.axis_size("fsdp")
    experts = groups // 2
    capacity = 2 * SEQ // experts
    factor = HEAD ** (-0.5)
    up_weight = w_up[0]
    down_weight = w_down[0]
    places = jnp.arange(SEQ, dtype=jnp.int32)
    causal = places[:, None] >= places[None, :]
    expert_ids = jnp.arange(experts, dtype=jnp.int32)
    saved = []
    mixed_parts = []
    weights = fetch_weights(gain_attn, w_qkv, w_proj, rel_table, gain_moe, w_router)
    gain_a = weights[0].astype(jnp.float32)
    gain_m = weights[4].astype(jnp.float32)
    router_float = weights[5].astype(jnp.float32)
    hot = distance_hot()
    bias = bias_matrix(weights[3], hot)
    for batch in range(MB):
        x_float = tokens[batch * SEQ : (batch + 1) * SEQ].astype(jnp.float32)
        live_keys = places < lengths[batch]
        live_col = live_keys.astype(jnp.float32)[:, None]
        allowed = causal & live_keys[None, :]
        normed = rms_norm(x_float, gain_a).astype(jnp.bfloat16)
        qkv_rows = (
            jnp.dot(normed, weights[1], preferred_element_type=jnp.float32)
            .astype(jnp.bfloat16)
            .reshape(SEQ, 3, HEADS, HEAD)
        )
        scores = masked_scores(qkv_rows, bias, allowed, factor)
        row_peak = jnp.max(scores, axis=-1, keepdims=True)
        exp_scores = jnp.exp(scores - row_peak)
        row_total = jnp.sum(exp_scores, axis=-1, keepdims=True)
        log_total = row_peak + jnp.log(row_total)
        probs_low = (exp_scores / row_total).astype(jnp.bfloat16)
        attended = jnp.einsum(
            "hqk,khd->qhd", probs_low, qkv_rows[:, 2], preferred_element_type=jnp.float32
        )
        attended = attended.astype(jnp.bfloat16).reshape(SEQ, D)
        branch = jnp.dot(attended, weights[2], preferred_element_type=jnp.float32)
        hidden = x_float + live_col * branch
        normed2 = rms_norm(hidden, gain_m).astype(jnp.bfloat16)
        logits = jnp.dot(normed2, weights[5], preferred_element_type=jnp.float32)
        route_rows = routes[batch * SEQ : (batch + 1) * SEQ]
        slot_rows = slots[batch * SEQ : (batch + 1) * SEQ]
        hot_first = (route_rows[:, 0:1] == expert_ids[None, :]).astype(jnp.float32)
        hot_second = (route_rows[:, 1:2] == expert_ids[None, :]).astype(jnp.float32)
        gate_first = jax.nn.sigmoid(
            jnp.sum(logits * hot_first, axis=-1) - jnp.sum(logits * hot_second, axis=-1)
        )
        row_place = route_rows * capacity + slot_rows
        target = jnp.where(live_keys[:, None], row_place, experts * capacity)
        outgoing = jnp.zeros((experts * capacity, D), jnp.bfloat16)
        outgoing = (
            outgoing.at[target[:, 0]]
            .set(normed2, mode="drop")
            .at[target[:, 1]]
            .set(normed2, mode="drop")
        )
        outgoing = jnp.repeat(outgoing.reshape(experts, capacity, D), 2, axis=0)
        expert_received = lax.all_to_all(outgoing, "fsdp", split_axis=0, concat_axis=0, tiled=True)
        expert_before = jnp.einsum(
            "scd,df->scf", expert_received, up_weight, preferred_element_type=jnp.float32
        )
        expert_active = exact_gelu(expert_before).astype(jnp.bfloat16)
        partial_value = jnp.einsum(
            "scf,fd->scd", expert_active, down_weight, preferred_element_type=jnp.float32
        ).astype(jnp.bfloat16)
        returned = lax.all_to_all(partial_value, "fsdp", split_axis=0, concat_axis=0, tiled=True)
        results = (returned, expert_received, expert_before)
        combined = (
            results[0]
            .astype(jnp.float32)
            .reshape(experts, 2, capacity, D)
            .sum(axis=1)
            .reshape(experts * capacity, D)
        )
        first_out = combined[row_place[:, 0]]
        second_out = combined[row_place[:, 1]]
        moe = live_col * (
            gate_first[:, None] * first_out + (1.0 - gate_first)[:, None] * second_out
        )
        mixed_parts.append((hidden + moe).astype(jnp.bfloat16))
        saved.append(
            {
                "normed": normed,
                "qkv_rows": qkv_rows,
                "log_total": log_total,
                "attended": attended,
                "hidden": hidden,
                "normed2": normed2,
                "gate_first": gate_first,
                "first_out": first_out,
                "second_out": second_out,
                "results": results,
                "target": target,
                "row_place": row_place,
                "hot_first": hot_first,
                "hot_second": hot_second,
            }
        )
    grad_qkv_w = jnp.zeros((D, 3 * D), jnp.float32)
    grad_proj_w = jnp.zeros((D, D), jnp.float32)
    grad_table = jnp.zeros((SEQ, HEADS), jnp.float32)
    grad_gain_a = jnp.zeros((D,), jnp.float32)
    grad_gain_m = jnp.zeros((D,), jnp.float32)
    grad_router = jnp.zeros((D, experts), jnp.float32)
    grad_up = jnp.zeros((D, FF // 2), jnp.float32)
    grad_down = jnp.zeros((FF // 2, D), jnp.float32)
    grad_parts = [None] * MB
    for batch in reversed(range(MB)):
        kept = saved[batch]
        x_float = tokens[batch * SEQ : (batch + 1) * SEQ].astype(jnp.float32)
        live_keys = places < lengths[batch]
        live_col = live_keys.astype(jnp.float32)[:, None]
        allowed = causal & live_keys[None, :]
        grad_out = cotangent[batch * SEQ : (batch + 1) * SEQ].astype(jnp.float32)
        grad_moe = live_col * grad_out
        gate_first = kept["gate_first"]
        gate_second = 1.0 - gate_first
        grad_gate_first = jnp.sum(grad_moe * kept["first_out"], axis=-1)
        grad_gate_second = jnp.sum(grad_moe * kept["second_out"], axis=-1)
        grad_first = (gate_first[:, None] * grad_moe).astype(jnp.bfloat16)
        grad_second = (gate_second[:, None] * grad_moe).astype(jnp.bfloat16)
        target = kept["target"]
        grad_send = jnp.zeros((experts * capacity, D), jnp.bfloat16)
        grad_send = (
            grad_send.at[target[:, 0]]
            .set(grad_first, mode="drop")
            .at[target[:, 1]]
            .set(grad_second, mode="drop")
        )
        grad_send = jnp.repeat(grad_send.reshape(experts, capacity, D), 2, axis=0)
        grad_recv = lax.all_to_all(grad_send, "fsdp", split_axis=0, concat_axis=0, tiled=True)
        received = kept["results"][1]
        before = kept["results"][2]
        active, gelu_back = jax.vjp(exact_gelu, before)
        active_low = active.astype(jnp.bfloat16)
        grad_active = jnp.einsum(
            "scd,fd->scf", grad_recv, down_weight, preferred_element_type=jnp.float32
        )
        grad_before = gelu_back(grad_active)[0].astype(jnp.bfloat16)
        grad_down = grad_down + jnp.einsum(
            "scf,scd->fd", active_low, grad_recv, preferred_element_type=jnp.float32
        )
        grad_up = grad_up + jnp.einsum(
            "scd,scf->df", received, grad_before, preferred_element_type=jnp.float32
        )
        grad_part = jnp.einsum(
            "scf,df->scd", grad_before, up_weight, preferred_element_type=jnp.float32
        ).astype(jnp.bfloat16)
        grad_back = lax.all_to_all(grad_part, "fsdp", split_axis=0, concat_axis=0, tiled=True)
        grad_rows = (
            grad_back.astype(jnp.float32)
            .reshape(experts, 2, capacity, D)
            .sum(axis=1)
            .reshape(experts * capacity, D)
        )
        row_place = kept["row_place"]
        grad_diff = (grad_gate_first - grad_gate_second) * gate_first * gate_second
        grad_logits = grad_diff[:, None] * (kept["hot_first"] - kept["hot_second"])
        normed2_float = kept["normed2"].astype(jnp.float32)
        grad_router = grad_router + jnp.dot(normed2_float.T, grad_logits, precision=exact_precision)
        grad_normed2 = live_col * (grad_rows[row_place[:, 0]] + grad_rows[row_place[:, 1]])
        grad_normed2 = grad_normed2 + jnp.dot(
            grad_logits, router_float.T, precision=exact_precision
        )
        _, norm_back_moe = jax.vjp(rms_norm, kept["hidden"], gain_m)
        grad_hidden_norm, grad_gain_part = norm_back_moe(grad_normed2)
        grad_gain_m = grad_gain_m + grad_gain_part
        grad_hidden = grad_out + grad_hidden_norm
        grad_branch = (live_col * grad_hidden).astype(jnp.bfloat16)
        grad_proj_w = grad_proj_w + jnp.einsum(
            "sd,se->de", kept["attended"], grad_branch, preferred_element_type=jnp.float32
        )
        grad_attended = jnp.einsum(
            "se,de->sd", grad_branch, weights[2], preferred_element_type=jnp.float32
        )
        grad_attended = grad_attended.astype(jnp.bfloat16).reshape(SEQ, HEADS, HEAD)
        qkv_rows = kept["qkv_rows"]
        scores = masked_scores(qkv_rows, bias, allowed, factor)
        probs = jnp.exp(scores - kept["log_total"])
        probs_low = probs.astype(jnp.bfloat16)
        grad_probs = jnp.einsum(
            "qhd,khd->hqk", grad_attended, qkv_rows[:, 2], preferred_element_type=jnp.float32
        )
        row_dot = jnp.sum(probs * grad_probs, axis=-1, keepdims=True)
        grad_scores = (probs * (grad_probs - row_dot)).astype(jnp.bfloat16)
        grad_table = grad_table + jnp.einsum(
            "dp,hp->dh",
            hot,
            jnp.where(allowed[None], grad_scores, 0).reshape(HEADS, SEQ * SEQ),
            preferred_element_type=jnp.float32,
        )
        grad_queries = (
            jnp.einsum(
                "hqk,khd->qhd", grad_scores, qkv_rows[:, 1], preferred_element_type=jnp.float32
            )
            * factor
        )
        grad_keys = (
            jnp.einsum(
                "hqk,qhd->khd", grad_scores, qkv_rows[:, 0], preferred_element_type=jnp.float32
            )
            * factor
        )
        grad_values = jnp.einsum(
            "hqk,qhd->khd", probs_low, grad_attended, preferred_element_type=jnp.float32
        )
        grad_qkv = (
            jnp.stack([grad_queries, grad_keys, grad_values], axis=1)
            .astype(jnp.bfloat16)
            .reshape(SEQ, 3 * D)
        )
        grad_qkv_w = grad_qkv_w + jnp.einsum(
            "sd,se->de", kept["normed"], grad_qkv, preferred_element_type=jnp.float32
        )
        grad_normed = jnp.einsum(
            "se,de->sd", grad_qkv, weights[1], preferred_element_type=jnp.float32
        )
        _, norm_back_attn = jax.vjp(rms_norm, x_float, gain_a)
        grad_x_norm, grad_gain_piece = norm_back_attn(grad_normed)
        grad_gain_a = grad_gain_a + grad_gain_piece
        grad_parts[batch] = grad_hidden + grad_x_norm
    small = jnp.concatenate(
        [
            grad_gain_a.reshape(groups, -1),
            grad_gain_m.reshape(groups, -1),
            grad_router.reshape(groups, -1),
            grad_table.reshape(groups, -1),
        ],
        axis=1,
    )
    small = lax.psum_scatter(small, "fsdp", scatter_dimension=0, tiled=True)
    shards = (
        small,
        lax.psum_scatter(grad_qkv_w, "fsdp", scatter_dimension=0, tiled=True),
        lax.psum_scatter(grad_proj_w, "fsdp", scatter_dimension=0, tiled=True),
    )
    sums = lax.psum((shards[0], shards[1], shards[2], grad_up[None], grad_down[None]), "replica")
    rows = D // groups
    edge = 2 * rows + rows * experts
    totals = (
        sums[0][0, :rows],
        sums[1],
        sums[2],
        sums[0][0, edge:].reshape(SEQ // groups, HEADS),
        sums[0][0, rows : 2 * rows],
        sums[0][0, 2 * rows : edge].reshape(rows, experts),
        sums[3],
        sums[4],
    )
    mixed = jnp.concatenate(mixed_parts, axis=0)
    grad_tokens = jnp.concatenate(grad_parts, axis=0)
    return (
        mixed,
        grad_tokens,
        totals[0],
        totals[1],
        totals[2],
        totals[3],
        totals[4],
        totals[5],
        totals[6],
        totals[7],
    )


def solution(mesh):
    in_specs = (
        P(("replica", "fsdp"), None),
        P(("replica", "fsdp"), None),
        P(("replica", "fsdp")),
        P(("replica", "fsdp"), None),
        P(("replica", "fsdp"), None),
        P("fsdp"),
        P("fsdp", None),
        P("fsdp", None),
        P("fsdp", None),
        P("fsdp"),
        P("fsdp", None),
        P("fsdp", None, None),
        P("fsdp", None, None),
    )
    out_specs = (
        P(("replica", "fsdp"), None),
        P(("replica", "fsdp"), None),
        P("fsdp"),
        P("fsdp", None),
        P("fsdp", None),
        P("fsdp", None),
        P("fsdp"),
        P("fsdp", None),
        P("fsdp", None, None),
        P("fsdp", None, None),
    )
    return jax.shard_map(body, mesh=mesh, in_specs=in_specs, out_specs=out_specs, check_vma=False)
```

```python
import functools

import jax
import jax.numpy as jnp
from jax import lax
from jax.experimental import pallas as pl
from jax.experimental.pallas import tpu as pltpu
from jax.sharding import PartitionSpec as P

D = 768
HEADS = 12
HEAD = 64
FF = 3072
SEQ = 128
MB = 2
MESH = pl.DeviceIdType.MESH
F32 = jnp.float32
BF16 = jnp.bfloat16
NEG = -1e30
HF = FF // 2
TOK = MB * SEQ
EXP = 4
CAP = 64
ROWS = MB * CAP
LOWC = 1152
EXTRA = D + 128
WALL = 2 * LOWC + EXTRA
SHARD = 96
HALF = SHARD // 2
PAIRS = HEADS // 2
SCALE = HEAD ** (-0.5)


def place():
    replica = lax.axis_index("replica")
    group = lax.axis_index("fsdp")
    return replica // 2, replica % 2, group // 2, group % 2


def device(x, c, z, y):
    return (x * 2 + c, z * 2 + y)


def remote(src, dst, send, recv, target):
    return pltpu.make_async_remote_copy(
        src_ref=src,
        dst_ref=dst,
        send_sem=send,
        recv_sem=recv,
        device_id=target,
        device_id_type=MESH,
    )


def greet():
    x, c, z, y = place()
    barrier = pltpu.get_barrier_semaphore()
    targets = [device(x, 1 - c, z, y), device(1 - x, c, z, y), device(x, c, z, 1 - y)]
    targets += [device(x, c, (z + k) % 4, y) for k in (1, 2, 3)]
    for target in targets:
        pl.semaphore_signal(barrier, inc=1, device_id=target, device_id_type=MESH)
    pl.semaphore_wait(barrier, len(targets))


def dot(a, b, ca=1, cb=0):
    return lax.dot_general(a, b, (((ca,), (cb,)), ((), ())), preferred_element_type=F32)


GATHER_SEMS = 40


def fill_own(wq, wp, sm, wall, local_sem):
    x, c, z, y = place()
    own = pl.ds(pl.multiple_of((z * 2 + y) * SHARD, 16), SHARD)
    fills = [
        pltpu.make_async_copy(wq.at[:, pl.ds(0, LOWC)], wall.at[own, pl.ds(0, LOWC)], local_sem.at[0]),
        pltpu.make_async_copy(
            wq.at[:, pl.ds(LOWC, LOWC)], wall.at[own, pl.ds(LOWC + EXTRA, LOWC)], local_sem.at[1]
        ),
        pltpu.make_async_copy(wp, wall.at[own, pl.ds(LOWC, D)], local_sem.at[2]),
        pltpu.make_async_copy(sm, wall.at[own, pl.ds(LOWC + D, 128)], local_sem.at[3]),
    ]
    for fill in fills:
        fill.start()
    for fill in fills:
        fill.wait()


def gather_weights(wall, send_sem, recv_sem):
    x, c, z, y = place()
    plane = pl.ds(pl.multiple_of(x * LOWC, 128), LOWC + EXTRA)
    share = pl.ds(pl.multiple_of(x * (LOWC + EXTRA), 128), LOWC)
    gained = pl.ds(pl.multiple_of((1 - x) * (LOWC + EXTRA), 128), LOWC)
    up, down = device(x, c, z + 1, y), device(x, c, z - 1, y)
    across, facing, twin = device(x, c, z, 1 - y), device(1 - x, c, z, y), device(x, 1 - c, z, y)
    started = []

    def part(zs, ys, half, cols):
        return wall.at[pl.ds(pl.multiple_of((zs * 2 + ys) * SHARD + half * HALF, 16), HALF), cols]

    def run(cond, what):
        if cond is None:
            what()
        else:
            pl.when(cond)(what)

    def go(cond, zs, ys, cols, send, recv, target):
        piece = part(zs, ys, c, cols)
        copy = remote(piece, piece, send_sem.at[send], recv_sem.at[recv], target)
        run(cond, copy.start)
        started.append((cond, copy))

    def arrive(cond, zs, ys, half, cols, recv):
        piece = part(zs, ys, half, cols)
        copy = remote(piece, piece, send_sem.at[0], recv_sem.at[recv], twin)
        run(cond, copy.wait_recv)

    def spread(cond, zs, ys, k):
        source = zs * 2 + ys
        go(cond, zs, ys, share, 13 + source, 8 + source, facing)
        go(cond, zs, ys, plane, 21 + source, 16 + source, twin)

    go(z < 3, z, y, plane, 0, z, up)
    go(z > 0, z, y, plane, 3, z, down)
    go(None, z, y, plane, 6, 4 + z, across)
    for k in (1, 2, 3):
        below, above = z - k, z + k
        for cond, zs, on, send, target in (
            (below >= 0, below, z < 3, k, up),
            (above <= 3, above, z > 0, 3 + k, down),
        ):
            arrive(cond, zs, y, c, plane, zs)
            if k < 3:
                go(cond & on, zs, y, plane, send, zs, target)
            go(cond, zs, y, plane, 6 + (k if target is up else 3 + k), 4 + zs, across)
            spread(cond, zs, y, k)
        if k == 1:
            arrive(None, z, 1 - y, c, plane, 4 + z)
            spread(None, z, 1 - y, 0)
        else:
            for cond, zs in ((z - k + 1 >= 0, z - k + 1), (z + k - 1 <= 3, z + k - 1)):
                arrive(cond, zs, 1 - y, c, plane, 4 + zs)
                spread(cond, zs, 1 - y, 0)
    for cond, zs in ((z == 3, z - 3), (z == 0, z + 3)):
        arrive(cond, zs, 1 - y, c, plane, 4 + zs)
        spread(cond, zs, 1 - y, 0)
    for zs in range(4):
        for ys in range(2):
            source = zs * 2 + ys
            other = (zs != z) | (ys != y)
            arrive(other, zs, ys, c, gained, 8 + source)
            go(other, zs, ys, gained, 29 + source, 24 + source, twin)
    for zs in range(4):
        for ys in range(2):
            source = zs * 2 + ys
            other = (zs != z) | (ys != y)
            arrive(other, zs, ys, 1 - c, plane, 16 + source)
            arrive(other, zs, ys, 1 - c, gained, 24 + source)
    return started


def finish(started):
    for cond, copy in started:
        if cond is None:
            copy.wait_send()
        else:
            pl.when(cond)(copy.wait_send)


def unit(values):
    return lax.rsqrt(jnp.mean(values * values, axis=-1, keepdims=True) + 1e-06)


def build_bias(wall, bias):
    table = jnp.concatenate(
        [wall[f * SHARD : f * SHARD + 16, LOWC + D : LOWC + EXTRA] for f in range(8)], axis=0
    )
    ahead = lax.broadcasted_iota(jnp.int32, (SEQ, SEQ), 0)
    lane = lax.broadcasted_iota(jnp.int32, (SEQ, SEQ), 1)
    turned = jnp.where(ahead + lane == SEQ, 1.0, jnp.where(ahead + lane == 0, 1.0, 0.0)).astype(BF16)
    lines = dot(table, turned, 0, 0)
    for h in range(HEADS):
        line = jnp.broadcast_to(lines[HEAD + h : HEAD + h + 1, :], (SEQ, SEQ))
        rolled = pltpu.roll(line, 0, 1, stride=1, stride_axis=0)
        bias[(h // 2) * SEQ : (h // 2 + 1) * SEQ, (h % 2) * SEQ : (h % 2 + 1) * SEQ] = jnp.where(ahead >= lane, rolled, NEG)


def routing(routes, slots, s):
    rows = slice(s * SEQ, (s + 1) * SEQ)
    lane = lax.broadcasted_iota(jnp.int32, (SEQ, EXP * CAP), 1)
    spots = routes[rows, :] * CAP + slots[rows, :]
    return spots[:, 0:1] == lane, spots[:, 1:2] == lane


def live_column(lengths, s):
    return lax.broadcasted_iota(jnp.int32, (SEQ, 1), 0) < lengths[s]


def attention_forward(
    x_ref, cot, lengths, routes, slots, wall, rows_t, board, normed, qkv, attended, hidden, normed2, gates,
    out_f, out_g,
):
    rows_t[...] = jnp.transpose(wall[:, LOWC + D : LOWC + EXTRA].astype(F32))[0:8]
    build_bias(wall, board)
    x = x_ref[...].astype(F32)
    normed[...] = (x * unit(x) * rows_t[0:1, :]).astype(BF16)
    qkv[:, 0:LOWC] = dot(normed[...], wall[:, 0:LOWC]).astype(BF16)
    qkv[:, LOWC : 2 * LOWC] = dot(normed[...], wall[:, LOWC + EXTRA : WALL]).astype(BF16)
    lane = lax.broadcasted_iota(jnp.int32, (SEQ, 128), 1)

    def pair(p, carry):
        blocks = pl.ds(pl.multiple_of(p * SEQ, SEQ), SEQ)
        for s in range(MB):
            rows = slice(s * SEQ, (s + 1) * SEQ)
            q = qkv[rows, pl.ds(pl.multiple_of(p * 128, 128), 128)]
            k = qkv[rows, pl.ds(pl.multiple_of(D + p * 128, 128), 128)]
            v = qkv[rows, pl.ds(pl.multiple_of(2 * D + p * 128, 128), 128)]
            alive = lane < lengths[s]
            got = []
            for j in range(2):
                mine = (lane < HEAD) if j == 0 else (lane >= HEAD)
                raw = dot(jnp.where(mine, q, jnp.zeros_like(q)), k, 1, 1)
                scores = jnp.where(alive, raw * SCALE + board[blocks, j * SEQ : (j + 1) * SEQ], NEG)
                scores = jnp.exp(scores - jnp.max(scores, axis=-1, keepdims=True))
                share = scores / jnp.sum(scores, axis=-1, keepdims=True)
                board[blocks, (2 + 2 * s + j) * SEQ : (3 + 2 * s + j) * SEQ] = share
                got.append(dot(share.astype(BF16), v))
            attended[rows, pl.ds(pl.multiple_of(p * 128, 128), 128)] = jnp.where(
                lane < HEAD, got[0], got[1]
            ).astype(BF16)
        return carry

    lax.fori_loop(0, PAIRS, pair, 0)
    branch = dot(attended[...], wall[:, LOWC : LOWC + D])
    for s in range(MB):
        rows = slice(s * SEQ, (s + 1) * SEQ)
        live = live_column(lengths, s)
        state = x_ref[rows, :].astype(F32) + jnp.where(live, branch[rows, :], 0.0)
        hidden[rows, :] = state
        low = (state * unit(state) * rows_t[1:2, :]).astype(BF16)
        normed2[rows, :] = low
        logits = dot(low, wall[:, LOWC + D : LOWC + EXTRA])
        kind = lane - 2
        picked = jnp.where(kind == routes[rows, 0:1], logits, 0.0) - jnp.where(
            kind == routes[rows, 1:2], logits, 0.0
        )
        gate = jax.nn.sigmoid(jnp.sum(picked, axis=-1, keepdims=True))
        gates[rows, :] = gate
        grad = jnp.where(live, cot[rows, :].astype(F32), 0.0)
        first, second = routing(routes, slots, s)
        first = jnp.where(first & live, 1.0, 0.0).astype(BF16)
        second = jnp.where(second & live, 1.0, 0.0).astype(BF16)
        sent = dot(first + second, low, 0, 0).astype(BF16)
        back = dot(first, (gate * grad).astype(BF16), 0, 0) + dot(
            second, ((1.0 - gate) * grad).astype(BF16), 0, 0
        )
        back = back.astype(BF16)
        for e in range(EXP):
            out_f[e, s * CAP : (s + 1) * CAP, :] = sent[e * CAP : (e + 1) * CAP, :]
            out_g[e, s * CAP : (s + 1) * CAP, :] = back[e * CAP : (e + 1) * CAP, :]


class Links:
    def __init__(self, send_sem, recv_sem):
        self.send_sem, self.recv_sem = send_sem, recv_sem
        self.started = []

    def go(self, cond, src, dst, send, recv, target):
        copy = remote(src, dst, self.send_sem.at[send], self.recv_sem.at[recv], target)
        run(cond, copy.start)
        self.started.append((cond, copy))
        return copy

    def arrive(self, cond, dst, recv, target):
        run(cond, remote(dst, dst, self.send_sem.at[0], self.recv_sem.at[recv], target).wait_recv)

    def leave(self, copy):
        copy.wait_send()
        self.started = [(cond, item) for cond, item in self.started if item is not copy]

    def finish(self):
        for cond, copy in self.started:
            run(cond, copy.wait_send)
        self.started = []


def run(cond, what):
    if cond is None:
        what()
    else:
        pl.when(cond)(what)


TILE = 512
Z_ROWS, Y_ROWS, Y_PART, Z_BACK = 40, 48, 56, 64
TWIN_W, FACE_W, TWIN_OUT = 72, 74, 76
RS_TWIN, RS_Y, RS_Z, RS_FACE, RS_OUT = 78, 80, 84, 92, 93
LINKS = 96


def quarter(zs):
    return pl.ds(pl.multiple_of(zs * 2 * ROWS, 2 * ROWS), 2 * ROWS)


def half_rows(zs, ys):
    return pl.ds(pl.multiple_of((zs * 2 + ys) * ROWS, ROWS), ROWS)


def expert_forward(zs, recv, up, down, act, slope, part):
    rows = quarter(zs)

    def tile(i, carry):
        cols = pl.ds(pl.multiple_of(i * TILE, TILE), TILE)
        before = dot(recv[rows, :], up[:, cols])
        below = 0.5 + 0.5 * lax.erf(before * 0.7071067811865476)
        act[rows, cols] = (before * below).astype(BF16)
        density = jnp.exp(before * before * -0.5) * 0.3989422804014327
        slope[rows, cols] = (below + before * density).astype(BF16)
        return carry

    lax.fori_loop(0, HF // TILE, tile, 0)
    got = dot(act[rows, 0:HF], down[...]).astype(BF16)
    part[zs, 0] = got[0:ROWS]
    part[zs, 1] = got[ROWS : 2 * ROWS]


def expert_backward(zs, recv, up, down, slope, part):
    rows = quarter(zs)

    def tile(i, carry):
        cols = pl.ds(pl.multiple_of(i * TILE, TILE), TILE)
        grad = dot(recv[rows, :], down[cols, :], 1, 1)
        slope[rows, cols] = (grad * slope[rows, cols].astype(F32)).astype(BF16)
        return carry

    lax.fori_loop(0, HF // TILE, tile, 0)
    got = dot(slope[rows, :], up[...], 1, 1).astype(BF16)
    part[zs, 0] = got[0:ROWS]
    part[zs, 1] = got[ROWS : 2 * ROWS]


def experts(links, out, recv, up, down, act, slope, part, take, back, w_down, w_up):
    x, c, z, y = place()
    across, facing, twin = device(x, c, z, 1 - y), device(1 - x, c, z, y), device(x, 1 - c, z, y)

    for kind in range(2):
        links.go(None, out[kind].at[z], recv[kind].at[half_rows(z, y), :], Y_ROWS + kind * 4, Y_ROWS + kind * 4 + z, across)
        for d in (1, 2, 3):
            to = (z + d) % 4
            links.go(
                None, out[kind].at[to], recv[kind].at[half_rows(z, y), :], Z_ROWS + kind * 4 + d,
                Z_ROWS + kind * 4 + z, device(x, c, to, y),
            )
        recv[kind][half_rows(z, y), :] = out[kind][z]

    def source(d):
        return (z + 4 - d) % 4

    def reach(kind, d):
        zs = source(d)
        rows = recv[kind].at[half_rows(zs, y), :]
        links.arrive(None, rows, Z_ROWS + kind * 4 + zs, across)
        links.go(None, rows, rows, Y_ROWS + kind * 4 + d, Y_ROWS + kind * 4 + zs, across)

    def compute(kind, d):
        zs = source(d)
        links.arrive(None, recv[kind].at[half_rows(zs, 1 - y), :], Y_ROWS + kind * 4 + zs, across)
        if kind == 0:
            expert_forward(zs, recv[0], up, down, act, slope, part[0])
        else:
            expert_backward(zs, recv[1], up, down, slope, part[1])
        links.go(
            None, part[kind].at[zs, 1 - y], take[kind].at[zs], Y_PART + kind * 4 + d, Y_PART + kind * 4 + zs, across
        )

    def merge(kind, d):
        zs = source(d)
        links.arrive(None, take[kind].at[zs], Y_PART + kind * 4 + zs, across)
        total = (part[kind][zs, y].astype(F32) + take[kind][zs].astype(F32)).astype(BF16)
        if d == 0:
            back[kind][z] = total
        else:
            part[kind][zs, y] = total
            links.go(
                None, part[kind].at[zs, y], back[kind].at[z], Z_BACK + kind * 4 + d, Z_BACK + kind * 4 + z,
                device(x, c, zs, y),
            )

    compute(0, 0)
    reach(0, 1)
    compute(1, 0)
    reach(0, 2)
    compute(0, 1)
    merge(0, 0)
    reach(0, 3)
    compute(0, 2)
    merge(1, 0)
    merge(0, 1)
    reach(1, 1)
    compute(0, 3)
    merge(0, 2)
    reach(1, 2)
    compute(1, 1)
    merge(0, 3)
    reach(1, 3)
    compute(1, 2)
    merge(1, 1)
    compute(1, 3)
    merge(1, 2)

    def down_tile(i, part_of, keep):
        cols = pl.ds(pl.multiple_of(part_of * (HF // 2) + i * 256, 128), 256)
        got = dot(act[:, cols], recv[1][...], 0, 0)
        keep[pl.ds(pl.multiple_of(i * 256, 256), 256), :] = got.astype(keep.dtype)

    def up_tile(i, part_of, keep):
        cols = pl.ds(pl.multiple_of(part_of * (D // 2) + i * 128, 128), 128)
        got = dot(recv[0][:, cols], slope[...], 0, 0)
        keep[pl.ds(pl.multiple_of(i * 128, 128), 128), :] = got.astype(keep.dtype)

    def tiles(one, part_of, keep):
        def step(i, carry):
            one(i, part_of, keep)
            return carry

        lax.fori_loop(0, 3, step, 0)

    sent = []
    for i, (one, w) in enumerate(((down_tile, w_down), (up_tile, w_up))):
        own, give, got, face = w
        tiles(one, 1 - c, give)
        sent.append(links.go(None, give, got, TWIN_W + i, TWIN_W + i, twin))
        if i == 0:
            merge(1, 3)
        tiles(one, c, own)
        links.arrive(None, got, TWIN_W + i, twin)
        links.leave(sent[i])
        give[...] = (own[...] + got[...].astype(F32)).astype(BF16)
        links.go(None, give, face, FACE_W + i, FACE_W + i, facing)
    for kind in range(2):
        for d in (1, 2, 3):
            zs = source(d)
            links.arrive(None, back[kind].at[zs], Z_BACK + kind * 4 + zs, across)


def expert_grads_out(links, w_down, w_up, out_down, out_up, local_sem):
    x, c, z, y = place()
    facing, twin = device(1 - x, c, z, y), device(x, 1 - c, z, y)
    pending = []
    for i, (w, target) in enumerate(((w_down, out_down), (w_up, out_up))):
        own, give, got, face = w
        count = own.shape[0]
        links.arrive(None, face, FACE_W + i, facing)
        own[...] = give[...].astype(F32) + face[...].astype(F32)
        rows = pl.ds(pl.multiple_of(c * count, 128), count)
        links.go(None, own, target.at[rows, :], TWIN_OUT + i, TWIN_OUT + i, twin)
        copy = pltpu.make_async_copy(own, target.at[rows, :], local_sem.at[i])
        copy.start()
        pending.append(copy)
    for i, (w, target) in enumerate(((w_down, out_down), (w_up, out_up))):
        count = w[0].shape[0]
        rows = pl.ds(pl.multiple_of((1 - c) * count, 128), count)
        links.arrive(None, target.at[rows, :], TWIN_OUT + i, twin)
    return pending


OWNC = 2 * D
SENTC = OWNC + 128


def combine(cot, lengths, routes, slots, rows_t, hidden, normed2, gates, back_f, back_g, mixed, rb, small_t):
    lane = lax.broadcasted_iota(jnp.int32, (SEQ, 128), 1)
    gain_grad = jnp.zeros((1, D), F32)
    router_grad = jnp.zeros((128, D), F32)
    for s in range(MB):
        rows = slice(s * SEQ, (s + 1) * SEQ)
        live = live_column(lengths, s)
        first, second = routing(routes, slots, s)
        first = jnp.where(first, 1.0, 0.0).astype(BF16)
        second = jnp.where(second, 1.0, 0.0).astype(BF16)
        given = jnp.concatenate([back_f[e, s * CAP : (s + 1) * CAP, :] for e in range(EXP)], axis=0)
        first_out = dot(first, given)
        second_out = dot(second, given)
        gate = gates[rows, :]
        grad = cot[rows, :].astype(F32)
        grad_live = jnp.where(live, grad, 0.0)
        state = hidden[rows, :]
        moe = gate * first_out + (1.0 - gate) * second_out
        mixed[rows, :] = (state + jnp.where(live, moe, 0.0)).astype(BF16)
        tilt = jnp.sum(grad_live * first_out, axis=-1, keepdims=True) - jnp.sum(
            grad_live * second_out, axis=-1, keepdims=True
        )
        tilt = tilt * gate * (1.0 - gate)
        kind = lane - 2
        hot = jnp.where(kind == routes[rows, 0:1], 1.0, 0.0) - jnp.where(kind == routes[rows, 1:2], 1.0, 0.0)
        grad_logits = tilt * hot
        high = grad_logits.astype(BF16)
        low = (grad_logits - high.astype(F32)).astype(BF16)
        router_grad = router_grad + dot(high, normed2[rows, :], 0, 0) + dot(low, normed2[rows, :], 0, 0)
        given = jnp.concatenate([back_g[e, s * CAP : (s + 1) * CAP, :] for e in range(EXP)], axis=0)
        grad_low = jnp.where(live, dot(first + second, given), 0.0)
        for e in range(EXP):
            grad_low = grad_low + grad_logits[:, 2 + e : 3 + e] * rows_t[2 + e : 3 + e, :]
        factor = unit(state)
        scaled = state * factor
        gain_grad = gain_grad + jnp.sum(grad_low * scaled, axis=0, keepdims=True)
        grad_low = grad_low * rows_t[1:2, :]
        inner = jnp.mean(grad_low * scaled, axis=-1, keepdims=True)
        grad_state = grad + factor * (grad_low - scaled * inner)
        hidden[rows, :] = grad_state
        rb[rows, 3 * D : 4 * D] = jnp.where(live, grad_state, 0.0).astype(BF16)
    small_t[...] = router_grad
    small_t[1:2, :] = gain_grad


def attention_backward(x_ref, wall, rows_t, left, qkv, board, hidden, grad_att, rb, rel_rows, small_t, grad_tokens):
    grad_att[...] = dot(rb[:, 3 * D : 4 * D], wall[:, LOWC : LOWC + D], 1, 1).astype(BF16)
    lane = lax.broadcasted_iota(jnp.int32, (SEQ, 128), 1)
    ahead = lax.broadcasted_iota(jnp.int32, (SEQ, 128), 0)
    flip = jnp.where(ahead + lane == SEQ - 1, 1.0, 0.0).astype(BF16)
    flip = jnp.concatenate([flip] * MB, axis=1)

    def pair(p, carry):
        blocks = pl.ds(pl.multiple_of(p * SEQ, SEQ), SEQ)
        scores = [[None] * MB, [None] * MB]
        for s in range(MB):
            rows = slice(s * SEQ, (s + 1) * SEQ)
            cols = [pl.ds(pl.multiple_of(i * D + p * 128, 128), 128) for i in range(3)]
            q, k, v = (qkv[rows, cols[i]] for i in range(3))
            grad = grad_att[rows, cols[0]]
            grads = [[], [], []]
            for j in range(2):
                mine = (lane < HEAD) if j == 0 else (lane >= HEAD)
                share = board[blocks, (2 + 2 * s + j) * SEQ : (3 + 2 * s + j) * SEQ]
                grad_probs = dot(jnp.where(mine, grad, jnp.zeros_like(grad)), v, 1, 1)
                inner = jnp.sum(share * grad_probs, axis=-1, keepdims=True)
                grad_scores = (share * (grad_probs - inner)).astype(BF16)
                scores[j][s] = grad_scores
                grads[0].append(dot(grad_scores, k) * SCALE)
                grads[1].append(dot(grad_scores, q, 0, 0) * SCALE)
                grads[2].append(dot(share.astype(BF16), grad, 0, 0))
            for i in range(3):
                rb[rows, cols[i]] = jnp.where(lane < HEAD, grads[i][0], grads[i][1]).astype(BF16)
        for j in range(2):
            flipped = dot(flip, jnp.concatenate(scores[j], axis=0))
            rolled = pltpu.roll(flipped, 1, 1, stride=1, stride_axis=0)
            rel_rows[pl.ds(2 * p + j, 1), :] = jnp.sum(rolled, axis=0, keepdims=True)
        return carry

    lax.fori_loop(0, PAIRS, pair, 0)
    grad_low = dot(rb[:, 0:LOWC], wall[:, 0:LOWC], 1, 1) + dot(
        rb[:, LOWC : 2 * LOWC], wall[:, LOWC + EXTRA : WALL], 1, 1
    )
    state = x_ref[...].astype(F32)
    factor = unit(state)
    scaled = state * factor
    small_t[0:1, :] = jnp.sum(grad_low * scaled, axis=0, keepdims=True)
    grad_low = grad_low * rows_t[0:1, :]
    inner = jnp.mean(grad_low * scaled, axis=-1, keepdims=True)
    grad_tokens[...] = hidden[...] + factor * (grad_low - scaled * inner)

    spot = lax.broadcasted_iota(jnp.int32, (SEQ, D), 0)
    column = lax.broadcasted_iota(jnp.int32, (SEQ, D), 1)
    distance = (SEQ - spot) & (SEQ - 1)
    picks = jnp.where(column == (distance >> 4) * SHARD + (distance & 15), 1.0, 0.0).astype(BF16)
    rest = rel_rows[...]
    spread = jnp.zeros((16, D), F32)
    for _ in range(3):
        high = rest.astype(BF16)
        spread = spread + dot(high, picks)
        rest = rest - high.astype(F32)
    small_t[HEAD : HEAD + 16, :] = spread


def reduce_grads(links, left, rb, small_t, give, take, total, y_take, z_take, face_give, face_take, last, out_qkv, out_proj, out_small, local_sem):
    x, c, z, y = place()
    across, facing, twin = device(x, c, z, 1 - y), device(1 - x, c, z, y), device(x, 1 - c, z, y)
    up, down = device(x, c, z + 1, y), device(x, c, z - 1, y)

    def tile(core, i, keep):
        def step(m, carry):
            rows = pl.ds(pl.multiple_of(m * 256, 256), 256)
            rhs = rb[:, pl.ds(pl.multiple_of((2 * core + i) * D, 128), D)]
            keep[rows, i * D : (i + 1) * D] = dot(left[core * i, :, rows], rhs, 0, 0).astype(keep.dtype)
            return carry

        lax.fori_loop(0, 3, step, 0)

    for i in range(2):
        tile(1 - c, i, give)
    small = jnp.transpose(small_t[...])
    give[:, OWNC:SENTC] = small.astype(BF16)
    first = links.go(None, give, take, RS_TWIN, RS_TWIN, twin)
    for i in range(2):
        tile(c, i, total)
    total[:, OWNC:SENTC] = small.astype(BF16).astype(F32)
    links.arrive(None, take, RS_TWIN, twin)
    links.leave(first)
    mirror = z // 2
    near = z + mirror * (3 - 2 * z)
    order = [o + mirror * (3 - 2 * o) for o in (3, 2, 1 - near, near)]

    def shard(zs, ys):
        return pl.ds(pl.multiple_of((zs * 2 + ys) * SHARD, 16), SHARD)

    for zs in order:
        rows = shard(zs, 1 - y)
        give[rows, :] = (total[rows, :] + take[rows, :].astype(F32)).astype(BF16)
        links.go(None, give.at[rows, :], y_take.at[zs], RS_Y + zs, RS_Y + zs, across)
    for zs in order:
        rows = shard(zs, y)
        total[rows, :] = total[rows, :] + take[rows, :].astype(F32)
    for k, zs in enumerate(order):
        rows = shard(zs, y)
        links.arrive(None, y_take.at[zs], RS_Y + zs, across)
        total[rows, :] = total[rows, :] + y_take[zs].astype(F32)
        if k < 3:
            climbs, sinks = zs > z, zs < z
            for cond, more, slot, target in ((climbs, z > 0, zs, up), (sinks, z < 3, 4 + zs, down)):

                @pl.when(cond & more)
                def _():
                    links.arrive(None, z_take.at[slot], RS_Z + slot, across)
                    total[rows, :] = total[rows, :] + z_take[slot].astype(F32)

                @pl.when(cond)
                def _():
                    give[rows, :] = total[rows, :].astype(BF16)

                links.go(cond, give.at[rows, :], z_take.at[slot], RS_Z + slot, RS_Z + slot, target)
    rows = shard(z, y)
    for cond, slot in ((z > 0, z), (z < 3, 4 + z)):

        @pl.when(cond)
        def _():
            links.arrive(None, z_take.at[slot], RS_Z + slot, across)
            total[rows, :] = total[rows, :] + z_take[slot].astype(F32)

    face_give[...] = total[rows, :].astype(BF16)
    links.go(None, face_give, face_take, RS_FACE, RS_FACE, facing)
    links.arrive(None, face_take, RS_FACE, facing)
    last[...] = face_give[...].astype(F32) + face_take[...].astype(F32)
    pieces = (
        (c == 0, slice(0, OWNC), out_qkv.at[:, 0:OWNC], 0),
        (c == 1, slice(0, D), out_qkv.at[:, OWNC : 3 * D], 1),
        (c == 1, slice(D, OWNC), out_proj, 2),
    )
    pending = []
    for cond, cols, target, i in pieces:
        links.go(cond, last.at[:, cols], target, RS_OUT + i, RS_OUT + i, twin)
        copy = pltpu.make_async_copy(last.at[:, cols], target, local_sem.at[2 + i])
        run(cond, copy.start)
        pending.append((cond, copy))
    copy = pltpu.make_async_copy(last.at[:, OWNC:SENTC], out_small, local_sem.at[5])
    copy.start()
    pending.append((None, copy))
    for cond, cols, target, i in pieces:
        links.arrive((c == 1) if i == 0 else (c == 0), target, RS_OUT + i, twin)
    return pending


def layer(
    x_ref, cot, lengths, routes, slots, wq, wp, sm, w_up, w_down,
    mixed, grad_tokens, out_qkv, out_proj, out_small, out_up, out_down,
    wall, rows_t, left, qkv, hidden, normed2, gates, out_f, out_g, recv_f, recv_g, up, down, act, slope,
    part_f, part_g, take_f, take_g, back_f, back_g, dn_own, dn_give, dn_take, dn_face, up_own, up_give, up_take, up_face,
    rb, rel_rows, small_t, take, total, y_take, z_take, face_give, face_take, last,
    local_sem, send_sem, recv_sem,
):
    fetch = [
        pltpu.make_async_copy(w_up.at[0], up, local_sem.at[4]),
        pltpu.make_async_copy(w_down.at[0], down, local_sem.at[5]),
    ]
    for copy in fetch:
        copy.start()
    greet()
    fill_own(wq, wp, sm, wall, local_sem)
    links = Links(send_sem, recv_sem)
    links.started += gather_weights(wall, send_sem, recv_sem)
    normed, attended = left.at[0], left.at[1]
    attention_forward(
        x_ref, cot, lengths, routes, slots, wall, rows_t, total, normed, qkv, attended, hidden, normed2, gates,
        out_f, out_g,
    )
    for copy in fetch:
        copy.wait()
    downs, ups = (dn_own, dn_give, dn_take, dn_face), (up_own, up_give, up_take, up_face)
    experts(
        links, (out_f, out_g), (recv_f, recv_g), up, down, act, slope, (part_f, part_g), (take_f, take_g),
        (back_f, back_g), downs, ups,
    )
    rel_rows[...] = jnp.zeros_like(rel_rows)
    combine(cot, lengths, routes, slots, rows_t, hidden, normed2, gates, back_f, back_g, mixed, rb, small_t)
    attention_backward(x_ref, wall, rows_t, left, qkv, total, hidden, normed2, rb, rel_rows, small_t, grad_tokens)
    pending = reduce_grads(
        links, left, rb, small_t, act.at[0:D, :], take, total, y_take, z_take, face_give, face_take, last, out_qkv, out_proj,
        out_small, local_sem,
    )
    more = expert_grads_out(links, downs, ups, out_down, out_up, local_sem)
    for cond, copy in pending + [(None, copy) for copy in more]:
        run(cond, copy.wait)
    links.finish()


def pack_small(gain_attn, gain_moe, w_router, rel_table):
    table = jnp.pad(rel_table, ((0, SHARD - rel_table.shape[0]), (0, 64 - HEADS)))
    side = jnp.concatenate([gain_attn[:, None], gain_moe[:, None], w_router], axis=1)
    return jnp.concatenate([jnp.pad(side, ((0, 0), (0, 64 - side.shape[1]))), table], axis=1)


def body_fast(
    tokens, cotangent, lengths, routes, slots, gain_attn, w_qkv, w_proj, rel_table, gain_moe, w_router, w_up, w_down
):
    small = pack_small(gain_attn, gain_moe, w_router, rel_table)
    vm = pl.BlockSpec(memory_space=pltpu.VMEM)
    hbm = pl.BlockSpec(memory_space=pl.ANY)
    sds = jax.ShapeDtypeStruct
    v = pltpu.VMEM
    out = pl.pallas_call(
        layer,
        out_shape=(
            sds((TOK, D), BF16), sds((TOK, D), F32), sds((SHARD, 3 * D), F32), sds((SHARD, D), F32),
            sds((SHARD, 128), F32), sds((D, HF), F32), sds((HF, D), F32),
        ),
        in_specs=[vm, vm, pl.BlockSpec(memory_space=pltpu.SMEM), vm, vm, hbm, hbm, hbm, hbm, hbm],
        out_specs=[vm, vm, hbm, hbm, hbm, hbm, hbm],
        scratch_shapes=[
            v((D, WALL), BF16), v((8, D), F32), v((2, TOK, D), BF16),
            v((TOK, 3 * D), BF16), v((TOK, D), F32), v((TOK, D), BF16),
            v((TOK, 1), F32), v((EXP, ROWS, D), BF16), v((EXP, ROWS, D), BF16),
            v((8 * ROWS, D), BF16), v((8 * ROWS, D), BF16), v((D, HF), BF16), v((HF, D), BF16),
            v((8 * ROWS, SENTC), BF16), v((8 * ROWS, HF), BF16),
            v((EXP, 2, ROWS, D), BF16), v((EXP, 2, ROWS, D), BF16), v((EXP, ROWS, D), BF16), v((EXP, ROWS, D), BF16),
            v((EXP, ROWS, D), BF16), v((EXP, ROWS, D), BF16),
            v((HF // 2, D), F32), v((HF // 2, D), BF16), v((HF // 2, D), BF16), v((HF // 2, D), BF16),
            v((D // 2, HF), F32), v((D // 2, HF), BF16), v((D // 2, HF), BF16), v((D // 2, HF), BF16),
            v((TOK, 4 * D), BF16), v((16, SEQ), F32), v((128, D), F32),
            v((D, SENTC), BF16), v((D, SENTC), F32), v((4, SHARD, SENTC), BF16), v((8, SHARD, SENTC), BF16),
            v((SHARD, SENTC), BF16), v((SHARD, SENTC), BF16), v((SHARD, SENTC), F32),
            pltpu.SemaphoreType.DMA((6,)), pltpu.SemaphoreType.DMA((LINKS,)), pltpu.SemaphoreType.DMA((LINKS,)),
        ],
        compiler_params=pltpu.CompilerParams(
            collective_id=0, has_side_effects=True, vmem_limit_bytes=67043328
        ),
        name="layer",
    )(tokens, cotangent, lengths, routes, slots, w_qkv, w_proj, small, w_up, w_down)
    mixed, grad_tokens, grad_qkv, grad_proj, side, grad_up, grad_down = out
    return (
        mixed,
        grad_tokens,
        side[:, 0],
        grad_qkv,
        grad_proj,
        side[: rel_table.shape[0], HEAD : HEAD + HEADS],
        side[:, 1],
        side[:, 2 : 2 + EXP],
        grad_up[None],
        grad_down[None],
    )


epsilon = 1e-06
exact_precision = lax.Precision.HIGHEST


def rms_norm(values, gain):
    factor = lax.rsqrt(jnp.mean(values * values, axis=-1, keepdims=True) + epsilon)
    return values * factor * gain


def distance_hot():
    places = jnp.arange(SEQ, dtype=jnp.int32)
    distance = jnp.clip(places[:, None] - places[None, :], 0, SEQ - 1).reshape(1, SEQ * SEQ)
    return (distance == places[:, None]).astype(jnp.bfloat16)


def bias_matrix(table, hot):
    flat = jnp.einsum("dh,dp->hp", table, hot, preferred_element_type=jnp.float32)
    return flat.reshape(table.shape[1], SEQ, SEQ)


def exact_gelu(values):
    return jax.nn.gelu(values, approximate=False)


def masked_scores(qkv_rows, bias, allowed, factor):
    raw = jnp.einsum(
        "qhd,khd->hqk", qkv_rows[:, 0], qkv_rows[:, 1], preferred_element_type=jnp.float32
    )
    return jnp.where(allowed[None], raw * factor + bias, -1e30)


def fetch_weights(gain_attn, w_qkv, w_proj, rel_table, gain_moe, w_router):
    rows, experts = w_router.shape
    spread = rel_table.shape[0]
    packed = jnp.concatenate(
        [gain_attn, gain_moe, w_router.reshape(-1), rel_table.reshape(-1)]
    )
    small = lax.all_gather(packed, "fsdp", axis=0, tiled=False)
    groups = small.shape[0]
    edge = 2 * rows + rows * experts
    return (
        small[:, :rows].reshape(-1),
        lax.all_gather(w_qkv, "fsdp", axis=0, tiled=True),
        lax.all_gather(w_proj, "fsdp", axis=0, tiled=True),
        small[:, edge:].reshape(groups * spread, HEADS),
        small[:, rows : 2 * rows].reshape(-1),
        small[:, 2 * rows : edge].reshape(groups * rows, experts),
    )


def body(
    tokens,
    cotangent,
    lengths,
    routes,
    slots,
    gain_attn,
    w_qkv,
    w_proj,
    rel_table,
    gain_moe,
    w_router,
    w_up,
    w_down,
):
    groups = lax.axis_size("fsdp")
    experts = groups // 2
    capacity = 2 * SEQ // experts
    factor = HEAD ** (-0.5)
    up_weight = w_up[0]
    down_weight = w_down[0]
    places = jnp.arange(SEQ, dtype=jnp.int32)
    causal = places[:, None] >= places[None, :]
    expert_ids = jnp.arange(experts, dtype=jnp.int32)
    saved = []
    mixed_parts = []
    weights = fetch_weights(gain_attn, w_qkv, w_proj, rel_table, gain_moe, w_router)
    gain_a = weights[0].astype(jnp.float32)
    gain_m = weights[4].astype(jnp.float32)
    router_float = weights[5].astype(jnp.float32)
    hot = distance_hot()
    bias = bias_matrix(weights[3], hot)
    for batch in range(MB):
        x_float = tokens[batch * SEQ : (batch + 1) * SEQ].astype(jnp.float32)
        live_keys = places < lengths[batch]
        live_col = live_keys.astype(jnp.float32)[:, None]
        allowed = causal & live_keys[None, :]
        normed = rms_norm(x_float, gain_a).astype(jnp.bfloat16)
        qkv_rows = (
            jnp.dot(normed, weights[1], preferred_element_type=jnp.float32)
            .astype(jnp.bfloat16)
            .reshape(SEQ, 3, HEADS, HEAD)
        )
        scores = masked_scores(qkv_rows, bias, allowed, factor)
        row_peak = jnp.max(scores, axis=-1, keepdims=True)
        exp_scores = jnp.exp(scores - row_peak)
        row_total = jnp.sum(exp_scores, axis=-1, keepdims=True)
        log_total = row_peak + jnp.log(row_total)
        probs_low = (exp_scores / row_total).astype(jnp.bfloat16)
        attended = jnp.einsum(
            "hqk,khd->qhd", probs_low, qkv_rows[:, 2], preferred_element_type=jnp.float32
        )
        attended = attended.astype(jnp.bfloat16).reshape(SEQ, D)
        branch = jnp.dot(attended, weights[2], preferred_element_type=jnp.float32)
        hidden = x_float + live_col * branch
        normed2 = rms_norm(hidden, gain_m).astype(jnp.bfloat16)
        logits = jnp.dot(normed2, weights[5], preferred_element_type=jnp.float32)
        route_rows = routes[batch * SEQ : (batch + 1) * SEQ]
        slot_rows = slots[batch * SEQ : (batch + 1) * SEQ]
        hot_first = (route_rows[:, 0:1] == expert_ids[None, :]).astype(jnp.float32)
        hot_second = (route_rows[:, 1:2] == expert_ids[None, :]).astype(jnp.float32)
        gate_first = jax.nn.sigmoid(
            jnp.sum(logits * hot_first, axis=-1) - jnp.sum(logits * hot_second, axis=-1)
        )
        row_place = route_rows * capacity + slot_rows
        target = jnp.where(live_keys[:, None], row_place, experts * capacity)
        outgoing = jnp.zeros((experts * capacity, D), jnp.bfloat16)
        outgoing = (
            outgoing.at[target[:, 0]]
            .set(normed2, mode="drop")
            .at[target[:, 1]]
            .set(normed2, mode="drop")
        )
        outgoing = jnp.repeat(outgoing.reshape(experts, capacity, D), 2, axis=0)
        expert_received = lax.all_to_all(outgoing, "fsdp", split_axis=0, concat_axis=0, tiled=True)
        expert_before = jnp.einsum(
            "scd,df->scf", expert_received, up_weight, preferred_element_type=jnp.float32
        )
        expert_active = exact_gelu(expert_before).astype(jnp.bfloat16)
        partial_value = jnp.einsum(
            "scf,fd->scd", expert_active, down_weight, preferred_element_type=jnp.float32
        ).astype(jnp.bfloat16)
        returned = lax.all_to_all(partial_value, "fsdp", split_axis=0, concat_axis=0, tiled=True)
        results = (returned, expert_received, expert_before)
        combined = (
            results[0]
            .astype(jnp.float32)
            .reshape(experts, 2, capacity, D)
            .sum(axis=1)
            .reshape(experts * capacity, D)
        )
        first_out = combined[row_place[:, 0]]
        second_out = combined[row_place[:, 1]]
        moe = live_col * (
            gate_first[:, None] * first_out + (1.0 - gate_first)[:, None] * second_out
        )
        mixed_parts.append((hidden + moe).astype(jnp.bfloat16))
        saved.append(
            {
                "normed": normed,
                "qkv_rows": qkv_rows,
                "log_total": log_total,
                "attended": attended,
                "hidden": hidden,
                "normed2": normed2,
                "gate_first": gate_first,
                "first_out": first_out,
                "second_out": second_out,
                "results": results,
                "target": target,
                "row_place": row_place,
                "hot_first": hot_first,
                "hot_second": hot_second,
            }
        )
    grad_qkv_w = jnp.zeros((D, 3 * D), jnp.float32)
    grad_proj_w = jnp.zeros((D, D), jnp.float32)
    grad_table = jnp.zeros((SEQ, HEADS), jnp.float32)
    grad_gain_a = jnp.zeros((D,), jnp.float32)
    grad_gain_m = jnp.zeros((D,), jnp.float32)
    grad_router = jnp.zeros((D, experts), jnp.float32)
    grad_up = jnp.zeros((D, FF // 2), jnp.float32)
    grad_down = jnp.zeros((FF // 2, D), jnp.float32)
    grad_parts = [None] * MB
    for batch in reversed(range(MB)):
        kept = saved[batch]
        x_float = tokens[batch * SEQ : (batch + 1) * SEQ].astype(jnp.float32)
        live_keys = places < lengths[batch]
        live_col = live_keys.astype(jnp.float32)[:, None]
        allowed = causal & live_keys[None, :]
        grad_out = cotangent[batch * SEQ : (batch + 1) * SEQ].astype(jnp.float32)
        grad_moe = live_col * grad_out
        gate_first = kept["gate_first"]
        gate_second = 1.0 - gate_first
        grad_gate_first = jnp.sum(grad_moe * kept["first_out"], axis=-1)
        grad_gate_second = jnp.sum(grad_moe * kept["second_out"], axis=-1)
        grad_first = (gate_first[:, None] * grad_moe).astype(jnp.bfloat16)
        grad_second = (gate_second[:, None] * grad_moe).astype(jnp.bfloat16)
        target = kept["target"]
        grad_send = jnp.zeros((experts * capacity, D), jnp.bfloat16)
        grad_send = (
            grad_send.at[target[:, 0]]
            .set(grad_first, mode="drop")
            .at[target[:, 1]]
            .set(grad_second, mode="drop")
        )
        grad_send = jnp.repeat(grad_send.reshape(experts, capacity, D), 2, axis=0)
        grad_recv = lax.all_to_all(grad_send, "fsdp", split_axis=0, concat_axis=0, tiled=True)
        received = kept["results"][1]
        before = kept["results"][2]
        active, gelu_back = jax.vjp(exact_gelu, before)
        active_low = active.astype(jnp.bfloat16)
        grad_active = jnp.einsum(
            "scd,fd->scf", grad_recv, down_weight, preferred_element_type=jnp.float32
        )
        grad_before = gelu_back(grad_active)[0].astype(jnp.bfloat16)
        grad_down = grad_down + jnp.einsum(
            "scf,scd->fd", active_low, grad_recv, preferred_element_type=jnp.float32
        )
        grad_up = grad_up + jnp.einsum(
            "scd,scf->df", received, grad_before, preferred_element_type=jnp.float32
        )
        grad_part = jnp.einsum(
            "scf,df->scd", grad_before, up_weight, preferred_element_type=jnp.float32
        ).astype(jnp.bfloat16)
        grad_back = lax.all_to_all(grad_part, "fsdp", split_axis=0, concat_axis=0, tiled=True)
        grad_rows = (
            grad_back.astype(jnp.float32)
            .reshape(experts, 2, capacity, D)
            .sum(axis=1)
            .reshape(experts * capacity, D)
        )
        row_place = kept["row_place"]
        grad_diff = (grad_gate_first - grad_gate_second) * gate_first * gate_second
        grad_logits = grad_diff[:, None] * (kept["hot_first"] - kept["hot_second"])
        normed2_float = kept["normed2"].astype(jnp.float32)
        grad_router = grad_router + jnp.dot(normed2_float.T, grad_logits, precision=exact_precision)
        grad_normed2 = live_col * (grad_rows[row_place[:, 0]] + grad_rows[row_place[:, 1]])
        grad_normed2 = grad_normed2 + jnp.dot(
            grad_logits, router_float.T, precision=exact_precision
        )
        _, norm_back_moe = jax.vjp(rms_norm, kept["hidden"], gain_m)
        grad_hidden_norm, grad_gain_part = norm_back_moe(grad_normed2)
        grad_gain_m = grad_gain_m + grad_gain_part
        grad_hidden = grad_out + grad_hidden_norm
        grad_branch = (live_col * grad_hidden).astype(jnp.bfloat16)
        grad_proj_w = grad_proj_w + jnp.einsum(
            "sd,se->de", kept["attended"], grad_branch, preferred_element_type=jnp.float32
        )
        grad_attended = jnp.einsum(
            "se,de->sd", grad_branch, weights[2], preferred_element_type=jnp.float32
        )
        grad_attended = grad_attended.astype(jnp.bfloat16).reshape(SEQ, HEADS, HEAD)
        qkv_rows = kept["qkv_rows"]
        scores = masked_scores(qkv_rows, bias, allowed, factor)
        probs = jnp.exp(scores - kept["log_total"])
        probs_low = probs.astype(jnp.bfloat16)
        grad_probs = jnp.einsum(
            "qhd,khd->hqk", grad_attended, qkv_rows[:, 2], preferred_element_type=jnp.float32
        )
        row_dot = jnp.sum(probs * grad_probs, axis=-1, keepdims=True)
        grad_scores = (probs * (grad_probs - row_dot)).astype(jnp.bfloat16)
        grad_table = grad_table + jnp.einsum(
            "dp,hp->dh",
            hot,
            jnp.where(allowed[None], grad_scores, 0).reshape(HEADS, SEQ * SEQ),
            preferred_element_type=jnp.float32,
        )
        grad_queries = (
            jnp.einsum(
                "hqk,khd->qhd", grad_scores, qkv_rows[:, 1], preferred_element_type=jnp.float32
            )
            * factor
        )
        grad_keys = (
            jnp.einsum(
                "hqk,qhd->khd", grad_scores, qkv_rows[:, 0], preferred_element_type=jnp.float32
            )
            * factor
        )
        grad_values = jnp.einsum(
            "hqk,qhd->khd", probs_low, grad_attended, preferred_element_type=jnp.float32
        )
        grad_qkv = (
            jnp.stack([grad_queries, grad_keys, grad_values], axis=1)
            .astype(jnp.bfloat16)
            .reshape(SEQ, 3 * D)
        )
        grad_qkv_w = grad_qkv_w + jnp.einsum(
            "sd,se->de", kept["normed"], grad_qkv, preferred_element_type=jnp.float32
        )
        grad_normed = jnp.einsum(
            "se,de->sd", grad_qkv, weights[1], preferred_element_type=jnp.float32
        )
        _, norm_back_attn = jax.vjp(rms_norm, x_float, gain_a)
        grad_x_norm, grad_gain_piece = norm_back_attn(grad_normed)
        grad_gain_a = grad_gain_a + grad_gain_piece
        grad_parts[batch] = grad_hidden + grad_x_norm
    small = jnp.concatenate(
        [
            grad_gain_a.reshape(groups, -1),
            grad_gain_m.reshape(groups, -1),
            grad_router.reshape(groups, -1),
            grad_table.reshape(groups, -1),
        ],
        axis=1,
    )
    small = lax.psum_scatter(small, "fsdp", scatter_dimension=0, tiled=True)
    shards = (
        small,
        lax.psum_scatter(grad_qkv_w, "fsdp", scatter_dimension=0, tiled=True),
        lax.psum_scatter(grad_proj_w, "fsdp", scatter_dimension=0, tiled=True),
    )
    sums = lax.psum((shards[0], shards[1], shards[2], grad_up[None], grad_down[None]), "replica")
    rows = D // groups
    edge = 2 * rows + rows * experts
    totals = (
        sums[0][0, :rows],
        sums[1],
        sums[2],
        sums[0][0, edge:].reshape(SEQ // groups, HEADS),
        sums[0][0, rows : 2 * rows],
        sums[0][0, 2 * rows : edge].reshape(rows, experts),
        sums[3],
        sums[4],
    )
    mixed = jnp.concatenate(mixed_parts, axis=0)
    grad_tokens = jnp.concatenate(grad_parts, axis=0)
    return (
        mixed,
        grad_tokens,
        totals[0],
        totals[1],
        totals[2],
        totals[3],
        totals[4],
        totals[5],
        totals[6],
        totals[7],
    )


def solution(mesh):
    in_specs = (
        P(("replica", "fsdp"), None),
        P(("replica", "fsdp"), None),
        P(("replica", "fsdp")),
        P(("replica", "fsdp"), None),
        P(("replica", "fsdp"), None),
        P("fsdp"),
        P("fsdp", None),
        P("fsdp", None),
        P("fsdp", None),
        P("fsdp"),
        P("fsdp", None),
        P("fsdp", None, None),
        P("fsdp", None, None),
    )
    out_specs = (
        P(("replica", "fsdp"), None),
        P(("replica", "fsdp"), None),
        P("fsdp"),
        P("fsdp", None),
        P("fsdp", None),
        P("fsdp", None),
        P("fsdp"),
        P("fsdp", None),
        P("fsdp", None, None),
        P("fsdp", None, None),
    )
    fast = dict(mesh.shape) == {"replica": 4, "fsdp": 8}
    return jax.shard_map(body_fast if fast else body, mesh=mesh, in_specs=in_specs, out_specs=out_specs, check_vma=False)
```

```python
import functools

import jax
import jax.numpy as jnp
from jax import lax
from jax.experimental import pallas as pl
from jax.experimental.pallas import tpu as pltpu
from jax.sharding import PartitionSpec as P

D = 768
HEADS = 12
HEAD = 64
FF = 3072
SEQ = 128
MB = 2
MESH = pl.DeviceIdType.MESH
F32 = jnp.float32
BF16 = jnp.bfloat16
NEG = -1e30
HF = FF // 2
TOK = MB * SEQ
EXP = 4
CAP = 64
ROWS = MB * CAP
LOW = 896
MID = 3 * D - 2 * LOW
MORE = MID + 128
SMALL = LOW + MID
PROJ = LOW + MORE
HIGH = PROJ + D
WALL = HIGH + LOW
LEFTC = LOW + MID
SHARD = 96
HALF = SHARD // 2
PAIRS = HEADS // 2
SCALE = HEAD ** (-0.5)


def place():
    replica = lax.axis_index("replica")
    group = lax.axis_index("fsdp")
    return replica // 2, replica % 2, group // 2, group % 2


def device(x, c, z, y):
    return (x * 2 + c, z * 2 + y)


def remote(src, dst, send, recv, target):
    return pltpu.make_async_remote_copy(
        src_ref=src,
        dst_ref=dst,
        send_sem=send,
        recv_sem=recv,
        device_id=target,
        device_id_type=MESH,
    )


def greet():
    x, c, z, y = place()
    barrier = pltpu.get_barrier_semaphore()
    targets = [device(x, 1 - c, z, y), device(1 - x, c, z, y), device(x, c, z, 1 - y)]
    targets += [device(x, c, (z + k) % 4, y) for k in (1, 2, 3)]
    for target in targets:
        pl.semaphore_signal(barrier, inc=1, device_id=target, device_id_type=MESH)
    pl.semaphore_wait(barrier, len(targets))


def dot(a, b, ca=1, cb=0):
    return lax.dot_general(a, b, (((ca,), (cb,)), ((), ())), preferred_element_type=F32)


def run(cond, what):
    if cond is None:
        what()
    else:
        pl.when(cond)(what)


class Links:
    def __init__(self, send_sem, recv_sem):
        self.send_sem, self.recv_sem = send_sem, recv_sem
        self.started = []

    def go(self, cond, src, dst, send, recv, target):
        copy = remote(src, dst, self.send_sem.at[send], self.recv_sem.at[recv], target)
        run(cond, copy.start)
        self.started.append((cond, copy))
        return copy

    def arrive(self, cond, dst, recv, target):
        run(cond, remote(dst, dst, self.send_sem.at[0], self.recv_sem.at[recv], target).wait_recv)

    def leave(self, copy):
        copy.wait_send()
        self.started = [(cond, item) for cond, item in self.started if item is not copy]

    def finish(self):
        for cond, copy in self.started:
            run(cond, copy.wait_send)
        self.started = []


def gather_weights(links, wq, wp, sm, wall, local_sem):
    x, c, z, y = place()
    own = pl.ds(pl.multiple_of((z * 2 + y) * SHARD, 16), SHARD)
    fills = [
        pltpu.make_async_copy(wq.at[:, pl.ds(0, LEFTC)], wall.at[own, pl.ds(0, LEFTC)], local_sem.at[0]),
        pltpu.make_async_copy(wq.at[:, pl.ds(LEFTC, LOW)], wall.at[own, pl.ds(HIGH, LOW)], local_sem.at[1]),
        pltpu.make_async_copy(wp, wall.at[own, pl.ds(PROJ, D)], local_sem.at[2]),
        pltpu.make_async_copy(sm, wall.at[own, pl.ds(SMALL, 128)], local_sem.at[3]),
    ]
    for fill in fills:
        fill.start()
    share = pl.ds(pl.multiple_of(x * HIGH, 128), LOW)
    gained = pl.ds(pl.multiple_of((1 - x) * HIGH, 128), LOW)
    columns = (share, pl.ds(LOW, MORE), pl.ds(PROJ, D))
    up, down = device(x, c, z + 1, y), device(x, c, z - 1, y)
    across, facing, twin = device(x, c, z, 1 - y), device(1 - x, c, z, y), device(x, 1 - c, z, y)

    def part(zs, ys, half, cols):
        return wall.at[pl.ds(pl.multiple_of((zs * 2 + ys) * SHARD + half * HALF, 16), HALF), cols]

    def go(cond, zs, ys, cols, send, recv, target, src=None):
        piece = part(zs, ys, c, cols)
        links.go(cond, piece if src is None else src, piece, send, recv, target)

    def arrive(cond, zs, ys, half, cols, recv):
        links.arrive(cond, part(zs, ys, half, cols), recv, twin)

    def spread(cond, sub, zs, ys):
        source = zs * 2 + ys
        if sub == 0:
            go(cond, zs, ys, share, 39 + source, 24 + source, facing)
        go(cond, zs, ys, columns[sub], 47 + sub * 8 + source, 32 + sub * 8 + source, twin)

    def begin(sub, src):
        go(z < 3, z, y, columns[sub], sub * 3, sub * 4 + z, up, src)
        go(z > 0, z, y, columns[sub], 9 + sub * 3, sub * 4 + z, down, src)
        go(None, z, y, columns[sub], 18 + sub * 7, 12 + sub * 4 + z, across, src)

    def along(sub, k):
        below, above = z - k, z + k
        for cond, zs, on, first, target, place_of in (
            (below >= 0, below, z < 3, 0, up, k),
            (above <= 3, above, z > 0, 9, down, 3 + k),
        ):
            arrive(cond, zs, y, c, columns[sub], sub * 4 + zs)
            if k < 3:
                go(cond & on, zs, y, columns[sub], first + sub * 3 + k, sub * 4 + zs, target)
            go(cond, zs, y, columns[sub], 18 + sub * 7 + place_of, 12 + sub * 4 + zs, across)
            spread(cond, sub, zs, y)

    def over(sub, k):
        if k == 0:
            arrive(None, z, 1 - y, c, columns[sub], 12 + sub * 4 + z)
            spread(None, sub, z, 1 - y)
            return
        for cond, zs in ((z - k >= 0, z - k), (z + k <= 3, z + k)):
            arrive(cond, zs, 1 - y, c, columns[sub], 12 + sub * 4 + zs)
            spread(cond, sub, zs, 1 - y)

    half = pl.ds(pl.multiple_of(c * HALF, 16), HALF)
    begin(0, wq.at[half, pl.ds(pl.multiple_of(x * LEFTC, 128), LOW)])
    for fill in fills:
        fill.wait()
    begin(1, None)
    begin(2, wp.at[half, :])
    for k in (1, 2, 3):
        for sub in range(3):
            along(sub, k)
            if k > 1 or sub < 2:
                over(sub, k - 1)
        if k == 1:
            over(2, 0)
    for sub in range(2):
        over(sub, 3)

    def each(what):
        for zs in range(4):
            for ys in range(2):
                what((zs != z) | (ys != y), zs, ys, zs * 2 + ys)

    def gain(other, zs, ys, source):
        arrive(other, zs, ys, c, gained, 24 + source)
        go(other, zs, ys, gained, 71 + source, 56 + source, twin)

    def mostly(other, zs, ys, source):
        for sub in range(2):
            arrive(other, zs, ys, 1 - c, columns[sub], 32 + sub * 8 + source)
        arrive(other, zs, ys, 1 - c, gained, 56 + source)

    def rest(other, zs, ys, source):
        arrive(other, zs, ys, 1 - c, columns[2], 32 + 16 + source)

    each(gain)
    each(mostly)

    def later():
        over(2, 3)
        each(rest)

    return later


def unit(values):
    return lax.rsqrt(jnp.mean(values * values, axis=-1, keepdims=True) + 1e-06)


def build_bias(wall, bias):
    table = jnp.concatenate(
        [wall[f * SHARD : f * SHARD + 16, SMALL : SMALL + 128] for f in range(8)], axis=0
    )
    ahead = lax.broadcasted_iota(jnp.int32, (SEQ, SEQ), 0)
    lane = lax.broadcasted_iota(jnp.int32, (SEQ, SEQ), 1)
    turned = jnp.where(ahead + lane == SEQ, 1.0, jnp.where(ahead + lane == 0, 1.0, 0.0)).astype(BF16)
    lines = dot(table, turned, 0, 0)
    for h in range(HEADS):
        line = jnp.broadcast_to(lines[HEAD + h : HEAD + h + 1, :], (SEQ, SEQ))
        rolled = pltpu.roll(line, 0, 1, stride=1, stride_axis=0)
        bias[(h // 2) * SEQ : (h // 2 + 1) * SEQ, (h % 2) * SEQ : (h % 2 + 1) * SEQ] = jnp.where(ahead >= lane, rolled, NEG)


def stand(routes, slots, lines, columns):
    chosen = routes[...]
    lines[...] = jnp.zeros_like(lines)
    lines[0:2, :] = (chosen * CAP + slots[...]).astype(F32)
    lines[2:4, :] = chosen.astype(F32)
    columns[...] = jnp.transpose(lines[...])


def routing(columns, s):
    spots = columns[s * SEQ : (s + 1) * SEQ, :]
    lane = lax.broadcasted_iota(jnp.int32, (SEQ, EXP * CAP), 1).astype(F32)
    return spots[:, 0:1] == lane, spots[:, 1:2] == lane


def named(columns, s):
    spots = columns[s * SEQ : (s + 1) * SEQ, :]
    lane = lax.broadcasted_iota(jnp.int32, (SEQ, 128), 1).astype(F32) - 2.0
    return spots[:, 2:3] == lane, spots[:, 3:4] == lane


def live_column(lengths, s):
    return lax.broadcasted_iota(jnp.int32, (SEQ, 1), 0) < lengths[s]


def attention_forward(
    later, x_ref, cot, lengths, columns, wall, rows_t, board, normed, qkv, attended, hidden, normed2, gates, out_f, out_g
):
    rows_t[...] = jnp.transpose(wall[:, SMALL : SMALL + 128].astype(F32))[0:8]
    build_bias(wall, board)
    x = x_ref[...].astype(F32)
    normed[...] = (x * unit(x) * rows_t[0:1, :]).astype(BF16)
    qkv[:, 0:LEFTC] = dot(normed[...], wall[:, 0:LEFTC]).astype(BF16)
    qkv[:, LEFTC : 3 * D] = dot(normed[...], wall[:, HIGH:WALL]).astype(BF16)
    lane = lax.broadcasted_iota(jnp.int32, (SEQ, 128), 1)

    def pair(p, carry):
        blocks = pl.ds(pl.multiple_of(p * SEQ, SEQ), SEQ)
        for s in range(MB):
            rows = slice(s * SEQ, (s + 1) * SEQ)
            q = qkv[rows, pl.ds(pl.multiple_of(p * 128, 128), 128)]
            k = qkv[rows, pl.ds(pl.multiple_of(D + p * 128, 128), 128)]
            v = qkv[rows, pl.ds(pl.multiple_of(2 * D + p * 128, 128), 128)]
            alive = lane < lengths[s]
            got = []
            for j in range(2):
                mine = (lane < HEAD) if j == 0 else (lane >= HEAD)
                raw = dot(jnp.where(mine, q, jnp.zeros_like(q)), k, 1, 1)
                scores = jnp.where(alive, raw * SCALE + board[blocks, j * SEQ : (j + 1) * SEQ], NEG)
                scores = jnp.exp(scores - jnp.max(scores, axis=-1, keepdims=True))
                share = scores * (1.0 / jnp.sum(scores, axis=-1, keepdims=True))
                board[blocks, (2 + 2 * s + j) * SEQ : (3 + 2 * s + j) * SEQ] = share
                got.append(dot(share.astype(BF16), v))
            attended[rows, pl.ds(pl.multiple_of(p * 128, 128), 128)] = jnp.where(
                lane < HEAD, got[0], got[1]
            ).astype(BF16)
        return carry

    lax.fori_loop(0, PAIRS, pair, 0)
    later()
    branch = dot(attended[...], wall[:, PROJ:HIGH])
    for s in range(MB):
        rows = slice(s * SEQ, (s + 1) * SEQ)
        live = live_column(lengths, s)
        state = x_ref[rows, :].astype(F32) + jnp.where(live, branch[rows, :], 0.0)
        hidden[rows, :] = state
        low = (state * unit(state) * rows_t[1:2, :]).astype(BF16)
        normed2[rows, :] = low
        logits = dot(low, wall[:, SMALL : SMALL + 128])
        one, two = named(columns, s)
        picked = jnp.where(one, logits, 0.0) - jnp.where(two, logits, 0.0)
        gate = jax.nn.sigmoid(jnp.sum(picked, axis=-1, keepdims=True))
        gates[rows, :] = gate
        grad = jnp.where(live, cot[rows, :].astype(F32), 0.0)
        first, second = routing(columns, s)
        first = jnp.where(first & live, 1.0, 0.0).astype(BF16)
        second = jnp.where(second & live, 1.0, 0.0).astype(BF16)
        sent = dot(first + second, low, 0, 0).astype(BF16)
        back = dot(first, (gate * grad).astype(BF16), 0, 0) + dot(
            second, ((1.0 - gate) * grad).astype(BF16), 0, 0
        )
        back = back.astype(BF16)
        for e in range(EXP):
            out_f[e, s * CAP : (s + 1) * CAP, :] = sent[e * CAP : (e + 1) * CAP, :]
            out_g[e, s * CAP : (s + 1) * CAP, :] = back[e * CAP : (e + 1) * CAP, :]


TILE = 512
Z_ROWS, Y_ROWS, Y_PART, Z_BACK = 80, 88, 96, 104
TWIN_W, FACE_W, TWIN_OUT = 112, 114, 120
RS_TWIN, RS_Y, RS_Z, RS_FACE, RS_OUT = 126, 130, 146, 178, 182
LINKS = 186


def quarter(zs):
    return pl.ds(pl.multiple_of(zs * 2 * ROWS, 2 * ROWS), 2 * ROWS)


def half_rows(zs, ys):
    return pl.ds(pl.multiple_of((zs * 2 + ys) * ROWS, ROWS), ROWS)


def expert_forward(zs, recv, up, down, act, slope, part):
    rows = quarter(zs)

    def tile(i, carry):
        cols = pl.ds(pl.multiple_of(i * TILE, TILE), TILE)
        before = dot(recv[rows, :], up[:, cols])
        below = 0.5 + 0.5 * lax.erf(before * 0.7071067811865476)
        act[rows, cols] = (before * below).astype(BF16)
        density = jnp.exp(before * before * -0.5) * 0.3989422804014327
        slope[rows, cols] = (below + before * density).astype(BF16)
        return carry

    lax.fori_loop(0, HF // TILE, tile, 0)
    got = dot(act[rows, 0:HF], down[...]).astype(BF16)
    part[zs, 0] = got[0:ROWS]
    part[zs, 1] = got[ROWS : 2 * ROWS]


def expert_backward(zs, recv, up, down, slope, part):
    rows = quarter(zs)

    def tile(i, carry):
        cols = pl.ds(pl.multiple_of(i * TILE, TILE), TILE)
        grad = dot(recv[rows, :], down[cols, :], 1, 1)
        slope[rows, cols] = (grad * slope[rows, cols].astype(F32)).astype(BF16)
        return carry

    lax.fori_loop(0, HF // TILE, tile, 0)
    got = dot(slope[rows, :], up[...], 1, 1).astype(BF16)
    part[zs, 0] = got[0:ROWS]
    part[zs, 1] = got[ROWS : 2 * ROWS]


def experts(links, out, recv, up, down, act, slope, part, take, back, w_down, w_up):
    x, c, z, y = place()
    across, facing, twin = device(x, c, z, 1 - y), device(1 - x, c, z, y), device(x, 1 - c, z, y)

    for kind in range(2):
        links.go(None, out[kind].at[z], recv[kind].at[half_rows(z, y), :], Y_ROWS + kind * 4, Y_ROWS + kind * 4 + z, across)
        for d in (1, 2, 3):
            to = (z + d) % 4
            links.go(
                None, out[kind].at[to], recv[kind].at[half_rows(z, y), :], Z_ROWS + kind * 4 + d,
                Z_ROWS + kind * 4 + z, device(x, c, to, y),
            )
        recv[kind][half_rows(z, y), :] = out[kind][z]

    def source(d):
        return (z + 4 - d) % 4

    def reach(kind, d):
        zs = source(d)
        rows = recv[kind].at[half_rows(zs, y), :]
        links.arrive(None, rows, Z_ROWS + kind * 4 + zs, across)
        links.go(None, rows, rows, Y_ROWS + kind * 4 + d, Y_ROWS + kind * 4 + zs, across)

    def compute(kind, d):
        zs = source(d)
        links.arrive(None, recv[kind].at[half_rows(zs, 1 - y), :], Y_ROWS + kind * 4 + zs, across)
        if kind == 0:
            expert_forward(zs, recv[0], up, down, act, slope, part[0])
        else:
            expert_backward(zs, recv[1], up, down, slope, part[1])

    def give_part(kind, d):
        zs = source(d)
        links.go(
            None, part[kind].at[zs, 1 - y], take[kind].at[zs], Y_PART + kind * 4 + d, Y_PART + kind * 4 + zs, across
        )

    def merge(kind, d):
        zs = source(d)
        links.arrive(None, take[kind].at[zs], Y_PART + kind * 4 + zs, across)
        total = (part[kind][zs, y].astype(F32) + take[kind][zs].astype(F32)).astype(BF16)
        if d == 0:
            back[kind][z] = total
        else:
            part[kind][zs, y] = total
            links.go(
                None, part[kind].at[zs, y], back[kind].at[z], Z_BACK + kind * 4 + d, Z_BACK + kind * 4 + z,
                device(x, c, zs, y),
            )

    reach(0, 1)
    compute(0, 0)
    reach(0, 2)
    compute(1, 0)
    reach(0, 3)
    compute(0, 1)
    reach(1, 1)
    give_part(0, 1)
    compute(0, 2)
    reach(1, 2)
    give_part(0, 2)
    compute(1, 1)
    reach(1, 3)
    give_part(1, 1)
    merge(0, 1)
    compute(0, 3)
    give_part(0, 3)
    merge(0, 2)
    compute(1, 2)
    give_part(1, 2)
    merge(1, 1)
    compute(1, 3)
    give_part(1, 3)
    give_part(0, 0)
    give_part(1, 0)

    def down_tile(i, part_of, keep):
        cols = pl.ds(pl.multiple_of(part_of * (HF // 2) + i * 256, 128), 256)
        got = dot(act[:, cols], recv[1][...], 0, 0)
        keep[pl.ds(pl.multiple_of(i * 256, 256), 256), :] = got.astype(keep.dtype)

    def up_tile(i, part_of, keep):
        cols = pl.ds(pl.multiple_of(part_of * (D // 2) + i * 128, 128), 128)
        got = dot(recv[0][:, cols], slope[...], 0, 0)
        keep[pl.ds(pl.multiple_of(i * 128, 128), 128), :] = got.astype(keep.dtype)

    def tiles(one, part_of, keep):
        def step(i, carry):
            one(i, part_of, keep)
            return carry

        lax.fori_loop(0, 3, step, 0)

    pairs = ((0, 3), (1, 2), (1, 3))
    for i, (one, w) in enumerate(((down_tile, w_down), (up_tile, w_up))):
        own, give, got, face = w
        tiles(one, 1 - c, give)
        sent = links.go(None, give, got, TWIN_W + i, TWIN_W + i, twin)
        tiles(one, c, own)
        links.arrive(None, got, TWIN_W + i, twin)
        links.leave(sent)
        count = own.shape[0] // 3
        for m in range(3):
            rows = slice(m * count, (m + 1) * count)
            give[rows, :] = (own[rows, :] + got[rows, :].astype(F32)).astype(BF16)
            links.go(None, give.at[rows, :], face.at[rows, :], FACE_W + i * 3 + m, FACE_W + i * 3 + m, facing)
        merge(*pairs[i])
    merge(*pairs[2])
    merge(0, 0)
    merge(1, 0)
    for kind in range(2):
        for d in (1, 2, 3):
            zs = source(d)
            links.arrive(None, back[kind].at[zs], Z_BACK + kind * 4 + zs, across)


def expert_grad_out(links, piece, w_down, w_up, out_down, out_up, local_sem):
    x, c, z, y = place()
    facing, twin = device(1 - x, c, z, y), device(x, 1 - c, z, y)
    (own, give, got, face), target = ((w_down, out_down), (w_up, out_up))[piece // 3]
    count = own.shape[0] // 3
    rows = slice((piece % 3) * count, (piece % 3 + 1) * count)
    links.arrive(None, face.at[rows, :], FACE_W + piece, facing)
    face[rows, :] = (give[rows, :].astype(F32) + face[rows, :].astype(F32)).astype(BF16)
    there = target.at[pl.ds(pl.multiple_of((c * 3 + piece % 3) * count, 128), count), :]
    links.go(None, face.at[rows, :], there, TWIN_OUT + piece, TWIN_OUT + piece, twin)
    copy = pltpu.make_async_copy(face.at[rows, :], there, local_sem.at[8 + piece])
    copy.start()
    return copy


def expert_grads_arrive(links, out_down, out_up):
    x, c, z, y = place()
    for piece in range(6):
        target = (out_down, out_up)[piece // 3]
        count = target.shape[0] // 6
        there = target.at[pl.ds(pl.multiple_of(((1 - c) * 3 + piece % 3) * count, 128), count), :]
        links.arrive(None, there, TWIN_OUT + piece, device(x, 1 - c, z, y))


SENTC = 2 * D + 128


def combine(cot, lengths, columns, rows_t, hidden, normed2, gates, back_f, back_g, mixed, rb, small_t):
    gain_grad = jnp.zeros((1, D), F32)
    router_grad = jnp.zeros((128, D), F32)
    for s in range(MB):
        rows = slice(s * SEQ, (s + 1) * SEQ)
        live = live_column(lengths, s)
        first, second = routing(columns, s)
        first = jnp.where(first, 1.0, 0.0).astype(BF16)
        second = jnp.where(second, 1.0, 0.0).astype(BF16)
        given = jnp.concatenate([back_f[e, s * CAP : (s + 1) * CAP, :] for e in range(EXP)], axis=0)
        first_out = dot(first, given)
        second_out = dot(second, given)
        gate = gates[rows, :]
        grad = cot[rows, :].astype(F32)
        grad_live = jnp.where(live, grad, 0.0)
        state = hidden[rows, :]
        moe = gate * first_out + (1.0 - gate) * second_out
        mixed[rows, :] = (state + jnp.where(live, moe, 0.0)).astype(BF16)
        tilt = jnp.sum(grad_live * first_out, axis=-1, keepdims=True) - jnp.sum(
            grad_live * second_out, axis=-1, keepdims=True
        )
        tilt = tilt * gate * (1.0 - gate)
        one, two = named(columns, s)
        hot = jnp.where(one, 1.0, 0.0) - jnp.where(two, 1.0, 0.0)
        grad_logits = tilt * hot
        high = grad_logits.astype(BF16)
        low = (grad_logits - high.astype(F32)).astype(BF16)
        router_grad = router_grad + dot(high, normed2[rows, :], 0, 0) + dot(low, normed2[rows, :], 0, 0)
        given = jnp.concatenate([back_g[e, s * CAP : (s + 1) * CAP, :] for e in range(EXP)], axis=0)
        grad_low = jnp.where(live, dot(first + second, given), 0.0)
        for e in range(EXP):
            grad_low = grad_low + grad_logits[:, 2 + e : 3 + e] * rows_t[2 + e : 3 + e, :]
        factor = unit(state)
        scaled = state * factor
        gain_grad = gain_grad + jnp.sum(grad_low * scaled, axis=0, keepdims=True)
        grad_low = grad_low * rows_t[1:2, :]
        inner = jnp.mean(grad_low * scaled, axis=-1, keepdims=True)
        grad_state = grad + factor * (grad_low - scaled * inner)
        hidden[rows, :] = grad_state
        rb[rows, 3 * D : 4 * D] = jnp.where(live, grad_state, 0.0).astype(BF16)
    small_t[...] = router_grad
    small_t[1:2, :] = gain_grad


def attention_backward(x_ref, wall, rows_t, qkv, board, hidden, grad_att, rb, rel_rows, small_t, grad_tokens, midway):
    grad_att[...] = dot(rb[:, 3 * D : 4 * D], wall[:, PROJ:HIGH], 1, 1).astype(BF16)
    midway()
    lane = lax.broadcasted_iota(jnp.int32, (SEQ, 128), 1)
    ahead = lax.broadcasted_iota(jnp.int32, (SEQ, 128), 0)
    flip = jnp.where(ahead + lane == SEQ - 1, 1.0, 0.0).astype(BF16)
    flip = jnp.concatenate([flip] * MB, axis=1)

    def pair(p, carry):
        blocks = pl.ds(pl.multiple_of(p * SEQ, SEQ), SEQ)
        scores = [[None] * MB, [None] * MB]
        for s in range(MB):
            rows = slice(s * SEQ, (s + 1) * SEQ)
            cols = [pl.ds(pl.multiple_of(i * D + p * 128, 128), 128) for i in range(3)]
            q, k, v = (qkv[rows, cols[i]] for i in range(3))
            grad = grad_att[rows, cols[0]]
            grads = [[], [], []]
            for j in range(2):
                mine = (lane < HEAD) if j == 0 else (lane >= HEAD)
                share = board[blocks, (2 + 2 * s + j) * SEQ : (3 + 2 * s + j) * SEQ]
                grad_probs = dot(jnp.where(mine, grad, jnp.zeros_like(grad)), v, 1, 1)
                inner = jnp.sum(share * grad_probs, axis=-1, keepdims=True)
                grad_scores = (share * (grad_probs - inner)).astype(BF16)
                scores[j][s] = grad_scores
                grads[0].append(dot(grad_scores, k) * SCALE)
                grads[1].append(dot(grad_scores, q, 0, 0) * SCALE)
                grads[2].append(dot(share.astype(BF16), grad, 0, 0))
            for i in range(3):
                rb[rows, cols[i]] = jnp.where(lane < HEAD, grads[i][0], grads[i][1]).astype(BF16)
        for j in range(2):
            flipped = dot(flip, jnp.concatenate(scores[j], axis=0))
            rolled = pltpu.roll(flipped, 1, 1, stride=1, stride_axis=0)
            rel_rows[pl.ds(2 * p + j, 1), :] = jnp.sum(rolled, axis=0, keepdims=True)
        return carry

    lax.fori_loop(0, PAIRS, pair, 0)
    grad_low = dot(rb[:, 0:LEFTC], wall[:, 0:LEFTC], 1, 1) + dot(
        rb[:, LEFTC : 3 * D], wall[:, HIGH:WALL], 1, 1
    )
    state = x_ref[...].astype(F32)
    factor = unit(state)
    scaled = state * factor
    small_t[0:1, :] = jnp.sum(grad_low * scaled, axis=0, keepdims=True)
    grad_low = grad_low * rows_t[0:1, :]
    inner = jnp.mean(grad_low * scaled, axis=-1, keepdims=True)
    grad_tokens[...] = hidden[...] + factor * (grad_low - scaled * inner)

    spot = lax.broadcasted_iota(jnp.int32, (SEQ, D), 0)
    column = lax.broadcasted_iota(jnp.int32, (SEQ, D), 1)
    distance = (SEQ - spot) & (SEQ - 1)
    picks = jnp.where(column == (distance >> 4) * SHARD + (distance & 15), 1.0, 0.0).astype(BF16)
    rest = rel_rows[...]
    spread = jnp.zeros((16, D), F32)
    for _ in range(3):
        high = rest.astype(BF16)
        spread = spread + dot(high, picks)
        rest = rest - high.astype(F32)
    small_t[HEAD : HEAD + 16, :] = spread


HC = D // 2
GROUPS = (
    (1, 2 * HC, HC, lambda core: 3 * D + core * HC, lambda core: core * HC),
    (0, HC, HC, lambda core: 2 * D + core * HC, lambda core: 2 * D + core * HC),
    (0, 0, HC, lambda core: core * D, lambda core: core * D),
    (0, 3 * HC, HC + 128, lambda core: core * D + HC, lambda core: core * D + HC),
)


class Reduction:
    def __init__(self, links, group, left, rb, small_t, give, take, total, y_take, z_take, face_give, face_take, last):
        self.links, self.group = links, group
        which, first, self.width, self.rhs, self.target = GROUPS[group]
        self.cols = slice(first, first + self.width)
        self.core_cols = slice(first, first + HC)
        self.small_cols = slice(first + HC, first + self.width)
        self.lhs, self.rb, self.small_t = left.at[which], rb, small_t
        self.give, self.take, self.total = give, take, total
        self.y_take, self.z_take, self.face_give, self.face_take, self.last = y_take, z_take, face_give, face_take, last
        x, c, z, y = self.place = place()
        self.across, self.facing, self.twin = device(x, c, z, 1 - y), device(1 - x, c, z, y), device(x, 1 - c, z, y)
        mirror = z // 2
        near = z + mirror * (3 - 2 * z)
        self.order = [o + mirror * (3 - 2 * o) for o in (3, 2, 1 - near, near)]

    def tile(self, core, keep):
        def step(m, carry):
            rows = pl.ds(pl.multiple_of(m * 256, 256), 256)
            rhs = self.rb[:, pl.ds(pl.multiple_of(self.rhs(core), 128), HC)]
            keep[rows, self.core_cols] = dot(self.lhs[:, rows], rhs, 0, 0).astype(keep.dtype)
            return carry

        lax.fori_loop(0, 3, step, 0)

    def form(self):
        x, c, z, y = self.place
        self.tile(1 - c, self.give)
        if self.group == 3:
            small = jnp.transpose(self.small_t[...]).astype(BF16)
            self.give[:, self.small_cols] = small
            self.total[:, self.small_cols] = small.astype(F32)
        slot = RS_TWIN + self.group
        self.sent = self.links.go(None, self.give.at[:, self.cols], self.take.at[:, self.cols], slot, slot, self.twin)
        self.tile(c, self.total)

    def shard(self, zs, ys):
        return pl.ds(pl.multiple_of((zs * 2 + ys) * SHARD, 16), SHARD)

    def halve(self):
        x, c, z, y = self.place
        links, cols = self.links, self.cols
        links.arrive(None, self.take.at[:, cols], RS_TWIN + self.group, self.twin)
        links.leave(self.sent)
        for zs in self.order:
            rows = self.shard(zs, 1 - y)
            self.give[rows, cols] = (self.total[rows, cols] + self.take[rows, cols].astype(F32)).astype(BF16)
            slot = RS_Y + self.group * 4 + zs
            links.go(None, self.give.at[rows, cols], self.y_take.at[zs, :, cols], slot, slot, self.across)
        for zs in self.order:
            rows = self.shard(zs, y)
            self.total[rows, cols] = self.total[rows, cols] + self.take[rows, cols].astype(F32)

    def chain(self, k):
        x, c, z, y = self.place
        links, cols, zs = self.links, self.cols, self.order[k]
        total, z_take = self.total, self.z_take
        rows = self.shard(zs, y)
        links.arrive(None, self.y_take.at[zs, :, cols], RS_Y + self.group * 4 + zs, self.across)
        total[rows, cols] = total[rows, cols] + self.y_take[zs, :, cols].astype(F32)
        if k == 3:
            return
        for cond, more, slot, target in (
            (zs > z, z > 0, zs, device(x, c, z + 1, y)),
            (zs < z, z < 3, 4 + zs, device(x, c, z - 1, y)),
        ):
            self.add_from_z(cond & more, slot, rows)

            @pl.when(cond)
            def _():
                self.give[rows, cols] = total[rows, cols].astype(BF16)

            index = RS_Z + self.group * 8 + slot
            links.go(cond, self.give.at[rows, cols], z_take.at[slot, :, cols], index, index, target)

    def add_from_z(self, cond, slot, rows):
        cols = self.cols

        @pl.when(cond)
        def _():
            part = self.z_take.at[slot, :, cols]
            self.links.arrive(None, part, RS_Z + self.group * 8 + slot, self.across)
            self.total[rows, cols] = self.total[rows, cols] + part[...].astype(F32)

    def face(self):
        x, c, z, y = self.place
        rows, cols = self.shard(z, y), self.cols
        self.add_from_z(z > 0, z, rows)
        self.add_from_z(z < 3, 4 + z, rows)
        self.face_give[:, cols] = self.total[rows, cols].astype(BF16)
        slot = RS_FACE + self.group
        self.links.go(None, self.face_give.at[:, cols], self.face_take.at[:, cols], slot, slot, self.facing)

    def publish(self, out_qkv, out_proj, out_small, local_sem):
        x, c, z, y = self.place
        cols = self.cols
        self.links.arrive(None, self.face_take.at[:, cols], RS_FACE + self.group, self.facing)
        self.last[:, cols] = self.face_give[:, cols].astype(F32) + self.face_take[:, cols].astype(F32)
        self.out = out_proj if self.group == 0 else out_qkv
        slot = RS_OUT + self.group
        part, there = self.last.at[:, self.core_cols], self.landing(c)
        self.links.go(None, part, there, slot, slot, self.twin)
        copies = [pltpu.make_async_copy(part, there, local_sem.at[self.group])]
        if self.group == 3:
            copies.append(pltpu.make_async_copy(self.last.at[:, self.small_cols], out_small, local_sem.at[6]))
        for copy in copies:
            copy.start()
        return copies

    def landing(self, core):
        return self.out.at[:, pl.ds(pl.multiple_of(self.target(core), 128), HC)]

    def landed(self):
        x, c, z, y = self.place
        self.links.arrive(None, self.landing(1 - c), RS_OUT + self.group, self.twin)


def layer(
    x_ref, cot, lengths, routes, slots, wq, wp, sm, w_up, w_down,
    mixed, grad_tokens, out_qkv, out_proj, out_small, out_up, out_down,
    wall, rows_t, lines, columns, left, qkv, hidden, normed2, gates, out_f, out_g, recv_f, recv_g, up, down, act, slope,
    part_f, part_g, take_f, take_g, back_f, back_g, dn_own, dn_give, dn_take, dn_face, up_own, up_give, up_take, up_face,
    rb, rel_rows, small_t, take, total, y_take, z_take, face_give, face_take, last,
    local_sem, send_sem, recv_sem,
):
    fetch = [
        pltpu.make_async_copy(w_up.at[0], up, local_sem.at[4]),
        pltpu.make_async_copy(w_down.at[0], down, local_sem.at[5]),
    ]
    greet()
    links = Links(send_sem, recv_sem)
    for copy in fetch:
        copy.start()
    stand(routes, slots, lines, columns)
    rel_rows[...] = jnp.zeros_like(rel_rows)
    later = gather_weights(links, wq, wp, sm, wall, local_sem)
    normed, attended = left.at[0], left.at[1]
    attention_forward(
        later, x_ref, cot, lengths, columns, wall, rows_t, total, normed, qkv, attended, hidden, normed2, gates, out_f, out_g
    )
    for copy in fetch:
        copy.wait()
    downs, ups = (dn_own, dn_give, dn_take, dn_face), (up_own, up_give, up_take, up_face)
    experts(
        links, (out_f, out_g), (recv_f, recv_g), up, down, act, slope, (part_f, part_g), (take_f, take_g),
        (back_f, back_g), downs, ups,
    )
    combine(cot, lengths, columns, rows_t, hidden, normed2, gates, back_f, back_g, mixed, rb, small_t)
    proj, values, first, second = (
        Reduction(
            links, group, left, rb, small_t, act.at[0:D, :], take, total, y_take, z_take, face_give, face_take, last
        )
        for group in range(4)
    )
    pending = []

    def grads(piece):
        pending.append(expert_grad_out(links, piece, downs, ups, out_down, out_up, local_sem))

    def publish(item):
        pending.extend(item.publish(out_qkv, out_proj, out_small, local_sem))

    proj.form()
    attention_backward(
        x_ref, wall, rows_t, qkv, total, hidden, normed2, rb, rel_rows, small_t, grad_tokens, proj.halve
    )
    values.form()
    proj.chain(0)
    values.halve()
    proj.chain(1)
    first.form()
    proj.chain(2)
    proj.chain(3)
    first.halve()
    values.chain(0)
    second.form()
    values.chain(1)
    second.halve()
    values.chain(2)
    values.chain(3)
    grads(0)
    grads(1)
    proj.face()
    for k in range(4):
        first.chain(k)
    values.face()
    grads(2)
    for k in range(4):
        second.chain(k)
    first.face()
    grads(3)
    second.face()
    grads(4)
    grads(5)
    for item in (proj, values, first, second):
        publish(item)
    for item in (proj, values, first, second):
        item.landed()
    expert_grads_arrive(links, out_down, out_up)
    for copy in pending:
        copy.wait()
    links.finish()


def pack_small(gain_attn, gain_moe, w_router, rel_table):
    table = jnp.pad(rel_table, ((0, SHARD - rel_table.shape[0]), (0, 64 - HEADS)))
    side = jnp.concatenate([gain_attn[:, None], gain_moe[:, None], w_router], axis=1)
    return jnp.concatenate([jnp.pad(side, ((0, 0), (0, 64 - side.shape[1]))), table], axis=1)


def hand_out(mixed, tokens, qkv, proj, small, up, down, to_mixed, to_tokens, to_qkv, to_proj, to_small, to_up, to_down):
    to_mixed[...] = mixed[...]
    to_tokens[...] = tokens[...]
    to_qkv[...] = qkv[...]
    to_proj[...] = proj[...]
    to_up[...] = up[...].astype(F32)
    to_down[...] = down[...].astype(F32)

    @pl.when(pl.program_id(0) == 0)
    def _():
        to_small[...] = jnp.transpose(small[...])


def rows_of(shape, steps):
    return pl.BlockSpec((shape[0] // steps, shape[1]), lambda i: (i, 0))


def body_fast(
    tokens, cotangent, lengths, routes, slots, gain_attn, w_qkv, w_proj, rel_table, gain_moe, w_router, w_up, w_down
):
    small = pack_small(gain_attn, gain_moe, w_router, rel_table)
    vm = pl.BlockSpec(memory_space=pltpu.VMEM)
    hbm = pl.BlockSpec(memory_space=pl.ANY)
    sds = jax.ShapeDtypeStruct
    v = pltpu.VMEM
    shapes = (
        sds((TOK, D), BF16), sds((TOK, D), F32), sds((SHARD, 3 * D), F32), sds((SHARD, D), F32),
        sds((SHARD, 128), F32), sds((D, HF), BF16), sds((HF, D), BF16),
    )
    out = pl.pallas_call(
        layer,
        out_shape=shapes,
        in_specs=[vm, vm, pl.BlockSpec(memory_space=pltpu.SMEM), vm, vm, hbm, hbm, hbm, hbm, hbm],
        out_specs=[vm, vm, hbm, hbm, hbm, hbm, hbm],
        scratch_shapes=[
            v((D, WALL), BF16), v((8, D), F32), v((8, TOK), F32), v((TOK, 8), F32), v((2, TOK, D), BF16),
            v((TOK, 3 * D), BF16), v((TOK, D), F32), v((TOK, D), BF16),
            v((TOK, 1), F32), v((EXP, ROWS, D), BF16), v((EXP, ROWS, D), BF16),
            v((8 * ROWS, D), BF16), v((8 * ROWS, D), BF16), v((D, HF), BF16), v((HF, D), BF16),
            v((8 * ROWS, SENTC), BF16), v((8 * ROWS, HF), BF16),
            v((EXP, 2, ROWS, D), BF16), v((EXP, 2, ROWS, D), BF16), v((EXP, ROWS, D), BF16), v((EXP, ROWS, D), BF16),
            v((EXP, ROWS, D), BF16), v((EXP, ROWS, D), BF16),
            v((HF // 2, D), F32), v((HF // 2, D), BF16), v((HF // 2, D), BF16), v((HF // 2, D), BF16),
            v((D // 2, HF), F32), v((D // 2, HF), BF16), v((D // 2, HF), BF16), v((D // 2, HF), BF16),
            v((TOK, 4 * D), BF16), v((16, SEQ), F32), v((128, D), F32),
            v((D, SENTC), BF16), v((D, SENTC), F32), v((4, SHARD, SENTC), BF16), v((8, SHARD, SENTC), BF16),
            v((SHARD, SENTC), BF16), v((SHARD, SENTC), BF16), v((SHARD, SENTC), F32),
            pltpu.SemaphoreType.DMA((14,)), pltpu.SemaphoreType.DMA((LINKS,)), pltpu.SemaphoreType.DMA((LINKS,)),
        ],
        compiler_params=pltpu.CompilerParams(
            collective_id=0, has_side_effects=True, vmem_limit_bytes=67043328
        ),
        name="layer",
    )(tokens, cotangent, lengths, routes.T, slots.T, w_qkv, w_proj, small, w_up, w_down)
    steps = 4
    final = list(shapes)
    final[5], final[6] = sds((D, HF), F32), sds((HF, D), F32)
    specs = [rows_of(item.shape, steps) for item in shapes]
    whole_in = pl.BlockSpec((SHARD, 128), lambda i: (0, 0))
    whole_out = pl.BlockSpec((128, SHARD), lambda i: (0, 0))
    final[4] = sds((128, SHARD), F32)
    mixed, grad_tokens, grad_qkv, grad_proj, side, grad_up, grad_down = pl.pallas_call(
        hand_out,
        out_shape=tuple(final),
        grid=(steps,),
        in_specs=specs[:4] + [whole_in] + specs[5:],
        out_specs=specs[:4] + [whole_out] + specs[5:],
        name="hand_out",
    )(*out)
    return (
        mixed,
        grad_tokens,
        side[0],
        grad_qkv,
        grad_proj,
        side[HEAD : HEAD + HEADS, : rel_table.shape[0]].T,
        side[1],
        side[2 : 2 + EXP].T,
        grad_up[None],
        grad_down[None],
    )


epsilon = 1e-06
exact_precision = lax.Precision.HIGHEST


def rms_norm(values, gain):
    factor = lax.rsqrt(jnp.mean(values * values, axis=-1, keepdims=True) + epsilon)
    return values * factor * gain


def distance_hot():
    places = jnp.arange(SEQ, dtype=jnp.int32)
    distance = jnp.clip(places[:, None] - places[None, :], 0, SEQ - 1).reshape(1, SEQ * SEQ)
    return (distance == places[:, None]).astype(jnp.bfloat16)


def bias_matrix(table, hot):
    flat = jnp.einsum("dh,dp->hp", table, hot, preferred_element_type=jnp.float32)
    return flat.reshape(table.shape[1], SEQ, SEQ)


def exact_gelu(values):
    return jax.nn.gelu(values, approximate=False)


def masked_scores(qkv_rows, bias, allowed, factor):
    raw = jnp.einsum(
        "qhd,khd->hqk", qkv_rows[:, 0], qkv_rows[:, 1], preferred_element_type=jnp.float32
    )
    return jnp.where(allowed[None], raw * factor + bias, -1e30)


def fetch_weights(gain_attn, w_qkv, w_proj, rel_table, gain_moe, w_router):
    rows, experts = w_router.shape
    spread = rel_table.shape[0]
    packed = jnp.concatenate(
        [gain_attn, gain_moe, w_router.reshape(-1), rel_table.reshape(-1)]
    )
    small = lax.all_gather(packed, "fsdp", axis=0, tiled=False)
    groups = small.shape[0]
    edge = 2 * rows + rows * experts
    return (
        small[:, :rows].reshape(-1),
        lax.all_gather(w_qkv, "fsdp", axis=0, tiled=True),
        lax.all_gather(w_proj, "fsdp", axis=0, tiled=True),
        small[:, edge:].reshape(groups * spread, HEADS),
        small[:, rows : 2 * rows].reshape(-1),
        small[:, 2 * rows : edge].reshape(groups * rows, experts),
    )


def body(
    tokens,
    cotangent,
    lengths,
    routes,
    slots,
    gain_attn,
    w_qkv,
    w_proj,
    rel_table,
    gain_moe,
    w_router,
    w_up,
    w_down,
):
    groups = lax.axis_size("fsdp")
    experts = groups // 2
    capacity = 2 * SEQ // experts
    factor = HEAD ** (-0.5)
    up_weight = w_up[0]
    down_weight = w_down[0]
    places = jnp.arange(SEQ, dtype=jnp.int32)
    causal = places[:, None] >= places[None, :]
    expert_ids = jnp.arange(experts, dtype=jnp.int32)
    saved = []
    mixed_parts = []
    weights = fetch_weights(gain_attn, w_qkv, w_proj, rel_table, gain_moe, w_router)
    gain_a = weights[0].astype(jnp.float32)
    gain_m = weights[4].astype(jnp.float32)
    router_float = weights[5].astype(jnp.float32)
    hot = distance_hot()
    bias = bias_matrix(weights[3], hot)
    for batch in range(MB):
        x_float = tokens[batch * SEQ : (batch + 1) * SEQ].astype(jnp.float32)
        live_keys = places < lengths[batch]
        live_col = live_keys.astype(jnp.float32)[:, None]
        allowed = causal & live_keys[None, :]
        normed = rms_norm(x_float, gain_a).astype(jnp.bfloat16)
        qkv_rows = (
            jnp.dot(normed, weights[1], preferred_element_type=jnp.float32)
            .astype(jnp.bfloat16)
            .reshape(SEQ, 3, HEADS, HEAD)
        )
        scores = masked_scores(qkv_rows, bias, allowed, factor)
        row_peak = jnp.max(scores, axis=-1, keepdims=True)
        exp_scores = jnp.exp(scores - row_peak)
        row_total = jnp.sum(exp_scores, axis=-1, keepdims=True)
        log_total = row_peak + jnp.log(row_total)
        probs_low = (exp_scores / row_total).astype(jnp.bfloat16)
        attended = jnp.einsum(
            "hqk,khd->qhd", probs_low, qkv_rows[:, 2], preferred_element_type=jnp.float32
        )
        attended = attended.astype(jnp.bfloat16).reshape(SEQ, D)
        branch = jnp.dot(attended, weights[2], preferred_element_type=jnp.float32)
        hidden = x_float + live_col * branch
        normed2 = rms_norm(hidden, gain_m).astype(jnp.bfloat16)
        logits = jnp.dot(normed2, weights[5], preferred_element_type=jnp.float32)
        route_rows = routes[batch * SEQ : (batch + 1) * SEQ]
        slot_rows = slots[batch * SEQ : (batch + 1) * SEQ]
        hot_first = (route_rows[:, 0:1] == expert_ids[None, :]).astype(jnp.float32)
        hot_second = (route_rows[:, 1:2] == expert_ids[None, :]).astype(jnp.float32)
        gate_first = jax.nn.sigmoid(
            jnp.sum(logits * hot_first, axis=-1) - jnp.sum(logits * hot_second, axis=-1)
        )
        row_place = route_rows * capacity + slot_rows
        target = jnp.where(live_keys[:, None], row_place, experts * capacity)
        outgoing = jnp.zeros((experts * capacity, D), jnp.bfloat16)
        outgoing = (
            outgoing.at[target[:, 0]]
            .set(normed2, mode="drop")
            .at[target[:, 1]]
            .set(normed2, mode="drop")
        )
        outgoing = jnp.repeat(outgoing.reshape(experts, capacity, D), 2, axis=0)
        expert_received = lax.all_to_all(outgoing, "fsdp", split_axis=0, concat_axis=0, tiled=True)
        expert_before = jnp.einsum(
            "scd,df->scf", expert_received, up_weight, preferred_element_type=jnp.float32
        )
        expert_active = exact_gelu(expert_before).astype(jnp.bfloat16)
        partial_value = jnp.einsum(
            "scf,fd->scd", expert_active, down_weight, preferred_element_type=jnp.float32
        ).astype(jnp.bfloat16)
        returned = lax.all_to_all(partial_value, "fsdp", split_axis=0, concat_axis=0, tiled=True)
        results = (returned, expert_received, expert_before)
        combined = (
            results[0]
            .astype(jnp.float32)
            .reshape(experts, 2, capacity, D)
            .sum(axis=1)
            .reshape(experts * capacity, D)
        )
        first_out = combined[row_place[:, 0]]
        second_out = combined[row_place[:, 1]]
        moe = live_col * (
            gate_first[:, None] * first_out + (1.0 - gate_first)[:, None] * second_out
        )
        mixed_parts.append((hidden + moe).astype(jnp.bfloat16))
        saved.append(
            {
                "normed": normed,
                "qkv_rows": qkv_rows,
                "log_total": log_total,
                "attended": attended,
                "hidden": hidden,
                "normed2": normed2,
                "gate_first": gate_first,
                "first_out": first_out,
                "second_out": second_out,
                "results": results,
                "target": target,
                "row_place": row_place,
                "hot_first": hot_first,
                "hot_second": hot_second,
            }
        )
    grad_qkv_w = jnp.zeros((D, 3 * D), jnp.float32)
    grad_proj_w = jnp.zeros((D, D), jnp.float32)
    grad_table = jnp.zeros((SEQ, HEADS), jnp.float32)
    grad_gain_a = jnp.zeros((D,), jnp.float32)
    grad_gain_m = jnp.zeros((D,), jnp.float32)
    grad_router = jnp.zeros((D, experts), jnp.float32)
    grad_up = jnp.zeros((D, FF // 2), jnp.float32)
    grad_down = jnp.zeros((FF // 2, D), jnp.float32)
    grad_parts = [None] * MB
    for batch in reversed(range(MB)):
        kept = saved[batch]
        x_float = tokens[batch * SEQ : (batch + 1) * SEQ].astype(jnp.float32)
        live_keys = places < lengths[batch]
        live_col = live_keys.astype(jnp.float32)[:, None]
        allowed = causal & live_keys[None, :]
        grad_out = cotangent[batch * SEQ : (batch + 1) * SEQ].astype(jnp.float32)
        grad_moe = live_col * grad_out
        gate_first = kept["gate_first"]
        gate_second = 1.0 - gate_first
        grad_gate_first = jnp.sum(grad_moe * kept["first_out"], axis=-1)
        grad_gate_second = jnp.sum(grad_moe * kept["second_out"], axis=-1)
        grad_first = (gate_first[:, None] * grad_moe).astype(jnp.bfloat16)
        grad_second = (gate_second[:, None] * grad_moe).astype(jnp.bfloat16)
        target = kept["target"]
        grad_send = jnp.zeros((experts * capacity, D), jnp.bfloat16)
        grad_send = (
            grad_send.at[target[:, 0]]
            .set(grad_first, mode="drop")
            .at[target[:, 1]]
            .set(grad_second, mode="drop")
        )
        grad_send = jnp.repeat(grad_send.reshape(experts, capacity, D), 2, axis=0)
        grad_recv = lax.all_to_all(grad_send, "fsdp", split_axis=0, concat_axis=0, tiled=True)
        received = kept["results"][1]
        before = kept["results"][2]
        active, gelu_back = jax.vjp(exact_gelu, before)
        active_low = active.astype(jnp.bfloat16)
        grad_active = jnp.einsum(
            "scd,fd->scf", grad_recv, down_weight, preferred_element_type=jnp.float32
        )
        grad_before = gelu_back(grad_active)[0].astype(jnp.bfloat16)
        grad_down = grad_down + jnp.einsum(
            "scf,scd->fd", active_low, grad_recv, preferred_element_type=jnp.float32
        )
        grad_up = grad_up + jnp.einsum(
            "scd,scf->df", received, grad_before, preferred_element_type=jnp.float32
        )
        grad_part = jnp.einsum(
            "scf,df->scd", grad_before, up_weight, preferred_element_type=jnp.float32
        ).astype(jnp.bfloat16)
        grad_back = lax.all_to_all(grad_part, "fsdp", split_axis=0, concat_axis=0, tiled=True)
        grad_rows = (
            grad_back.astype(jnp.float32)
            .reshape(experts, 2, capacity, D)
            .sum(axis=1)
            .reshape(experts * capacity, D)
        )
        row_place = kept["row_place"]
        grad_diff = (grad_gate_first - grad_gate_second) * gate_first * gate_second
        grad_logits = grad_diff[:, None] * (kept["hot_first"] - kept["hot_second"])
        normed2_float = kept["normed2"].astype(jnp.float32)
        grad_router = grad_router + jnp.dot(normed2_float.T, grad_logits, precision=exact_precision)
        grad_normed2 = live_col * (grad_rows[row_place[:, 0]] + grad_rows[row_place[:, 1]])
        grad_normed2 = grad_normed2 + jnp.dot(
            grad_logits, router_float.T, precision=exact_precision
        )
        _, norm_back_moe = jax.vjp(rms_norm, kept["hidden"], gain_m)
        grad_hidden_norm, grad_gain_part = norm_back_moe(grad_normed2)
        grad_gain_m = grad_gain_m + grad_gain_part
        grad_hidden = grad_out + grad_hidden_norm
        grad_branch = (live_col * grad_hidden).astype(jnp.bfloat16)
        grad_proj_w = grad_proj_w + jnp.einsum(
            "sd,se->de", kept["attended"], grad_branch, preferred_element_type=jnp.float32
        )
        grad_attended = jnp.einsum(
            "se,de->sd", grad_branch, weights[2], preferred_element_type=jnp.float32
        )
        grad_attended = grad_attended.astype(jnp.bfloat16).reshape(SEQ, HEADS, HEAD)
        qkv_rows = kept["qkv_rows"]
        scores = masked_scores(qkv_rows, bias, allowed, factor)
        probs = jnp.exp(scores - kept["log_total"])
        probs_low = probs.astype(jnp.bfloat16)
        grad_probs = jnp.einsum(
            "qhd,khd->hqk", grad_attended, qkv_rows[:, 2], preferred_element_type=jnp.float32
        )
        row_dot = jnp.sum(probs * grad_probs, axis=-1, keepdims=True)
        grad_scores = (probs * (grad_probs - row_dot)).astype(jnp.bfloat16)
        grad_table = grad_table + jnp.einsum(
            "dp,hp->dh",
            hot,
            jnp.where(allowed[None], grad_scores, 0).reshape(HEADS, SEQ * SEQ),
            preferred_element_type=jnp.float32,
        )
        grad_queries = (
            jnp.einsum(
                "hqk,khd->qhd", grad_scores, qkv_rows[:, 1], preferred_element_type=jnp.float32
            )
            * factor
        )
        grad_keys = (
            jnp.einsum(
                "hqk,qhd->khd", grad_scores, qkv_rows[:, 0], preferred_element_type=jnp.float32
            )
            * factor
        )
        grad_values = jnp.einsum(
            "hqk,qhd->khd", probs_low, grad_attended, preferred_element_type=jnp.float32
        )
        grad_qkv = (
            jnp.stack([grad_queries, grad_keys, grad_values], axis=1)
            .astype(jnp.bfloat16)
            .reshape(SEQ, 3 * D)
        )
        grad_qkv_w = grad_qkv_w + jnp.einsum(
            "sd,se->de", kept["normed"], grad_qkv, preferred_element_type=jnp.float32
        )
        grad_normed = jnp.einsum(
            "se,de->sd", grad_qkv, weights[1], preferred_element_type=jnp.float32
        )
        _, norm_back_attn = jax.vjp(rms_norm, x_float, gain_a)
        grad_x_norm, grad_gain_piece = norm_back_attn(grad_normed)
        grad_gain_a = grad_gain_a + grad_gain_piece
        grad_parts[batch] = grad_hidden + grad_x_norm
    small = jnp.concatenate(
        [
            grad_gain_a.reshape(groups, -1),
            grad_gain_m.reshape(groups, -1),
            grad_router.reshape(groups, -1),
            grad_table.reshape(groups, -1),
        ],
        axis=1,
    )
    small = lax.psum_scatter(small, "fsdp", scatter_dimension=0, tiled=True)
    shards = (
        small,
        lax.psum_scatter(grad_qkv_w, "fsdp", scatter_dimension=0, tiled=True),
        lax.psum_scatter(grad_proj_w, "fsdp", scatter_dimension=0, tiled=True),
    )
    sums = lax.psum((shards[0], shards[1], shards[2], grad_up[None], grad_down[None]), "replica")
    rows = D // groups
    edge = 2 * rows + rows * experts
    totals = (
        sums[0][0, :rows],
        sums[1],
        sums[2],
        sums[0][0, edge:].reshape(SEQ // groups, HEADS),
        sums[0][0, rows : 2 * rows],
        sums[0][0, 2 * rows : edge].reshape(rows, experts),
        sums[3],
        sums[4],
    )
    mixed = jnp.concatenate(mixed_parts, axis=0)
    grad_tokens = jnp.concatenate(grad_parts, axis=0)
    return (
        mixed,
        grad_tokens,
        totals[0],
        totals[1],
        totals[2],
        totals[3],
        totals[4],
        totals[5],
        totals[6],
        totals[7],
    )


def solution(mesh):
    in_specs = (
        P(("replica", "fsdp"), None),
        P(("replica", "fsdp"), None),
        P(("replica", "fsdp")),
        P(("replica", "fsdp"), None),
        P(("replica", "fsdp"), None),
        P("fsdp"),
        P("fsdp", None),
        P("fsdp", None),
        P("fsdp", None),
        P("fsdp"),
        P("fsdp", None),
        P("fsdp", None, None),
        P("fsdp", None, None),
    )
    out_specs = (
        P(("replica", "fsdp"), None),
        P(("replica", "fsdp"), None),
        P("fsdp"),
        P("fsdp", None),
        P("fsdp", None),
        P("fsdp", None),
        P("fsdp"),
        P("fsdp", None),
        P("fsdp", None, None),
        P("fsdp", None, None),
    )
    fast = dict(mesh.shape) == {"replica": 4, "fsdp": 8}
    return jax.shard_map(body_fast if fast else body, mesh=mesh, in_specs=in_specs, out_specs=out_specs, check_vma=False)
```

```python
import functools

import jax
import jax.numpy as jnp
from jax import lax
from jax.experimental import pallas as pl
from jax.experimental.pallas import tpu as pltpu
from jax.sharding import PartitionSpec as P

D = 768
HEADS = 12
HEAD = 64
FF = 3072
SEQ = 128
MB = 2
MESH = pl.DeviceIdType.MESH
F32 = jnp.float32
BF16 = jnp.bfloat16
NEG = -1e30
HF = FF // 2
TOK = MB * SEQ
EXP = 4
CAP = 64
ROWS = MB * CAP
LOW = 896
MID = 3 * D - 2 * LOW
MORE = MID + 128
SMALL = LOW + MID
PROJ = LOW + MORE
HIGH = PROJ + D
WALL = HIGH + LOW
LEFTC = LOW + MID
SHARD = 96
HALF = SHARD // 2
PAIRS = HEADS // 2
SCALE = HEAD ** (-0.5)


def place():
    replica = lax.axis_index("replica")
    group = lax.axis_index("fsdp")
    return replica // 2, replica % 2, group // 2, group % 2


def device(x, c, z, y):
    return (x * 2 + c, z * 2 + y)


def remote(src, dst, send, recv, target):
    return pltpu.make_async_remote_copy(
        src_ref=src,
        dst_ref=dst,
        send_sem=send,
        recv_sem=recv,
        device_id=target,
        device_id_type=MESH,
    )


def greet():
    x, c, z, y = place()
    barrier = pltpu.get_barrier_semaphore()
    targets = [device(x, 1 - c, z, y), device(1 - x, c, z, y), device(x, c, z, 1 - y)]
    targets += [device(x, c, (z + k) % 4, y) for k in (1, 2, 3)]
    for target in targets:
        pl.semaphore_signal(barrier, inc=1, device_id=target, device_id_type=MESH)
    pl.semaphore_wait(barrier, len(targets))


def dot(a, b, ca=1, cb=0):
    return lax.dot_general(a, b, (((ca,), (cb,)), ((), ())), preferred_element_type=F32)


def run(cond, what):
    if cond is None:
        what()
    else:
        pl.when(cond)(what)


class Links:
    def __init__(self, send_sem, recv_sem):
        self.send_sem, self.recv_sem = send_sem, recv_sem
        self.started = []

    def go(self, cond, src, dst, send, recv, target):
        copy = remote(src, dst, self.send_sem.at[send], self.recv_sem.at[recv], target)
        run(cond, copy.start)
        self.started.append((cond, copy))
        return copy

    def arrive(self, cond, dst, recv, target):
        run(cond, remote(dst, dst, self.send_sem.at[0], self.recv_sem.at[recv], target).wait_recv)

    def leave(self, copy):
        copy.wait_send()
        self.started = [(cond, item) for cond, item in self.started if item is not copy]

    def finish(self):
        for cond, copy in self.started:
            run(cond, copy.wait_send)
        self.started = []


def gather_weights(links, wq, wp, wall, local_sem, others):
    x, c, z, y = place()
    own = pl.ds(pl.multiple_of((z * 2 + y) * SHARD, 16), SHARD)
    fills = [
        pltpu.make_async_copy(wq.at[:, pl.ds(0, LEFTC)], wall.at[own, pl.ds(0, LEFTC)], local_sem.at[0]),
        pltpu.make_async_copy(wq.at[:, pl.ds(LEFTC, LOW)], wall.at[own, pl.ds(HIGH, LOW)], local_sem.at[1]),
        pltpu.make_async_copy(wp, wall.at[own, pl.ds(PROJ, D)], local_sem.at[2]),
    ]
    for fill in fills:
        fill.start()
    share = pl.ds(pl.multiple_of(x * HIGH, 128), LOW)
    gained = pl.ds(pl.multiple_of((1 - x) * HIGH, 128), LOW)
    columns = (share, pl.ds(LOW, MORE), pl.ds(PROJ, D))
    up, down = device(x, c, z + 1, y), device(x, c, z - 1, y)
    across, facing, twin = device(x, c, z, 1 - y), device(1 - x, c, z, y), device(x, 1 - c, z, y)

    def part(zs, ys, half, cols):
        return wall.at[pl.ds(pl.multiple_of((zs * 2 + ys) * SHARD + half * HALF, 16), HALF), cols]

    def go(cond, zs, ys, cols, send, recv, target, src=None):
        piece = part(zs, ys, c, cols)
        links.go(cond, piece if src is None else src, piece, send, recv, target)

    def arrive(cond, zs, ys, half, cols, recv):
        links.arrive(cond, part(zs, ys, half, cols), recv, twin)

    def spread(cond, sub, zs, ys):
        source = zs * 2 + ys
        if sub == 0:
            go(cond, zs, ys, share, 39 + source, 24 + source, facing)
        go(cond, zs, ys, columns[sub], 47 + sub * 8 + source, 32 + sub * 8 + source, twin)

    def begin(sub, src):
        go(z < 3, z, y, columns[sub], sub * 3, sub * 4 + z, up, src)
        go(z > 0, z, y, columns[sub], 9 + sub * 3, sub * 4 + z, down, src)
        go(None, z, y, columns[sub], 18 + sub * 7, 12 + sub * 4 + z, across, src)

    def along(sub, k):
        below, above = z - k, z + k
        for cond, zs, on, first, target, place_of in (
            (below >= 0, below, z < 3, 0, up, k),
            (above <= 3, above, z > 0, 9, down, 3 + k),
        ):
            arrive(cond, zs, y, c, columns[sub], sub * 4 + zs)
            if k < 3:
                go(cond & on, zs, y, columns[sub], first + sub * 3 + k, sub * 4 + zs, target)
            go(cond, zs, y, columns[sub], 18 + sub * 7 + place_of, 12 + sub * 4 + zs, across)
            spread(cond, sub, zs, y)

    def over(sub, k):
        if k == 0:
            arrive(None, z, 1 - y, c, columns[sub], 12 + sub * 4 + z)
            spread(None, sub, z, 1 - y)
            return
        for cond, zs in ((z - k >= 0, z - k), (z + k <= 3, z + k)):
            arrive(cond, zs, 1 - y, c, columns[sub], 12 + sub * 4 + zs)
            spread(cond, sub, zs, 1 - y)

    half = pl.ds(pl.multiple_of(c * HALF, 16), HALF)
    begin(0, wq.at[half, pl.ds(pl.multiple_of(x * LEFTC, 128), LOW)])
    for copy in others:
        copy.start()
    for fill in fills:
        fill.wait()
    begin(1, None)
    for k in (1, 2, 3):
        for sub in range(2):
            along(sub, k)
            over(sub, k - 1)
        if k == 2:
            begin(2, wp.at[half, :])
    along(2, 1)
    for sub in range(2):
        over(sub, 3)

    def each(what):
        for zs in range(4):
            for ys in range(2):
                what((zs != z) | (ys != y), zs, ys, zs * 2 + ys)

    def gain(other, zs, ys, source):
        arrive(other, zs, ys, c, gained, 24 + source)
        go(other, zs, ys, gained, 71 + source, 56 + source, twin)

    def mostly(other, zs, ys, source):
        for sub in range(2):
            arrive(other, zs, ys, 1 - c, columns[sub], 32 + sub * 8 + source)
        arrive(other, zs, ys, 1 - c, gained, 56 + source)

    def rest(other, zs, ys, source):
        arrive(other, zs, ys, 1 - c, columns[2], 32 + 16 + source)

    each(gain)
    each(mostly)

    def first():
        along(2, 2)
        over(2, 0)

    def second():
        along(2, 3)
        over(2, 1)
        over(2, 2)

    return first, second, lambda: over(2, 3), lambda: each(rest)


def unit(values):
    return lax.rsqrt(jnp.mean(values * values, axis=-1, keepdims=True) + 1e-06)


def build_bias(wall, bias):
    table = jnp.concatenate(
        [wall[f * SHARD : f * SHARD + 16, SMALL : SMALL + 128] for f in range(8)], axis=0
    )
    ahead = lax.broadcasted_iota(jnp.int32, (SEQ, SEQ), 0)
    lane = lax.broadcasted_iota(jnp.int32, (SEQ, SEQ), 1)
    turned = jnp.where(ahead + lane == SEQ, 1.0, jnp.where(ahead + lane == 0, 1.0, 0.0)).astype(BF16)
    lines = dot(table, turned, 0, 0)
    for h in range(HEADS):
        line = jnp.broadcast_to(lines[HEAD + h : HEAD + h + 1, :], (SEQ, SEQ))
        rolled = pltpu.roll(line, 0, 1, stride=1, stride_axis=0)
        bias[(h // 2) * SEQ : (h // 2 + 1) * SEQ, (h % 2) * SEQ : (h % 2 + 1) * SEQ] = jnp.where(ahead >= lane, rolled, NEG)


def pack(gain_attn, gain_moe, router_t, rel, board, wall):
    x, c, z, y = place()
    board[0:SEQ, 0:SEQ] = jnp.zeros((SEQ, SEQ), F32)
    board[0:1, 0:SHARD] = gain_attn[...].astype(F32)
    board[1:2, 0:SHARD] = gain_moe[...].astype(F32)
    board[2 : 2 + EXP, 0:SHARD] = router_t[...].astype(F32)
    turned = jnp.transpose(board[0:SEQ, 0:SEQ])
    board[0:SEQ, 0:SEQ] = turned
    board[0:16, HEAD : HEAD + HEADS] = rel[...].astype(F32)
    own = pl.ds(pl.multiple_of((z * 2 + y) * SHARD, 16), SHARD)
    wall[own, SMALL : SMALL + 128] = board[0:SHARD, 0:SEQ].astype(BF16)


def stand(routes, slots, lines, columns):
    chosen = routes[...]
    lines[...] = jnp.zeros_like(lines)
    lines[0:2, :] = (chosen * CAP + slots[...]).astype(F32)
    lines[2:4, :] = chosen.astype(F32)
    columns[...] = jnp.transpose(lines[...])


def routing(columns, s):
    spots = columns[s * SEQ : (s + 1) * SEQ, :]
    lane = lax.broadcasted_iota(jnp.int32, (SEQ, EXP * CAP), 1).astype(F32)
    return spots[:, 0:1] == lane, spots[:, 1:2] == lane


def named(columns, s):
    spots = columns[s * SEQ : (s + 1) * SEQ, :]
    lane = lax.broadcasted_iota(jnp.int32, (SEQ, 128), 1).astype(F32) - 2.0
    return spots[:, 2:3] == lane, spots[:, 3:4] == lane


def live_column(lengths, s):
    return lax.broadcasted_iota(jnp.int32, (SEQ, 1), 0) < lengths[s]


def attention_forward(
    later, x_ref, cot, lengths, columns, wall, rows_t, board, normed, qkv, attended, hidden, normed2, gates, out_f, out_g
):
    rows_t[...] = jnp.transpose(wall[:, SMALL : SMALL + 128].astype(F32))[0:8]
    build_bias(wall, board)
    x = x_ref[...].astype(F32)
    normed[...] = (x * unit(x) * rows_t[0:1, :]).astype(BF16)
    qkv[:, 0:LEFTC] = dot(normed[...], wall[:, 0:LEFTC]).astype(BF16)
    qkv[:, LEFTC : 3 * D] = dot(normed[...], wall[:, HIGH:WALL]).astype(BF16)
    lane = lax.broadcasted_iota(jnp.int32, (SEQ, 128), 1)

    def pair(p, carry):
        blocks = pl.ds(pl.multiple_of(p * SEQ, SEQ), SEQ)
        for s in range(MB):
            rows = slice(s * SEQ, (s + 1) * SEQ)
            q = qkv[rows, pl.ds(pl.multiple_of(p * 128, 128), 128)]
            k = qkv[rows, pl.ds(pl.multiple_of(D + p * 128, 128), 128)]
            v = qkv[rows, pl.ds(pl.multiple_of(2 * D + p * 128, 128), 128)]
            alive = lane < lengths[s]
            got = []
            for j in range(2):
                mine = (lane < HEAD) if j == 0 else (lane >= HEAD)
                raw = dot(jnp.where(mine, q, jnp.zeros_like(q)), k, 1, 1)
                scores = jnp.where(alive, raw * SCALE + board[blocks, j * SEQ : (j + 1) * SEQ], NEG)
                scores = jnp.exp(scores - jnp.max(scores, axis=-1, keepdims=True))
                share = scores * (1.0 / jnp.sum(scores, axis=-1, keepdims=True))
                board[blocks, (2 + 2 * s + j) * SEQ : (3 + 2 * s + j) * SEQ] = share
                got.append(dot(share.astype(BF16), v))
            attended[rows, pl.ds(pl.multiple_of(p * 128, 128), 128)] = jnp.where(
                lane < HEAD, got[0], got[1]
            ).astype(BF16)
        return carry

    for t in range(3):
        later[t]()
        lax.fori_loop(2 * t, 2 * t + 2, pair, 0)
    later[3]()
    branch = dot(attended[...], wall[:, PROJ:HIGH])
    for s in range(MB):
        rows = slice(s * SEQ, (s + 1) * SEQ)
        live = live_column(lengths, s)
        state = x_ref[rows, :].astype(F32) + jnp.where(live, branch[rows, :], 0.0)
        hidden[rows, :] = state
        low = (state * unit(state) * rows_t[1:2, :]).astype(BF16)
        normed2[rows, :] = low
        logits = dot(low, wall[:, SMALL : SMALL + 128])
        one, two = named(columns, s)
        picked = jnp.where(one, logits, 0.0) - jnp.where(two, logits, 0.0)
        gate = jax.nn.sigmoid(jnp.sum(picked, axis=-1, keepdims=True))
        gates[rows, :] = gate
        grad = jnp.where(live, cot[rows, :].astype(F32), 0.0)
        first, second = routing(columns, s)
        first = jnp.where(first & live, 1.0, 0.0).astype(BF16)
        second = jnp.where(second & live, 1.0, 0.0).astype(BF16)
        sent = dot(first + second, low, 0, 0).astype(BF16)
        back = dot(first, (gate * grad).astype(BF16), 0, 0) + dot(
            second, ((1.0 - gate) * grad).astype(BF16), 0, 0
        )
        back = back.astype(BF16)
        for e in range(EXP):
            out_f[e, s * CAP : (s + 1) * CAP, :] = sent[e * CAP : (e + 1) * CAP, :]
            out_g[e, s * CAP : (s + 1) * CAP, :] = back[e * CAP : (e + 1) * CAP, :]


TILE = 512
Z_ROWS, Y_ROWS, Y_PART, Z_BACK = 80, 88, 96, 104
TWIN_W, FACE_W, TWIN_OUT = 112, 114, 120
RS_TWIN, RS_Y, RS_Z, RS_FACE, RS_OUT = 126, 131, 147, 179, 183
LINKS = 191


def quarter(zs):
    return pl.ds(pl.multiple_of(zs * 2 * ROWS, 2 * ROWS), 2 * ROWS)


def half_rows(zs, ys):
    return pl.ds(pl.multiple_of((zs * 2 + ys) * ROWS, ROWS), ROWS)


def expert_forward(zs, recv, up, down, act, slope, part):
    rows = quarter(zs)

    def tile(i, carry):
        cols = pl.ds(pl.multiple_of(i * TILE, TILE), TILE)
        before = dot(recv[rows, :], up[:, cols])
        below = 0.5 + 0.5 * lax.erf(before * 0.7071067811865476)
        act[rows, cols] = (before * below).astype(BF16)
        density = jnp.exp(before * before * -0.5) * 0.3989422804014327
        slope[rows, cols] = (below + before * density).astype(BF16)
        return carry

    lax.fori_loop(0, HF // TILE, tile, 0)
    got = dot(act[rows, 0:HF], down[...]).astype(BF16)
    part[zs, 0] = got[0:ROWS]
    part[zs, 1] = got[ROWS : 2 * ROWS]


def expert_backward(zs, recv, up, down, slope, part):
    rows = quarter(zs)

    def tile(i, carry):
        cols = pl.ds(pl.multiple_of(i * TILE, TILE), TILE)
        grad = dot(recv[rows, :], down[cols, :], 1, 1)
        slope[rows, cols] = (grad * slope[rows, cols].astype(F32)).astype(BF16)
        return carry

    lax.fori_loop(0, HF // TILE, tile, 0)
    got = dot(slope[rows, :], up[...], 1, 1).astype(BF16)
    part[zs, 0] = got[0:ROWS]
    part[zs, 1] = got[ROWS : 2 * ROWS]


def experts(links, out, recv, up, down, act, slope, part, take, back, w_down, w_up):
    x, c, z, y = place()
    across, facing, twin = device(x, c, z, 1 - y), device(1 - x, c, z, y), device(x, 1 - c, z, y)

    for kind in range(2):
        links.go(None, out[kind].at[z], recv[kind].at[half_rows(z, y), :], Y_ROWS + kind * 4, Y_ROWS + kind * 4 + z, across)
        for d in (1, 2, 3):
            to = (z + d) % 4
            links.go(
                None, out[kind].at[to], recv[kind].at[half_rows(z, y), :], Z_ROWS + kind * 4 + d,
                Z_ROWS + kind * 4 + z, device(x, c, to, y),
            )
        recv[kind][half_rows(z, y), :] = out[kind][z]

    def source(d):
        return (z + 4 - d) % 4

    def reach(kind, d):
        zs = source(d)
        rows = recv[kind].at[half_rows(zs, y), :]
        links.arrive(None, rows, Z_ROWS + kind * 4 + zs, across)
        links.go(None, rows, rows, Y_ROWS + kind * 4 + d, Y_ROWS + kind * 4 + zs, across)

    def compute(kind, d):
        zs = source(d)
        links.arrive(None, recv[kind].at[half_rows(zs, 1 - y), :], Y_ROWS + kind * 4 + zs, across)
        if kind == 0:
            expert_forward(zs, recv[0], up, down, act, slope, part[0])
        else:
            expert_backward(zs, recv[1], up, down, slope, part[1])

    def give_part(kind, d):
        zs = source(d)
        links.go(
            None, part[kind].at[zs, 1 - y], take[kind].at[zs], Y_PART + kind * 4 + d, Y_PART + kind * 4 + zs, across
        )

    def merge(kind, d):
        zs = source(d)
        links.arrive(None, take[kind].at[zs], Y_PART + kind * 4 + zs, across)
        total = (part[kind][zs, y].astype(F32) + take[kind][zs].astype(F32)).astype(BF16)
        if d == 0:
            back[kind][z] = total
        else:
            part[kind][zs, y] = total
            links.go(
                None, part[kind].at[zs, y], back[kind].at[z], Z_BACK + kind * 4 + d, Z_BACK + kind * 4 + z,
                device(x, c, zs, y),
            )

    reach(0, 1)
    compute(0, 0)
    reach(0, 2)
    compute(1, 0)
    reach(0, 3)
    compute(0, 1)
    reach(1, 1)
    give_part(0, 1)
    compute(0, 2)
    reach(1, 2)
    give_part(0, 2)
    compute(1, 1)
    reach(1, 3)
    give_part(1, 1)
    merge(0, 1)
    compute(0, 3)
    give_part(0, 3)
    merge(0, 2)
    compute(1, 2)
    give_part(1, 2)
    merge(1, 1)
    compute(1, 3)
    give_part(1, 3)
    give_part(0, 0)
    give_part(1, 0)

    def down_tile(i, part_of, keep):
        cols = pl.ds(pl.multiple_of(part_of * (HF // 2) + i * 256, 128), 256)
        got = dot(act[:, cols], recv[1][...], 0, 0)
        keep[pl.ds(pl.multiple_of(i * 256, 256), 256), :] = got.astype(keep.dtype)

    def up_tile(i, part_of, keep):
        cols = pl.ds(pl.multiple_of(part_of * (D // 2) + i * 128, 128), 128)
        got = dot(recv[0][:, cols], slope[...], 0, 0)
        keep[pl.ds(pl.multiple_of(i * 128, 128), 128), :] = got.astype(keep.dtype)

    def tiles(one, part_of, keep):
        def step(i, carry):
            one(i, part_of, keep)
            return carry

        lax.fori_loop(0, 3, step, 0)

    pairs = ((0, 3), (1, 2), (1, 3))
    for i, (one, w) in enumerate(((down_tile, w_down), (up_tile, w_up))):
        own, give, got, face = w
        tiles(one, 1 - c, give)
        sent = links.go(None, give, got, TWIN_W + i, TWIN_W + i, twin)
        tiles(one, c, own)
        links.arrive(None, got, TWIN_W + i, twin)
        links.leave(sent)
        count = own.shape[0] // 3
        for m in range(3):
            rows = slice(m * count, (m + 1) * count)
            give[rows, :] = (own[rows, :] + got[rows, :].astype(F32)).astype(BF16)
            links.go(None, give.at[rows, :], face.at[rows, :], FACE_W + i * 3 + m, FACE_W + i * 3 + m, facing)
        merge(*pairs[i])
    merge(*pairs[2])
    merge(0, 0)
    merge(1, 0)
    for kind in range(2):
        for d in (1, 2, 3):
            zs = source(d)
            links.arrive(None, back[kind].at[zs], Z_BACK + kind * 4 + zs, across)


def expert_grad_out(links, piece, w_down, w_up, out_down, out_up, local_sem):
    x, c, z, y = place()
    facing, twin = device(1 - x, c, z, y), device(x, 1 - c, z, y)
    (own, give, got, face), target = ((w_down, out_down), (w_up, out_up))[piece // 3]
    count = own.shape[0] // 3
    rows = slice((piece % 3) * count, (piece % 3 + 1) * count)
    links.arrive(None, face.at[rows, :], FACE_W + piece, facing)
    face[rows, :] = (give[rows, :].astype(F32) + face[rows, :].astype(F32)).astype(BF16)
    there = target.at[pl.ds(pl.multiple_of((c * 3 + piece % 3) * count, 128), count), :]
    links.go(None, face.at[rows, :], there, TWIN_OUT + piece, TWIN_OUT + piece, twin)
    copy = pltpu.make_async_copy(face.at[rows, :], there, local_sem.at[8 + piece])
    copy.start()
    return copy


def expert_grads_arrive(links, out_down, out_up):
    x, c, z, y = place()
    for piece in range(6):
        target = (out_down, out_up)[piece // 3]
        count = target.shape[0] // 6
        there = target.at[pl.ds(pl.multiple_of(((1 - c) * 3 + piece % 3) * count, 128), count), :]
        links.arrive(None, there, TWIN_OUT + piece, device(x, 1 - c, z, y))


SENTC = 2 * D + 128


def combine(cot, lengths, columns, rows_t, hidden, normed2, gates, back_f, back_g, mixed, rb, small_t):
    gain_grad = jnp.zeros((1, D), F32)
    router_grad = jnp.zeros((128, D), F32)
    for s in range(MB):
        rows = slice(s * SEQ, (s + 1) * SEQ)
        live = live_column(lengths, s)
        first, second = routing(columns, s)
        first = jnp.where(first, 1.0, 0.0).astype(BF16)
        second = jnp.where(second, 1.0, 0.0).astype(BF16)
        given = jnp.concatenate([back_f[e, s * CAP : (s + 1) * CAP, :] for e in range(EXP)], axis=0)
        first_out = dot(first, given)
        second_out = dot(second, given)
        gate = gates[rows, :]
        grad = cot[rows, :].astype(F32)
        grad_live = jnp.where(live, grad, 0.0)
        state = hidden[rows, :]
        moe = gate * first_out + (1.0 - gate) * second_out
        mixed[rows, :] = (state + jnp.where(live, moe, 0.0)).astype(BF16)
        tilt = jnp.sum(grad_live * first_out, axis=-1, keepdims=True) - jnp.sum(
            grad_live * second_out, axis=-1, keepdims=True
        )
        tilt = tilt * gate * (1.0 - gate)
        one, two = named(columns, s)
        hot = jnp.where(one, 1.0, 0.0) - jnp.where(two, 1.0, 0.0)
        grad_logits = tilt * hot
        high = grad_logits.astype(BF16)
        low = (grad_logits - high.astype(F32)).astype(BF16)
        router_grad = router_grad + dot(high, normed2[rows, :], 0, 0) + dot(low, normed2[rows, :], 0, 0)
        given = jnp.concatenate([back_g[e, s * CAP : (s + 1) * CAP, :] for e in range(EXP)], axis=0)
        grad_low = jnp.where(live, dot(first + second, given), 0.0)
        for e in range(EXP):
            grad_low = grad_low + grad_logits[:, 2 + e : 3 + e] * rows_t[2 + e : 3 + e, :]
        factor = unit(state)
        scaled = state * factor
        gain_grad = gain_grad + jnp.sum(grad_low * scaled, axis=0, keepdims=True)
        grad_low = grad_low * rows_t[1:2, :]
        inner = jnp.mean(grad_low * scaled, axis=-1, keepdims=True)
        grad_state = grad + factor * (grad_low - scaled * inner)
        hidden[rows, :] = grad_state
        rb[rows, 3 * D : 4 * D] = jnp.where(live, grad_state, 0.0).astype(BF16)
    small_t[...] = router_grad
    small_t[1:2, :] = gain_grad


def attention_backward(x_ref, wall, rows_t, qkv, board, hidden, grad_att, rb, rel_rows, small_t, grad_tokens, midway, formed):
    grad_att[...] = dot(rb[:, 3 * D : 4 * D], wall[:, PROJ:HIGH], 1, 1).astype(BF16)
    midway()
    lane = lax.broadcasted_iota(jnp.int32, (SEQ, 128), 1)
    ahead = lax.broadcasted_iota(jnp.int32, (SEQ, 128), 0)
    flip = jnp.where(ahead + lane == SEQ - 1, 1.0, 0.0).astype(BF16)
    flip = jnp.concatenate([flip] * MB, axis=1)

    def pair(p, carry):
        blocks = pl.ds(pl.multiple_of(p * SEQ, SEQ), SEQ)
        scores = [[None] * MB, [None] * MB]
        for s in range(MB):
            rows = slice(s * SEQ, (s + 1) * SEQ)
            cols = [pl.ds(pl.multiple_of(i * D + p * 128, 128), 128) for i in range(3)]
            q, k, v = (qkv[rows, cols[i]] for i in range(3))
            grad = grad_att[rows, cols[0]]
            grads = [[], [], []]
            for j in range(2):
                mine = (lane < HEAD) if j == 0 else (lane >= HEAD)
                share = board[blocks, (2 + 2 * s + j) * SEQ : (3 + 2 * s + j) * SEQ]
                grad_probs = dot(jnp.where(mine, grad, jnp.zeros_like(grad)), v, 1, 1)
                inner = jnp.sum(share * grad_probs, axis=-1, keepdims=True)
                grad_scores = (share * (grad_probs - inner)).astype(BF16)
                scores[j][s] = grad_scores
                grads[0].append(dot(grad_scores, k) * SCALE)
                grads[1].append(dot(grad_scores, q, 0, 0) * SCALE)
                grads[2].append(dot(share.astype(BF16), grad, 0, 0))
            for i in range(3):
                rb[rows, cols[i]] = jnp.where(lane < HEAD, grads[i][0], grads[i][1]).astype(BF16)
        for j in range(2):
            flipped = dot(flip, jnp.concatenate(scores[j], axis=0))
            rolled = pltpu.roll(flipped, 1, 1, stride=1, stride_axis=0)
            rel_rows[pl.ds(2 * p + j, 1), :] = jnp.sum(rolled, axis=0, keepdims=True)
        return carry

    for t in range(3):
        lax.fori_loop(2 * t, 2 * t + 2, pair, 0)
        formed[t]()
    grad_low = dot(rb[:, 0:LEFTC], wall[:, 0:LEFTC], 1, 1) + dot(
        rb[:, LEFTC : 3 * D], wall[:, HIGH:WALL], 1, 1
    )
    state = x_ref[...].astype(F32)
    factor = unit(state)
    scaled = state * factor
    small_t[0:1, :] = jnp.sum(grad_low * scaled, axis=0, keepdims=True)
    grad_low = grad_low * rows_t[0:1, :]
    inner = jnp.mean(grad_low * scaled, axis=-1, keepdims=True)
    grad_tokens[...] = hidden[...] + factor * (grad_low - scaled * inner)

    spot = lax.broadcasted_iota(jnp.int32, (SEQ, D), 0)
    column = lax.broadcasted_iota(jnp.int32, (SEQ, D), 1)
    distance = (SEQ - spot) & (SEQ - 1)
    picks = jnp.where(column == (distance >> 4) * SHARD + (distance & 15), 1.0, 0.0).astype(BF16)
    rest = rel_rows[...]
    spread = jnp.zeros((16, D), F32)
    for _ in range(3):
        high = rest.astype(BF16)
        spread = spread + dot(high, picks)
        rest = rest - high.astype(F32)
    small_t[HEAD : HEAD + 16, :] = spread


HC = D // 2
SMALLS = SENTC - 128


def portions(group):
    if group == 0:
        return 1, 2 * HC, HC, ((0, HC, lambda core: 3 * D + core * HC, lambda core: core * HC),)
    t = group - 1
    both = (
        (0, 256, lambda core: core * D + 256 * t, lambda core: core * D + 256 * t),
        (256, 128, lambda core: 2 * D + 256 * t + 128 * core, lambda core: 2 * D + 256 * t + 128 * core),
    )
    return 0, (0, HC, 3 * HC)[t], HC + 128 * (t == 2), both


class Reduction:
    def __init__(self, links, group, left, rb, small_t, give, take, total, y_take, z_take, face_give, face_take, last):
        self.links, self.group = links, group
        which, first, width, portion = portions(group)
        self.cols = slice(first, first + width)
        self.core_cols = slice(first, first + HC)
        self.portion = [(slice(first + at, first + at + wide), wide, rhs, target) for at, wide, rhs, target in portion]
        self.lhs, self.rb, self.small_t = left.at[which], rb, small_t
        self.give, self.take, self.total = give, take, total
        self.y_take, self.z_take, self.face_give, self.face_take, self.last = y_take, z_take, face_give, face_take, last
        x, c, z, y = self.place = place()
        self.across, self.facing, self.twin = device(x, c, z, 1 - y), device(1 - x, c, z, y), device(x, 1 - c, z, y)
        mirror = z // 2
        near = z + mirror * (3 - 2 * z)
        self.order = [o + mirror * (3 - 2 * o) for o in (3, 2, 1 - near, near)]

    def tile(self, core, keep):
        def step(m, carry):
            rows = pl.ds(pl.multiple_of(m * 256, 256), 256)
            for cols, wide, rhs, target in self.portion:
                right = self.rb[:, pl.ds(pl.multiple_of(rhs(core), 128), wide)]
                keep[rows, cols] = dot(self.lhs[:, rows], right, 0, 0).astype(keep.dtype)
            return carry

        lax.fori_loop(0, 3, step, 0)

    def form(self):
        x, c, z, y = self.place
        self.tile(1 - c, self.give)
        self.sent = [self.to_twin(self.core_cols, RS_TWIN + self.group)]
        self.tile(c, self.total)

    def to_twin(self, cols, slot):
        return self.links.go(None, self.give.at[:, cols], self.take.at[:, cols], slot, slot, self.twin)

    def form_small(self):
        small = jnp.transpose(self.small_t[...])
        self.give[:, SMALLS:SENTC] = small.astype(BF16)
        self.total[:, SMALLS:SENTC] = small.astype(BF16).astype(F32)
        self.sent.append(self.to_twin(slice(SMALLS, SENTC), RS_TWIN + 4))

    def shard(self, zs, ys):
        return pl.ds(pl.multiple_of((zs * 2 + ys) * SHARD, 16), SHARD)

    def halve(self):
        x, c, z, y = self.place
        links, cols = self.links, self.cols
        links.arrive(None, self.take.at[:, self.core_cols], RS_TWIN + self.group, self.twin)
        if self.group == 3:
            links.arrive(None, self.take.at[:, SMALLS:SENTC], RS_TWIN + 4, self.twin)
        for copy in self.sent:
            links.leave(copy)
        for zs in self.order:
            rows = self.shard(zs, 1 - y)
            self.give[rows, cols] = (self.total[rows, cols] + self.take[rows, cols].astype(F32)).astype(BF16)
            slot = RS_Y + self.group * 4 + zs
            links.go(None, self.give.at[rows, cols], self.y_take.at[zs, :, cols], slot, slot, self.across)
        for zs in self.order:
            rows = self.shard(zs, y)
            self.total[rows, cols] = self.total[rows, cols] + self.take[rows, cols].astype(F32)

    def chain(self, k):
        x, c, z, y = self.place
        links, cols, zs = self.links, self.cols, self.order[k]
        total, z_take = self.total, self.z_take
        rows = self.shard(zs, y)
        links.arrive(None, self.y_take.at[zs, :, cols], RS_Y + self.group * 4 + zs, self.across)
        total[rows, cols] = total[rows, cols] + self.y_take[zs, :, cols].astype(F32)
        if k == 3:
            return
        for cond, more, slot, target in (
            (zs > z, z > 0, zs, device(x, c, z + 1, y)),
            (zs < z, z < 3, 4 + zs, device(x, c, z - 1, y)),
        ):
            self.add_from_z(cond & more, slot, rows)

            @pl.when(cond)
            def _():
                self.give[rows, cols] = total[rows, cols].astype(BF16)

            index = RS_Z + self.group * 8 + slot
            links.go(cond, self.give.at[rows, cols], z_take.at[slot, :, cols], index, index, target)

    def add_from_z(self, cond, slot, rows):
        cols = self.cols

        @pl.when(cond)
        def _():
            part = self.z_take.at[slot, :, cols]
            self.links.arrive(None, part, RS_Z + self.group * 8 + slot, self.across)
            self.total[rows, cols] = self.total[rows, cols] + part[...].astype(F32)

    def face(self):
        x, c, z, y = self.place
        rows, cols = self.shard(z, y), self.cols
        self.add_from_z(z > 0, z, rows)
        self.add_from_z(z < 3, 4 + z, rows)
        self.face_give[:, cols] = self.total[rows, cols].astype(BF16)
        slot = RS_FACE + self.group
        self.links.go(None, self.face_give.at[:, cols], self.face_take.at[:, cols], slot, slot, self.facing)

    def publish(self, out_qkv, out_proj, out_small, local_sem):
        x, c, z, y = self.place
        cols = self.cols
        self.links.arrive(None, self.face_take.at[:, cols], RS_FACE + self.group, self.facing)
        self.last[:, cols] = self.face_give[:, cols].astype(F32) + self.face_take[:, cols].astype(F32)
        self.out = out_proj if self.group == 0 else out_qkv
        copies = []
        for i, (part, there) in enumerate(self.landing(c)):
            slot = RS_OUT + self.group * 2 + i
            self.links.go(None, part, there, slot, slot, self.twin)
            copies.append(pltpu.make_async_copy(part, there, local_sem.at[16 + self.group * 2 + i]))
        if self.group == 3:
            copies.append(pltpu.make_async_copy(self.last.at[:, SMALLS:SENTC], out_small, local_sem.at[6]))
        for copy in copies:
            copy.start()
        return copies

    def landing(self, core):
        return [
            (self.last.at[:, cols], self.out.at[:, pl.ds(pl.multiple_of(target(core), 128), wide)])
            for cols, wide, rhs, target in self.portion
        ]

    def landed(self):
        x, c, z, y = self.place
        for i, (part, there) in enumerate(self.landing(1 - c)):
            self.links.arrive(None, there, RS_OUT + self.group * 2 + i, self.twin)


def layer(
    x_in, cot_in, lengths, routes, slots, gain_attn, gain_moe, router_t, rel, wq, wp, w_up, w_down,
    mixed_out, tokens_out, out_qkv, out_proj, out_small, out_up, out_down,
    x_ref, cot, mixed, grad_tokens, board,
    wall, rows_t, lines, columns, left, qkv, hidden, normed2, gates, out_f, out_g, recv_f, recv_g, up, down, act, slope,
    part_f, part_g, take_f, take_g, back_f, back_g, dn_own, dn_give, dn_take, dn_face, up_own, up_give, up_take, up_face,
    rb, rel_rows, small_t, take, total, y_take, z_take, face_give, face_take, last,
    local_sem, send_sem, recv_sem,
):
    inputs = [
        pltpu.make_async_copy(x_in, x_ref, local_sem.at[24]),
        pltpu.make_async_copy(cot_in, cot, local_sem.at[25]),
    ]
    fetch = [
        pltpu.make_async_copy(w_up.at[0], up, local_sem.at[4]),
        pltpu.make_async_copy(w_down.at[0], down, local_sem.at[5]),
    ]
    pack(gain_attn, gain_moe, router_t, rel, board, wall)
    greet()
    links = Links(send_sem, recv_sem)
    later = gather_weights(links, wq, wp, wall, local_sem, inputs + fetch)
    stand(routes, slots, lines, columns)
    rel_rows[...] = jnp.zeros_like(rel_rows)
    for copy in inputs:
        copy.wait()
    normed, attended = left.at[0], left.at[1]
    attention_forward(
        later, x_ref, cot, lengths, columns, wall, rows_t, board, normed, qkv, attended, hidden, normed2, gates, out_f, out_g
    )
    for copy in fetch:
        copy.wait()
    downs, ups = (dn_own, dn_give, dn_take, dn_face), (up_own, up_give, up_take, up_face)
    experts(
        links, (out_f, out_g), (recv_f, recv_g), up, down, act, slope, (part_f, part_g), (take_f, take_g),
        (back_f, back_g), downs, ups,
    )
    combine(cot, lengths, columns, rows_t, hidden, normed2, gates, back_f, back_g, mixed, rb, small_t)
    pending = []

    def put(src, dst, i):
        copy = pltpu.make_async_copy(src, dst, local_sem.at[i])
        copy.start()
        pending.append(copy)

    put(mixed, mixed_out, 26)
    proj, one, two, three = (
        Reduction(
            links, group, left, rb, small_t, act.at[0:D, :], take, total, y_take, z_take, face_give, face_take, last
        )
        for group in range(4)
    )

    def grads(piece):
        pending.append(expert_grad_out(links, piece, downs, ups, out_down, out_up, local_sem))

    def publish(item):
        pending.extend(item.publish(out_qkv, out_proj, out_small, local_sem))

    def early():
        one.form()
        proj.chain(0)

    def middle():
        one.halve()
        two.form()
        proj.chain(1)

    def late():
        two.halve()
        three.form()
        proj.chain(2)
        one.chain(0)

    proj.form()
    attention_backward(
        x_ref, wall, rows_t, qkv, board, hidden, normed2, rb, rel_rows, small_t, grad_tokens, proj.halve,
        (early, middle, late),
    )
    three.form_small()
    put(grad_tokens, tokens_out, 27)
    proj.chain(3)
    one.chain(1)
    three.halve()
    two.chain(0)
    one.chain(2)
    grads(0)
    proj.face()
    two.chain(1)
    one.chain(3)
    grads(1)
    three.chain(0)
    two.chain(2)
    grads(2)
    one.face()
    three.chain(1)
    two.chain(3)
    grads(3)
    three.chain(2)
    two.face()
    grads(4)
    three.chain(3)
    grads(5)
    three.face()
    items = (proj, one, two, three)
    for item in items:
        publish(item)
    for item in items:
        item.landed()
    expert_grads_arrive(links, out_down, out_up)
    for copy in pending:
        copy.wait()
    links.finish()


def hand_out(
    mixed, tokens, qkv, proj, small, up, down,
    to_mixed, to_tokens, to_qkv, to_proj, to_gain_attn, to_gain_moe, to_router, to_rel, to_up, to_down,
):
    to_mixed[...] = mixed[...]
    to_tokens[...] = tokens[...]
    to_qkv[...] = qkv[...]
    to_proj[...] = proj[...]
    to_up[...] = up[...].astype(F32)
    to_down[...] = down[...].astype(F32)

    @pl.when(pl.program_id(0) == 0)
    def _():
        turned = jnp.transpose(small[...])
        to_gain_attn[...] = turned[0]
        to_gain_moe[...] = turned[1]
        to_router[...] = turned[2 : 2 + EXP]
        to_rel[...] = small[0:16, HEAD : HEAD + HEADS]


def rows_of(shape, steps):
    return pl.BlockSpec((shape[0] // steps, shape[1]), lambda i: (i, 0))


def body_fast(
    tokens, cotangent, lengths, routes, slots, gain_attn, w_qkv, w_proj, rel_table, gain_moe, w_router, w_up, w_down
):
    vm = pl.BlockSpec(memory_space=pltpu.VMEM)
    hbm = pl.BlockSpec(memory_space=pl.ANY)
    sds = jax.ShapeDtypeStruct
    v = pltpu.VMEM
    shapes = (
        sds((TOK, D), BF16), sds((TOK, D), F32), sds((SHARD, 3 * D), F32), sds((SHARD, D), F32),
        sds((SHARD, 128), F32), sds((D, HF), BF16), sds((HF, D), BF16),
    )
    out = pl.pallas_call(
        layer,
        out_shape=shapes,
        in_specs=[hbm, hbm, pl.BlockSpec(memory_space=pltpu.SMEM), vm, vm, vm, vm, vm, vm, hbm, hbm, hbm, hbm],
        out_specs=[hbm, hbm, hbm, hbm, hbm, hbm, hbm],
        scratch_shapes=[
            v((TOK, D), BF16), v((TOK, D), BF16), v((TOK, D), BF16), v((TOK, D), F32), v((D, D), F32),
            v((D, WALL), BF16), v((8, D), F32), v((8, TOK), F32), v((TOK, 8), F32), v((2, TOK, D), BF16),
            v((TOK, 3 * D), BF16), v((TOK, D), F32), v((TOK, D), BF16),
            v((TOK, 1), F32), v((EXP, ROWS, D), BF16), v((EXP, ROWS, D), BF16),
            v((8 * ROWS, D), BF16), v((8 * ROWS, D), BF16), v((D, HF), BF16), v((HF, D), BF16),
            v((8 * ROWS, SENTC), BF16), v((8 * ROWS, HF), BF16),
            v((EXP, 2, ROWS, D), BF16), v((EXP, 2, ROWS, D), BF16), v((EXP, ROWS, D), BF16), v((EXP, ROWS, D), BF16),
            v((EXP, ROWS, D), BF16), v((EXP, ROWS, D), BF16),
            v((HF // 2, D), F32), v((HF // 2, D), BF16), v((HF // 2, D), BF16), v((HF // 2, D), BF16),
            v((D // 2, HF), F32), v((D // 2, HF), BF16), v((D // 2, HF), BF16), v((D // 2, HF), BF16),
            v((TOK, 4 * D), BF16), v((16, SEQ), F32), v((128, D), F32),
            v((D, SENTC), BF16), v((D, SENTC), F32), v((4, SHARD, SENTC), BF16), v((8, SHARD, SENTC), BF16),
            v((SHARD, SENTC), BF16), v((SHARD, SENTC), BF16), v((SHARD, SENTC), F32),
            pltpu.SemaphoreType.DMA((28,)), pltpu.SemaphoreType.DMA((LINKS,)), pltpu.SemaphoreType.DMA((LINKS,)),
        ],
        compiler_params=pltpu.CompilerParams(
            collective_id=0, has_side_effects=True, vmem_limit_bytes=67043328
        ),
        name="layer",
    )(
        tokens, cotangent, lengths, routes.T, slots.T, gain_attn[None], gain_moe[None], w_router.T, rel_table, w_qkv, w_proj,
        w_up, w_down,
    )
    steps = 4
    tall = [rows_of(item.shape, steps) for item in shapes]
    small_in = pl.BlockSpec((SHARD, 128), lambda i: (0, 0))
    small_out = [
        pl.BlockSpec((SHARD,), lambda i: (0,)), pl.BlockSpec((SHARD,), lambda i: (0,)),
        pl.BlockSpec((EXP, SHARD), lambda i: (0, 0)), pl.BlockSpec((16, HEADS), lambda i: (0, 0)),
    ]
    small = (sds((SHARD,), F32), sds((SHARD,), F32), sds((EXP, SHARD), F32), sds((16, HEADS), F32))
    mixed, grad_tokens, grad_qkv, grad_proj, grad_gain_attn, grad_gain_moe, grad_router, grad_rel, grad_up, grad_down = (
        pl.pallas_call(
            hand_out,
            out_shape=shapes[:4] + small + (sds((D, HF), F32), sds((HF, D), F32)),
            grid=(steps,),
            in_specs=tall[:4] + [small_in] + tall[5:],
            out_specs=tall[:4] + small_out + tall[5:],
            name="hand_out",
        )(*out)
    )
    return (
        mixed,
        grad_tokens,
        grad_gain_attn,
        grad_qkv,
        grad_proj,
        grad_rel,
        grad_gain_moe,
        grad_router.T,
        grad_up[None],
        grad_down[None],
    )


epsilon = 1e-06
exact_precision = lax.Precision.HIGHEST


def rms_norm(values, gain):
    factor = lax.rsqrt(jnp.mean(values * values, axis=-1, keepdims=True) + epsilon)
    return values * factor * gain


def distance_hot():
    places = jnp.arange(SEQ, dtype=jnp.int32)
    distance = jnp.clip(places[:, None] - places[None, :], 0, SEQ - 1).reshape(1, SEQ * SEQ)
    return (distance == places[:, None]).astype(jnp.bfloat16)


def bias_matrix(table, hot):
    flat = jnp.einsum("dh,dp->hp", table, hot, preferred_element_type=jnp.float32)
    return flat.reshape(table.shape[1], SEQ, SEQ)


def exact_gelu(values):
    return jax.nn.gelu(values, approximate=False)


def masked_scores(qkv_rows, bias, allowed, factor):
    raw = jnp.einsum(
        "qhd,khd->hqk", qkv_rows[:, 0], qkv_rows[:, 1], preferred_element_type=jnp.float32
    )
    return jnp.where(allowed[None], raw * factor + bias, -1e30)


def fetch_weights(gain_attn, w_qkv, w_proj, rel_table, gain_moe, w_router):
    rows, experts = w_router.shape
    spread = rel_table.shape[0]
    packed = jnp.concatenate(
        [gain_attn, gain_moe, w_router.reshape(-1), rel_table.reshape(-1)]
    )
    small = lax.all_gather(packed, "fsdp", axis=0, tiled=False)
    groups = small.shape[0]
    edge = 2 * rows + rows * experts
    return (
        small[:, :rows].reshape(-1),
        lax.all_gather(w_qkv, "fsdp", axis=0, tiled=True),
        lax.all_gather(w_proj, "fsdp", axis=0, tiled=True),
        small[:, edge:].reshape(groups * spread, HEADS),
        small[:, rows : 2 * rows].reshape(-1),
        small[:, 2 * rows : edge].reshape(groups * rows, experts),
    )


def body(
    tokens,
    cotangent,
    lengths,
    routes,
    slots,
    gain_attn,
    w_qkv,
    w_proj,
    rel_table,
    gain_moe,
    w_router,
    w_up,
    w_down,
):
    groups = lax.axis_size("fsdp")
    experts = groups // 2
    capacity = 2 * SEQ // experts
    factor = HEAD ** (-0.5)
    up_weight = w_up[0]
    down_weight = w_down[0]
    places = jnp.arange(SEQ, dtype=jnp.int32)
    causal = places[:, None] >= places[None, :]
    expert_ids = jnp.arange(experts, dtype=jnp.int32)
    saved = []
    mixed_parts = []
    weights = fetch_weights(gain_attn, w_qkv, w_proj, rel_table, gain_moe, w_router)
    gain_a = weights[0].astype(jnp.float32)
    gain_m = weights[4].astype(jnp.float32)
    router_float = weights[5].astype(jnp.float32)
    hot = distance_hot()
    bias = bias_matrix(weights[3], hot)
    for batch in range(MB):
        x_float = tokens[batch * SEQ : (batch + 1) * SEQ].astype(jnp.float32)
        live_keys = places < lengths[batch]
        live_col = live_keys.astype(jnp.float32)[:, None]
        allowed = causal & live_keys[None, :]
        normed = rms_norm(x_float, gain_a).astype(jnp.bfloat16)
        qkv_rows = (
            jnp.dot(normed, weights[1], preferred_element_type=jnp.float32)
            .astype(jnp.bfloat16)
            .reshape(SEQ, 3, HEADS, HEAD)
        )
        scores = masked_scores(qkv_rows, bias, allowed, factor)
        row_peak = jnp.max(scores, axis=-1, keepdims=True)
        exp_scores = jnp.exp(scores - row_peak)
        row_total = jnp.sum(exp_scores, axis=-1, keepdims=True)
        log_total = row_peak + jnp.log(row_total)
        probs_low = (exp_scores / row_total).astype(jnp.bfloat16)
        attended = jnp.einsum(
            "hqk,khd->qhd", probs_low, qkv_rows[:, 2], preferred_element_type=jnp.float32
        )
        attended = attended.astype(jnp.bfloat16).reshape(SEQ, D)
        branch = jnp.dot(attended, weights[2], preferred_element_type=jnp.float32)
        hidden = x_float + live_col * branch
        normed2 = rms_norm(hidden, gain_m).astype(jnp.bfloat16)
        logits = jnp.dot(normed2, weights[5], preferred_element_type=jnp.float32)
        route_rows = routes[batch * SEQ : (batch + 1) * SEQ]
        slot_rows = slots[batch * SEQ : (batch + 1) * SEQ]
        hot_first = (route_rows[:, 0:1] == expert_ids[None, :]).astype(jnp.float32)
        hot_second = (route_rows[:, 1:2] == expert_ids[None, :]).astype(jnp.float32)
        gate_first = jax.nn.sigmoid(
            jnp.sum(logits * hot_first, axis=-1) - jnp.sum(logits * hot_second, axis=-1)
        )
        row_place = route_rows * capacity + slot_rows
        target = jnp.where(live_keys[:, None], row_place, experts * capacity)
        outgoing = jnp.zeros((experts * capacity, D), jnp.bfloat16)
        outgoing = (
            outgoing.at[target[:, 0]]
            .set(normed2, mode="drop")
            .at[target[:, 1]]
            .set(normed2, mode="drop")
        )
        outgoing = jnp.repeat(outgoing.reshape(experts, capacity, D), 2, axis=0)
        expert_received = lax.all_to_all(outgoing, "fsdp", split_axis=0, concat_axis=0, tiled=True)
        expert_before = jnp.einsum(
            "scd,df->scf", expert_received, up_weight, preferred_element_type=jnp.float32
        )
        expert_active = exact_gelu(expert_before).astype(jnp.bfloat16)
        partial_value = jnp.einsum(
            "scf,fd->scd", expert_active, down_weight, preferred_element_type=jnp.float32
        ).astype(jnp.bfloat16)
        returned = lax.all_to_all(partial_value, "fsdp", split_axis=0, concat_axis=0, tiled=True)
        results = (returned, expert_received, expert_before)
        combined = (
            results[0]
            .astype(jnp.float32)
            .reshape(experts, 2, capacity, D)
            .sum(axis=1)
            .reshape(experts * capacity, D)
        )
        first_out = combined[row_place[:, 0]]
        second_out = combined[row_place[:, 1]]
        moe = live_col * (
            gate_first[:, None] * first_out + (1.0 - gate_first)[:, None] * second_out
        )
        mixed_parts.append((hidden + moe).astype(jnp.bfloat16))
        saved.append(
            {
                "normed": normed,
                "qkv_rows": qkv_rows,
                "log_total": log_total,
                "attended": attended,
                "hidden": hidden,
                "normed2": normed2,
                "gate_first": gate_first,
                "first_out": first_out,
                "second_out": second_out,
                "results": results,
                "target": target,
                "row_place": row_place,
                "hot_first": hot_first,
                "hot_second": hot_second,
            }
        )
    grad_qkv_w = jnp.zeros((D, 3 * D), jnp.float32)
    grad_proj_w = jnp.zeros((D, D), jnp.float32)
    grad_table = jnp.zeros((SEQ, HEADS), jnp.float32)
    grad_gain_a = jnp.zeros((D,), jnp.float32)
    grad_gain_m = jnp.zeros((D,), jnp.float32)
    grad_router = jnp.zeros((D, experts), jnp.float32)
    grad_up = jnp.zeros((D, FF // 2), jnp.float32)
    grad_down = jnp.zeros((FF // 2, D), jnp.float32)
    grad_parts = [None] * MB
    for batch in reversed(range(MB)):
        kept = saved[batch]
        x_float = tokens[batch * SEQ : (batch + 1) * SEQ].astype(jnp.float32)
        live_keys = places < lengths[batch]
        live_col = live_keys.astype(jnp.float32)[:, None]
        allowed = causal & live_keys[None, :]
        grad_out = cotangent[batch * SEQ : (batch + 1) * SEQ].astype(jnp.float32)
        grad_moe = live_col * grad_out
        gate_first = kept["gate_first"]
        gate_second = 1.0 - gate_first
        grad_gate_first = jnp.sum(grad_moe * kept["first_out"], axis=-1)
        grad_gate_second = jnp.sum(grad_moe * kept["second_out"], axis=-1)
        grad_first = (gate_first[:, None] * grad_moe).astype(jnp.bfloat16)
        grad_second = (gate_second[:, None] * grad_moe).astype(jnp.bfloat16)
        target = kept["target"]
        grad_send = jnp.zeros((experts * capacity, D), jnp.bfloat16)
        grad_send = (
            grad_send.at[target[:, 0]]
            .set(grad_first, mode="drop")
            .at[target[:, 1]]
            .set(grad_second, mode="drop")
        )
        grad_send = jnp.repeat(grad_send.reshape(experts, capacity, D), 2, axis=0)
        grad_recv = lax.all_to_all(grad_send, "fsdp", split_axis=0, concat_axis=0, tiled=True)
        received = kept["results"][1]
        before = kept["results"][2]
        active, gelu_back = jax.vjp(exact_gelu, before)
        active_low = active.astype(jnp.bfloat16)
        grad_active = jnp.einsum(
            "scd,fd->scf", grad_recv, down_weight, preferred_element_type=jnp.float32
        )
        grad_before = gelu_back(grad_active)[0].astype(jnp.bfloat16)
        grad_down = grad_down + jnp.einsum(
            "scf,scd->fd", active_low, grad_recv, preferred_element_type=jnp.float32
        )
        grad_up = grad_up + jnp.einsum(
            "scd,scf->df", received, grad_before, preferred_element_type=jnp.float32
        )
        grad_part = jnp.einsum(
            "scf,df->scd", grad_before, up_weight, preferred_element_type=jnp.float32
        ).astype(jnp.bfloat16)
        grad_back = lax.all_to_all(grad_part, "fsdp", split_axis=0, concat_axis=0, tiled=True)
        grad_rows = (
            grad_back.astype(jnp.float32)
            .reshape(experts, 2, capacity, D)
            .sum(axis=1)
            .reshape(experts * capacity, D)
        )
        row_place = kept["row_place"]
        grad_diff = (grad_gate_first - grad_gate_second) * gate_first * gate_second
        grad_logits = grad_diff[:, None] * (kept["hot_first"] - kept["hot_second"])
        normed2_float = kept["normed2"].astype(jnp.float32)
        grad_router = grad_router + jnp.dot(normed2_float.T, grad_logits, precision=exact_precision)
        grad_normed2 = live_col * (grad_rows[row_place[:, 0]] + grad_rows[row_place[:, 1]])
        grad_normed2 = grad_normed2 + jnp.dot(
            grad_logits, router_float.T, precision=exact_precision
        )
        _, norm_back_moe = jax.vjp(rms_norm, kept["hidden"], gain_m)
        grad_hidden_norm, grad_gain_part = norm_back_moe(grad_normed2)
        grad_gain_m = grad_gain_m + grad_gain_part
        grad_hidden = grad_out + grad_hidden_norm
        grad_branch = (live_col * grad_hidden).astype(jnp.bfloat16)
        grad_proj_w = grad_proj_w + jnp.einsum(
            "sd,se->de", kept["attended"], grad_branch, preferred_element_type=jnp.float32
        )
        grad_attended = jnp.einsum(
            "se,de->sd", grad_branch, weights[2], preferred_element_type=jnp.float32
        )
        grad_attended = grad_attended.astype(jnp.bfloat16).reshape(SEQ, HEADS, HEAD)
        qkv_rows = kept["qkv_rows"]
        scores = masked_scores(qkv_rows, bias, allowed, factor)
        probs = jnp.exp(scores - kept["log_total"])
        probs_low = probs.astype(jnp.bfloat16)
        grad_probs = jnp.einsum(
            "qhd,khd->hqk", grad_attended, qkv_rows[:, 2], preferred_element_type=jnp.float32
        )
        row_dot = jnp.sum(probs * grad_probs, axis=-1, keepdims=True)
        grad_scores = (probs * (grad_probs - row_dot)).astype(jnp.bfloat16)
        grad_table = grad_table + jnp.einsum(
            "dp,hp->dh",
            hot,
            jnp.where(allowed[None], grad_scores, 0).reshape(HEADS, SEQ * SEQ),
            preferred_element_type=jnp.float32,
        )
        grad_queries = (
            jnp.einsum(
                "hqk,khd->qhd", grad_scores, qkv_rows[:, 1], preferred_element_type=jnp.float32
            )
            * factor
        )
        grad_keys = (
            jnp.einsum(
                "hqk,qhd->khd", grad_scores, qkv_rows[:, 0], preferred_element_type=jnp.float32
            )
            * factor
        )
        grad_values = jnp.einsum(
            "hqk,qhd->khd", probs_low, grad_attended, preferred_element_type=jnp.float32
        )
        grad_qkv = (
            jnp.stack([grad_queries, grad_keys, grad_values], axis=1)
            .astype(jnp.bfloat16)
            .reshape(SEQ, 3 * D)
        )
        grad_qkv_w = grad_qkv_w + jnp.einsum(
            "sd,se->de", kept["normed"], grad_qkv, preferred_element_type=jnp.float32
        )
        grad_normed = jnp.einsum(
            "se,de->sd", grad_qkv, weights[1], preferred_element_type=jnp.float32
        )
        _, norm_back_attn = jax.vjp(rms_norm, x_float, gain_a)
        grad_x_norm, grad_gain_piece = norm_back_attn(grad_normed)
        grad_gain_a = grad_gain_a + grad_gain_piece
        grad_parts[batch] = grad_hidden + grad_x_norm
    small = jnp.concatenate(
        [
            grad_gain_a.reshape(groups, -1),
            grad_gain_m.reshape(groups, -1),
            grad_router.reshape(groups, -1),
            grad_table.reshape(groups, -1),
        ],
        axis=1,
    )
    small = lax.psum_scatter(small, "fsdp", scatter_dimension=0, tiled=True)
    shards = (
        small,
        lax.psum_scatter(grad_qkv_w, "fsdp", scatter_dimension=0, tiled=True),
        lax.psum_scatter(grad_proj_w, "fsdp", scatter_dimension=0, tiled=True),
    )
    sums = lax.psum((shards[0], shards[1], shards[2], grad_up[None], grad_down[None]), "replica")
    rows = D // groups
    edge = 2 * rows + rows * experts
    totals = (
        sums[0][0, :rows],
        sums[1],
        sums[2],
        sums[0][0, edge:].reshape(SEQ // groups, HEADS),
        sums[0][0, rows : 2 * rows],
        sums[0][0, 2 * rows : edge].reshape(rows, experts),
        sums[3],
        sums[4],
    )
    mixed = jnp.concatenate(mixed_parts, axis=0)
    grad_tokens = jnp.concatenate(grad_parts, axis=0)
    return (
        mixed,
        grad_tokens,
        totals[0],
        totals[1],
        totals[2],
        totals[3],
        totals[4],
        totals[5],
        totals[6],
        totals[7],
    )


def solution(mesh):
    in_specs = (
        P(("replica", "fsdp"), None),
        P(("replica", "fsdp"), None),
        P(("replica", "fsdp")),
        P(("replica", "fsdp"), None),
        P(("replica", "fsdp"), None),
        P("fsdp"),
        P("fsdp", None),
        P("fsdp", None),
        P("fsdp", None),
        P("fsdp"),
        P("fsdp", None),
        P("fsdp", None, None),
        P("fsdp", None, None),
    )
    out_specs = (
        P(("replica", "fsdp"), None),
        P(("replica", "fsdp"), None),
        P("fsdp"),
        P("fsdp", None),
        P("fsdp", None),
        P("fsdp", None),
        P("fsdp"),
        P("fsdp", None),
        P("fsdp", None, None),
        P("fsdp", None, None),
    )
    fast = dict(mesh.shape) == {"replica": 4, "fsdp": 8}
    return jax.shard_map(body_fast if fast else body, mesh=mesh, in_specs=in_specs, out_specs=out_specs, check_vma=False)
```

```python
import functools

import jax
import jax.numpy as jnp
from jax import lax
from jax.experimental import pallas as pl
from jax.experimental.pallas import tpu as pltpu
from jax.sharding import PartitionSpec as P

D = 768
HEADS = 12
HEAD = 64
FF = 3072
SEQ = 128
MB = 2
MESH = pl.DeviceIdType.MESH
F32 = jnp.float32
BF16 = jnp.bfloat16
NEG = -1e30
HF = FF // 2
TOK = MB * SEQ
EXP = 4
CAP = 64
ROWS = MB * CAP
LOW = 896
MID = 3 * D - 2 * LOW
MORE = MID + 128
SMALL = LOW + MID
PROJ = LOW + MORE
HIGH = PROJ + D
WALL = HIGH + LOW
LEFTC = LOW + MID
SHARD = 96
HALF = SHARD // 2
PAIRS = HEADS // 2
SCALE = HEAD ** (-0.5)


def place():
    replica = lax.axis_index("replica")
    group = lax.axis_index("fsdp")
    return replica // 2, replica % 2, group // 2, group % 2


def device(x, c, z, y):
    return (x * 2 + c, z * 2 + y)


def remote(src, dst, send, recv, target):
    return pltpu.make_async_remote_copy(
        src_ref=src,
        dst_ref=dst,
        send_sem=send,
        recv_sem=recv,
        device_id=target,
        device_id_type=MESH,
    )


def greet():
    x, c, z, y = place()
    barrier = pltpu.get_barrier_semaphore()
    targets = [device(x, 1 - c, z, y), device(1 - x, c, z, y), device(x, c, z, 1 - y)]
    targets += [device(x, c, (z + k) % 4, y) for k in (1, 2, 3)]
    for target in targets:
        pl.semaphore_signal(barrier, inc=1, device_id=target, device_id_type=MESH)
    return lambda: pl.semaphore_wait(barrier, len(targets))


def dot(a, b, ca=1, cb=0):
    return lax.dot_general(a, b, (((ca,), (cb,)), ((), ())), preferred_element_type=F32)


def run(cond, what):
    if cond is None:
        what()
    else:
        pl.when(cond)(what)


class Links:
    def __init__(self, send_sem, recv_sem):
        self.send_sem, self.recv_sem = send_sem, recv_sem
        self.started = []

    def go(self, cond, src, dst, send, recv, target):
        copy = remote(src, dst, self.send_sem.at[send], self.recv_sem.at[recv], target)
        run(cond, copy.start)
        self.started.append((cond, copy))
        return copy

    def arrive(self, cond, dst, recv, target):
        run(cond, remote(dst, dst, self.send_sem.at[0], self.recv_sem.at[recv], target).wait_recv)

    def leave(self, copy):
        copy.wait_send()
        self.started = [(cond, item) for cond, item in self.started if item is not copy]

    def finish(self):
        for cond, copy in self.started:
            run(cond, copy.wait_send)
        self.started = []


def gather_weights(links, wq, wp, wall, local_sem, others, ready):
    x, c, z, y = place()
    own = pl.ds(pl.multiple_of((z * 2 + y) * SHARD, 16), SHARD)
    fills = [
        pltpu.make_async_copy(wq.at[:, pl.ds(0, LEFTC)], wall.at[own, pl.ds(0, LEFTC)], local_sem.at[0]),
        pltpu.make_async_copy(wq.at[:, pl.ds(LEFTC, LOW)], wall.at[own, pl.ds(HIGH, LOW)], local_sem.at[1]),
        pltpu.make_async_copy(wp, wall.at[own, pl.ds(PROJ, D)], local_sem.at[2]),
    ]
    for copy in fills + others:
        copy.start()
    ready()
    share = pl.ds(pl.multiple_of(x * HIGH, 128), LOW)
    gained = pl.ds(pl.multiple_of((1 - x) * HIGH, 128), LOW)
    columns = (share, pl.ds(LOW, MORE), pl.ds(PROJ, D))
    up, down = device(x, c, z + 1, y), device(x, c, z - 1, y)
    across, facing, twin = device(x, c, z, 1 - y), device(1 - x, c, z, y), device(x, 1 - c, z, y)

    def part(zs, ys, half, cols):
        return wall.at[pl.ds(pl.multiple_of((zs * 2 + ys) * SHARD + half * HALF, 16), HALF), cols]

    def go(cond, zs, ys, cols, send, recv, target, src=None):
        piece = part(zs, ys, c, cols)
        links.go(cond, piece if src is None else src, piece, send, recv, target)

    def arrive(cond, zs, ys, half, cols, recv):
        links.arrive(cond, part(zs, ys, half, cols), recv, twin)

    def spread(cond, sub, zs, ys):
        source = zs * 2 + ys
        if sub == 0:
            go(cond, zs, ys, share, 39 + source, 24 + source, facing)
        go(cond, zs, ys, columns[sub], 47 + sub * 8 + source, 32 + sub * 8 + source, twin)

    def begin(sub, src):
        go(z < 3, z, y, columns[sub], sub * 3, sub * 4 + z, up, src)
        go(z > 0, z, y, columns[sub], 9 + sub * 3, sub * 4 + z, down, src)
        go(None, z, y, columns[sub], 18 + sub * 7, 12 + sub * 4 + z, across, src)

    def along(sub, k):
        below, above = z - k, z + k
        for cond, zs, on, first, target, place_of in (
            (below >= 0, below, z < 3, 0, up, k),
            (above <= 3, above, z > 0, 9, down, 3 + k),
        ):
            arrive(cond, zs, y, c, columns[sub], sub * 4 + zs)
            if k < 3:
                go(cond & on, zs, y, columns[sub], first + sub * 3 + k, sub * 4 + zs, target)
            go(cond, zs, y, columns[sub], 18 + sub * 7 + place_of, 12 + sub * 4 + zs, across)
            spread(cond, sub, zs, y)

    def over(sub, k):
        if k == 0:
            arrive(None, z, 1 - y, c, columns[sub], 12 + sub * 4 + z)
            spread(None, sub, z, 1 - y)
            return
        for cond, zs in ((z - k >= 0, z - k), (z + k <= 3, z + k)):
            arrive(cond, zs, 1 - y, c, columns[sub], 12 + sub * 4 + zs)
            spread(cond, sub, zs, 1 - y)

    half = pl.ds(pl.multiple_of(c * HALF, 16), HALF)
    begin(0, wq.at[half, pl.ds(pl.multiple_of(x * LEFTC, 128), LOW)])
    for fill in fills:
        fill.wait()
    begin(1, None)
    for k in (1, 2, 3):
        for sub in range(2):
            along(sub, k)
            over(sub, k - 1)
        if k == 2:
            begin(2, wp.at[half, :])
    along(2, 1)
    for sub in range(2):
        over(sub, 3)

    def each(what):
        for zs in range(4):
            for ys in range(2):
                what((zs != z) | (ys != y), zs, ys, zs * 2 + ys)

    def gain(other, zs, ys, source):
        arrive(other, zs, ys, c, gained, 24 + source)
        go(other, zs, ys, gained, 71 + source, 56 + source, twin)

    def mostly(other, zs, ys, source):
        for sub in range(2):
            arrive(other, zs, ys, 1 - c, columns[sub], 32 + sub * 8 + source)
        arrive(other, zs, ys, 1 - c, gained, 56 + source)

    def rest(other, zs, ys, source):
        arrive(other, zs, ys, 1 - c, columns[2], 32 + 16 + source)

    each(gain)
    each(mostly)

    def first():
        along(2, 2)
        over(2, 0)

    def second():
        along(2, 3)
        over(2, 1)
        over(2, 2)

    return first, second, lambda: over(2, 3), lambda: each(rest)


def unit(values):
    return lax.rsqrt(jnp.mean(values * values, axis=-1, keepdims=True) + 1e-06)


def heads(rows):
    lane = lax.broadcasted_iota(jnp.int32, rows.shape, 1)
    none = jnp.zeros_like(rows)
    return jnp.concatenate([jnp.where(lane < HEAD, rows, none), jnp.where(lane < HEAD, none, rows)], axis=0)


def beside(blocks):
    return jnp.concatenate([blocks[0:SEQ], blocks[SEQ : 2 * SEQ]], axis=1)


def build_bias(wall, bias):
    table = jnp.concatenate(
        [wall[f * SHARD : f * SHARD + 16, SMALL : SMALL + 128] for f in range(8)], axis=0
    )
    ahead = lax.broadcasted_iota(jnp.int32, (SEQ, SEQ), 0)
    lane = lax.broadcasted_iota(jnp.int32, (SEQ, SEQ), 1)
    turned = jnp.where(ahead + lane == SEQ, 1.0, jnp.where(ahead + lane == 0, 1.0, 0.0)).astype(BF16)
    lines = dot(table, turned, 0, 0)
    for h in range(HEADS):
        line = jnp.broadcast_to(lines[HEAD + h : HEAD + h + 1, :], (SEQ, SEQ))
        rolled = pltpu.roll(line, 0, 1, stride=1, stride_axis=0)
        bias[h * SEQ : (h + 1) * SEQ, 0:SEQ] = jnp.where(ahead >= lane, rolled, NEG)


def pack(gain_attn, gain_moe, router_t, rel, board, wall):
    x, c, z, y = place()
    board[0:SEQ, 0:SEQ] = jnp.zeros((SEQ, SEQ), F32)
    board[0:1, 0:SHARD] = gain_attn[...].astype(F32)
    board[1:2, 0:SHARD] = gain_moe[...].astype(F32)
    board[2 : 2 + EXP, 0:SHARD] = router_t[...].astype(F32)
    turned = jnp.transpose(board[0:SEQ, 0:SEQ])
    board[0:SEQ, 0:SEQ] = turned
    board[0:16, HEAD : HEAD + HEADS] = rel[...].astype(F32)
    own = pl.ds(pl.multiple_of((z * 2 + y) * SHARD, 16), SHARD)
    wall[own, SMALL : SMALL + 128] = board[0:SHARD, 0:SEQ].astype(BF16)


def stand(routes, slots, lines, columns):
    chosen = routes[...]
    lines[...] = jnp.zeros_like(lines)
    lines[0:2, :] = (chosen * CAP + slots[...]).astype(F32)
    lines[2:4, :] = chosen.astype(F32)
    columns[...] = jnp.transpose(lines[...])


def routing(columns, s):
    spots = columns[s * SEQ : (s + 1) * SEQ, :]
    lane = lax.broadcasted_iota(jnp.int32, (SEQ, EXP * CAP), 1).astype(F32)
    return spots[:, 0:1] == lane, spots[:, 1:2] == lane


def named(columns, s):
    spots = columns[s * SEQ : (s + 1) * SEQ, :]
    lane = lax.broadcasted_iota(jnp.int32, (SEQ, 128), 1).astype(F32) - 2.0
    return spots[:, 2:3] == lane, spots[:, 3:4] == lane


def live_column(lengths, s):
    return lax.broadcasted_iota(jnp.int32, (SEQ, 1), 0) < lengths[s]


def attention_forward(
    later, x_ref, cot, lengths, columns, wall, rows_t, board, normed, qkv, attended, hidden, normed2, gates, out_f, out_g
):
    rows_t[...] = jnp.transpose(wall[:, SMALL : SMALL + 128].astype(F32))[0:8]
    build_bias(wall, board)
    x = x_ref[...].astype(F32)
    normed[...] = (x * unit(x) * rows_t[0:1, :]).astype(BF16)
    qkv[:, 0:LEFTC] = dot(normed[...], wall[:, 0:LEFTC]).astype(BF16)
    qkv[:, LEFTC : 3 * D] = dot(normed[...], wall[:, HIGH:WALL]).astype(BF16)
    lane = lax.broadcasted_iota(jnp.int32, (2 * SEQ, 128), 1)

    def pair(p, carry):
        blocks = pl.ds(pl.multiple_of(p * 2 * SEQ, SEQ), 2 * SEQ)
        for s in range(MB):
            rows = slice(s * SEQ, (s + 1) * SEQ)
            q = qkv[rows, pl.ds(pl.multiple_of(p * 128, 128), 128)]
            k = qkv[rows, pl.ds(pl.multiple_of(D + p * 128, 128), 128)]
            v = qkv[rows, pl.ds(pl.multiple_of(2 * D + p * 128, 128), 128)]
            scores = jnp.where(lane < lengths[s], dot(heads(q), k, 1, 1) * SCALE + board[blocks, 0:SEQ], NEG)
            scores = jnp.exp(scores - jnp.max(scores, axis=-1, keepdims=True))
            share = scores * (1.0 / jnp.sum(scores, axis=-1, keepdims=True))
            board[blocks, (1 + s) * SEQ : (2 + s) * SEQ] = share
            attended[rows, pl.ds(pl.multiple_of(p * 128, 128), 128)] = dot(
                beside(share.astype(BF16)), heads(v)
            ).astype(BF16)
        return carry

    for t in range(3):
        later[t]()
        lax.fori_loop(2 * t, 2 * t + 2, pair, 0)
    later[3]()
    branch = dot(attended[...], wall[:, PROJ:HIGH])
    for s in range(MB):
        rows = slice(s * SEQ, (s + 1) * SEQ)
        live = live_column(lengths, s)
        state = x_ref[rows, :].astype(F32) + jnp.where(live, branch[rows, :], 0.0)
        hidden[rows, :] = state
        low = (state * unit(state) * rows_t[1:2, :]).astype(BF16)
        normed2[rows, :] = low
        logits = dot(low, wall[:, SMALL : SMALL + 128])
        one, two = named(columns, s)
        picked = jnp.where(one, logits, 0.0) - jnp.where(two, logits, 0.0)
        gate = jax.nn.sigmoid(jnp.sum(picked, axis=-1, keepdims=True))
        gates[rows, :] = gate
        grad = jnp.where(live, cot[rows, :].astype(F32), 0.0)
        first, second = routing(columns, s)
        first = jnp.where(first & live, 1.0, 0.0).astype(BF16)
        second = jnp.where(second & live, 1.0, 0.0).astype(BF16)
        sent = dot(first + second, low, 0, 0).astype(BF16)
        back = dot(first, (gate * grad).astype(BF16), 0, 0) + dot(
            second, ((1.0 - gate) * grad).astype(BF16), 0, 0
        )
        back = back.astype(BF16)
        for e in range(EXP):
            out_f[e, s * CAP : (s + 1) * CAP, :] = sent[e * CAP : (e + 1) * CAP, :]
            out_g[e, s * CAP : (s + 1) * CAP, :] = back[e * CAP : (e + 1) * CAP, :]


TILE = 512
Z_ROWS, Y_ROWS, Y_PART, Z_BACK = 80, 88, 96, 104
TWIN_W, FACE_W, TWIN_OUT = 112, 114, 120
RS_TWIN, RS_Y, RS_Z, RS_FACE, RS_OUT = 126, 131, 147, 179, 183
LINKS = 191


def quarter(zs):
    return pl.ds(pl.multiple_of(zs * 2 * ROWS, 2 * ROWS), 2 * ROWS)


def half_rows(zs, ys):
    return pl.ds(pl.multiple_of((zs * 2 + ys) * ROWS, ROWS), ROWS)


def expert_forward(zs, recv, up, down, act, slope, part):
    rows = quarter(zs)

    def tile(i, carry):
        cols = pl.ds(pl.multiple_of(i * TILE, TILE), TILE)
        before = dot(recv[rows, :], up[:, cols])
        below = 0.5 + 0.5 * lax.erf(before * 0.7071067811865476)
        act[rows, cols] = (before * below).astype(BF16)
        density = jnp.exp(before * before * -0.5) * 0.3989422804014327
        slope[rows, cols] = (below + before * density).astype(BF16)
        return carry

    lax.fori_loop(0, HF // TILE, tile, 0)
    got = dot(act[rows, 0:HF], down[...]).astype(BF16)
    part[zs, 0] = got[0:ROWS]
    part[zs, 1] = got[ROWS : 2 * ROWS]


def expert_backward(zs, recv, up, down, slope, part):
    rows = quarter(zs)

    def tile(i, carry):
        cols = pl.ds(pl.multiple_of(i * TILE, TILE), TILE)
        grad = dot(recv[rows, :], down[cols, :], 1, 1)
        slope[rows, cols] = (grad * slope[rows, cols].astype(F32)).astype(BF16)
        return carry

    lax.fori_loop(0, HF // TILE, tile, 0)
    got = dot(slope[rows, :], up[...], 1, 1).astype(BF16)
    part[zs, 0] = got[0:ROWS]
    part[zs, 1] = got[ROWS : 2 * ROWS]


def experts(links, out, recv, up, down, act, slope, part, take, back, w_down, w_up):
    x, c, z, y = place()
    across, facing, twin = device(x, c, z, 1 - y), device(1 - x, c, z, y), device(x, 1 - c, z, y)

    for kind in range(2):
        links.go(None, out[kind].at[z], recv[kind].at[half_rows(z, y), :], Y_ROWS + kind * 4, Y_ROWS + kind * 4 + z, across)
        for d in (1, 2, 3):
            to = (z + d) % 4
            links.go(
                None, out[kind].at[to], recv[kind].at[half_rows(z, y), :], Z_ROWS + kind * 4 + d,
                Z_ROWS + kind * 4 + z, device(x, c, to, y),
            )
        recv[kind][half_rows(z, y), :] = out[kind][z]

    def source(d):
        return (z + 4 - d) % 4

    def reach(kind, d):
        zs = source(d)
        rows = recv[kind].at[half_rows(zs, y), :]
        links.arrive(None, rows, Z_ROWS + kind * 4 + zs, across)
        links.go(None, rows, rows, Y_ROWS + kind * 4 + d, Y_ROWS + kind * 4 + zs, across)

    def compute(kind, d):
        zs = source(d)
        links.arrive(None, recv[kind].at[half_rows(zs, 1 - y), :], Y_ROWS + kind * 4 + zs, across)
        if kind == 0:
            expert_forward(zs, recv[0], up, down, act, slope, part[0])
        else:
            expert_backward(zs, recv[1], up, down, slope, part[1])

    def give_part(kind, d):
        zs = source(d)
        links.go(
            None, part[kind].at[zs, 1 - y], take[kind].at[zs], Y_PART + kind * 4 + d, Y_PART + kind * 4 + zs, across
        )

    def merge(kind, d):
        zs = source(d)
        links.arrive(None, take[kind].at[zs], Y_PART + kind * 4 + zs, across)
        total = (part[kind][zs, y].astype(F32) + take[kind][zs].astype(F32)).astype(BF16)
        if d == 0:
            back[kind][z] = total
        else:
            part[kind][zs, y] = total
            links.go(
                None, part[kind].at[zs, y], back[kind].at[z], Z_BACK + kind * 4 + d, Z_BACK + kind * 4 + z,
                device(x, c, zs, y),
            )

    reach(0, 1)
    compute(0, 0)
    reach(0, 2)
    compute(1, 0)
    reach(0, 3)
    compute(0, 1)
    reach(1, 1)
    give_part(0, 1)
    compute(0, 2)
    reach(1, 2)
    give_part(0, 2)
    compute(1, 1)
    reach(1, 3)
    give_part(1, 1)
    merge(0, 1)
    compute(0, 3)
    give_part(0, 3)
    merge(0, 2)
    compute(1, 2)
    give_part(1, 2)
    merge(1, 1)
    compute(1, 3)
    give_part(1, 3)
    give_part(0, 0)
    give_part(1, 0)

    def down_tile(i, part_of, keep):
        cols = pl.ds(pl.multiple_of(part_of * (HF // 2) + i * 256, 128), 256)
        got = dot(act[:, cols], recv[1][...], 0, 0)
        keep[pl.ds(pl.multiple_of(i * 256, 256), 256), :] = got.astype(keep.dtype)

    def up_tile(i, part_of, keep):
        cols = pl.ds(pl.multiple_of(part_of * (D // 2) + i * 128, 128), 128)
        got = dot(recv[0][:, cols], slope[...], 0, 0)
        keep[pl.ds(pl.multiple_of(i * 128, 128), 128), :] = got.astype(keep.dtype)

    def tiles(one, part_of, keep):
        def step(i, carry):
            one(i, part_of, keep)
            return carry

        lax.fori_loop(0, 3, step, 0)

    def spread(i, sent):
        own, give, got, face = (w_down, w_up)[i]
        links.arrive(None, got, TWIN_W + i, twin)
        links.leave(sent)
        count = own.shape[0] // 3
        for m in range(3):
            rows = slice(m * count, (m + 1) * count)
            give[rows, :] = (own[rows, :] + got[rows, :].astype(F32)).astype(BF16)
            links.go(None, give.at[rows, :], face.at[rows, :], FACE_W + i * 3 + m, FACE_W + i * 3 + m, facing)

    tiles(down_tile, 1 - c, w_down[1])
    sent = links.go(None, w_down[1], w_down[2], TWIN_W, TWIN_W, twin)
    merge(0, 3)
    tiles(down_tile, c, w_down[0])
    spread(0, sent)
    merge(1, 2)
    tiles(up_tile, 1 - c, w_up[1])
    sent = links.go(None, w_up[1], w_up[2], TWIN_W + 1, TWIN_W + 1, twin)
    merge(1, 3)
    tiles(up_tile, c, w_up[0])
    spread(1, sent)
    merge(0, 0)
    merge(1, 0)
    for kind in range(2):
        for d in (1, 2, 3):
            zs = source(d)
            links.arrive(None, back[kind].at[zs], Z_BACK + kind * 4 + zs, across)


def expert_grad_out(links, piece, w_down, w_up, out_down, out_up, local_sem):
    x, c, z, y = place()
    facing, twin = device(1 - x, c, z, y), device(x, 1 - c, z, y)
    (own, give, got, face), target = ((w_down, out_down), (w_up, out_up))[piece // 3]
    count = own.shape[0] // 3
    rows = slice((piece % 3) * count, (piece % 3 + 1) * count)
    links.arrive(None, face.at[rows, :], FACE_W + piece, facing)
    face[rows, :] = (give[rows, :].astype(F32) + face[rows, :].astype(F32)).astype(BF16)
    there = target.at[pl.ds(pl.multiple_of((c * 3 + piece % 3) * count, 128), count), :]
    links.go(None, face.at[rows, :], there, TWIN_OUT + piece, TWIN_OUT + piece, twin)
    copy = pltpu.make_async_copy(face.at[rows, :], there, local_sem.at[8 + piece])
    copy.start()
    return copy


def expert_grads_arrive(links, out_down, out_up):
    x, c, z, y = place()
    for piece in range(6):
        target = (out_down, out_up)[piece // 3]
        count = target.shape[0] // 6
        there = target.at[pl.ds(pl.multiple_of(((1 - c) * 3 + piece % 3) * count, 128), count), :]
        links.arrive(None, there, TWIN_OUT + piece, device(x, 1 - c, z, y))


SENTC = 2 * D + 128


def combine(cot, lengths, columns, rows_t, hidden, normed2, gates, back_f, back_g, mixed, rb, small_t):
    gain_grad = jnp.zeros((1, D), F32)
    router_grad = jnp.zeros((128, D), F32)
    for s in range(MB):
        rows = slice(s * SEQ, (s + 1) * SEQ)
        live = live_column(lengths, s)
        first, second = routing(columns, s)
        first = jnp.where(first, 1.0, 0.0).astype(BF16)
        second = jnp.where(second, 1.0, 0.0).astype(BF16)
        given = jnp.concatenate([back_f[e, s * CAP : (s + 1) * CAP, :] for e in range(EXP)], axis=0)
        first_out = dot(first, given)
        second_out = dot(second, given)
        gate = gates[rows, :]
        grad = cot[rows, :].astype(F32)
        grad_live = jnp.where(live, grad, 0.0)
        state = hidden[rows, :]
        moe = gate * first_out + (1.0 - gate) * second_out
        mixed[rows, :] = (state + jnp.where(live, moe, 0.0)).astype(BF16)
        tilt = jnp.sum(grad_live * first_out, axis=-1, keepdims=True) - jnp.sum(
            grad_live * second_out, axis=-1, keepdims=True
        )
        tilt = tilt * gate * (1.0 - gate)
        one, two = named(columns, s)
        hot = jnp.where(one, 1.0, 0.0) - jnp.where(two, 1.0, 0.0)
        grad_logits = tilt * hot
        high = grad_logits.astype(BF16)
        low = (grad_logits - high.astype(F32)).astype(BF16)
        router_grad = router_grad + dot(high, normed2[rows, :], 0, 0) + dot(low, normed2[rows, :], 0, 0)
        given = jnp.concatenate([back_g[e, s * CAP : (s + 1) * CAP, :] for e in range(EXP)], axis=0)
        grad_low = jnp.where(live, dot(first + second, given), 0.0)
        for e in range(EXP):
            grad_low = grad_low + grad_logits[:, 2 + e : 3 + e] * rows_t[2 + e : 3 + e, :]
        factor = unit(state)
        scaled = state * factor
        gain_grad = gain_grad + jnp.sum(grad_low * scaled, axis=0, keepdims=True)
        grad_low = grad_low * rows_t[1:2, :]
        inner = jnp.mean(grad_low * scaled, axis=-1, keepdims=True)
        grad_state = grad + factor * (grad_low - scaled * inner)
        hidden[rows, :] = grad_state
        rb[rows, 3 * D : 4 * D] = jnp.where(live, grad_state, 0.0).astype(BF16)
    small_t[...] = router_grad
    small_t[1:2, :] = gain_grad


def attention_backward(x_ref, wall, rows_t, qkv, board, hidden, grad_att, rb, rel_rows, small_t, grad_tokens, midway, formed):
    grad_att[...] = dot(rb[:, 3 * D : 4 * D], wall[:, PROJ:HIGH], 1, 1).astype(BF16)
    midway()
    lane = lax.broadcasted_iota(jnp.int32, (SEQ, 128), 1)
    ahead = lax.broadcasted_iota(jnp.int32, (SEQ, 128), 0)
    flip = jnp.where(ahead + lane == SEQ - 1, 1.0, 0.0).astype(BF16)
    flip = jnp.concatenate([flip] * MB, axis=1)

    def pair(p, carry):
        blocks = pl.ds(pl.multiple_of(p * 2 * SEQ, SEQ), 2 * SEQ)
        scores = []
        for s in range(MB):
            rows = slice(s * SEQ, (s + 1) * SEQ)
            cols = [pl.ds(pl.multiple_of(i * D + p * 128, 128), 128) for i in range(3)]
            q, k, v = (qkv[rows, cols[i]] for i in range(3))
            grad = heads(grad_att[rows, cols[0]])
            share = board[blocks, (1 + s) * SEQ : (2 + s) * SEQ]
            grad_probs = dot(grad, v, 1, 1)
            inner = jnp.sum(share * grad_probs, axis=-1, keepdims=True)
            grad_scores = (share * (grad_probs - inner)).astype(BF16)
            scores.append(beside(grad_scores))
            rb[rows, cols[0]] = (dot(scores[s], heads(k)) * SCALE).astype(BF16)
            rb[rows, cols[1]] = (dot(grad_scores, heads(q), 0, 0) * SCALE).astype(BF16)
            rb[rows, cols[2]] = dot(share.astype(BF16), grad, 0, 0).astype(BF16)
        flipped = dot(flip, jnp.concatenate(scores, axis=0))
        for j in range(2):
            rolled = pltpu.roll(flipped[:, j * SEQ : (j + 1) * SEQ], 1, 1, stride=1, stride_axis=0)
            rel_rows[pl.ds(2 * p + j, 1), :] = jnp.sum(rolled, axis=0, keepdims=True)
        return carry

    for t in range(3):
        lax.fori_loop(2 * t, 2 * t + 2, pair, 0)
        formed[t]()
    grad_low = dot(rb[:, 0:LEFTC], wall[:, 0:LEFTC], 1, 1) + dot(
        rb[:, LEFTC : 3 * D], wall[:, HIGH:WALL], 1, 1
    )
    state = x_ref[...].astype(F32)
    factor = unit(state)
    scaled = state * factor
    small_t[0:1, :] = jnp.sum(grad_low * scaled, axis=0, keepdims=True)
    grad_low = grad_low * rows_t[0:1, :]
    inner = jnp.mean(grad_low * scaled, axis=-1, keepdims=True)
    grad_tokens[...] = hidden[...] + factor * (grad_low - scaled * inner)

    spot = lax.broadcasted_iota(jnp.int32, (SEQ, D), 0)
    column = lax.broadcasted_iota(jnp.int32, (SEQ, D), 1)
    distance = (SEQ - spot) & (SEQ - 1)
    picks = jnp.where(column == (distance >> 4) * SHARD + (distance & 15), 1.0, 0.0).astype(BF16)
    rest = rel_rows[...]
    spread = jnp.zeros((16, D), F32)
    for _ in range(3):
        high = rest.astype(BF16)
        spread = spread + dot(high, picks)
        rest = rest - high.astype(F32)
    small_t[HEAD : HEAD + 16, :] = spread


HC = D // 2
SMALLS = SENTC - 128


def portions(group):
    if group == 0:
        return 1, 2 * HC, HC, ((0, HC, lambda core: 3 * D + core * HC, lambda core: core * HC),)
    t = group - 1
    both = (
        (0, 256, lambda core: core * D + 256 * t, lambda core: core * D + 256 * t),
        (256, 128, lambda core: 2 * D + 256 * t + 128 * core, lambda core: 2 * D + 256 * t + 128 * core),
    )
    return 0, (0, HC, 3 * HC)[t], HC + 128 * (t == 2), both


class Reduction:
    def __init__(self, links, group, left, rb, small_t, give, take, total, y_take, z_take, face_give, face_take, last):
        self.links, self.group = links, group
        which, first, width, portion = portions(group)
        self.cols = slice(first, first + width)
        self.core_cols = slice(first, first + HC)
        self.portion = [(slice(first + at, first + at + wide), wide, rhs, target) for at, wide, rhs, target in portion]
        self.lhs, self.rb, self.small_t = left.at[which], rb, small_t
        self.give, self.take, self.total = give, take, total
        self.y_take, self.z_take, self.face_give, self.face_take, self.last = y_take, z_take, face_give, face_take, last
        x, c, z, y = self.place = place()
        self.across, self.facing, self.twin = device(x, c, z, 1 - y), device(1 - x, c, z, y), device(x, 1 - c, z, y)
        mirror = z // 2
        near = z + mirror * (3 - 2 * z)
        self.order = [o + mirror * (3 - 2 * o) for o in (3, 2, 1 - near, near)]

    def tile(self, core, keep):
        def step(m, carry):
            rows = pl.ds(pl.multiple_of(m * 256, 256), 256)
            for cols, wide, rhs, target in self.portion:
                right = self.rb[:, pl.ds(pl.multiple_of(rhs(core), 128), wide)]
                keep[rows, cols] = dot(self.lhs[:, rows], right, 0, 0).astype(keep.dtype)
            return carry

        lax.fori_loop(0, 3, step, 0)

    def form(self):
        x, c, z, y = self.place
        self.tile(1 - c, self.give)
        self.sent = [self.to_twin(self.core_cols, RS_TWIN + self.group)]
        self.tile(c, self.total)

    def to_twin(self, cols, slot):
        return self.links.go(None, self.give.at[:, cols], self.take.at[:, cols], slot, slot, self.twin)

    def form_small(self):
        small = jnp.transpose(self.small_t[...])
        self.give[:, SMALLS:SENTC] = small.astype(BF16)
        self.total[:, SMALLS:SENTC] = small.astype(BF16).astype(F32)
        self.sent.append(self.to_twin(slice(SMALLS, SENTC), RS_TWIN + 4))

    def shard(self, zs, ys):
        return pl.ds(pl.multiple_of((zs * 2 + ys) * SHARD, 16), SHARD)

    def halve(self):
        x, c, z, y = self.place
        links, cols = self.links, self.cols
        links.arrive(None, self.take.at[:, self.core_cols], RS_TWIN + self.group, self.twin)
        if self.group == 3:
            links.arrive(None, self.take.at[:, SMALLS:SENTC], RS_TWIN + 4, self.twin)
        for copy in self.sent:
            links.leave(copy)
        for zs in self.order:
            rows = self.shard(zs, 1 - y)
            self.give[rows, cols] = (self.total[rows, cols] + self.take[rows, cols].astype(F32)).astype(BF16)
            slot = RS_Y + self.group * 4 + zs
            links.go(None, self.give.at[rows, cols], self.y_take.at[zs, :, cols], slot, slot, self.across)
        for zs in self.order:
            rows = self.shard(zs, y)
            self.total[rows, cols] = self.total[rows, cols] + self.take[rows, cols].astype(F32)

    def chain(self, k):
        x, c, z, y = self.place
        links, cols, zs = self.links, self.cols, self.order[k]
        total, z_take = self.total, self.z_take
        rows = self.shard(zs, y)
        links.arrive(None, self.y_take.at[zs, :, cols], RS_Y + self.group * 4 + zs, self.across)
        total[rows, cols] = total[rows, cols] + self.y_take[zs, :, cols].astype(F32)
        if k == 3:
            return
        for cond, more, slot, target in (
            (zs > z, z > 0, zs, device(x, c, z + 1, y)),
            (zs < z, z < 3, 4 + zs, device(x, c, z - 1, y)),
        ):
            self.add_from_z(cond & more, slot, rows)

            @pl.when(cond)
            def _():
                self.give[rows, cols] = total[rows, cols].astype(BF16)

            index = RS_Z + self.group * 8 + slot
            links.go(cond, self.give.at[rows, cols], z_take.at[slot, :, cols], index, index, target)

    def add_from_z(self, cond, slot, rows):
        cols = self.cols

        @pl.when(cond)
        def _():
            part = self.z_take.at[slot, :, cols]
            self.links.arrive(None, part, RS_Z + self.group * 8 + slot, self.across)
            self.total[rows, cols] = self.total[rows, cols] + part[...].astype(F32)

    def face(self):
        x, c, z, y = self.place
        rows, cols = self.shard(z, y), self.cols
        self.add_from_z(z > 0, z, rows)
        self.add_from_z(z < 3, 4 + z, rows)
        self.face_give[:, cols] = self.total[rows, cols].astype(BF16)
        slot = RS_FACE + self.group
        self.links.go(None, self.face_give.at[:, cols], self.face_take.at[:, cols], slot, slot, self.facing)

    def publish(self, out_qkv, out_proj, out_small, local_sem):
        x, c, z, y = self.place
        cols = self.cols
        self.links.arrive(None, self.face_take.at[:, cols], RS_FACE + self.group, self.facing)
        self.last[:, cols] = self.face_give[:, cols].astype(F32) + self.face_take[:, cols].astype(F32)
        self.out = out_proj if self.group == 0 else out_qkv
        copies = []
        for i, (part, there) in enumerate(self.landing(c)):
            slot = RS_OUT + self.group * 2 + i
            self.links.go(None, part, there, slot, slot, self.twin)
            copies.append(pltpu.make_async_copy(part, there, local_sem.at[16 + self.group * 2 + i]))
        if self.group == 3:
            copies.append(pltpu.make_async_copy(self.last.at[:, SMALLS:SENTC], out_small, local_sem.at[6]))
        for copy in copies:
            copy.start()
        return copies

    def landing(self, core):
        return [
            (self.last.at[:, cols], self.out.at[:, pl.ds(pl.multiple_of(target(core), 128), wide)])
            for cols, wide, rhs, target in self.portion
        ]

    def landed(self):
        x, c, z, y = self.place
        for i, (part, there) in enumerate(self.landing(1 - c)):
            self.links.arrive(None, there, RS_OUT + self.group * 2 + i, self.twin)


def layer(
    x_in, cot_in, lengths, routes, slots, gain_attn, gain_moe, router_t, rel, wq, wp, w_up, w_down,
    mixed_out, tokens_out, out_qkv, out_proj, out_small, out_up, out_down,
    x_ref, cot, mixed, grad_tokens, board,
    wall, rows_t, lines, columns, left, qkv, hidden, normed2, gates, out_f, out_g, recv_f, recv_g, up, down, act, slope,
    part_f, part_g, take_f, take_g, back_f, back_g, dn_own, dn_give, dn_take, dn_face, up_own, up_give, up_take, up_face,
    rb, rel_rows, small_t, take, total, y_take, z_take, face_give, face_take, last,
    local_sem, send_sem, recv_sem,
):
    inputs = [
        pltpu.make_async_copy(x_in, x_ref, local_sem.at[24]),
        pltpu.make_async_copy(cot_in, cot, local_sem.at[25]),
    ]
    fetch = [
        pltpu.make_async_copy(w_up.at[0], up, local_sem.at[4]),
        pltpu.make_async_copy(w_down.at[0], down, local_sem.at[5]),
    ]
    met = greet()
    links = Links(send_sem, recv_sem)

    def ready():
        pack(gain_attn, gain_moe, router_t, rel, board, wall)
        stand(routes, slots, lines, columns)
        rel_rows[...] = jnp.zeros_like(rel_rows)
        met()

    later = gather_weights(links, wq, wp, wall, local_sem, inputs + fetch, ready)
    for copy in inputs:
        copy.wait()
    normed, attended = left.at[0], left.at[1]
    attention_forward(
        later, x_ref, cot, lengths, columns, wall, rows_t, board, normed, qkv, attended, hidden, normed2, gates, out_f, out_g
    )
    for copy in fetch:
        copy.wait()
    downs, ups = (dn_own, dn_give, dn_take, dn_face), (up_own, up_give, up_take, up_face)
    experts(
        links, (out_f, out_g), (recv_f, recv_g), up, down, act, slope, (part_f, part_g), (take_f, take_g),
        (back_f, back_g), downs, ups,
    )
    combine(cot, lengths, columns, rows_t, hidden, normed2, gates, back_f, back_g, mixed, rb, small_t)
    pending = []

    def put(src, dst, i):
        copy = pltpu.make_async_copy(src, dst, local_sem.at[i])
        copy.start()
        pending.append(copy)

    put(mixed, mixed_out, 26)
    proj, one, two, three = (
        Reduction(
            links, group, left, rb, small_t, act.at[0:D, :], take, total, y_take, z_take, face_give, face_take, last
        )
        for group in range(4)
    )

    def grads(piece):
        pending.append(expert_grad_out(links, piece, downs, ups, out_down, out_up, local_sem))

    def publish(item):
        pending.extend(item.publish(out_qkv, out_proj, out_small, local_sem))

    def early():
        one.form()
        proj.chain(0)

    def middle():
        one.halve()
        two.form()
        proj.chain(1)

    def late():
        two.halve()
        three.form()
        proj.chain(2)
        one.chain(0)

    proj.form()
    attention_backward(
        x_ref, wall, rows_t, qkv, board, hidden, normed2, rb, rel_rows, small_t, grad_tokens, proj.halve,
        (early, middle, late),
    )
    three.form_small()
    put(grad_tokens, tokens_out, 27)
    proj.chain(3)
    one.chain(1)
    three.halve()
    two.chain(0)
    one.chain(2)
    grads(0)
    proj.face()
    two.chain(1)
    one.chain(3)
    grads(1)
    three.chain(0)
    two.chain(2)
    grads(2)
    one.face()
    three.chain(1)
    two.chain(3)
    grads(3)
    three.chain(2)
    two.face()
    grads(4)
    three.chain(3)
    grads(5)
    three.face()
    items = (proj, one, two, three)
    for item in items:
        publish(item)
    for item in items:
        item.landed()
    expert_grads_arrive(links, out_down, out_up)
    for copy in pending:
        copy.wait()
    links.finish()


PARTS = 6


def hand_out(
    mixed, tokens, qkv, proj, small, up, down,
    to_mixed, to_tokens, to_qkv, to_proj, to_gain_attn, to_gain_moe, to_router, to_rel, to_up, to_down,
    v_mixed, v_tokens, v_qkv, v_proj, v_small, v_up, v_down,
    v_gain_attn, v_gain_moe, v_router, v_rel, wide_up, wide_down, in_sem, out_sem,
):
    def rows(array, i):
        count = array.shape[0] // PARTS
        return pl.ds(i * count, count)

    def copy(src, dst, sem, i):
        item = pltpu.make_async_copy(src, dst, sem.at[i])
        item.start()
        return item

    halves = [
        (source, held, wide, out, rows(source, i))
        for i in range(PARTS)
        for source, held, wide, out in ((up, v_up, wide_up, to_up), (down, v_down, wide_down, to_down))
    ]
    coming = [copy(source.at[at], held.at[at], in_sem, i) for i, (source, held, _, _, at) in enumerate(halves)]
    plain = ((tokens, v_tokens, to_tokens), (qkv, v_qkv, to_qkv), (mixed, v_mixed, to_mixed), (proj, v_proj, to_proj))
    first = len(halves)
    little = copy(small, v_small, in_sem, first + len(plain))
    others = [copy(source, held, in_sem, first + i) for i, (source, held, _) in enumerate(plain)]
    going = []

    def put(src, dst):
        going.append(copy(src, dst, out_sem, len(going)))

    for item, (source, held, wide, out, at) in zip(coming, halves):
        item.wait()
        wide[at] = held[at].astype(F32)
        put(wide.at[at], out.at[at])
    little.wait()
    turned = jnp.transpose(v_small[...])
    v_gain_attn[...] = turned[0]
    v_gain_moe[...] = turned[1]
    v_router[...] = turned[2 : 2 + EXP]
    v_rel[...] = v_small[0:16, HEAD : HEAD + HEADS]
    put(v_gain_attn, to_gain_attn)
    put(v_gain_moe, to_gain_moe)
    put(v_router, to_router)
    put(v_rel, to_rel)
    for item, (_, held, out) in zip(others, plain):
        item.wait()
        put(held, out)
    for item in going:
        item.wait()


def body_fast(
    tokens, cotangent, lengths, routes, slots, gain_attn, w_qkv, w_proj, rel_table, gain_moe, w_router, w_up, w_down
):
    vm = pl.BlockSpec(memory_space=pltpu.VMEM)
    hbm = pl.BlockSpec(memory_space=pl.ANY)
    sds = jax.ShapeDtypeStruct
    v = pltpu.VMEM
    shapes = (
        sds((TOK, D), BF16), sds((TOK, D), F32), sds((SHARD, 3 * D), F32), sds((SHARD, D), F32),
        sds((SHARD, 128), F32), sds((D, HF), BF16), sds((HF, D), BF16),
    )
    out = pl.pallas_call(
        layer,
        out_shape=shapes,
        in_specs=[hbm, hbm, pl.BlockSpec(memory_space=pltpu.SMEM), vm, vm, vm, vm, vm, vm, hbm, hbm, hbm, hbm],
        out_specs=[hbm, hbm, hbm, hbm, hbm, hbm, hbm],
        scratch_shapes=[
            v((TOK, D), BF16), v((TOK, D), BF16), v((TOK, D), BF16), v((TOK, D), F32), v((HEADS * SEQ, 3 * SEQ), F32),
            v((D, WALL), BF16), v((8, D), F32), v((8, TOK), F32), v((TOK, 8), F32), v((2, TOK, D), BF16),
            v((TOK, 3 * D), BF16), v((TOK, D), F32), v((TOK, D), BF16),
            v((TOK, 1), F32), v((EXP, ROWS, D), BF16), v((EXP, ROWS, D), BF16),
            v((8 * ROWS, D), BF16), v((8 * ROWS, D), BF16), v((D, HF), BF16), v((HF, D), BF16),
            v((8 * ROWS, SENTC), BF16), v((8 * ROWS, HF), BF16),
            v((EXP, 2, ROWS, D), BF16), v((EXP, 2, ROWS, D), BF16), v((EXP, ROWS, D), BF16), v((EXP, ROWS, D), BF16),
            v((EXP, ROWS, D), BF16), v((EXP, ROWS, D), BF16),
            v((HF // 2, D), F32), v((HF // 2, D), BF16), v((HF // 2, D), BF16), v((HF // 2, D), BF16),
            v((D // 2, HF), F32), v((D // 2, HF), BF16), v((D // 2, HF), BF16), v((D // 2, HF), BF16),
            v((TOK, 4 * D), BF16), v((16, SEQ), F32), v((128, D), F32),
            v((D, SENTC), BF16), v((D, SENTC), F32), v((4, SHARD, SENTC), BF16), v((8, SHARD, SENTC), BF16),
            v((SHARD, SENTC), BF16), v((SHARD, SENTC), BF16), v((SHARD, SENTC), F32),
            pltpu.SemaphoreType.DMA((28,)), pltpu.SemaphoreType.DMA((LINKS,)), pltpu.SemaphoreType.DMA((LINKS,)),
        ],
        compiler_params=pltpu.CompilerParams(
            collective_id=0, has_side_effects=True, vmem_limit_bytes=67043328
        ),
        name="layer",
    )(
        tokens, cotangent, lengths, routes.T, slots.T, gain_attn[None], gain_moe[None], w_router.T, rel_table, w_qkv, w_proj,
        w_up, w_down,
    )
    small = (sds((SHARD,), F32), sds((SHARD,), F32), sds((EXP, SHARD), F32), sds((16, HEADS), F32))
    final = shapes[:4] + small + (sds((D, HF), F32), sds((HF, D), F32))
    mixed, grad_tokens, grad_qkv, grad_proj, grad_gain_attn, grad_gain_moe, grad_router, grad_rel, grad_up, grad_down = (
        pl.pallas_call(
            hand_out,
            out_shape=final,
            in_specs=[hbm] * len(shapes),
            out_specs=[hbm] * len(final),
            scratch_shapes=[v(item.shape, item.dtype) for item in shapes + small + final[-2:]]
            + [pltpu.SemaphoreType.DMA((2 * PARTS + 5,)), pltpu.SemaphoreType.DMA((2 * PARTS + 8,))],
            name="hand_out",
        )(*out)
    )
    return (
        mixed,
        grad_tokens,
        grad_gain_attn,
        grad_qkv,
        grad_proj,
        grad_rel,
        grad_gain_moe,
        grad_router.T,
        grad_up[None],
        grad_down[None],
    )


epsilon = 1e-06
exact_precision = lax.Precision.HIGHEST


def rms_norm(values, gain):
    factor = lax.rsqrt(jnp.mean(values * values, axis=-1, keepdims=True) + epsilon)
    return values * factor * gain


def distance_hot():
    places = jnp.arange(SEQ, dtype=jnp.int32)
    distance = jnp.clip(places[:, None] - places[None, :], 0, SEQ - 1).reshape(1, SEQ * SEQ)
    return (distance == places[:, None]).astype(jnp.bfloat16)


def bias_matrix(table, hot):
    flat = jnp.einsum("dh,dp->hp", table, hot, preferred_element_type=jnp.float32)
    return flat.reshape(table.shape[1], SEQ, SEQ)


def exact_gelu(values):
    return jax.nn.gelu(values, approximate=False)


def masked_scores(qkv_rows, bias, allowed, factor):
    raw = jnp.einsum(
        "qhd,khd->hqk", qkv_rows[:, 0], qkv_rows[:, 1], preferred_element_type=jnp.float32
    )
    return jnp.where(allowed[None], raw * factor + bias, -1e30)


def fetch_weights(gain_attn, w_qkv, w_proj, rel_table, gain_moe, w_router):
    rows, experts = w_router.shape
    spread = rel_table.shape[0]
    packed = jnp.concatenate(
        [gain_attn, gain_moe, w_router.reshape(-1), rel_table.reshape(-1)]
    )
    small = lax.all_gather(packed, "fsdp", axis=0, tiled=False)
    groups = small.shape[0]
    edge = 2 * rows + rows * experts
    return (
        small[:, :rows].reshape(-1),
        lax.all_gather(w_qkv, "fsdp", axis=0, tiled=True),
        lax.all_gather(w_proj, "fsdp", axis=0, tiled=True),
        small[:, edge:].reshape(groups * spread, HEADS),
        small[:, rows : 2 * rows].reshape(-1),
        small[:, 2 * rows : edge].reshape(groups * rows, experts),
    )


def body(
    tokens,
    cotangent,
    lengths,
    routes,
    slots,
    gain_attn,
    w_qkv,
    w_proj,
    rel_table,
    gain_moe,
    w_router,
    w_up,
    w_down,
):
    groups = lax.axis_size("fsdp")
    experts = groups // 2
    capacity = 2 * SEQ // experts
    factor = HEAD ** (-0.5)
    up_weight = w_up[0]
    down_weight = w_down[0]
    places = jnp.arange(SEQ, dtype=jnp.int32)
    causal = places[:, None] >= places[None, :]
    expert_ids = jnp.arange(experts, dtype=jnp.int32)
    saved = []
    mixed_parts = []
    weights = fetch_weights(gain_attn, w_qkv, w_proj, rel_table, gain_moe, w_router)
    gain_a = weights[0].astype(jnp.float32)
    gain_m = weights[4].astype(jnp.float32)
    router_float = weights[5].astype(jnp.float32)
    hot = distance_hot()
    bias = bias_matrix(weights[3], hot)
    for batch in range(MB):
        x_float = tokens[batch * SEQ : (batch + 1) * SEQ].astype(jnp.float32)
        live_keys = places < lengths[batch]
        live_col = live_keys.astype(jnp.float32)[:, None]
        allowed = causal & live_keys[None, :]
        normed = rms_norm(x_float, gain_a).astype(jnp.bfloat16)
        qkv_rows = (
            jnp.dot(normed, weights[1], preferred_element_type=jnp.float32)
            .astype(jnp.bfloat16)
            .reshape(SEQ, 3, HEADS, HEAD)
        )
        scores = masked_scores(qkv_rows, bias, allowed, factor)
        row_peak = jnp.max(scores, axis=-1, keepdims=True)
        exp_scores = jnp.exp(scores - row_peak)
        row_total = jnp.sum(exp_scores, axis=-1, keepdims=True)
        log_total = row_peak + jnp.log(row_total)
        probs_low = (exp_scores / row_total).astype(jnp.bfloat16)
        attended = jnp.einsum(
            "hqk,khd->qhd", probs_low, qkv_rows[:, 2], preferred_element_type=jnp.float32
        )
        attended = attended.astype(jnp.bfloat16).reshape(SEQ, D)
        branch = jnp.dot(attended, weights[2], preferred_element_type=jnp.float32)
        hidden = x_float + live_col * branch
        normed2 = rms_norm(hidden, gain_m).astype(jnp.bfloat16)
        logits = jnp.dot(normed2, weights[5], preferred_element_type=jnp.float32)
        route_rows = routes[batch * SEQ : (batch + 1) * SEQ]
        slot_rows = slots[batch * SEQ : (batch + 1) * SEQ]
        hot_first = (route_rows[:, 0:1] == expert_ids[None, :]).astype(jnp.float32)
        hot_second = (route_rows[:, 1:2] == expert_ids[None, :]).astype(jnp.float32)
        gate_first = jax.nn.sigmoid(
            jnp.sum(logits * hot_first, axis=-1) - jnp.sum(logits * hot_second, axis=-1)
        )
        row_place = route_rows * capacity + slot_rows
        target = jnp.where(live_keys[:, None], row_place, experts * capacity)
        outgoing = jnp.zeros((experts * capacity, D), jnp.bfloat16)
        outgoing = (
            outgoing.at[target[:, 0]]
            .set(normed2, mode="drop")
            .at[target[:, 1]]
            .set(normed2, mode="drop")
        )
        outgoing = jnp.repeat(outgoing.reshape(experts, capacity, D), 2, axis=0)
        expert_received = lax.all_to_all(outgoing, "fsdp", split_axis=0, concat_axis=0, tiled=True)
        expert_before = jnp.einsum(
            "scd,df->scf", expert_received, up_weight, preferred_element_type=jnp.float32
        )
        expert_active = exact_gelu(expert_before).astype(jnp.bfloat16)
        partial_value = jnp.einsum(
            "scf,fd->scd", expert_active, down_weight, preferred_element_type=jnp.float32
        ).astype(jnp.bfloat16)
        returned = lax.all_to_all(partial_value, "fsdp", split_axis=0, concat_axis=0, tiled=True)
        results = (returned, expert_received, expert_before)
        combined = (
            results[0]
            .astype(jnp.float32)
            .reshape(experts, 2, capacity, D)
            .sum(axis=1)
            .reshape(experts * capacity, D)
        )
        first_out = combined[row_place[:, 0]]
        second_out = combined[row_place[:, 1]]
        moe = live_col * (
            gate_first[:, None] * first_out + (1.0 - gate_first)[:, None] * second_out
        )
        mixed_parts.append((hidden + moe).astype(jnp.bfloat16))
        saved.append(
            {
                "normed": normed,
                "qkv_rows": qkv_rows,
                "log_total": log_total,
                "attended": attended,
                "hidden": hidden,
                "normed2": normed2,
                "gate_first": gate_first,
                "first_out": first_out,
                "second_out": second_out,
                "results": results,
                "target": target,
                "row_place": row_place,
                "hot_first": hot_first,
                "hot_second": hot_second,
            }
        )
    grad_qkv_w = jnp.zeros((D, 3 * D), jnp.float32)
    grad_proj_w = jnp.zeros((D, D), jnp.float32)
    grad_table = jnp.zeros((SEQ, HEADS), jnp.float32)
    grad_gain_a = jnp.zeros((D,), jnp.float32)
    grad_gain_m = jnp.zeros((D,), jnp.float32)
    grad_router = jnp.zeros((D, experts), jnp.float32)
    grad_up = jnp.zeros((D, FF // 2), jnp.float32)
    grad_down = jnp.zeros((FF // 2, D), jnp.float32)
    grad_parts = [None] * MB
    for batch in reversed(range(MB)):
        kept = saved[batch]
        x_float = tokens[batch * SEQ : (batch + 1) * SEQ].astype(jnp.float32)
        live_keys = places < lengths[batch]
        live_col = live_keys.astype(jnp.float32)[:, None]
        allowed = causal & live_keys[None, :]
        grad_out = cotangent[batch * SEQ : (batch + 1) * SEQ].astype(jnp.float32)
        grad_moe = live_col * grad_out
        gate_first = kept["gate_first"]
        gate_second = 1.0 - gate_first
        grad_gate_first = jnp.sum(grad_moe * kept["first_out"], axis=-1)
        grad_gate_second = jnp.sum(grad_moe * kept["second_out"], axis=-1)
        grad_first = (gate_first[:, None] * grad_moe).astype(jnp.bfloat16)
        grad_second = (gate_second[:, None] * grad_moe).astype(jnp.bfloat16)
        target = kept["target"]
        grad_send = jnp.zeros((experts * capacity, D), jnp.bfloat16)
        grad_send = (
            grad_send.at[target[:, 0]]
            .set(grad_first, mode="drop")
            .at[target[:, 1]]
            .set(grad_second, mode="drop")
        )
        grad_send = jnp.repeat(grad_send.reshape(experts, capacity, D), 2, axis=0)
        grad_recv = lax.all_to_all(grad_send, "fsdp", split_axis=0, concat_axis=0, tiled=True)
        received = kept["results"][1]
        before = kept["results"][2]
        active, gelu_back = jax.vjp(exact_gelu, before)
        active_low = active.astype(jnp.bfloat16)
        grad_active = jnp.einsum(
            "scd,fd->scf", grad_recv, down_weight, preferred_element_type=jnp.float32
        )
        grad_before = gelu_back(grad_active)[0].astype(jnp.bfloat16)
        grad_down = grad_down + jnp.einsum(
            "scf,scd->fd", active_low, grad_recv, preferred_element_type=jnp.float32
        )
        grad_up = grad_up + jnp.einsum(
            "scd,scf->df", received, grad_before, preferred_element_type=jnp.float32
        )
        grad_part = jnp.einsum(
            "scf,df->scd", grad_before, up_weight, preferred_element_type=jnp.float32
        ).astype(jnp.bfloat16)
        grad_back = lax.all_to_all(grad_part, "fsdp", split_axis=0, concat_axis=0, tiled=True)
        grad_rows = (
            grad_back.astype(jnp.float32)
            .reshape(experts, 2, capacity, D)
            .sum(axis=1)
            .reshape(experts * capacity, D)
        )
        row_place = kept["row_place"]
        grad_diff = (grad_gate_first - grad_gate_second) * gate_first * gate_second
        grad_logits = grad_diff[:, None] * (kept["hot_first"] - kept["hot_second"])
        normed2_float = kept["normed2"].astype(jnp.float32)
        grad_router = grad_router + jnp.dot(normed2_float.T, grad_logits, precision=exact_precision)
        grad_normed2 = live_col * (grad_rows[row_place[:, 0]] + grad_rows[row_place[:, 1]])
        grad_normed2 = grad_normed2 + jnp.dot(
            grad_logits, router_float.T, precision=exact_precision
        )
        _, norm_back_moe = jax.vjp(rms_norm, kept["hidden"], gain_m)
        grad_hidden_norm, grad_gain_part = norm_back_moe(grad_normed2)
        grad_gain_m = grad_gain_m + grad_gain_part
        grad_hidden = grad_out + grad_hidden_norm
        grad_branch = (live_col * grad_hidden).astype(jnp.bfloat16)
        grad_proj_w = grad_proj_w + jnp.einsum(
            "sd,se->de", kept["attended"], grad_branch, preferred_element_type=jnp.float32
        )
        grad_attended = jnp.einsum(
            "se,de->sd", grad_branch, weights[2], preferred_element_type=jnp.float32
        )
        grad_attended = grad_attended.astype(jnp.bfloat16).reshape(SEQ, HEADS, HEAD)
        qkv_rows = kept["qkv_rows"]
        scores = masked_scores(qkv_rows, bias, allowed, factor)
        probs = jnp.exp(scores - kept["log_total"])
        probs_low = probs.astype(jnp.bfloat16)
        grad_probs = jnp.einsum(
            "qhd,khd->hqk", grad_attended, qkv_rows[:, 2], preferred_element_type=jnp.float32
        )
        row_dot = jnp.sum(probs * grad_probs, axis=-1, keepdims=True)
        grad_scores = (probs * (grad_probs - row_dot)).astype(jnp.bfloat16)
        grad_table = grad_table + jnp.einsum(
            "dp,hp->dh",
            hot,
            jnp.where(allowed[None], grad_scores, 0).reshape(HEADS, SEQ * SEQ),
            preferred_element_type=jnp.float32,
        )
        grad_queries = (
            jnp.einsum(
                "hqk,khd->qhd", grad_scores, qkv_rows[:, 1], preferred_element_type=jnp.float32
            )
            * factor
        )
        grad_keys = (
            jnp.einsum(
                "hqk,qhd->khd", grad_scores, qkv_rows[:, 0], preferred_element_type=jnp.float32
            )
            * factor
        )
        grad_values = jnp.einsum(
            "hqk,qhd->khd", probs_low, grad_attended, preferred_element_type=jnp.float32
        )
        grad_qkv = (
            jnp.stack([grad_queries, grad_keys, grad_values], axis=1)
            .astype(jnp.bfloat16)
            .reshape(SEQ, 3 * D)
        )
        grad_qkv_w = grad_qkv_w + jnp.einsum(
            "sd,se->de", kept["normed"], grad_qkv, preferred_element_type=jnp.float32
        )
        grad_normed = jnp.einsum(
            "se,de->sd", grad_qkv, weights[1], preferred_element_type=jnp.float32
        )
        _, norm_back_attn = jax.vjp(rms_norm, x_float, gain_a)
        grad_x_norm, grad_gain_piece = norm_back_attn(grad_normed)
        grad_gain_a = grad_gain_a + grad_gain_piece
        grad_parts[batch] = grad_hidden + grad_x_norm
    small = jnp.concatenate(
        [
            grad_gain_a.reshape(groups, -1),
            grad_gain_m.reshape(groups, -1),
            grad_router.reshape(groups, -1),
            grad_table.reshape(groups, -1),
        ],
        axis=1,
    )
    small = lax.psum_scatter(small, "fsdp", scatter_dimension=0, tiled=True)
    shards = (
        small,
        lax.psum_scatter(grad_qkv_w, "fsdp", scatter_dimension=0, tiled=True),
        lax.psum_scatter(grad_proj_w, "fsdp", scatter_dimension=0, tiled=True),
    )
    sums = lax.psum((shards[0], shards[1], shards[2], grad_up[None], grad_down[None]), "replica")
    rows = D // groups
    edge = 2 * rows + rows * experts
    totals = (
        sums[0][0, :rows],
        sums[1],
        sums[2],
        sums[0][0, edge:].reshape(SEQ // groups, HEADS),
        sums[0][0, rows : 2 * rows],
        sums[0][0, 2 * rows : edge].reshape(rows, experts),
        sums[3],
        sums[4],
    )
    mixed = jnp.concatenate(mixed_parts, axis=0)
    grad_tokens = jnp.concatenate(grad_parts, axis=0)
    return (
        mixed,
        grad_tokens,
        totals[0],
        totals[1],
        totals[2],
        totals[3],
        totals[4],
        totals[5],
        totals[6],
        totals[7],
    )


def solution(mesh):
    in_specs = (
        P(("replica", "fsdp"), None),
        P(("replica", "fsdp"), None),
        P(("replica", "fsdp")),
        P(("replica", "fsdp"), None),
        P(("replica", "fsdp"), None),
        P("fsdp"),
        P("fsdp", None),
        P("fsdp", None),
        P("fsdp", None),
        P("fsdp"),
        P("fsdp", None),
        P("fsdp", None, None),
        P("fsdp", None, None),
    )
    out_specs = (
        P(("replica", "fsdp"), None),
        P(("replica", "fsdp"), None),
        P("fsdp"),
        P("fsdp", None),
        P("fsdp", None),
        P("fsdp", None),
        P("fsdp"),
        P("fsdp", None),
        P("fsdp", None, None),
        P("fsdp", None, None),
    )
    fast = dict(mesh.shape) == {"replica": 4, "fsdp": 8}
    return jax.shard_map(body_fast if fast else body, mesh=mesh, in_specs=in_specs, out_specs=out_specs, check_vma=False)
```

```python
import functools

import jax
import jax.numpy as jnp
from jax import lax
from jax.experimental import pallas as pl
from jax.experimental.pallas import tpu as pltpu
from jax.sharding import PartitionSpec as P

D = 768
HEADS = 12
HEAD = 64
FF = 3072
SEQ = 128
MB = 2
MESH = pl.DeviceIdType.MESH
F32 = jnp.float32
BF16 = jnp.bfloat16
NEG = -1e30
HF = FF // 2
TOK = MB * SEQ
EXP = 4
CAP = 64
ROWS = MB * CAP
LOW = 896
MID = 3 * D - 2 * LOW
MORE = MID + 128
SMALL = LOW + MID
PROJ = LOW + MORE
HIGH = PROJ + D
WALL = HIGH + LOW
LEFTC = LOW + MID
SHARD = 96
HALF = SHARD // 2
PAIRS = HEADS // 2
SCALE = HEAD ** (-0.5)


def place():
    replica = lax.axis_index("replica")
    group = lax.axis_index("fsdp")
    return replica // 2, replica % 2, group // 2, group % 2


def device(x, c, z, y):
    return (x * 2 + c, z * 2 + y)


def remote(src, dst, send, recv, target):
    return pltpu.make_async_remote_copy(
        src_ref=src,
        dst_ref=dst,
        send_sem=send,
        recv_sem=recv,
        device_id=target,
        device_id_type=MESH,
    )


def greet():
    x, c, z, y = place()
    barrier = pltpu.get_barrier_semaphore()
    targets = [device(x, 1 - c, z, y), device(1 - x, c, z, y), device(x, c, z, 1 - y)]
    targets += [device(x, c, (z + k) % 4, y) for k in (1, 2, 3)]
    for target in targets:
        pl.semaphore_signal(barrier, inc=1, device_id=target, device_id_type=MESH)
    return lambda: pl.semaphore_wait(barrier, len(targets))


def dot(a, b, ca=1, cb=0):
    return lax.dot_general(a, b, (((ca,), (cb,)), ((), ())), preferred_element_type=F32)


def run(cond, what):
    if cond is None:
        what()
    else:
        pl.when(cond)(what)


class Links:
    def __init__(self, send_sem, recv_sem):
        self.send_sem, self.recv_sem = send_sem, recv_sem
        self.started = []

    def go(self, cond, src, dst, send, recv, target):
        copy = remote(src, dst, self.send_sem.at[send], self.recv_sem.at[recv], target)
        run(cond, copy.start)
        self.started.append((cond, copy))
        return copy

    def arrive(self, cond, dst, recv, target):
        run(cond, remote(dst, dst, self.send_sem.at[0], self.recv_sem.at[recv], target).wait_recv)

    def leave(self, copy):
        copy.wait_send()
        self.started = [(cond, item) for cond, item in self.started if item is not copy]

    def finish(self):
        for cond, copy in self.started:
            run(cond, copy.wait_send)
        self.started = []


def gather_weights(links, wq, wp, wall, local_sem, others, ready):
    x, c, z, y = place()
    own = pl.ds(pl.multiple_of((z * 2 + y) * SHARD, 16), SHARD)
    fills = [
        pltpu.make_async_copy(wq.at[:, pl.ds(0, LEFTC)], wall.at[own, pl.ds(0, LEFTC)], local_sem.at[0]),
        pltpu.make_async_copy(wq.at[:, pl.ds(LEFTC, LOW)], wall.at[own, pl.ds(HIGH, LOW)], local_sem.at[1]),
        pltpu.make_async_copy(wp, wall.at[own, pl.ds(PROJ, D)], local_sem.at[2]),
    ]
    for copy in fills + others:
        copy.start()
    ready()
    share = pl.ds(pl.multiple_of(x * HIGH, 128), LOW)
    gained = pl.ds(pl.multiple_of((1 - x) * HIGH, 128), LOW)
    columns = (share, pl.ds(LOW, MORE), pl.ds(PROJ, D))
    up, down = device(x, c, z + 1, y), device(x, c, z - 1, y)
    across, facing, twin = device(x, c, z, 1 - y), device(1 - x, c, z, y), device(x, 1 - c, z, y)

    def part(zs, ys, half, cols):
        return wall.at[pl.ds(pl.multiple_of((zs * 2 + ys) * SHARD + half * HALF, 16), HALF), cols]

    def go(cond, zs, ys, cols, send, recv, target, src=None):
        piece = part(zs, ys, c, cols)
        links.go(cond, piece if src is None else src, piece, send, recv, target)

    def arrive(cond, zs, ys, half, cols, recv):
        links.arrive(cond, part(zs, ys, half, cols), recv, twin)

    def spread(cond, sub, zs, ys):
        source = zs * 2 + ys
        if sub == 0:
            go(cond, zs, ys, share, 39 + source, 24 + source, facing)
        go(cond, zs, ys, columns[sub], 47 + sub * 8 + source, 32 + sub * 8 + source, twin)

    def begin(sub, src):
        go(z < 3, z, y, columns[sub], sub * 3, sub * 4 + z, up, src)
        go(z > 0, z, y, columns[sub], 9 + sub * 3, sub * 4 + z, down, src)
        go(None, z, y, columns[sub], 18 + sub * 7, 12 + sub * 4 + z, across, src)

    def along(sub, k):
        below, above = z - k, z + k
        for cond, zs, on, first, target, place_of in (
            (below >= 0, below, z < 3, 0, up, k),
            (above <= 3, above, z > 0, 9, down, 3 + k),
        ):
            arrive(cond, zs, y, c, columns[sub], sub * 4 + zs)
            if k < 3:
                go(cond & on, zs, y, columns[sub], first + sub * 3 + k, sub * 4 + zs, target)
            go(cond, zs, y, columns[sub], 18 + sub * 7 + place_of, 12 + sub * 4 + zs, across)
            spread(cond, sub, zs, y)

    def over(sub, k):
        if k == 0:
            arrive(None, z, 1 - y, c, columns[sub], 12 + sub * 4 + z)
            spread(None, sub, z, 1 - y)
            return
        for cond, zs in ((z - k >= 0, z - k), (z + k <= 3, z + k)):
            arrive(cond, zs, 1 - y, c, columns[sub], 12 + sub * 4 + zs)
            spread(cond, sub, zs, 1 - y)

    half = pl.ds(pl.multiple_of(c * HALF, 16), HALF)
    begin(0, wq.at[half, pl.ds(pl.multiple_of(x * LEFTC, 128), LOW)])
    for fill in fills:
        fill.wait()
    begin(1, None)
    for k in (1, 2, 3):
        for sub in range(2):
            along(sub, k)
            over(sub, k - 1)
        if k == 2:
            begin(2, wp.at[half, :])
    along(2, 1)
    for sub in range(2):
        over(sub, 3)

    def each(what):
        for zs in range(4):
            for ys in range(2):
                what((zs != z) | (ys != y), zs, ys, zs * 2 + ys)

    def gain(other, zs, ys, source):
        arrive(other, zs, ys, c, gained, 24 + source)
        go(other, zs, ys, gained, 71 + source, 56 + source, twin)

    def mostly(other, zs, ys, source):
        for sub in range(2):
            arrive(other, zs, ys, 1 - c, columns[sub], 32 + sub * 8 + source)
        arrive(other, zs, ys, 1 - c, gained, 56 + source)

    def rest(other, zs, ys, source):
        arrive(other, zs, ys, 1 - c, columns[2], 32 + 16 + source)

    each(gain)
    each(mostly)

    def first():
        along(2, 2)
        over(2, 0)

    def second():
        along(2, 3)
        over(2, 1)
        over(2, 2)

    return first, second, lambda: over(2, 3), lambda: each(rest)


def unit(values):
    return lax.rsqrt(jnp.mean(values * values, axis=-1, keepdims=True) + 1e-06)


def heads(rows):
    lane = lax.broadcasted_iota(jnp.int32, rows.shape, 1)
    none = jnp.zeros_like(rows)
    return jnp.concatenate([jnp.where(lane < HEAD, rows, none), jnp.where(lane < HEAD, none, rows)], axis=0)


def beside(blocks):
    return jnp.concatenate([blocks[0:SEQ], blocks[SEQ : 2 * SEQ]], axis=1)


def build_bias(wall, bias):
    table = jnp.concatenate(
        [wall[f * SHARD : f * SHARD + 16, SMALL : SMALL + 128] for f in range(8)], axis=0
    )
    ahead = lax.broadcasted_iota(jnp.int32, (SEQ, SEQ), 0)
    lane = lax.broadcasted_iota(jnp.int32, (SEQ, SEQ), 1)
    turned = jnp.where(ahead + lane == SEQ, 1.0, jnp.where(ahead + lane == 0, 1.0, 0.0)).astype(BF16)
    lines = dot(table, turned, 0, 0)
    for h in range(HEADS):
        line = jnp.broadcast_to(lines[HEAD + h : HEAD + h + 1, :], (SEQ, SEQ))
        rolled = pltpu.roll(line, 0, 1, stride=1, stride_axis=0)
        bias[h * SEQ : (h + 1) * SEQ, 0:SEQ] = jnp.where(ahead >= lane, rolled, NEG)


def pack(gain_attn, gain_moe, router_t, rel, board, wall):
    x, c, z, y = place()
    board[0:SEQ, 0:SEQ] = jnp.zeros((SEQ, SEQ), F32)
    board[0:1, 0:SHARD] = gain_attn[...].astype(F32)
    board[1:2, 0:SHARD] = gain_moe[...].astype(F32)
    board[2 : 2 + EXP, 0:SHARD] = router_t[...].astype(F32)
    turned = jnp.transpose(board[0:SEQ, 0:SEQ])
    board[0:SEQ, 0:SEQ] = turned
    board[0:16, HEAD : HEAD + HEADS] = rel[...].astype(F32)
    own = pl.ds(pl.multiple_of((z * 2 + y) * SHARD, 16), SHARD)
    wall[own, SMALL : SMALL + 128] = board[0:SHARD, 0:SEQ].astype(BF16)


def stand(routes, slots, lines, columns):
    chosen = routes[...]
    lines[...] = jnp.zeros_like(lines)
    lines[0:2, :] = (chosen * CAP + slots[...]).astype(F32)
    lines[2:4, :] = chosen.astype(F32)
    columns[...] = jnp.transpose(lines[...])


def routing(columns, s):
    spots = columns[s * SEQ : (s + 1) * SEQ, :]
    lane = lax.broadcasted_iota(jnp.int32, (SEQ, EXP * CAP), 1).astype(F32)
    return spots[:, 0:1] == lane, spots[:, 1:2] == lane


def named(columns, s):
    spots = columns[s * SEQ : (s + 1) * SEQ, :]
    lane = lax.broadcasted_iota(jnp.int32, (SEQ, 128), 1).astype(F32) - 2.0
    return spots[:, 2:3] == lane, spots[:, 3:4] == lane


def live_column(lengths, s):
    return lax.broadcasted_iota(jnp.int32, (SEQ, 1), 0) < lengths[s]


def attention_forward(
    later, x_ref, cot, lengths, columns, wall, rows_t, board, normed, qkv, attended, hidden, normed2, gates, out_f, out_g
):
    rows_t[...] = jnp.transpose(wall[:, SMALL : SMALL + 128].astype(F32))[0:8]
    build_bias(wall, board)
    x = x_ref[...].astype(F32)
    normed[...] = (x * unit(x) * rows_t[0:1, :]).astype(BF16)
    qkv[:, 0:LEFTC] = dot(normed[...], wall[:, 0:LEFTC]).astype(BF16)
    qkv[:, LEFTC : 3 * D] = dot(normed[...], wall[:, HIGH:WALL]).astype(BF16)
    lane = lax.broadcasted_iota(jnp.int32, (2 * SEQ, 128), 1)

    def pair(p, carry):
        blocks = pl.ds(pl.multiple_of(p * 2 * SEQ, SEQ), 2 * SEQ)
        for s in range(MB):
            rows = slice(s * SEQ, (s + 1) * SEQ)
            q = qkv[rows, pl.ds(pl.multiple_of(p * 128, 128), 128)]
            k = qkv[rows, pl.ds(pl.multiple_of(D + p * 128, 128), 128)]
            v = qkv[rows, pl.ds(pl.multiple_of(2 * D + p * 128, 128), 128)]
            scores = jnp.where(lane < lengths[s], dot(heads(q), k, 1, 1) * SCALE + board[blocks, 0:SEQ], NEG)
            scores = jnp.exp(scores - jnp.max(scores, axis=-1, keepdims=True))
            share = scores * (1.0 / jnp.sum(scores, axis=-1, keepdims=True))
            board[blocks, (1 + s) * SEQ : (2 + s) * SEQ] = share
            attended[rows, pl.ds(pl.multiple_of(p * 128, 128), 128)] = dot(
                beside(share.astype(BF16)), heads(v)
            ).astype(BF16)
        return carry

    for t in range(3):
        later[t]()
        lax.fori_loop(2 * t, 2 * t + 2, pair, 0)
    later[3]()
    branch = dot(attended[...], wall[:, PROJ:HIGH])
    for s in range(MB):
        rows = slice(s * SEQ, (s + 1) * SEQ)
        live = live_column(lengths, s)
        state = x_ref[rows, :].astype(F32) + jnp.where(live, branch[rows, :], 0.0)
        hidden[rows, :] = state
        low = (state * unit(state) * rows_t[1:2, :]).astype(BF16)
        normed2[rows, :] = low
        logits = dot(low, wall[:, SMALL : SMALL + 128])
        one, two = named(columns, s)
        picked = jnp.where(one, logits, 0.0) - jnp.where(two, logits, 0.0)
        gate = jax.nn.sigmoid(jnp.sum(picked, axis=-1, keepdims=True))
        gates[rows, :] = gate
        grad = jnp.where(live, cot[rows, :].astype(F32), 0.0)
        first, second = routing(columns, s)
        first = jnp.where(first & live, 1.0, 0.0).astype(BF16)
        second = jnp.where(second & live, 1.0, 0.0).astype(BF16)
        sent = dot(first + second, low, 0, 0).astype(BF16)
        back = dot(first, (gate * grad).astype(BF16), 0, 0) + dot(
            second, ((1.0 - gate) * grad).astype(BF16), 0, 0
        )
        back = back.astype(BF16)
        for e in range(EXP):
            out_f[e, s * CAP : (s + 1) * CAP, :] = sent[e * CAP : (e + 1) * CAP, :]
            out_g[e, s * CAP : (s + 1) * CAP, :] = back[e * CAP : (e + 1) * CAP, :]


TILE = 512
Z_ROWS, Y_ROWS, Y_PART, Z_BACK = 80, 88, 96, 104
TWIN_W, FACE_W, TWIN_OUT = 112, 114, 120
RS_TWIN, RS_Y, RS_Z, RS_FACE, RS_OUT = 126, 131, 151, 191, 196
LINKS = 206


def quarter(zs):
    return pl.ds(pl.multiple_of(zs * 2 * ROWS, 2 * ROWS), 2 * ROWS)


def half_rows(zs, ys):
    return pl.ds(pl.multiple_of((zs * 2 + ys) * ROWS, ROWS), ROWS)


def expert_forward(zs, recv, up, down, act, slope, part):
    rows = quarter(zs)

    def tile(i, carry):
        cols = pl.ds(pl.multiple_of(i * TILE, TILE), TILE)
        before = dot(recv[rows, :], up[:, cols])
        below = 0.5 + 0.5 * lax.erf(before * 0.7071067811865476)
        act[rows, cols] = (before * below).astype(BF16)
        density = jnp.exp(before * before * -0.5) * 0.3989422804014327
        slope[rows, cols] = (below + before * density).astype(BF16)
        return carry

    lax.fori_loop(0, HF // TILE, tile, 0)
    got = dot(act[rows, 0:HF], down[...]).astype(BF16)
    part[zs, 0] = got[0:ROWS]
    part[zs, 1] = got[ROWS : 2 * ROWS]


def expert_backward(zs, recv, up, down, slope, part):
    rows = quarter(zs)

    def tile(i, carry):
        cols = pl.ds(pl.multiple_of(i * TILE, TILE), TILE)
        grad = dot(recv[rows, :], down[cols, :], 1, 1)
        slope[rows, cols] = (grad * slope[rows, cols].astype(F32)).astype(BF16)
        return carry

    lax.fori_loop(0, HF // TILE, tile, 0)
    got = dot(slope[rows, :], up[...], 1, 1).astype(BF16)
    part[zs, 0] = got[0:ROWS]
    part[zs, 1] = got[ROWS : 2 * ROWS]


def experts(links, out, recv, up, down, act, slope, part, take, back, w_down, w_up):
    x, c, z, y = place()
    across, facing, twin = device(x, c, z, 1 - y), device(1 - x, c, z, y), device(x, 1 - c, z, y)

    for kind in range(2):
        links.go(None, out[kind].at[z], recv[kind].at[half_rows(z, y), :], Y_ROWS + kind * 4, Y_ROWS + kind * 4 + z, across)
        for d in (1, 2, 3):
            to = (z + d) % 4
            links.go(
                None, out[kind].at[to], recv[kind].at[half_rows(z, y), :], Z_ROWS + kind * 4 + d,
                Z_ROWS + kind * 4 + z, device(x, c, to, y),
            )
        recv[kind][half_rows(z, y), :] = out[kind][z]

    def source(d):
        return (z + 4 - d) % 4

    def reach(kind, d):
        zs = source(d)
        rows = recv[kind].at[half_rows(zs, y), :]
        links.arrive(None, rows, Z_ROWS + kind * 4 + zs, across)
        links.go(None, rows, rows, Y_ROWS + kind * 4 + d, Y_ROWS + kind * 4 + zs, across)

    def compute(kind, d):
        zs = source(d)
        links.arrive(None, recv[kind].at[half_rows(zs, 1 - y), :], Y_ROWS + kind * 4 + zs, across)
        if kind == 0:
            expert_forward(zs, recv[0], up, down, act, slope, part[0])
        else:
            expert_backward(zs, recv[1], up, down, slope, part[1])

    def give_part(kind, d):
        zs = source(d)
        links.go(
            None, part[kind].at[zs, 1 - y], take[kind].at[zs], Y_PART + kind * 4 + d, Y_PART + kind * 4 + zs, across
        )

    def merge(kind, d):
        zs = source(d)
        links.arrive(None, take[kind].at[zs], Y_PART + kind * 4 + zs, across)
        total = (part[kind][zs, y].astype(F32) + take[kind][zs].astype(F32)).astype(BF16)
        if d == 0:
            back[kind][z] = total
        else:
            part[kind][zs, y] = total
            links.go(
                None, part[kind].at[zs, y], back[kind].at[z], Z_BACK + kind * 4 + d, Z_BACK + kind * 4 + z,
                device(x, c, zs, y),
            )

    reach(0, 1)
    compute(0, 0)
    reach(0, 2)
    compute(1, 0)
    reach(0, 3)
    compute(0, 1)
    reach(1, 1)
    give_part(0, 1)
    compute(0, 2)
    reach(1, 2)
    give_part(0, 2)
    compute(1, 1)
    reach(1, 3)
    give_part(1, 1)
    merge(0, 1)
    compute(0, 3)
    give_part(0, 3)
    merge(0, 2)
    compute(1, 2)
    give_part(1, 2)
    compute(1, 3)
    give_part(1, 3)
    give_part(0, 0)
    give_part(1, 0)

    def down_tile(i, part_of, keep):
        cols = pl.ds(pl.multiple_of(part_of * (HF // 2) + i * 256, 128), 256)
        got = dot(act[:, cols], recv[1][...], 0, 0)
        keep[pl.ds(pl.multiple_of(i * 256, 256), 256), :] = got.astype(keep.dtype)

    def up_tile(i, part_of, keep):
        cols = pl.ds(pl.multiple_of(part_of * (D // 2) + i * 128, 128), 128)
        got = dot(recv[0][:, cols], slope[...], 0, 0)
        keep[pl.ds(pl.multiple_of(i * 128, 128), 128), :] = got.astype(keep.dtype)

    def tiles(one, part_of, keep):
        def step(i, carry):
            one(i, part_of, keep)
            return carry

        lax.fori_loop(0, 3, step, 0)

    def spread(i, sent):
        own, give, got, face = (w_down, w_up)[i]
        links.arrive(None, got, TWIN_W + i, twin)
        links.leave(sent)
        count = own.shape[0] // 3
        for m in range(3):
            rows = slice(m * count, (m + 1) * count)
            give[rows, :] = (own[rows, :] + got[rows, :].astype(F32)).astype(BF16)
            links.go(None, give.at[rows, :], face.at[rows, :], FACE_W + i * 3 + m, FACE_W + i * 3 + m, facing)

    tiles(down_tile, 1 - c, w_down[1])
    sent = links.go(None, w_down[1], w_down[2], TWIN_W, TWIN_W, twin)
    merge(1, 1)
    tiles(down_tile, c, w_down[0])
    spread(0, sent)
    merge(0, 3)
    tiles(up_tile, 1 - c, w_up[1])
    sent = links.go(None, w_up[1], w_up[2], TWIN_W + 1, TWIN_W + 1, twin)
    merge(1, 2)
    tiles(up_tile, c, w_up[0])
    spread(1, sent)
    merge(1, 3)
    merge(0, 0)
    merge(1, 0)
    for kind in range(2):
        for d in (1, 2, 3):
            zs = source(d)
            links.arrive(None, back[kind].at[zs], Z_BACK + kind * 4 + zs, across)


def expert_grad_out(links, piece, w_down, w_up, out_down, out_up, local_sem):
    x, c, z, y = place()
    facing, twin = device(1 - x, c, z, y), device(x, 1 - c, z, y)
    (own, give, got, face), target = ((w_down, out_down), (w_up, out_up))[piece // 3]
    count = own.shape[0] // 3
    rows = slice((piece % 3) * count, (piece % 3 + 1) * count)
    links.arrive(None, face.at[rows, :], FACE_W + piece, facing)
    face[rows, :] = (give[rows, :].astype(F32) + face[rows, :].astype(F32)).astype(BF16)
    there = target.at[pl.ds(pl.multiple_of((c * 3 + piece % 3) * count, 128), count), :]
    links.go(None, face.at[rows, :], there, TWIN_OUT + piece, TWIN_OUT + piece, twin)
    copy = pltpu.make_async_copy(face.at[rows, :], there, local_sem.at[8 + piece])
    copy.start()
    return copy


def expert_grads_arrive(links, out_down, out_up):
    x, c, z, y = place()
    for piece in range(6):
        target = (out_down, out_up)[piece // 3]
        count = target.shape[0] // 6
        there = target.at[pl.ds(pl.multiple_of(((1 - c) * 3 + piece % 3) * count, 128), count), :]
        links.arrive(None, there, TWIN_OUT + piece, device(x, 1 - c, z, y))


SENTC = 2 * D + 128


def combine(cot, lengths, columns, rows_t, hidden, normed2, gates, back_f, back_g, mixed, rb, small_t):
    gain_grad = jnp.zeros((1, D), F32)
    router_grad = jnp.zeros((128, D), F32)
    for s in range(MB):
        rows = slice(s * SEQ, (s + 1) * SEQ)
        live = live_column(lengths, s)
        first, second = routing(columns, s)
        first = jnp.where(first, 1.0, 0.0).astype(BF16)
        second = jnp.where(second, 1.0, 0.0).astype(BF16)
        given = jnp.concatenate([back_f[e, s * CAP : (s + 1) * CAP, :] for e in range(EXP)], axis=0)
        first_out = dot(first, given)
        second_out = dot(second, given)
        gate = gates[rows, :]
        grad = cot[rows, :].astype(F32)
        grad_live = jnp.where(live, grad, 0.0)
        state = hidden[rows, :]
        moe = gate * first_out + (1.0 - gate) * second_out
        mixed[rows, :] = (state + jnp.where(live, moe, 0.0)).astype(BF16)
        tilt = jnp.sum(grad_live * first_out, axis=-1, keepdims=True) - jnp.sum(
            grad_live * second_out, axis=-1, keepdims=True
        )
        tilt = tilt * gate * (1.0 - gate)
        one, two = named(columns, s)
        hot = jnp.where(one, 1.0, 0.0) - jnp.where(two, 1.0, 0.0)
        grad_logits = tilt * hot
        high = grad_logits.astype(BF16)
        low = (grad_logits - high.astype(F32)).astype(BF16)
        router_grad = router_grad + dot(high, normed2[rows, :], 0, 0) + dot(low, normed2[rows, :], 0, 0)
        given = jnp.concatenate([back_g[e, s * CAP : (s + 1) * CAP, :] for e in range(EXP)], axis=0)
        grad_low = jnp.where(live, dot(first + second, given), 0.0)
        for e in range(EXP):
            grad_low = grad_low + grad_logits[:, 2 + e : 3 + e] * rows_t[2 + e : 3 + e, :]
        factor = unit(state)
        scaled = state * factor
        gain_grad = gain_grad + jnp.sum(grad_low * scaled, axis=0, keepdims=True)
        grad_low = grad_low * rows_t[1:2, :]
        inner = jnp.mean(grad_low * scaled, axis=-1, keepdims=True)
        grad_state = grad + factor * (grad_low - scaled * inner)
        hidden[rows, :] = grad_state
        rb[rows, 3 * D : 4 * D] = jnp.where(live, grad_state, 0.0).astype(BF16)
    small_t[...] = router_grad
    small_t[1:2, :] = gain_grad


def attention_backward(x_ref, wall, rows_t, qkv, board, hidden, grad_att, rb, rel_rows, small_t, grad_tokens, midway, formed):
    grad_att[...] = dot(rb[:, 3 * D : 4 * D], wall[:, PROJ:HIGH], 1, 1).astype(BF16)
    midway()
    lane = lax.broadcasted_iota(jnp.int32, (SEQ, 128), 1)
    ahead = lax.broadcasted_iota(jnp.int32, (SEQ, 128), 0)
    flip = jnp.where(ahead + lane == SEQ - 1, 1.0, 0.0).astype(BF16)
    flip = jnp.concatenate([flip] * MB, axis=1)

    def pair(p, carry):
        blocks = pl.ds(pl.multiple_of(p * 2 * SEQ, SEQ), 2 * SEQ)
        scores = []
        for s in range(MB):
            rows = slice(s * SEQ, (s + 1) * SEQ)
            cols = [pl.ds(pl.multiple_of(i * D + p * 128, 128), 128) for i in range(3)]
            q, k, v = (qkv[rows, cols[i]] for i in range(3))
            grad = heads(grad_att[rows, cols[0]])
            share = board[blocks, (1 + s) * SEQ : (2 + s) * SEQ]
            grad_probs = dot(grad, v, 1, 1)
            inner = jnp.sum(share * grad_probs, axis=-1, keepdims=True)
            grad_scores = (share * (grad_probs - inner)).astype(BF16)
            scores.append(beside(grad_scores))
            rb[rows, cols[0]] = (dot(scores[s], heads(k)) * SCALE).astype(BF16)
            rb[rows, cols[1]] = (dot(grad_scores, heads(q), 0, 0) * SCALE).astype(BF16)
            rb[rows, cols[2]] = dot(share.astype(BF16), grad, 0, 0).astype(BF16)
        flipped = dot(flip, jnp.concatenate(scores, axis=0))
        for j in range(2):
            rolled = pltpu.roll(flipped[:, j * SEQ : (j + 1) * SEQ], 1, 1, stride=1, stride_axis=0)
            rel_rows[pl.ds(2 * p + j, 1), :] = jnp.sum(rolled, axis=0, keepdims=True)
        return carry

    for t in range(3):
        lax.fori_loop(2 * t, 2 * t + 2, pair, 0)
        formed[t]()
    grad_low = dot(rb[:, 0:LEFTC], wall[:, 0:LEFTC], 1, 1) + dot(
        rb[:, LEFTC : 3 * D], wall[:, HIGH:WALL], 1, 1
    )
    state = x_ref[...].astype(F32)
    factor = unit(state)
    scaled = state * factor
    small_t[0:1, :] = jnp.sum(grad_low * scaled, axis=0, keepdims=True)
    grad_low = grad_low * rows_t[0:1, :]
    inner = jnp.mean(grad_low * scaled, axis=-1, keepdims=True)
    grad_tokens[...] = hidden[...] + factor * (grad_low - scaled * inner)

    spot = lax.broadcasted_iota(jnp.int32, (SEQ, D), 0)
    column = lax.broadcasted_iota(jnp.int32, (SEQ, D), 1)
    distance = (SEQ - spot) & (SEQ - 1)
    picks = jnp.where(column == (distance >> 4) * SHARD + (distance & 15), 1.0, 0.0).astype(BF16)
    rest = rel_rows[...]
    spread = jnp.zeros((16, D), F32)
    for _ in range(3):
        high = rest.astype(BF16)
        spread = spread + dot(high, picks)
        rest = rest - high.astype(F32)
    small_t[HEAD : HEAD + 16, :] = spread


HC = D // 2
SMALLS = SENTC - 128
STRAIGHT = (0, 1, 2, 3, 4)


def portions(group):
    if group == 0:
        return 1, 2 * HC, HC, ((0, HC, lambda core: 3 * D + core * HC, lambda core: core * HC),)
    if group == 4:
        return 0, SMALLS, 128, ()
    t = group - 1
    both = (
        (0, 256, lambda core: core * D + 256 * t, lambda core: core * D + 256 * t),
        (256, 128, lambda core: 2 * D + 256 * t + 128 * core, lambda core: 2 * D + 256 * t + 128 * core),
    )
    return 0, (0, HC, 3 * HC)[t], HC, both


class Reduction:
    def __init__(self, links, group, left, rb, small_t, give, take, total, y_take, z_take, face_give, face_take, last):
        self.links, self.group = links, group
        which, first, width, portion = portions(group)
        self.cols = slice(first, first + width)
        self.portion = [(slice(first + at, first + at + wide), wide, rhs, target) for at, wide, rhs, target in portion]
        self.lhs, self.rb, self.small_t = left.at[which], rb, small_t
        self.give, self.take, self.total = give, take, total
        self.y_take, self.z_take, self.face_give, self.face_take, self.last = y_take, z_take, face_give, face_take, last
        x, c, z, y = self.place = place()
        self.across, self.facing, self.twin = device(x, c, z, 1 - y), device(1 - x, c, z, y), device(x, 1 - c, z, y)
        mirror = z // 2
        near = z + mirror * (3 - 2 * z)
        self.order = [o + mirror * (3 - 2 * o) for o in (3, 2, 1 - near, near)]

    def tile(self, core, keep):
        def step(m, carry):
            rows = pl.ds(pl.multiple_of(m * 256, 256), 256)
            for cols, wide, rhs, target in self.portion:
                right = self.rb[:, pl.ds(pl.multiple_of(rhs(core), 128), wide)]
                keep[rows, cols] = dot(self.lhs[:, rows], right, 0, 0).astype(keep.dtype)
            return carry

        lax.fori_loop(0, 3, step, 0)

    def form(self):
        x, c, z, y = self.place
        self.tile(1 - c, self.give)
        self.to_twin()
        self.tile(c, self.total)

    def to_twin(self):
        slot, cols = RS_TWIN + self.group, self.cols
        self.sent = self.links.go(None, self.give.at[:, cols], self.take.at[:, cols], slot, slot, self.twin)

    def form_small(self):
        small = jnp.transpose(self.small_t[...]).astype(BF16)
        self.give[:, self.cols] = small
        self.to_twin()
        self.total[:, self.cols] = small.astype(F32)

    def shard(self, zs, ys):
        return pl.ds(pl.multiple_of((zs * 2 + ys) * SHARD, 16), SHARD)

    def halve(self):
        x, c, z, y = self.place
        links, cols = self.links, self.cols
        links.arrive(None, self.take.at[:, cols], RS_TWIN + self.group, self.twin)
        links.leave(self.sent)
        for zs in self.order:
            rows = self.shard(zs, 1 - y)
            self.give[rows, cols] = (self.total[rows, cols] + self.take[rows, cols].astype(F32)).astype(BF16)
            slot = RS_Y + self.group * 4 + zs
            links.go(None, self.give.at[rows, cols], self.y_take.at[zs, :, cols], slot, slot, self.across)
        for zs in self.order:
            rows = self.shard(zs, y)
            self.total[rows, cols] = self.total[rows, cols] + self.take[rows, cols].astype(F32)

    def chain(self, k):
        x, c, z, y = self.place
        links, cols, zs = self.links, self.cols, self.order[k]
        total, z_take = self.total, self.z_take
        rows = self.shard(zs, y)
        links.arrive(None, self.y_take.at[zs, :, cols], RS_Y + self.group * 4 + zs, self.across)
        total[rows, cols] = total[rows, cols] + self.y_take[zs, :, cols].astype(F32)
        if k == 3:
            return
        if self.group in STRAIGHT:
            self.give[rows, cols] = total[rows, cols].astype(BF16)
            base = RS_Z + self.group * 8
            links.go(None, self.give.at[rows, cols], z_take.at[z, :, cols], base + k, base + z, device(x, c, zs, y))
            return
        for cond, more, slot, target in (
            (zs > z, z > 0, zs, device(x, c, z + 1, y)),
            (zs < z, z < 3, 4 + zs, device(x, c, z - 1, y)),
        ):
            self.add_from_z(cond & more, slot, rows)

            @pl.when(cond)
            def _():
                self.give[rows, cols] = total[rows, cols].astype(BF16)

            index = RS_Z + self.group * 8 + slot
            links.go(cond, self.give.at[rows, cols], z_take.at[slot, :, cols], index, index, target)

    def add_from_z(self, cond, slot, rows):
        cols = self.cols

        @pl.when(cond)
        def _():
            part = self.z_take.at[slot, :, cols]
            self.links.arrive(None, part, RS_Z + self.group * 8 + slot, self.across)
            self.total[rows, cols] = self.total[rows, cols] + part[...].astype(F32)

    def face(self):
        x, c, z, y = self.place
        rows, cols = self.shard(z, y), self.cols
        if self.group in STRAIGHT:
            for d in (1, 2, 3):
                zs = (z + d) % 4
                self.links.arrive(None, self.z_take.at[zs, :, cols], RS_Z + self.group * 8 + zs, self.across)
                self.total[rows, cols] = self.total[rows, cols] + self.z_take[zs, :, cols].astype(F32)
        else:
            self.add_from_z(z > 0, z, rows)
            self.add_from_z(z < 3, 4 + z, rows)
        self.face_give[:, cols] = self.total[rows, cols].astype(BF16)
        slot = RS_FACE + self.group
        self.links.go(None, self.face_give.at[:, cols], self.face_take.at[:, cols], slot, slot, self.facing)

    def publish(self, out_qkv, out_proj, out_small, local_sem):
        x, c, z, y = self.place
        cols = self.cols
        self.links.arrive(None, self.face_take.at[:, cols], RS_FACE + self.group, self.facing)
        self.last[:, cols] = self.face_give[:, cols].astype(F32) + self.face_take[:, cols].astype(F32)
        self.out = out_proj if self.group == 0 else out_qkv
        copies = []
        for i, (part, there) in enumerate(self.landing(c)):
            slot = RS_OUT + self.group * 2 + i
            self.links.go(None, part, there, slot, slot, self.twin)
            copies.append(pltpu.make_async_copy(part, there, local_sem.at[16 + self.group * 2 + i]))
        if self.group == 4:
            copies.append(pltpu.make_async_copy(self.last.at[:, cols], out_small, local_sem.at[6]))
        for copy in copies:
            copy.start()
        return copies

    def landing(self, core):
        return [
            (self.last.at[:, cols], self.out.at[:, pl.ds(pl.multiple_of(target(core), 128), wide)])
            for cols, wide, rhs, target in self.portion
        ]

    def landed(self):
        x, c, z, y = self.place
        for i, (part, there) in enumerate(self.landing(1 - c)):
            self.links.arrive(None, there, RS_OUT + self.group * 2 + i, self.twin)


def layer(
    x_in, cot_in, lengths, routes, slots, gain_attn, gain_moe, router_t, rel, wq, wp, w_up, w_down,
    mixed_out, tokens_out, out_qkv, out_proj, out_small, out_up, out_down,
    x_ref, cot, mixed, grad_tokens, board,
    wall, rows_t, lines, columns, left, qkv, hidden, normed2, gates, out_f, out_g, recv_f, recv_g, up, down, act, slope,
    part_f, part_g, take_f, take_g, back_f, back_g, dn_own, dn_give, dn_take, dn_face, up_own, up_give, up_take, up_face,
    rb, rel_rows, small_t, take, total, y_take, z_take, face_give, face_take, last,
    local_sem, send_sem, recv_sem,
):
    inputs = [
        pltpu.make_async_copy(x_in, x_ref, local_sem.at[24]),
        pltpu.make_async_copy(cot_in, cot, local_sem.at[25]),
    ]
    fetch = [
        pltpu.make_async_copy(w_up.at[0], up, local_sem.at[4]),
        pltpu.make_async_copy(w_down.at[0], down, local_sem.at[5]),
    ]
    met = greet()
    links = Links(send_sem, recv_sem)

    def ready():
        pack(gain_attn, gain_moe, router_t, rel, board, wall)
        stand(routes, slots, lines, columns)
        rel_rows[...] = jnp.zeros_like(rel_rows)
        met()

    later = gather_weights(links, wq, wp, wall, local_sem, inputs + fetch, ready)
    for copy in inputs:
        copy.wait()
    normed, attended = left.at[0], left.at[1]
    attention_forward(
        later, x_ref, cot, lengths, columns, wall, rows_t, board, normed, qkv, attended, hidden, normed2, gates, out_f, out_g
    )
    for copy in fetch:
        copy.wait()
    downs, ups = (dn_own, dn_give, dn_take, dn_face), (up_own, up_give, up_take, up_face)
    experts(
        links, (out_f, out_g), (recv_f, recv_g), up, down, act, slope, (part_f, part_g), (take_f, take_g),
        (back_f, back_g), downs, ups,
    )
    combine(cot, lengths, columns, rows_t, hidden, normed2, gates, back_f, back_g, mixed, rb, small_t)
    pending = []

    def put(src, dst, i):
        copy = pltpu.make_async_copy(src, dst, local_sem.at[i])
        copy.start()
        pending.append(copy)

    put(mixed, mixed_out, 26)
    proj, one, two, three, small = (
        Reduction(
            links, group, left, rb, small_t, act.at[0:D, :], take, total, y_take, z_take, face_give, face_take, last
        )
        for group in range(5)
    )

    def grads(piece):
        pending.append(expert_grad_out(links, piece, downs, ups, out_down, out_up, local_sem))

    def publish(item):
        pending.extend(item.publish(out_qkv, out_proj, out_small, local_sem))

    def early():
        one.form()
        proj.chain(0)

    def middle():
        one.halve()
        two.form()
        proj.chain(1)

    def late():
        two.halve()
        three.form()
        proj.chain(2)
        one.chain(0)
        three.halve()

    proj.form()
    attention_backward(
        x_ref, wall, rows_t, qkv, board, hidden, normed2, rb, rel_rows, small_t, grad_tokens, proj.halve,
        (early, middle, late),
    )
    small.form_small()
    put(grad_tokens, tokens_out, 27)
    proj.chain(3)
    one.chain(1)
    small.halve()
    two.chain(0)
    one.chain(2)
    grads(0)
    proj.face()
    two.chain(1)
    one.chain(3)
    grads(1)
    three.chain(0)
    two.chain(2)
    three.chain(1)
    grads(2)
    one.face()
    three.chain(2)
    small.chain(0)
    two.chain(3)
    small.chain(1)
    small.chain(2)
    grads(3)
    publish(proj)
    two.face()
    grads(4)
    three.chain(3)
    small.chain(3)
    grads(5)
    publish(one)
    three.face()
    small.face()
    publish(two)
    publish(three)
    publish(small)
    for item in (proj, one, two, three):
        item.landed()
    expert_grads_arrive(links, out_down, out_up)
    for copy in pending:
        copy.wait()
    links.finish()


PARTS = 6


def hand_out(
    mixed, tokens, qkv, proj, small, up, down,
    to_mixed, to_tokens, to_qkv, to_proj, to_gain_attn, to_gain_moe, to_router, to_rel, to_up, to_down,
    v_mixed, v_tokens, v_qkv, v_proj, v_small, v_up, v_down,
    v_gain_attn, v_gain_moe, v_router, v_rel, wide_up, wide_down, in_sem, out_sem,
):
    def rows(array, i):
        count = array.shape[0] // PARTS
        return pl.ds(i * count, count)

    def copy(src, dst, sem, i):
        item = pltpu.make_async_copy(src, dst, sem.at[i])
        item.start()
        return item

    halves = [
        (source, held, wide, out, rows(source, i))
        for i in range(PARTS)
        for source, held, wide, out in ((up, v_up, wide_up, to_up), (down, v_down, wide_down, to_down))
    ]
    coming = [copy(source.at[at], held.at[at], in_sem, i) for i, (source, held, _, _, at) in enumerate(halves)]
    plain = ((tokens, v_tokens, to_tokens), (qkv, v_qkv, to_qkv), (mixed, v_mixed, to_mixed), (proj, v_proj, to_proj))
    first = len(halves)
    little = copy(small, v_small, in_sem, first + len(plain))
    others = [copy(source, held, in_sem, first + i) for i, (source, held, _) in enumerate(plain)]
    going = []

    def put(src, dst):
        going.append(copy(src, dst, out_sem, len(going)))

    for item, (source, held, wide, out, at) in zip(coming, halves):
        item.wait()
        wide[at] = held[at].astype(F32)
        put(wide.at[at], out.at[at])
    little.wait()
    turned = jnp.transpose(v_small[...])
    v_gain_attn[...] = turned[0]
    v_gain_moe[...] = turned[1]
    v_router[...] = turned[2 : 2 + EXP]
    v_rel[...] = v_small[0:16, HEAD : HEAD + HEADS]
    put(v_gain_attn, to_gain_attn)
    put(v_gain_moe, to_gain_moe)
    put(v_router, to_router)
    put(v_rel, to_rel)
    for item, (_, held, out) in zip(others, plain):
        item.wait()
        put(held, out)
    for item in going:
        item.wait()


def body_fast(
    tokens, cotangent, lengths, routes, slots, gain_attn, w_qkv, w_proj, rel_table, gain_moe, w_router, w_up, w_down
):
    vm = pl.BlockSpec(memory_space=pltpu.VMEM)
    hbm = pl.BlockSpec(memory_space=pl.ANY)
    sds = jax.ShapeDtypeStruct
    v = pltpu.VMEM
    shapes = (
        sds((TOK, D), BF16), sds((TOK, D), F32), sds((SHARD, 3 * D), F32), sds((SHARD, D), F32),
        sds((SHARD, 128), F32), sds((D, HF), BF16), sds((HF, D), BF16),
    )
    out = pl.pallas_call(
        layer,
        out_shape=shapes,
        in_specs=[hbm, hbm, pl.BlockSpec(memory_space=pltpu.SMEM), vm, vm, vm, vm, vm, vm, hbm, hbm, hbm, hbm],
        out_specs=[hbm, hbm, hbm, hbm, hbm, hbm, hbm],
        scratch_shapes=[
            v((TOK, D), BF16), v((TOK, D), BF16), v((TOK, D), BF16), v((TOK, D), F32), v((HEADS * SEQ, 3 * SEQ), F32),
            v((D, WALL), BF16), v((8, D), F32), v((8, TOK), F32), v((TOK, 8), F32), v((2, TOK, D), BF16),
            v((TOK, 3 * D), BF16), v((TOK, D), F32), v((TOK, D), BF16),
            v((TOK, 1), F32), v((EXP, ROWS, D), BF16), v((EXP, ROWS, D), BF16),
            v((8 * ROWS, D), BF16), v((8 * ROWS, D), BF16), v((D, HF), BF16), v((HF, D), BF16),
            v((8 * ROWS, SENTC), BF16), v((8 * ROWS, HF), BF16),
            v((EXP, 2, ROWS, D), BF16), v((EXP, 2, ROWS, D), BF16), v((EXP, ROWS, D), BF16), v((EXP, ROWS, D), BF16),
            v((EXP, ROWS, D), BF16), v((EXP, ROWS, D), BF16),
            v((HF // 2, D), F32), v((HF // 2, D), BF16), v((HF // 2, D), BF16), v((HF // 2, D), BF16),
            v((D // 2, HF), F32), v((D // 2, HF), BF16), v((D // 2, HF), BF16), v((D // 2, HF), BF16),
            v((TOK, 4 * D), BF16), v((16, SEQ), F32), v((128, D), F32),
            v((D, SENTC), BF16), v((D, SENTC), F32), v((4, SHARD, SENTC), BF16), v((8, SHARD, SENTC), BF16),
            v((SHARD, SENTC), BF16), v((SHARD, SENTC), BF16), v((SHARD, SENTC), F32),
            pltpu.SemaphoreType.DMA((28,)), pltpu.SemaphoreType.DMA((LINKS,)), pltpu.SemaphoreType.DMA((LINKS,)),
        ],
        compiler_params=pltpu.CompilerParams(
            collective_id=0, has_side_effects=True, vmem_limit_bytes=67043328
        ),
        name="layer",
    )(
        tokens, cotangent, lengths, routes.T, slots.T, gain_attn[None], gain_moe[None], w_router.T, rel_table, w_qkv, w_proj,
        w_up, w_down,
    )
    small = (sds((SHARD,), F32), sds((SHARD,), F32), sds((EXP, SHARD), F32), sds((16, HEADS), F32))
    final = shapes[:4] + small + (sds((D, HF), F32), sds((HF, D), F32))
    mixed, grad_tokens, grad_qkv, grad_proj, grad_gain_attn, grad_gain_moe, grad_router, grad_rel, grad_up, grad_down = (
        pl.pallas_call(
            hand_out,
            out_shape=final,
            in_specs=[hbm] * len(shapes),
            out_specs=[hbm] * len(final),
            scratch_shapes=[v(item.shape, item.dtype) for item in shapes + small + final[-2:]]
            + [pltpu.SemaphoreType.DMA((2 * PARTS + 5,)), pltpu.SemaphoreType.DMA((2 * PARTS + 8,))],
            name="hand_out",
        )(*out)
    )
    return (
        mixed,
        grad_tokens,
        grad_gain_attn,
        grad_qkv,
        grad_proj,
        grad_rel,
        grad_gain_moe,
        grad_router.T,
        grad_up[None],
        grad_down[None],
    )


epsilon = 1e-06
exact_precision = lax.Precision.HIGHEST


def rms_norm(values, gain):
    factor = lax.rsqrt(jnp.mean(values * values, axis=-1, keepdims=True) + epsilon)
    return values * factor * gain


def distance_hot():
    places = jnp.arange(SEQ, dtype=jnp.int32)
    distance = jnp.clip(places[:, None] - places[None, :], 0, SEQ - 1).reshape(1, SEQ * SEQ)
    return (distance == places[:, None]).astype(jnp.bfloat16)


def bias_matrix(table, hot):
    flat = jnp.einsum("dh,dp->hp", table, hot, preferred_element_type=jnp.float32)
    return flat.reshape(table.shape[1], SEQ, SEQ)


def exact_gelu(values):
    return jax.nn.gelu(values, approximate=False)


def masked_scores(qkv_rows, bias, allowed, factor):
    raw = jnp.einsum(
        "qhd,khd->hqk", qkv_rows[:, 0], qkv_rows[:, 1], preferred_element_type=jnp.float32
    )
    return jnp.where(allowed[None], raw * factor + bias, -1e30)


def fetch_weights(gain_attn, w_qkv, w_proj, rel_table, gain_moe, w_router):
    rows, experts = w_router.shape
    spread = rel_table.shape[0]
    packed = jnp.concatenate(
        [gain_attn, gain_moe, w_router.reshape(-1), rel_table.reshape(-1)]
    )
    small = lax.all_gather(packed, "fsdp", axis=0, tiled=False)
    groups = small.shape[0]
    edge = 2 * rows + rows * experts
    return (
        small[:, :rows].reshape(-1),
        lax.all_gather(w_qkv, "fsdp", axis=0, tiled=True),
        lax.all_gather(w_proj, "fsdp", axis=0, tiled=True),
        small[:, edge:].reshape(groups * spread, HEADS),
        small[:, rows : 2 * rows].reshape(-1),
        small[:, 2 * rows : edge].reshape(groups * rows, experts),
    )


def body(
    tokens,
    cotangent,
    lengths,
    routes,
    slots,
    gain_attn,
    w_qkv,
    w_proj,
    rel_table,
    gain_moe,
    w_router,
    w_up,
    w_down,
):
    groups = lax.axis_size("fsdp")
    experts = groups // 2
    capacity = 2 * SEQ // experts
    factor = HEAD ** (-0.5)
    up_weight = w_up[0]
    down_weight = w_down[0]
    places = jnp.arange(SEQ, dtype=jnp.int32)
    causal = places[:, None] >= places[None, :]
    expert_ids = jnp.arange(experts, dtype=jnp.int32)
    saved = []
    mixed_parts = []
    weights = fetch_weights(gain_attn, w_qkv, w_proj, rel_table, gain_moe, w_router)
    gain_a = weights[0].astype(jnp.float32)
    gain_m = weights[4].astype(jnp.float32)
    router_float = weights[5].astype(jnp.float32)
    hot = distance_hot()
    bias = bias_matrix(weights[3], hot)
    for batch in range(MB):
        x_float = tokens[batch * SEQ : (batch + 1) * SEQ].astype(jnp.float32)
        live_keys = places < lengths[batch]
        live_col = live_keys.astype(jnp.float32)[:, None]
        allowed = causal & live_keys[None, :]
        normed = rms_norm(x_float, gain_a).astype(jnp.bfloat16)
        qkv_rows = (
            jnp.dot(normed, weights[1], preferred_element_type=jnp.float32)
            .astype(jnp.bfloat16)
            .reshape(SEQ, 3, HEADS, HEAD)
        )
        scores = masked_scores(qkv_rows, bias, allowed, factor)
        row_peak = jnp.max(scores, axis=-1, keepdims=True)
        exp_scores = jnp.exp(scores - row_peak)
        row_total = jnp.sum(exp_scores, axis=-1, keepdims=True)
        log_total = row_peak + jnp.log(row_total)
        probs_low = (exp_scores / row_total).astype(jnp.bfloat16)
        attended = jnp.einsum(
            "hqk,khd->qhd", probs_low, qkv_rows[:, 2], preferred_element_type=jnp.float32
        )
        attended = attended.astype(jnp.bfloat16).reshape(SEQ, D)
        branch = jnp.dot(attended, weights[2], preferred_element_type=jnp.float32)
        hidden = x_float + live_col * branch
        normed2 = rms_norm(hidden, gain_m).astype(jnp.bfloat16)
        logits = jnp.dot(normed2, weights[5], preferred_element_type=jnp.float32)
        route_rows = routes[batch * SEQ : (batch + 1) * SEQ]
        slot_rows = slots[batch * SEQ : (batch + 1) * SEQ]
        hot_first = (route_rows[:, 0:1] == expert_ids[None, :]).astype(jnp.float32)
        hot_second = (route_rows[:, 1:2] == expert_ids[None, :]).astype(jnp.float32)
        gate_first = jax.nn.sigmoid(
            jnp.sum(logits * hot_first, axis=-1) - jnp.sum(logits * hot_second, axis=-1)
        )
        row_place = route_rows * capacity + slot_rows
        target = jnp.where(live_keys[:, None], row_place, experts * capacity)
        outgoing = jnp.zeros((experts * capacity, D), jnp.bfloat16)
        outgoing = (
            outgoing.at[target[:, 0]]
            .set(normed2, mode="drop")
            .at[target[:, 1]]
            .set(normed2, mode="drop")
        )
        outgoing = jnp.repeat(outgoing.reshape(experts, capacity, D), 2, axis=0)
        expert_received = lax.all_to_all(outgoing, "fsdp", split_axis=0, concat_axis=0, tiled=True)
        expert_before = jnp.einsum(
            "scd,df->scf", expert_received, up_weight, preferred_element_type=jnp.float32
        )
        expert_active = exact_gelu(expert_before).astype(jnp.bfloat16)
        partial_value = jnp.einsum(
            "scf,fd->scd", expert_active, down_weight, preferred_element_type=jnp.float32
        ).astype(jnp.bfloat16)
        returned = lax.all_to_all(partial_value, "fsdp", split_axis=0, concat_axis=0, tiled=True)
        results = (returned, expert_received, expert_before)
        combined = (
            results[0]
            .astype(jnp.float32)
            .reshape(experts, 2, capacity, D)
            .sum(axis=1)
            .reshape(experts * capacity, D)
        )
        first_out = combined[row_place[:, 0]]
        second_out = combined[row_place[:, 1]]
        moe = live_col * (
            gate_first[:, None] * first_out + (1.0 - gate_first)[:, None] * second_out
        )
        mixed_parts.append((hidden + moe).astype(jnp.bfloat16))
        saved.append(
            {
                "normed": normed,
                "qkv_rows": qkv_rows,
                "log_total": log_total,
                "attended": attended,
                "hidden": hidden,
                "normed2": normed2,
                "gate_first": gate_first,
                "first_out": first_out,
                "second_out": second_out,
                "results": results,
                "target": target,
                "row_place": row_place,
                "hot_first": hot_first,
                "hot_second": hot_second,
            }
        )
    grad_qkv_w = jnp.zeros((D, 3 * D), jnp.float32)
    grad_proj_w = jnp.zeros((D, D), jnp.float32)
    grad_table = jnp.zeros((SEQ, HEADS), jnp.float32)
    grad_gain_a = jnp.zeros((D,), jnp.float32)
    grad_gain_m = jnp.zeros((D,), jnp.float32)
    grad_router = jnp.zeros((D, experts), jnp.float32)
    grad_up = jnp.zeros((D, FF // 2), jnp.float32)
    grad_down = jnp.zeros((FF // 2, D), jnp.float32)
    grad_parts = [None] * MB
    for batch in reversed(range(MB)):
        kept = saved[batch]
        x_float = tokens[batch * SEQ : (batch + 1) * SEQ].astype(jnp.float32)
        live_keys = places < lengths[batch]
        live_col = live_keys.astype(jnp.float32)[:, None]
        allowed = causal & live_keys[None, :]
        grad_out = cotangent[batch * SEQ : (batch + 1) * SEQ].astype(jnp.float32)
        grad_moe = live_col * grad_out
        gate_first = kept["gate_first"]
        gate_second = 1.0 - gate_first
        grad_gate_first = jnp.sum(grad_moe * kept["first_out"], axis=-1)
        grad_gate_second = jnp.sum(grad_moe * kept["second_out"], axis=-1)
        grad_first = (gate_first[:, None] * grad_moe).astype(jnp.bfloat16)
        grad_second = (gate_second[:, None] * grad_moe).astype(jnp.bfloat16)
        target = kept["target"]
        grad_send = jnp.zeros((experts * capacity, D), jnp.bfloat16)
        grad_send = (
            grad_send.at[target[:, 0]]
            .set(grad_first, mode="drop")
            .at[target[:, 1]]
            .set(grad_second, mode="drop")
        )
        grad_send = jnp.repeat(grad_send.reshape(experts, capacity, D), 2, axis=0)
        grad_recv = lax.all_to_all(grad_send, "fsdp", split_axis=0, concat_axis=0, tiled=True)
        received = kept["results"][1]
        before = kept["results"][2]
        active, gelu_back = jax.vjp(exact_gelu, before)
        active_low = active.astype(jnp.bfloat16)
        grad_active = jnp.einsum(
            "scd,fd->scf", grad_recv, down_weight, preferred_element_type=jnp.float32
        )
        grad_before = gelu_back(grad_active)[0].astype(jnp.bfloat16)
        grad_down = grad_down + jnp.einsum(
            "scf,scd->fd", active_low, grad_recv, preferred_element_type=jnp.float32
        )
        grad_up = grad_up + jnp.einsum(
            "scd,scf->df", received, grad_before, preferred_element_type=jnp.float32
        )
        grad_part = jnp.einsum(
            "scf,df->scd", grad_before, up_weight, preferred_element_type=jnp.float32
        ).astype(jnp.bfloat16)
        grad_back = lax.all_to_all(grad_part, "fsdp", split_axis=0, concat_axis=0, tiled=True)
        grad_rows = (
            grad_back.astype(jnp.float32)
            .reshape(experts, 2, capacity, D)
            .sum(axis=1)
            .reshape(experts * capacity, D)
        )
        row_place = kept["row_place"]
        grad_diff = (grad_gate_first - grad_gate_second) * gate_first * gate_second
        grad_logits = grad_diff[:, None] * (kept["hot_first"] - kept["hot_second"])
        normed2_float = kept["normed2"].astype(jnp.float32)
        grad_router = grad_router + jnp.dot(normed2_float.T, grad_logits, precision=exact_precision)
        grad_normed2 = live_col * (grad_rows[row_place[:, 0]] + grad_rows[row_place[:, 1]])
        grad_normed2 = grad_normed2 + jnp.dot(
            grad_logits, router_float.T, precision=exact_precision
        )
        _, norm_back_moe = jax.vjp(rms_norm, kept["hidden"], gain_m)
        grad_hidden_norm, grad_gain_part = norm_back_moe(grad_normed2)
        grad_gain_m = grad_gain_m + grad_gain_part
        grad_hidden = grad_out + grad_hidden_norm
        grad_branch = (live_col * grad_hidden).astype(jnp.bfloat16)
        grad_proj_w = grad_proj_w + jnp.einsum(
            "sd,se->de", kept["attended"], grad_branch, preferred_element_type=jnp.float32
        )
        grad_attended = jnp.einsum(
            "se,de->sd", grad_branch, weights[2], preferred_element_type=jnp.float32
        )
        grad_attended = grad_attended.astype(jnp.bfloat16).reshape(SEQ, HEADS, HEAD)
        qkv_rows = kept["qkv_rows"]
        scores = masked_scores(qkv_rows, bias, allowed, factor)
        probs = jnp.exp(scores - kept["log_total"])
        probs_low = probs.astype(jnp.bfloat16)
        grad_probs = jnp.einsum(
            "qhd,khd->hqk", grad_attended, qkv_rows[:, 2], preferred_element_type=jnp.float32
        )
        row_dot = jnp.sum(probs * grad_probs, axis=-1, keepdims=True)
        grad_scores = (probs * (grad_probs - row_dot)).astype(jnp.bfloat16)
        grad_table = grad_table + jnp.einsum(
            "dp,hp->dh",
            hot,
            jnp.where(allowed[None], grad_scores, 0).reshape(HEADS, SEQ * SEQ),
            preferred_element_type=jnp.float32,
        )
        grad_queries = (
            jnp.einsum(
                "hqk,khd->qhd", grad_scores, qkv_rows[:, 1], preferred_element_type=jnp.float32
            )
            * factor
        )
        grad_keys = (
            jnp.einsum(
                "hqk,qhd->khd", grad_scores, qkv_rows[:, 0], preferred_element_type=jnp.float32
            )
            * factor
        )
        grad_values = jnp.einsum(
            "hqk,qhd->khd", probs_low, grad_attended, preferred_element_type=jnp.float32
        )
        grad_qkv = (
            jnp.stack([grad_queries, grad_keys, grad_values], axis=1)
            .astype(jnp.bfloat16)
            .reshape(SEQ, 3 * D)
        )
        grad_qkv_w = grad_qkv_w + jnp.einsum(
            "sd,se->de", kept["normed"], grad_qkv, preferred_element_type=jnp.float32
        )
        grad_normed = jnp.einsum(
            "se,de->sd", grad_qkv, weights[1], preferred_element_type=jnp.float32
        )
        _, norm_back_attn = jax.vjp(rms_norm, x_float, gain_a)
        grad_x_norm, grad_gain_piece = norm_back_attn(grad_normed)
        grad_gain_a = grad_gain_a + grad_gain_piece
        grad_parts[batch] = grad_hidden + grad_x_norm
    small = jnp.concatenate(
        [
            grad_gain_a.reshape(groups, -1),
            grad_gain_m.reshape(groups, -1),
            grad_router.reshape(groups, -1),
            grad_table.reshape(groups, -1),
        ],
        axis=1,
    )
    small = lax.psum_scatter(small, "fsdp", scatter_dimension=0, tiled=True)
    shards = (
        small,
        lax.psum_scatter(grad_qkv_w, "fsdp", scatter_dimension=0, tiled=True),
        lax.psum_scatter(grad_proj_w, "fsdp", scatter_dimension=0, tiled=True),
    )
    sums = lax.psum((shards[0], shards[1], shards[2], grad_up[None], grad_down[None]), "replica")
    rows = D // groups
    edge = 2 * rows + rows * experts
    totals = (
        sums[0][0, :rows],
        sums[1],
        sums[2],
        sums[0][0, edge:].reshape(SEQ // groups, HEADS),
        sums[0][0, rows : 2 * rows],
        sums[0][0, 2 * rows : edge].reshape(rows, experts),
        sums[3],
        sums[4],
    )
    mixed = jnp.concatenate(mixed_parts, axis=0)
    grad_tokens = jnp.concatenate(grad_parts, axis=0)
    return (
        mixed,
        grad_tokens,
        totals[0],
        totals[1],
        totals[2],
        totals[3],
        totals[4],
        totals[5],
        totals[6],
        totals[7],
    )


def solution(mesh):
    in_specs = (
        P(("replica", "fsdp"), None),
        P(("replica", "fsdp"), None),
        P(("replica", "fsdp")),
        P(("replica", "fsdp"), None),
        P(("replica", "fsdp"), None),
        P("fsdp"),
        P("fsdp", None),
        P("fsdp", None),
        P("fsdp", None),
        P("fsdp"),
        P("fsdp", None),
        P("fsdp", None, None),
        P("fsdp", None, None),
    )
    out_specs = (
        P(("replica", "fsdp"), None),
        P(("replica", "fsdp"), None),
        P("fsdp"),
        P("fsdp", None),
        P("fsdp", None),
        P("fsdp", None),
        P("fsdp"),
        P("fsdp", None),
        P("fsdp", None, None),
        P("fsdp", None, None),
    )
    fast = dict(mesh.shape) == {"replica": 4, "fsdp": 8}
    return jax.shard_map(body_fast if fast else body, mesh=mesh, in_specs=in_specs, out_specs=out_specs, check_vma=False)
```

```python
import functools

import jax
import jax.numpy as jnp
from jax import lax
from jax.experimental import pallas as pl
from jax.experimental.pallas import tpu as pltpu
from jax.sharding import PartitionSpec as P

D = 768
HEADS = 12
HEAD = 64
FF = 3072
SEQ = 128
MB = 2
MESH = pl.DeviceIdType.MESH
F32 = jnp.float32
BF16 = jnp.bfloat16
NEG = -1e30
HF = FF // 2
TOK = MB * SEQ
EXP = 4
CAP = 64
ROWS = MB * CAP
LOW = 896
MID = 3 * D - 2 * LOW
MORE = MID + 128
SMALL = LOW + MID
PROJ = LOW + MORE
HIGH = PROJ + D
WALL = HIGH + LOW
LEFTC = LOW + MID
SHARD = 96
HALF = SHARD // 2
PAIRS = HEADS // 2
SCALE = HEAD ** (-0.5)


def place():
    replica = lax.axis_index("replica")
    group = lax.axis_index("fsdp")
    return replica // 2, replica % 2, group // 2, group % 2


def device(x, c, z, y):
    return (x * 2 + c, z * 2 + y)


def remote(src, dst, send, recv, target):
    return pltpu.make_async_remote_copy(
        src_ref=src,
        dst_ref=dst,
        send_sem=send,
        recv_sem=recv,
        device_id=target,
        device_id_type=MESH,
    )


def greet():
    x, c, z, y = place()
    barrier = pltpu.get_barrier_semaphore()
    targets = [device(x, 1 - c, z, y), device(1 - x, c, z, y), device(x, c, z, 1 - y)]
    targets += [device(x, c, (z + k) % 4, y) for k in (1, 2, 3)]
    for target in targets:
        pl.semaphore_signal(barrier, inc=1, device_id=target, device_id_type=MESH)
    return lambda: pl.semaphore_wait(barrier, len(targets))


def dot(a, b, ca=1, cb=0):
    return lax.dot_general(a, b, (((ca,), (cb,)), ((), ())), preferred_element_type=F32)


def run(cond, what):
    if cond is None:
        what()
    else:
        pl.when(cond)(what)


class Links:
    def __init__(self, send_sem, recv_sem):
        self.send_sem, self.recv_sem = send_sem, recv_sem
        self.started = []

    def go(self, cond, src, dst, send, recv, target):
        copy = remote(src, dst, self.send_sem.at[send], self.recv_sem.at[recv], target)
        run(cond, copy.start)
        self.started.append((cond, copy))
        return copy

    def arrive(self, cond, dst, recv, target):
        run(cond, remote(dst, dst, self.send_sem.at[0], self.recv_sem.at[recv], target).wait_recv)

    def leave(self, copy):
        copy.wait_send()
        self.started = [(cond, item) for cond, item in self.started if item is not copy]

    def finish(self):
        for cond, copy in self.started:
            run(cond, copy.wait_send)
        self.started = []


def gather_weights(links, wq, wp, wall, local_sem, others, ready):
    x, c, z, y = place()
    own = pl.ds(pl.multiple_of((z * 2 + y) * SHARD, 16), SHARD)
    fills = [
        pltpu.make_async_copy(wq.at[:, pl.ds(0, LEFTC)], wall.at[own, pl.ds(0, LEFTC)], local_sem.at[0]),
        pltpu.make_async_copy(wq.at[:, pl.ds(LEFTC, LOW)], wall.at[own, pl.ds(HIGH, LOW)], local_sem.at[1]),
        pltpu.make_async_copy(wp, wall.at[own, pl.ds(PROJ, D)], local_sem.at[2]),
    ]
    for copy in fills + others:
        copy.start()
    ready()
    share = pl.ds(pl.multiple_of(x * HIGH, 128), LOW)
    gained = pl.ds(pl.multiple_of((1 - x) * HIGH, 128), LOW)
    columns = (share, pl.ds(LOW, MORE), pl.ds(PROJ, D))
    up, down = device(x, c, z + 1, y), device(x, c, z - 1, y)
    across, facing, twin = device(x, c, z, 1 - y), device(1 - x, c, z, y), device(x, 1 - c, z, y)

    def part(zs, ys, half, cols):
        return wall.at[pl.ds(pl.multiple_of((zs * 2 + ys) * SHARD + half * HALF, 16), HALF), cols]

    def go(cond, zs, ys, cols, send, recv, target, src=None):
        piece = part(zs, ys, c, cols)
        links.go(cond, piece if src is None else src, piece, send, recv, target)

    def arrive(cond, zs, ys, half, cols, recv):
        links.arrive(cond, part(zs, ys, half, cols), recv, twin)

    def spread(cond, sub, zs, ys):
        source = zs * 2 + ys
        if sub == 0:
            go(cond, zs, ys, share, 39 + source, 24 + source, facing)
        go(cond, zs, ys, columns[sub], 47 + sub * 8 + source, 32 + sub * 8 + source, twin)

    def begin(sub, src):
        go(z < 3, z, y, columns[sub], sub * 3, sub * 4 + z, up, src)
        go(z > 0, z, y, columns[sub], 9 + sub * 3, sub * 4 + z, down, src)
        go(None, z, y, columns[sub], 18 + sub * 7, 12 + sub * 4 + z, across, src)

    def along(sub, k):
        below, above = z - k, z + k
        for cond, zs, on, first, target, place_of in (
            (below >= 0, below, z < 3, 0, up, k),
            (above <= 3, above, z > 0, 9, down, 3 + k),
        ):
            arrive(cond, zs, y, c, columns[sub], sub * 4 + zs)
            if k < 3:
                go(cond & on, zs, y, columns[sub], first + sub * 3 + k, sub * 4 + zs, target)
            go(cond, zs, y, columns[sub], 18 + sub * 7 + place_of, 12 + sub * 4 + zs, across)
            spread(cond, sub, zs, y)

    def over(sub, k):
        if k == 0:
            arrive(None, z, 1 - y, c, columns[sub], 12 + sub * 4 + z)
            spread(None, sub, z, 1 - y)
            return
        for cond, zs in ((z - k >= 0, z - k), (z + k <= 3, z + k)):
            arrive(cond, zs, 1 - y, c, columns[sub], 12 + sub * 4 + zs)
            spread(cond, sub, zs, 1 - y)

    half = pl.ds(pl.multiple_of(c * HALF, 16), HALF)
    begin(0, wq.at[half, pl.ds(pl.multiple_of(x * LEFTC, 128), LOW)])
    for fill in fills:
        fill.wait()
    begin(1, None)
    for k in (1, 2, 3):
        for sub in range(2):
            along(sub, k)
            over(sub, k - 1)
        if k == 2:
            begin(2, wp.at[half, :])
    along(2, 1)
    for sub in range(2):
        over(sub, 3)

    def each(what):
        for zs in range(4):
            for ys in range(2):
                what((zs != z) | (ys != y), zs, ys, zs * 2 + ys)

    def gain(other, zs, ys, source):
        arrive(other, zs, ys, c, gained, 24 + source)
        go(other, zs, ys, gained, 71 + source, 56 + source, twin)

    def mostly(other, zs, ys, source):
        for sub in range(2):
            arrive(other, zs, ys, 1 - c, columns[sub], 32 + sub * 8 + source)
        arrive(other, zs, ys, 1 - c, gained, 56 + source)

    def rest(other, zs, ys, source):
        arrive(other, zs, ys, 1 - c, columns[2], 32 + 16 + source)

    each(gain)
    each(mostly)

    def first():
        along(2, 2)
        over(2, 0)

    def second():
        along(2, 3)
        over(2, 1)
        over(2, 2)

    return first, second, lambda: over(2, 3), lambda: each(rest)


def unit(values):
    return lax.rsqrt(jnp.mean(values * values, axis=-1, keepdims=True) + 1e-06)


def heads(rows):
    lane = lax.broadcasted_iota(jnp.int32, rows.shape, 1)
    none = jnp.zeros_like(rows)
    return jnp.concatenate([jnp.where(lane < HEAD, rows, none), jnp.where(lane < HEAD, none, rows)], axis=0)


def beside(blocks):
    return jnp.concatenate([blocks[0:SEQ], blocks[SEQ : 2 * SEQ]], axis=1)


def build_bias(wall, bias):
    table = jnp.concatenate(
        [wall[f * SHARD : f * SHARD + 16, SMALL : SMALL + 128] for f in range(8)], axis=0
    )
    ahead = lax.broadcasted_iota(jnp.int32, (SEQ, SEQ), 0)
    lane = lax.broadcasted_iota(jnp.int32, (SEQ, SEQ), 1)
    turned = jnp.where(ahead + lane == SEQ, 1.0, jnp.where(ahead + lane == 0, 1.0, 0.0)).astype(BF16)
    lines = dot(table, turned, 0, 0)
    for h in range(HEADS):
        line = jnp.broadcast_to(lines[HEAD + h : HEAD + h + 1, :], (SEQ, SEQ))
        rolled = pltpu.roll(line, 0, 1, stride=1, stride_axis=0)
        bias[h * SEQ : (h + 1) * SEQ, 0:SEQ] = jnp.where(ahead >= lane, rolled, NEG)


def pack(gain_attn, gain_moe, router_t, rel, board, wall):
    x, c, z, y = place()
    board[0:SEQ, 0:SEQ] = jnp.zeros((SEQ, SEQ), F32)
    board[0:1, 0:SHARD] = gain_attn[...].astype(F32)
    board[1:2, 0:SHARD] = gain_moe[...].astype(F32)
    board[2 : 2 + EXP, 0:SHARD] = router_t[...].astype(F32)
    turned = jnp.transpose(board[0:SEQ, 0:SEQ])
    board[0:SEQ, 0:SEQ] = turned
    board[0:16, HEAD : HEAD + HEADS] = rel[...].astype(F32)
    own = pl.ds(pl.multiple_of((z * 2 + y) * SHARD, 16), SHARD)
    wall[own, SMALL : SMALL + 128] = board[0:SHARD, 0:SEQ].astype(BF16)


def stand(routes, slots, lines, columns):
    chosen = routes[...]
    lines[...] = jnp.zeros_like(lines)
    lines[0:2, :] = (chosen * CAP + slots[...]).astype(F32)
    lines[2:4, :] = chosen.astype(F32)
    columns[...] = jnp.transpose(lines[...])


def routing(columns, s):
    spots = columns[s * SEQ : (s + 1) * SEQ, :]
    lane = lax.broadcasted_iota(jnp.int32, (SEQ, EXP * CAP), 1).astype(F32)
    return spots[:, 0:1] == lane, spots[:, 1:2] == lane


def named(columns, s):
    spots = columns[s * SEQ : (s + 1) * SEQ, :]
    lane = lax.broadcasted_iota(jnp.int32, (SEQ, 128), 1).astype(F32) - 2.0
    return spots[:, 2:3] == lane, spots[:, 3:4] == lane


def live_column(lengths, s):
    return lax.broadcasted_iota(jnp.int32, (SEQ, 1), 0) < lengths[s]


def attention_forward(
    later, dispatch, x_ref, cot, lengths, columns, wall, rows_t, board, normed, qkv, attended, hidden, normed2, gates,
    out_f, out_g,
):
    rows_t[...] = jnp.transpose(wall[:, SMALL : SMALL + 128].astype(F32))[0:8]
    build_bias(wall, board)
    x = x_ref[...].astype(F32)
    normed[...] = (x * unit(x) * rows_t[0:1, :]).astype(BF16)
    qkv[:, 0:LEFTC] = dot(normed[...], wall[:, 0:LEFTC]).astype(BF16)
    qkv[:, LEFTC : 3 * D] = dot(normed[...], wall[:, HIGH:WALL]).astype(BF16)
    lane = lax.broadcasted_iota(jnp.int32, (2 * SEQ, 128), 1)

    def pair(s, p):
        blocks = pl.ds(pl.multiple_of(p * 2 * SEQ, SEQ), 2 * SEQ)
        rows = slice(s * SEQ, (s + 1) * SEQ)
        q = qkv[rows, pl.ds(pl.multiple_of(p * 128, 128), 128)]
        k = qkv[rows, pl.ds(pl.multiple_of(D + p * 128, 128), 128)]
        v = qkv[rows, pl.ds(pl.multiple_of(2 * D + p * 128, 128), 128)]
        scores = jnp.where(lane < lengths[s], dot(heads(q), k, 1, 1) * SCALE + board[blocks, 0:SEQ], NEG)
        scores = jnp.exp(scores - jnp.max(scores, axis=-1, keepdims=True))
        share = scores * (1.0 / jnp.sum(scores, axis=-1, keepdims=True))
        board[blocks, (1 + s) * SEQ : (2 + s) * SEQ] = share
        attended[rows, pl.ds(pl.multiple_of(p * 128, 128), 128)] = dot(
            beside(share.astype(BF16)), heads(v)
        ).astype(BF16)

    def pairs(s, first, last):
        def step(i, carry):
            pair(s, 2 * i)
            pair(s, 2 * i + 1)
            return carry

        lax.fori_loop(first, last, step, 0)

    def finish(s):
        rows = slice(s * SEQ, (s + 1) * SEQ)
        live = live_column(lengths, s)
        branch = dot(attended[rows, :], wall[:, PROJ:HIGH])
        state = x_ref[rows, :].astype(F32) + jnp.where(live, branch, 0.0)
        hidden[rows, :] = state
        low = (state * unit(state) * rows_t[1:2, :]).astype(BF16)
        normed2[rows, :] = low
        first, second = routing(columns, s)
        first = jnp.where(first & live, 1.0, 0.0).astype(BF16)
        second = jnp.where(second & live, 1.0, 0.0).astype(BF16)
        sent = dot(first + second, low, 0, 0).astype(BF16)
        for e in range(EXP):
            out_f[e, s * CAP : (s + 1) * CAP, :] = sent[e * CAP : (e + 1) * CAP, :]
        dispatch(s)
        logits = dot(low, wall[:, SMALL : SMALL + 128])
        one, two = named(columns, s)
        picked = jnp.where(one, logits, 0.0) - jnp.where(two, logits, 0.0)
        gate = jax.nn.sigmoid(jnp.sum(picked, axis=-1, keepdims=True))
        gates[rows, :] = gate
        grad = jnp.where(live, cot[rows, :].astype(F32), 0.0)
        back = dot(first, (gate * grad).astype(BF16), 0, 0) + dot(
            second, ((1.0 - gate) * grad).astype(BF16), 0, 0
        )
        back = back.astype(BF16)
        for e in range(EXP):
            out_g[e, s * CAP : (s + 1) * CAP, :] = back[e * CAP : (e + 1) * CAP, :]

    for t in range(3):
        later[t]()
        pairs(0, t, t + 1)
    later[3]()
    finish(0)
    pairs(1, 0, 3)
    finish(1)


TILE = 512
Z_ROWS, Y_ROWS, Y_PART, Z_BACK = 80, 88, 96, 104
TWIN_W, FACE_W, TWIN_OUT = 112, 114, 120
RS_TWIN, RS_Y, RS_Z, RS_FACE, RS_OUT = 126, 131, 151, 191, 196
Z_FIRST, Y_FIRST = 206, 214
LINKS = 216


def quarter(zs):
    return pl.ds(pl.multiple_of(zs * 2 * ROWS, 2 * ROWS), 2 * ROWS)


def half_rows(zs, ys):
    return pl.ds(pl.multiple_of((zs * 2 + ys) * ROWS, ROWS), ROWS)


def expert_forward(zs, recv, up, down, act, slope, part):
    rows = quarter(zs)

    def tile(i, carry):
        cols = pl.ds(pl.multiple_of(i * TILE, TILE), TILE)
        before = dot(recv[rows, :], up[:, cols])
        below = 0.5 + 0.5 * lax.erf(before * 0.7071067811865476)
        act[rows, cols] = (before * below).astype(BF16)
        density = jnp.exp(before * before * -0.5) * 0.3989422804014327
        slope[rows, cols] = (below + before * density).astype(BF16)
        return carry

    lax.fori_loop(0, HF // TILE, tile, 0)
    got = dot(act[rows, 0:HF], down[...]).astype(BF16)
    part[zs, 0] = got[0:ROWS]
    part[zs, 1] = got[ROWS : 2 * ROWS]


def expert_backward(zs, recv, up, down, slope, part):
    rows = quarter(zs)

    def tile(i, carry):
        cols = pl.ds(pl.multiple_of(i * TILE, TILE), TILE)
        grad = dot(recv[rows, :], down[cols, :], 1, 1)
        slope[rows, cols] = (grad * slope[rows, cols].astype(F32)).astype(BF16)
        return carry

    lax.fori_loop(0, HF // TILE, tile, 0)
    got = dot(slope[rows, :], up[...], 1, 1).astype(BF16)
    part[zs, 0] = got[0:ROWS]
    part[zs, 1] = got[ROWS : 2 * ROWS]


def one_sequence(zs, ys, s):
    return pl.ds(pl.multiple_of((zs * 2 + ys) * ROWS + s * CAP, CAP), CAP)


def dispatch_forward(links, out, recv, s):
    x, c, z, y = place()
    rows = slice(s * CAP, (s + 1) * CAP)
    there = recv.at[one_sequence(z, y, s), :]
    links.go(None, out.at[z, rows, :], there, Y_FIRST + s, Y_FIRST + s, device(x, c, z, 1 - y))
    for d in (1, 2, 3):
        to = (z + d) % 4
        slot = Z_FIRST + s * 4
        links.go(None, out.at[to, rows, :], there, slot + d, slot + z, device(x, c, to, y))
    recv[one_sequence(z, y, s), :] = out[z, rows, :]


def experts(links, out, recv, up, down, act, slope, part, take, back, w_down, w_up):
    x, c, z, y = place()
    across, facing, twin = device(x, c, z, 1 - y), device(1 - x, c, z, y), device(x, 1 - c, z, y)

    for kind in (1,):
        links.go(None, out[kind].at[z], recv[kind].at[half_rows(z, y), :], Y_ROWS + kind * 4, Y_ROWS + kind * 4 + z, across)
        for d in (1, 2, 3):
            to = (z + d) % 4
            links.go(
                None, out[kind].at[to], recv[kind].at[half_rows(z, y), :], Z_ROWS + kind * 4 + d,
                Z_ROWS + kind * 4 + z, device(x, c, to, y),
            )
        recv[kind][half_rows(z, y), :] = out[kind][z]

    def source(d):
        return (z + 4 - d) % 4

    def reach(kind, d):
        zs = source(d)
        rows = recv[kind].at[half_rows(zs, y), :]
        if kind == 0:
            for s in range(MB):
                links.arrive(None, recv[0].at[one_sequence(zs, y, s), :], Z_FIRST + s * 4 + zs, across)
        else:
            links.arrive(None, rows, Z_ROWS + kind * 4 + zs, across)
        links.go(None, rows, rows, Y_ROWS + kind * 4 + d, Y_ROWS + kind * 4 + zs, across)

    def compute(kind, d):
        zs = source(d)
        if kind == 0 and d == 0:
            for s in range(MB):
                links.arrive(None, recv[0].at[one_sequence(z, 1 - y, s), :], Y_FIRST + s, across)
        else:
            links.arrive(None, recv[kind].at[half_rows(zs, 1 - y), :], Y_ROWS + kind * 4 + zs, across)
        if kind == 0:
            expert_forward(zs, recv[0], up, down, act, slope, part[0])
        else:
            expert_backward(zs, recv[1], up, down, slope, part[1])

    def give_part(kind, d):
        zs = source(d)
        links.go(
            None, part[kind].at[zs, 1 - y], take[kind].at[zs], Y_PART + kind * 4 + d, Y_PART + kind * 4 + zs, across
        )

    def merge(kind, d):
        zs = source(d)
        links.arrive(None, take[kind].at[zs], Y_PART + kind * 4 + zs, across)
        total = (part[kind][zs, y].astype(F32) + take[kind][zs].astype(F32)).astype(BF16)
        if d == 0:
            back[kind][z] = total
        else:
            part[kind][zs, y] = total
            links.go(
                None, part[kind].at[zs, y], back[kind].at[z], Z_BACK + kind * 4 + d, Z_BACK + kind * 4 + z,
                device(x, c, zs, y),
            )

    reach(0, 1)
    compute(0, 0)
    reach(0, 2)
    compute(1, 0)
    reach(0, 3)
    compute(0, 1)
    reach(1, 1)
    give_part(0, 1)
    compute(0, 2)
    reach(1, 2)
    give_part(0, 2)
    compute(1, 1)
    reach(1, 3)
    give_part(1, 1)
    merge(0, 1)
    compute(0, 3)
    give_part(0, 3)
    merge(0, 2)
    compute(1, 2)
    give_part(1, 2)
    compute(1, 3)
    give_part(1, 3)
    give_part(0, 0)
    give_part(1, 0)

    def down_tile(i, part_of, keep):
        cols = pl.ds(pl.multiple_of(part_of * (HF // 2) + i * 256, 128), 256)
        got = dot(act[:, cols], recv[1][...], 0, 0)
        keep[pl.ds(pl.multiple_of(i * 256, 256), 256), :] = got.astype(keep.dtype)

    def up_tile(i, part_of, keep):
        cols = pl.ds(pl.multiple_of(part_of * (D // 2) + i * 128, 128), 128)
        got = dot(recv[0][:, cols], slope[...], 0, 0)
        keep[pl.ds(pl.multiple_of(i * 128, 128), 128), :] = got.astype(keep.dtype)

    def tiles(one, part_of, keep):
        def step(i, carry):
            one(i, part_of, keep)
            return carry

        lax.fori_loop(0, 3, step, 0)

    def spread(i, sent):
        own, give, got, face = (w_down, w_up)[i]
        links.arrive(None, got, TWIN_W + i, twin)
        links.leave(sent)
        count = own.shape[0] // 3
        for m in range(3):
            rows = slice(m * count, (m + 1) * count)
            give[rows, :] = (own[rows, :] + got[rows, :].astype(F32)).astype(BF16)
            links.go(None, give.at[rows, :], face.at[rows, :], FACE_W + i * 3 + m, FACE_W + i * 3 + m, facing)

    tiles(down_tile, 1 - c, w_down[1])
    sent = links.go(None, w_down[1], w_down[2], TWIN_W, TWIN_W, twin)
    merge(1, 1)
    tiles(down_tile, c, w_down[0])
    spread(0, sent)
    merge(0, 3)
    tiles(up_tile, 1 - c, w_up[1])
    sent = links.go(None, w_up[1], w_up[2], TWIN_W + 1, TWIN_W + 1, twin)
    merge(1, 2)
    tiles(up_tile, c, w_up[0])
    spread(1, sent)
    merge(1, 3)
    merge(0, 0)
    merge(1, 0)
    for kind in range(2):
        for d in (1, 2, 3):
            zs = source(d)
            links.arrive(None, back[kind].at[zs], Z_BACK + kind * 4 + zs, across)


def expert_grad_out(links, piece, w_down, w_up, out_down, out_up, local_sem):
    x, c, z, y = place()
    facing, twin = device(1 - x, c, z, y), device(x, 1 - c, z, y)
    (own, give, got, face), target = ((w_down, out_down), (w_up, out_up))[piece // 3]
    count = own.shape[0] // 3
    rows = slice((piece % 3) * count, (piece % 3 + 1) * count)
    links.arrive(None, face.at[rows, :], FACE_W + piece, facing)
    face[rows, :] = (give[rows, :].astype(F32) + face[rows, :].astype(F32)).astype(BF16)
    there = target.at[pl.ds(pl.multiple_of((c * 3 + piece % 3) * count, 128), count), :]
    links.go(None, face.at[rows, :], there, TWIN_OUT + piece, TWIN_OUT + piece, twin)
    copy = pltpu.make_async_copy(face.at[rows, :], there, local_sem.at[8 + piece])
    copy.start()
    return copy


def expert_grads_arrive(links, out_down, out_up):
    x, c, z, y = place()
    for piece in range(6):
        target = (out_down, out_up)[piece // 3]
        count = target.shape[0] // 6
        there = target.at[pl.ds(pl.multiple_of(((1 - c) * 3 + piece % 3) * count, 128), count), :]
        links.arrive(None, there, TWIN_OUT + piece, device(x, 1 - c, z, y))


SENTC = 2 * D + 128


def combine(cot, lengths, columns, rows_t, hidden, normed2, gates, back_f, back_g, mixed, rb, small_t):
    gain_grad = jnp.zeros((1, D), F32)
    router_grad = jnp.zeros((128, D), F32)
    for s in range(MB):
        rows = slice(s * SEQ, (s + 1) * SEQ)
        live = live_column(lengths, s)
        first, second = routing(columns, s)
        first = jnp.where(first, 1.0, 0.0).astype(BF16)
        second = jnp.where(second, 1.0, 0.0).astype(BF16)
        given = jnp.concatenate([back_f[e, s * CAP : (s + 1) * CAP, :] for e in range(EXP)], axis=0)
        first_out = dot(first, given)
        second_out = dot(second, given)
        gate = gates[rows, :]
        grad = cot[rows, :].astype(F32)
        grad_live = jnp.where(live, grad, 0.0)
        state = hidden[rows, :]
        moe = gate * first_out + (1.0 - gate) * second_out
        mixed[rows, :] = (state + jnp.where(live, moe, 0.0)).astype(BF16)
        tilt = jnp.sum(grad_live * first_out, axis=-1, keepdims=True) - jnp.sum(
            grad_live * second_out, axis=-1, keepdims=True
        )
        tilt = tilt * gate * (1.0 - gate)
        one, two = named(columns, s)
        hot = jnp.where(one, 1.0, 0.0) - jnp.where(two, 1.0, 0.0)
        grad_logits = tilt * hot
        high = grad_logits.astype(BF16)
        low = (grad_logits - high.astype(F32)).astype(BF16)
        router_grad = router_grad + dot(high, normed2[rows, :], 0, 0) + dot(low, normed2[rows, :], 0, 0)
        given = jnp.concatenate([back_g[e, s * CAP : (s + 1) * CAP, :] for e in range(EXP)], axis=0)
        grad_low = jnp.where(live, dot(first + second, given), 0.0)
        for e in range(EXP):
            grad_low = grad_low + grad_logits[:, 2 + e : 3 + e] * rows_t[2 + e : 3 + e, :]
        factor = unit(state)
        scaled = state * factor
        gain_grad = gain_grad + jnp.sum(grad_low * scaled, axis=0, keepdims=True)
        grad_low = grad_low * rows_t[1:2, :]
        inner = jnp.mean(grad_low * scaled, axis=-1, keepdims=True)
        grad_state = grad + factor * (grad_low - scaled * inner)
        hidden[rows, :] = grad_state
        rb[rows, 3 * D : 4 * D] = jnp.where(live, grad_state, 0.0).astype(BF16)
    small_t[...] = router_grad
    small_t[1:2, :] = gain_grad


def attention_backward(x_ref, wall, rows_t, qkv, board, hidden, grad_att, rb, rel_rows, small_t, grad_tokens, midway, formed):
    grad_att[...] = dot(rb[:, 3 * D : 4 * D], wall[:, PROJ:HIGH], 1, 1).astype(BF16)
    midway()
    lane = lax.broadcasted_iota(jnp.int32, (SEQ, 128), 1)
    ahead = lax.broadcasted_iota(jnp.int32, (SEQ, 128), 0)
    flip = jnp.where(ahead + lane == SEQ - 1, 1.0, 0.0).astype(BF16)
    flip = jnp.concatenate([flip] * MB, axis=1)

    def pair(p, carry):
        blocks = pl.ds(pl.multiple_of(p * 2 * SEQ, SEQ), 2 * SEQ)
        scores = []
        for s in range(MB):
            rows = slice(s * SEQ, (s + 1) * SEQ)
            cols = [pl.ds(pl.multiple_of(i * D + p * 128, 128), 128) for i in range(3)]
            q, k, v = (qkv[rows, cols[i]] for i in range(3))
            grad = heads(grad_att[rows, cols[0]])
            share = board[blocks, (1 + s) * SEQ : (2 + s) * SEQ]
            grad_probs = dot(grad, v, 1, 1)
            inner = jnp.sum(share * grad_probs, axis=-1, keepdims=True)
            grad_scores = (share * (grad_probs - inner)).astype(BF16)
            scores.append(beside(grad_scores))
            rb[rows, cols[0]] = (dot(scores[s], heads(k)) * SCALE).astype(BF16)
            rb[rows, cols[1]] = (dot(grad_scores, heads(q), 0, 0) * SCALE).astype(BF16)
            rb[rows, cols[2]] = dot(share.astype(BF16), grad, 0, 0).astype(BF16)
        flipped = dot(flip, jnp.concatenate(scores, axis=0))
        for j in range(2):
            rolled = pltpu.roll(flipped[:, j * SEQ : (j + 1) * SEQ], 1, 1, stride=1, stride_axis=0)
            rel_rows[pl.ds(2 * p + j, 1), :] = jnp.sum(rolled, axis=0, keepdims=True)
        return carry

    for t in range(3):
        lax.fori_loop(2 * t, 2 * t + 2, pair, 0)
        formed[t]()
    grad_low = dot(rb[:, 0:LEFTC], wall[:, 0:LEFTC], 1, 1) + dot(
        rb[:, LEFTC : 3 * D], wall[:, HIGH:WALL], 1, 1
    )
    state = x_ref[...].astype(F32)
    factor = unit(state)
    scaled = state * factor
    small_t[0:1, :] = jnp.sum(grad_low * scaled, axis=0, keepdims=True)
    grad_low = grad_low * rows_t[0:1, :]
    inner = jnp.mean(grad_low * scaled, axis=-1, keepdims=True)
    grad_tokens[...] = hidden[...] + factor * (grad_low - scaled * inner)

    spot = lax.broadcasted_iota(jnp.int32, (SEQ, D), 0)
    column = lax.broadcasted_iota(jnp.int32, (SEQ, D), 1)
    distance = (SEQ - spot) & (SEQ - 1)
    picks = jnp.where(column == (distance >> 4) * SHARD + (distance & 15), 1.0, 0.0).astype(BF16)
    rest = rel_rows[...]
    spread = jnp.zeros((16, D), F32)
    for _ in range(3):
        high = rest.astype(BF16)
        spread = spread + dot(high, picks)
        rest = rest - high.astype(F32)
    small_t[HEAD : HEAD + 16, :] = spread


HC = D // 2
SMALLS = SENTC - 128
STRAIGHT = (0, 1, 2, 3, 4)


def portions(group):
    if group == 0:
        return 1, 2 * HC, HC, ((0, HC, lambda core: 3 * D + core * HC, lambda core: core * HC),)
    if group == 4:
        return 0, SMALLS, 128, ()
    t = group - 1
    both = (
        (0, 256, lambda core: core * D + 256 * t, lambda core: core * D + 256 * t),
        (256, 128, lambda core: 2 * D + 256 * t + 128 * core, lambda core: 2 * D + 256 * t + 128 * core),
    )
    return 0, (0, HC, 3 * HC)[t], HC, both


class Reduction:
    def __init__(self, links, group, left, rb, small_t, give, take, total, y_take, z_take, face_give, face_take, last):
        self.links, self.group = links, group
        which, first, width, portion = portions(group)
        self.cols = slice(first, first + width)
        self.portion = [(slice(first + at, first + at + wide), wide, rhs, target) for at, wide, rhs, target in portion]
        self.lhs, self.rb, self.small_t = left.at[which], rb, small_t
        self.give, self.take, self.total = give, take, total
        self.y_take, self.z_take, self.face_give, self.face_take, self.last = y_take, z_take, face_give, face_take, last
        x, c, z, y = self.place = place()
        self.across, self.facing, self.twin = device(x, c, z, 1 - y), device(1 - x, c, z, y), device(x, 1 - c, z, y)
        mirror = z // 2
        near = z + mirror * (3 - 2 * z)
        self.order = [o + mirror * (3 - 2 * o) for o in (3, 2, 1 - near, near)]

    def tile(self, core, keep):
        def step(m, carry):
            rows = pl.ds(pl.multiple_of(m * 256, 256), 256)
            for cols, wide, rhs, target in self.portion:
                right = self.rb[:, pl.ds(pl.multiple_of(rhs(core), 128), wide)]
                keep[rows, cols] = dot(self.lhs[:, rows], right, 0, 0).astype(keep.dtype)
            return carry

        lax.fori_loop(0, 3, step, 0)

    def form(self):
        x, c, z, y = self.place
        self.tile(1 - c, self.give)
        self.to_twin()
        self.tile(c, self.total)

    def to_twin(self):
        slot, cols = RS_TWIN + self.group, self.cols
        self.sent = self.links.go(None, self.give.at[:, cols], self.take.at[:, cols], slot, slot, self.twin)

    def form_small(self):
        small = jnp.transpose(self.small_t[...]).astype(BF16)
        self.give[:, self.cols] = small
        self.to_twin()
        self.total[:, self.cols] = small.astype(F32)

    def shard(self, zs, ys):
        return pl.ds(pl.multiple_of((zs * 2 + ys) * SHARD, 16), SHARD)

    def halve(self):
        x, c, z, y = self.place
        links, cols = self.links, self.cols
        links.arrive(None, self.take.at[:, cols], RS_TWIN + self.group, self.twin)
        links.leave(self.sent)
        for zs in self.order:
            rows = self.shard(zs, 1 - y)
            self.give[rows, cols] = (self.total[rows, cols] + self.take[rows, cols].astype(F32)).astype(BF16)
            slot = RS_Y + self.group * 4 + zs
            links.go(None, self.give.at[rows, cols], self.y_take.at[zs, :, cols], slot, slot, self.across)
        for zs in self.order:
            rows = self.shard(zs, y)
            self.total[rows, cols] = self.total[rows, cols] + self.take[rows, cols].astype(F32)

    def chain(self, k):
        x, c, z, y = self.place
        links, cols, zs = self.links, self.cols, self.order[k]
        total, z_take = self.total, self.z_take
        rows = self.shard(zs, y)
        links.arrive(None, self.y_take.at[zs, :, cols], RS_Y + self.group * 4 + zs, self.across)
        total[rows, cols] = total[rows, cols] + self.y_take[zs, :, cols].astype(F32)
        if k == 3:
            return
        if self.group in STRAIGHT:
            self.give[rows, cols] = total[rows, cols].astype(BF16)
            base = RS_Z + self.group * 8
            links.go(None, self.give.at[rows, cols], z_take.at[z, :, cols], base + k, base + z, device(x, c, zs, y))
            return
        for cond, more, slot, target in (
            (zs > z, z > 0, zs, device(x, c, z + 1, y)),
            (zs < z, z < 3, 4 + zs, device(x, c, z - 1, y)),
        ):
            self.add_from_z(cond & more, slot, rows)

            @pl.when(cond)
            def _():
                self.give[rows, cols] = total[rows, cols].astype(BF16)

            index = RS_Z + self.group * 8 + slot
            links.go(cond, self.give.at[rows, cols], z_take.at[slot, :, cols], index, index, target)

    def add_from_z(self, cond, slot, rows):
        cols = self.cols

        @pl.when(cond)
        def _():
            part = self.z_take.at[slot, :, cols]
            self.links.arrive(None, part, RS_Z + self.group * 8 + slot, self.across)
            self.total[rows, cols] = self.total[rows, cols] + part[...].astype(F32)

    def face(self):
        x, c, z, y = self.place
        rows, cols = self.shard(z, y), self.cols
        if self.group in STRAIGHT:
            for d in (1, 2, 3):
                zs = (z + d) % 4
                self.links.arrive(None, self.z_take.at[zs, :, cols], RS_Z + self.group * 8 + zs, self.across)
                self.total[rows, cols] = self.total[rows, cols] + self.z_take[zs, :, cols].astype(F32)
        else:
            self.add_from_z(z > 0, z, rows)
            self.add_from_z(z < 3, 4 + z, rows)
        self.face_give[:, cols] = self.total[rows, cols].astype(BF16)
        slot = RS_FACE + self.group
        self.links.go(None, self.face_give.at[:, cols], self.face_take.at[:, cols], slot, slot, self.facing)

    def publish(self, out_qkv, out_proj, out_small, local_sem):
        x, c, z, y = self.place
        cols = self.cols
        self.links.arrive(None, self.face_take.at[:, cols], RS_FACE + self.group, self.facing)
        self.last[:, cols] = self.face_give[:, cols].astype(F32) + self.face_take[:, cols].astype(F32)
        self.out = out_proj if self.group == 0 else out_qkv
        copies = []
        for i, (part, there) in enumerate(self.landing(c)):
            slot = RS_OUT + self.group * 2 + i
            self.links.go(None, part, there, slot, slot, self.twin)
            copies.append(pltpu.make_async_copy(part, there, local_sem.at[16 + self.group * 2 + i]))
        if self.group == 4:
            copies.append(pltpu.make_async_copy(self.last.at[:, cols], out_small, local_sem.at[6]))
        for copy in copies:
            copy.start()
        return copies

    def landing(self, core):
        return [
            (self.last.at[:, cols], self.out.at[:, pl.ds(pl.multiple_of(target(core), 128), wide)])
            for cols, wide, rhs, target in self.portion
        ]

    def landed(self):
        x, c, z, y = self.place
        for i, (part, there) in enumerate(self.landing(1 - c)):
            self.links.arrive(None, there, RS_OUT + self.group * 2 + i, self.twin)


def layer(
    x_in, cot_in, lengths, routes, slots, gain_attn, gain_moe, router_t, rel, wq, wp, w_up, w_down,
    mixed_out, tokens_out, out_qkv, out_proj, out_small, out_up, out_down,
    x_ref, cot, mixed, grad_tokens, board,
    wall, rows_t, lines, columns, left, qkv, hidden, normed2, gates, out_f, out_g, recv_f, recv_g, up, down, act, slope,
    part_f, part_g, take_f, take_g, back_f, back_g, dn_own, dn_give, dn_take, dn_face, up_own, up_give, up_take, up_face,
    rb, rel_rows, small_t, take, total, y_take, z_take, face_give, face_take, last,
    local_sem, send_sem, recv_sem,
):
    inputs = [
        pltpu.make_async_copy(x_in, x_ref, local_sem.at[24]),
        pltpu.make_async_copy(cot_in, cot, local_sem.at[25]),
    ]
    fetch = [
        pltpu.make_async_copy(w_up.at[0], up, local_sem.at[4]),
        pltpu.make_async_copy(w_down.at[0], down, local_sem.at[5]),
    ]
    met = greet()
    links = Links(send_sem, recv_sem)

    def ready():
        pack(gain_attn, gain_moe, router_t, rel, board, wall)
        stand(routes, slots, lines, columns)
        rel_rows[...] = jnp.zeros_like(rel_rows)
        met()

    later = gather_weights(links, wq, wp, wall, local_sem, inputs + fetch, ready)
    for copy in inputs:
        copy.wait()
    normed, attended = left.at[0], left.at[1]
    attention_forward(
        later, functools.partial(dispatch_forward, links, out_f, recv_f), x_ref, cot, lengths, columns, wall, rows_t, board, normed, qkv, attended, hidden, normed2, gates,
        out_f, out_g,
    )
    for copy in fetch:
        copy.wait()
    downs, ups = (dn_own, dn_give, dn_take, dn_face), (up_own, up_give, up_take, up_face)
    experts(
        links, (out_f, out_g), (recv_f, recv_g), up, down, act, slope, (part_f, part_g), (take_f, take_g),
        (back_f, back_g), downs, ups,
    )
    combine(cot, lengths, columns, rows_t, hidden, normed2, gates, back_f, back_g, mixed, rb, small_t)
    pending = []

    def put(src, dst, i):
        copy = pltpu.make_async_copy(src, dst, local_sem.at[i])
        copy.start()
        pending.append(copy)

    put(mixed, mixed_out, 26)
    proj, one, two, three, small = (
        Reduction(
            links, group, left, rb, small_t, act.at[0:D, :], take, total, y_take, z_take, face_give, face_take, last
        )
        for group in range(5)
    )

    def grads(piece):
        pending.append(expert_grad_out(links, piece, downs, ups, out_down, out_up, local_sem))

    def publish(item):
        pending.extend(item.publish(out_qkv, out_proj, out_small, local_sem))

    def early():
        one.form()
        proj.chain(0)

    def middle():
        one.halve()
        two.form()
        proj.chain(1)

    def late():
        two.halve()
        three.form()
        proj.chain(2)
        one.chain(0)
        three.halve()

    proj.form()
    attention_backward(
        x_ref, wall, rows_t, qkv, board, hidden, normed2, rb, rel_rows, small_t, grad_tokens, proj.halve,
        (early, middle, late),
    )
    small.form_small()
    put(grad_tokens, tokens_out, 27)
    proj.chain(3)
    one.chain(1)
    small.halve()
    two.chain(0)
    one.chain(2)
    grads(0)
    proj.face()
    two.chain(1)
    one.chain(3)
    grads(1)
    three.chain(0)
    two.chain(2)
    three.chain(1)
    grads(2)
    one.face()
    three.chain(2)
    small.chain(0)
    two.chain(3)
    small.chain(1)
    small.chain(2)
    grads(3)
    publish(proj)
    two.face()
    grads(4)
    three.chain(3)
    small.chain(3)
    grads(5)
    publish(one)
    three.face()
    small.face()
    publish(two)
    publish(three)
    publish(small)
    for item in (proj, one, two, three):
        item.landed()
    expert_grads_arrive(links, out_down, out_up)
    for copy in pending:
        copy.wait()
    links.finish()


PARTS = 6


def hand_out(
    mixed, tokens, qkv, proj, small, up, down,
    to_mixed, to_tokens, to_qkv, to_proj, to_gain_attn, to_gain_moe, to_router, to_rel, to_up, to_down,
    v_mixed, v_tokens, v_qkv, v_proj, v_small, v_up, v_down,
    v_gain_attn, v_gain_moe, v_router, v_rel, wide_up, wide_down, in_sem, out_sem,
):
    def rows(array, i):
        count = array.shape[0] // PARTS
        return pl.ds(i * count, count)

    def copy(src, dst, sem, i):
        item = pltpu.make_async_copy(src, dst, sem.at[i])
        item.start()
        return item

    halves = [
        (source, held, wide, out, rows(source, i))
        for i in range(PARTS)
        for source, held, wide, out in ((up, v_up, wide_up, to_up), (down, v_down, wide_down, to_down))
    ]
    coming = [copy(source.at[at], held.at[at], in_sem, i) for i, (source, held, _, _, at) in enumerate(halves)]
    plain = ((tokens, v_tokens, to_tokens), (qkv, v_qkv, to_qkv), (mixed, v_mixed, to_mixed), (proj, v_proj, to_proj))
    first = len(halves)
    little = copy(small, v_small, in_sem, first + len(plain))
    others = [copy(source, held, in_sem, first + i) for i, (source, held, _) in enumerate(plain)]
    going = []

    def put(src, dst):
        going.append(copy(src, dst, out_sem, len(going)))

    for item, (source, held, wide, out, at) in zip(coming, halves):
        item.wait()
        wide[at] = held[at].astype(F32)
        put(wide.at[at], out.at[at])
    little.wait()
    turned = jnp.transpose(v_small[...])
    v_gain_attn[...] = turned[0]
    v_gain_moe[...] = turned[1]
    v_router[...] = turned[2 : 2 + EXP]
    v_rel[...] = v_small[0:16, HEAD : HEAD + HEADS]
    put(v_gain_attn, to_gain_attn)
    put(v_gain_moe, to_gain_moe)
    put(v_router, to_router)
    put(v_rel, to_rel)
    for item, (_, held, out) in zip(others, plain):
        item.wait()
        put(held, out)
    for item in going:
        item.wait()


def body_fast(
    tokens, cotangent, lengths, routes, slots, gain_attn, w_qkv, w_proj, rel_table, gain_moe, w_router, w_up, w_down
):
    vm = pl.BlockSpec(memory_space=pltpu.VMEM)
    hbm = pl.BlockSpec(memory_space=pl.ANY)
    sds = jax.ShapeDtypeStruct
    v = pltpu.VMEM
    shapes = (
        sds((TOK, D), BF16), sds((TOK, D), F32), sds((SHARD, 3 * D), F32), sds((SHARD, D), F32),
        sds((SHARD, 128), F32), sds((D, HF), BF16), sds((HF, D), BF16),
    )
    out = pl.pallas_call(
        layer,
        out_shape=shapes,
        in_specs=[hbm, hbm, pl.BlockSpec(memory_space=pltpu.SMEM), vm, vm, vm, vm, vm, vm, hbm, hbm, hbm, hbm],
        out_specs=[hbm, hbm, hbm, hbm, hbm, hbm, hbm],
        scratch_shapes=[
            v((TOK, D), BF16), v((TOK, D), BF16), v((TOK, D), BF16), v((TOK, D), F32), v((HEADS * SEQ, 3 * SEQ), F32),
            v((D, WALL), BF16), v((8, D), F32), v((8, TOK), F32), v((TOK, 8), F32), v((2, TOK, D), BF16),
            v((TOK, 3 * D), BF16), v((TOK, D), F32), v((TOK, D), BF16),
            v((TOK, 1), F32), v((EXP, ROWS, D), BF16), v((EXP, ROWS, D), BF16),
            v((8 * ROWS, D), BF16), v((8 * ROWS, D), BF16), v((D, HF), BF16), v((HF, D), BF16),
            v((8 * ROWS, SENTC), BF16), v((8 * ROWS, HF), BF16),
            v((EXP, 2, ROWS, D), BF16), v((EXP, 2, ROWS, D), BF16), v((EXP, ROWS, D), BF16), v((EXP, ROWS, D), BF16),
            v((EXP, ROWS, D), BF16), v((EXP, ROWS, D), BF16),
            v((HF // 2, D), F32), v((HF // 2, D), BF16), v((HF // 2, D), BF16), v((HF // 2, D), BF16),
            v((D // 2, HF), F32), v((D // 2, HF), BF16), v((D // 2, HF), BF16), v((D // 2, HF), BF16),
            v((TOK, 4 * D), BF16), v((16, SEQ), F32), v((128, D), F32),
            v((D, SENTC), BF16), v((D, SENTC), F32), v((4, SHARD, SENTC), BF16), v((8, SHARD, SENTC), BF16),
            v((SHARD, SENTC), BF16), v((SHARD, SENTC), BF16), v((SHARD, SENTC), F32),
            pltpu.SemaphoreType.DMA((28,)), pltpu.SemaphoreType.DMA((LINKS,)), pltpu.SemaphoreType.DMA((LINKS,)),
        ],
        compiler_params=pltpu.CompilerParams(
            collective_id=0, has_side_effects=True, vmem_limit_bytes=67043328
        ),
        name="layer",
    )(
        tokens, cotangent, lengths, routes.T, slots.T, gain_attn[None], gain_moe[None], w_router.T, rel_table, w_qkv, w_proj,
        w_up, w_down,
    )
    small = (sds((SHARD,), F32), sds((SHARD,), F32), sds((EXP, SHARD), F32), sds((16, HEADS), F32))
    final = shapes[:4] + small + (sds((D, HF), F32), sds((HF, D), F32))
    mixed, grad_tokens, grad_qkv, grad_proj, grad_gain_attn, grad_gain_moe, grad_router, grad_rel, grad_up, grad_down = (
        pl.pallas_call(
            hand_out,
            out_shape=final,
            in_specs=[hbm] * len(shapes),
            out_specs=[hbm] * len(final),
            scratch_shapes=[v(item.shape, item.dtype) for item in shapes + small + final[-2:]]
            + [pltpu.SemaphoreType.DMA((2 * PARTS + 5,)), pltpu.SemaphoreType.DMA((2 * PARTS + 8,))],
            name="hand_out",
        )(*out)
    )
    return (
        mixed,
        grad_tokens,
        grad_gain_attn,
        grad_qkv,
        grad_proj,
        grad_rel,
        grad_gain_moe,
        grad_router.T,
        grad_up[None],
        grad_down[None],
    )


epsilon = 1e-06
exact_precision = lax.Precision.HIGHEST


def rms_norm(values, gain):
    factor = lax.rsqrt(jnp.mean(values * values, axis=-1, keepdims=True) + epsilon)
    return values * factor * gain


def distance_hot():
    places = jnp.arange(SEQ, dtype=jnp.int32)
    distance = jnp.clip(places[:, None] - places[None, :], 0, SEQ - 1).reshape(1, SEQ * SEQ)
    return (distance == places[:, None]).astype(jnp.bfloat16)


def bias_matrix(table, hot):
    flat = jnp.einsum("dh,dp->hp", table, hot, preferred_element_type=jnp.float32)
    return flat.reshape(table.shape[1], SEQ, SEQ)


def exact_gelu(values):
    return jax.nn.gelu(values, approximate=False)


def masked_scores(qkv_rows, bias, allowed, factor):
    raw = jnp.einsum(
        "qhd,khd->hqk", qkv_rows[:, 0], qkv_rows[:, 1], preferred_element_type=jnp.float32
    )
    return jnp.where(allowed[None], raw * factor + bias, -1e30)


def fetch_weights(gain_attn, w_qkv, w_proj, rel_table, gain_moe, w_router):
    rows, experts = w_router.shape
    spread = rel_table.shape[0]
    packed = jnp.concatenate(
        [gain_attn, gain_moe, w_router.reshape(-1), rel_table.reshape(-1)]
    )
    small = lax.all_gather(packed, "fsdp", axis=0, tiled=False)
    groups = small.shape[0]
    edge = 2 * rows + rows * experts
    return (
        small[:, :rows].reshape(-1),
        lax.all_gather(w_qkv, "fsdp", axis=0, tiled=True),
        lax.all_gather(w_proj, "fsdp", axis=0, tiled=True),
        small[:, edge:].reshape(groups * spread, HEADS),
        small[:, rows : 2 * rows].reshape(-1),
        small[:, 2 * rows : edge].reshape(groups * rows, experts),
    )


def body(
    tokens,
    cotangent,
    lengths,
    routes,
    slots,
    gain_attn,
    w_qkv,
    w_proj,
    rel_table,
    gain_moe,
    w_router,
    w_up,
    w_down,
):
    groups = lax.axis_size("fsdp")
    experts = groups // 2
    capacity = 2 * SEQ // experts
    factor = HEAD ** (-0.5)
    up_weight = w_up[0]
    down_weight = w_down[0]
    places = jnp.arange(SEQ, dtype=jnp.int32)
    causal = places[:, None] >= places[None, :]
    expert_ids = jnp.arange(experts, dtype=jnp.int32)
    saved = []
    mixed_parts = []
    weights = fetch_weights(gain_attn, w_qkv, w_proj, rel_table, gain_moe, w_router)
    gain_a = weights[0].astype(jnp.float32)
    gain_m = weights[4].astype(jnp.float32)
    router_float = weights[5].astype(jnp.float32)
    hot = distance_hot()
    bias = bias_matrix(weights[3], hot)
    for batch in range(MB):
        x_float = tokens[batch * SEQ : (batch + 1) * SEQ].astype(jnp.float32)
        live_keys = places < lengths[batch]
        live_col = live_keys.astype(jnp.float32)[:, None]
        allowed = causal & live_keys[None, :]
        normed = rms_norm(x_float, gain_a).astype(jnp.bfloat16)
        qkv_rows = (
            jnp.dot(normed, weights[1], preferred_element_type=jnp.float32)
            .astype(jnp.bfloat16)
            .reshape(SEQ, 3, HEADS, HEAD)
        )
        scores = masked_scores(qkv_rows, bias, allowed, factor)
        row_peak = jnp.max(scores, axis=-1, keepdims=True)
        exp_scores = jnp.exp(scores - row_peak)
        row_total = jnp.sum(exp_scores, axis=-1, keepdims=True)
        log_total = row_peak + jnp.log(row_total)
        probs_low = (exp_scores / row_total).astype(jnp.bfloat16)
        attended = jnp.einsum(
            "hqk,khd->qhd", probs_low, qkv_rows[:, 2], preferred_element_type=jnp.float32
        )
        attended = attended.astype(jnp.bfloat16).reshape(SEQ, D)
        branch = jnp.dot(attended, weights[2], preferred_element_type=jnp.float32)
        hidden = x_float + live_col * branch
        normed2 = rms_norm(hidden, gain_m).astype(jnp.bfloat16)
        logits = jnp.dot(normed2, weights[5], preferred_element_type=jnp.float32)
        route_rows = routes[batch * SEQ : (batch + 1) * SEQ]
        slot_rows = slots[batch * SEQ : (batch + 1) * SEQ]
        hot_first = (route_rows[:, 0:1] == expert_ids[None, :]).astype(jnp.float32)
        hot_second = (route_rows[:, 1:2] == expert_ids[None, :]).astype(jnp.float32)
        gate_first = jax.nn.sigmoid(
            jnp.sum(logits * hot_first, axis=-1) - jnp.sum(logits * hot_second, axis=-1)
        )
        row_place = route_rows * capacity + slot_rows
        target = jnp.where(live_keys[:, None], row_place, experts * capacity)
        outgoing = jnp.zeros((experts * capacity, D), jnp.bfloat16)
        outgoing = (
            outgoing.at[target[:, 0]]
            .set(normed2, mode="drop")
            .at[target[:, 1]]
            .set(normed2, mode="drop")
        )
        outgoing = jnp.repeat(outgoing.reshape(experts, capacity, D), 2, axis=0)
        expert_received = lax.all_to_all(outgoing, "fsdp", split_axis=0, concat_axis=0, tiled=True)
        expert_before = jnp.einsum(
            "scd,df->scf", expert_received, up_weight, preferred_element_type=jnp.float32
        )
        expert_active = exact_gelu(expert_before).astype(jnp.bfloat16)
        partial_value = jnp.einsum(
            "scf,fd->scd", expert_active, down_weight, preferred_element_type=jnp.float32
        ).astype(jnp.bfloat16)
        returned = lax.all_to_all(partial_value, "fsdp", split_axis=0, concat_axis=0, tiled=True)
        results = (returned, expert_received, expert_before)
        combined = (
            results[0]
            .astype(jnp.float32)
            .reshape(experts, 2, capacity, D)
            .sum(axis=1)
            .reshape(experts * capacity, D)
        )
        first_out = combined[row_place[:, 0]]
        second_out = combined[row_place[:, 1]]
        moe = live_col * (
            gate_first[:, None] * first_out + (1.0 - gate_first)[:, None] * second_out
        )
        mixed_parts.append((hidden + moe).astype(jnp.bfloat16))
        saved.append(
            {
                "normed": normed,
                "qkv_rows": qkv_rows,
                "log_total": log_total,
                "attended": attended,
                "hidden": hidden,
                "normed2": normed2,
                "gate_first": gate_first,
                "first_out": first_out,
                "second_out": second_out,
                "results": results,
                "target": target,
                "row_place": row_place,
                "hot_first": hot_first,
                "hot_second": hot_second,
            }
        )
    grad_qkv_w = jnp.zeros((D, 3 * D), jnp.float32)
    grad_proj_w = jnp.zeros((D, D), jnp.float32)
    grad_table = jnp.zeros((SEQ, HEADS), jnp.float32)
    grad_gain_a = jnp.zeros((D,), jnp.float32)
    grad_gain_m = jnp.zeros((D,), jnp.float32)
    grad_router = jnp.zeros((D, experts), jnp.float32)
    grad_up = jnp.zeros((D, FF // 2), jnp.float32)
    grad_down = jnp.zeros((FF // 2, D), jnp.float32)
    grad_parts = [None] * MB
    for batch in reversed(range(MB)):
        kept = saved[batch]
        x_float = tokens[batch * SEQ : (batch + 1) * SEQ].astype(jnp.float32)
        live_keys = places < lengths[batch]
        live_col = live_keys.astype(jnp.float32)[:, None]
        allowed = causal & live_keys[None, :]
        grad_out = cotangent[batch * SEQ : (batch + 1) * SEQ].astype(jnp.float32)
        grad_moe = live_col * grad_out
        gate_first = kept["gate_first"]
        gate_second = 1.0 - gate_first
        grad_gate_first = jnp.sum(grad_moe * kept["first_out"], axis=-1)
        grad_gate_second = jnp.sum(grad_moe * kept["second_out"], axis=-1)
        grad_first = (gate_first[:, None] * grad_moe).astype(jnp.bfloat16)
        grad_second = (gate_second[:, None] * grad_moe).astype(jnp.bfloat16)
        target = kept["target"]
        grad_send = jnp.zeros((experts * capacity, D), jnp.bfloat16)
        grad_send = (
            grad_send.at[target[:, 0]]
            .set(grad_first, mode="drop")
            .at[target[:, 1]]
            .set(grad_second, mode="drop")
        )
        grad_send = jnp.repeat(grad_send.reshape(experts, capacity, D), 2, axis=0)
        grad_recv = lax.all_to_all(grad_send, "fsdp", split_axis=0, concat_axis=0, tiled=True)
        received = kept["results"][1]
        before = kept["results"][2]
        active, gelu_back = jax.vjp(exact_gelu, before)
        active_low = active.astype(jnp.bfloat16)
        grad_active = jnp.einsum(
            "scd,fd->scf", grad_recv, down_weight, preferred_element_type=jnp.float32
        )
        grad_before = gelu_back(grad_active)[0].astype(jnp.bfloat16)
        grad_down = grad_down + jnp.einsum(
            "scf,scd->fd", active_low, grad_recv, preferred_element_type=jnp.float32
        )
        grad_up = grad_up + jnp.einsum(
            "scd,scf->df", received, grad_before, preferred_element_type=jnp.float32
        )
        grad_part = jnp.einsum(
            "scf,df->scd", grad_before, up_weight, preferred_element_type=jnp.float32
        ).astype(jnp.bfloat16)
        grad_back = lax.all_to_all(grad_part, "fsdp", split_axis=0, concat_axis=0, tiled=True)
        grad_rows = (
            grad_back.astype(jnp.float32)
            .reshape(experts, 2, capacity, D)
            .sum(axis=1)
            .reshape(experts * capacity, D)
        )
        row_place = kept["row_place"]
        grad_diff = (grad_gate_first - grad_gate_second) * gate_first * gate_second
        grad_logits = grad_diff[:, None] * (kept["hot_first"] - kept["hot_second"])
        normed2_float = kept["normed2"].astype(jnp.float32)
        grad_router = grad_router + jnp.dot(normed2_float.T, grad_logits, precision=exact_precision)
        grad_normed2 = live_col * (grad_rows[row_place[:, 0]] + grad_rows[row_place[:, 1]])
        grad_normed2 = grad_normed2 + jnp.dot(
            grad_logits, router_float.T, precision=exact_precision
        )
        _, norm_back_moe = jax.vjp(rms_norm, kept["hidden"], gain_m)
        grad_hidden_norm, grad_gain_part = norm_back_moe(grad_normed2)
        grad_gain_m = grad_gain_m + grad_gain_part
        grad_hidden = grad_out + grad_hidden_norm
        grad_branch = (live_col * grad_hidden).astype(jnp.bfloat16)
        grad_proj_w = grad_proj_w + jnp.einsum(
            "sd,se->de", kept["attended"], grad_branch, preferred_element_type=jnp.float32
        )
        grad_attended = jnp.einsum(
            "se,de->sd", grad_branch, weights[2], preferred_element_type=jnp.float32
        )
        grad_attended = grad_attended.astype(jnp.bfloat16).reshape(SEQ, HEADS, HEAD)
        qkv_rows = kept["qkv_rows"]
        scores = masked_scores(qkv_rows, bias, allowed, factor)
        probs = jnp.exp(scores - kept["log_total"])
        probs_low = probs.astype(jnp.bfloat16)
        grad_probs = jnp.einsum(
            "qhd,khd->hqk", grad_attended, qkv_rows[:, 2], preferred_element_type=jnp.float32
        )
        row_dot = jnp.sum(probs * grad_probs, axis=-1, keepdims=True)
        grad_scores = (probs * (grad_probs - row_dot)).astype(jnp.bfloat16)
        grad_table = grad_table + jnp.einsum(
            "dp,hp->dh",
            hot,
            jnp.where(allowed[None], grad_scores, 0).reshape(HEADS, SEQ * SEQ),
            preferred_element_type=jnp.float32,
        )
        grad_queries = (
            jnp.einsum(
                "hqk,khd->qhd", grad_scores, qkv_rows[:, 1], preferred_element_type=jnp.float32
            )
            * factor
        )
        grad_keys = (
            jnp.einsum(
                "hqk,qhd->khd", grad_scores, qkv_rows[:, 0], preferred_element_type=jnp.float32
            )
            * factor
        )
        grad_values = jnp.einsum(
            "hqk,qhd->khd", probs_low, grad_attended, preferred_element_type=jnp.float32
        )
        grad_qkv = (
            jnp.stack([grad_queries, grad_keys, grad_values], axis=1)
            .astype(jnp.bfloat16)
            .reshape(SEQ, 3 * D)
        )
        grad_qkv_w = grad_qkv_w + jnp.einsum(
            "sd,se->de", kept["normed"], grad_qkv, preferred_element_type=jnp.float32
        )
        grad_normed = jnp.einsum(
            "se,de->sd", grad_qkv, weights[1], preferred_element_type=jnp.float32
        )
        _, norm_back_attn = jax.vjp(rms_norm, x_float, gain_a)
        grad_x_norm, grad_gain_piece = norm_back_attn(grad_normed)
        grad_gain_a = grad_gain_a + grad_gain_piece
        grad_parts[batch] = grad_hidden + grad_x_norm
    small = jnp.concatenate(
        [
            grad_gain_a.reshape(groups, -1),
            grad_gain_m.reshape(groups, -1),
            grad_router.reshape(groups, -1),
            grad_table.reshape(groups, -1),
        ],
        axis=1,
    )
    small = lax.psum_scatter(small, "fsdp", scatter_dimension=0, tiled=True)
    shards = (
        small,
        lax.psum_scatter(grad_qkv_w, "fsdp", scatter_dimension=0, tiled=True),
        lax.psum_scatter(grad_proj_w, "fsdp", scatter_dimension=0, tiled=True),
    )
    sums = lax.psum((shards[0], shards[1], shards[2], grad_up[None], grad_down[None]), "replica")
    rows = D // groups
    edge = 2 * rows + rows * experts
    totals = (
        sums[0][0, :rows],
        sums[1],
        sums[2],
        sums[0][0, edge:].reshape(SEQ // groups, HEADS),
        sums[0][0, rows : 2 * rows],
        sums[0][0, 2 * rows : edge].reshape(rows, experts),
        sums[3],
        sums[4],
    )
    mixed = jnp.concatenate(mixed_parts, axis=0)
    grad_tokens = jnp.concatenate(grad_parts, axis=0)
    return (
        mixed,
        grad_tokens,
        totals[0],
        totals[1],
        totals[2],
        totals[3],
        totals[4],
        totals[5],
        totals[6],
        totals[7],
    )


def solution(mesh):
    in_specs = (
        P(("replica", "fsdp"), None),
        P(("replica", "fsdp"), None),
        P(("replica", "fsdp")),
        P(("replica", "fsdp"), None),
        P(("replica", "fsdp"), None),
        P("fsdp"),
        P("fsdp", None),
        P("fsdp", None),
        P("fsdp", None),
        P("fsdp"),
        P("fsdp", None),
        P("fsdp", None, None),
        P("fsdp", None, None),
    )
    out_specs = (
        P(("replica", "fsdp"), None),
        P(("replica", "fsdp"), None),
        P("fsdp"),
        P("fsdp", None),
        P("fsdp", None),
        P("fsdp", None),
        P("fsdp"),
        P("fsdp", None),
        P("fsdp", None, None),
        P("fsdp", None, None),
    )
    fast = dict(mesh.shape) == {"replica": 4, "fsdp": 8}
    return jax.shard_map(body_fast if fast else body, mesh=mesh, in_specs=in_specs, out_specs=out_specs, check_vma=False)
```

```python
import functools

import jax
import jax.numpy as jnp
from jax import lax
from jax.experimental import pallas as pl
from jax.experimental.pallas import tpu as pltpu
from jax.sharding import PartitionSpec as P

D = 768
HEADS = 12
HEAD = 64
FF = 3072
SEQ = 128
MB = 2
MESH = pl.DeviceIdType.MESH
F32 = jnp.float32
BF16 = jnp.bfloat16
NEG = -1e30
HF = FF // 2
TOK = MB * SEQ
EXP = 4
CAP = 64
ROWS = MB * CAP
LOW = 896
MID = 3 * D - 2 * LOW
MORE = MID + 128
SMALL = LOW + MID
PROJ = LOW + MORE
HIGH = PROJ + D
WALL = HIGH + LOW
LEFTC = LOW + MID
SHARD = 96
HALF = SHARD // 2
PAIRS = HEADS // 2
SCALE = HEAD ** (-0.5)


def place():
    replica = lax.axis_index("replica")
    group = lax.axis_index("fsdp")
    return replica // 2, replica % 2, group // 2, group % 2


def device(x, c, z, y):
    return (x * 2 + c, z * 2 + y)


def remote(src, dst, send, recv, target):
    return pltpu.make_async_remote_copy(
        src_ref=src,
        dst_ref=dst,
        send_sem=send,
        recv_sem=recv,
        device_id=target,
        device_id_type=MESH,
    )


def greet():
    x, c, z, y = place()
    barrier = pltpu.get_barrier_semaphore()
    targets = [device(x, 1 - c, z, y), device(1 - x, c, z, y), device(x, c, z, 1 - y)]
    targets += [device(x, c, (z + k) % 4, y) for k in (1, 2, 3)]
    for target in targets:
        pl.semaphore_signal(barrier, inc=1, device_id=target, device_id_type=MESH)
    return lambda: pl.semaphore_wait(barrier, len(targets))


def dot(a, b, ca=1, cb=0):
    return lax.dot_general(a, b, (((ca,), (cb,)), ((), ())), preferred_element_type=F32)


def run(cond, what):
    if cond is None:
        what()
    else:
        pl.when(cond)(what)


class Links:
    def __init__(self, send_sem, recv_sem):
        self.send_sem, self.recv_sem = send_sem, recv_sem
        self.started = []

    def go(self, cond, src, dst, send, recv, target):
        copy = remote(src, dst, self.send_sem.at[send], self.recv_sem.at[recv], target)
        run(cond, copy.start)
        self.started.append((cond, copy))
        return copy

    def arrive(self, cond, dst, recv, target):
        run(cond, remote(dst, dst, self.send_sem.at[0], self.recv_sem.at[recv], target).wait_recv)

    def leave(self, copy):
        copy.wait_send()
        self.started = [(cond, item) for cond, item in self.started if item is not copy]

    def finish(self):
        for cond, copy in self.started:
            run(cond, copy.wait_send)
        self.started = []


def gather_weights(links, wq, wp, wall, local_sem, others, ready):
    x, c, z, y = place()
    own = pl.ds(pl.multiple_of((z * 2 + y) * SHARD, 16), SHARD)
    fills = [
        pltpu.make_async_copy(wq.at[:, pl.ds(0, LEFTC)], wall.at[own, pl.ds(0, LEFTC)], local_sem.at[0]),
        pltpu.make_async_copy(wq.at[:, pl.ds(LEFTC, LOW)], wall.at[own, pl.ds(HIGH, LOW)], local_sem.at[1]),
        pltpu.make_async_copy(wp, wall.at[own, pl.ds(PROJ, D)], local_sem.at[2]),
    ]
    for copy in fills + others:
        copy.start()
    ready()
    share = pl.ds(pl.multiple_of(x * HIGH, 128), LOW)
    gained = pl.ds(pl.multiple_of((1 - x) * HIGH, 128), LOW)
    columns = (share, pl.ds(LOW, MORE), pl.ds(PROJ, D))
    up, down = device(x, c, z + 1, y), device(x, c, z - 1, y)
    across, facing, twin = device(x, c, z, 1 - y), device(1 - x, c, z, y), device(x, 1 - c, z, y)

    def part(zs, ys, half, cols):
        return wall.at[pl.ds(pl.multiple_of((zs * 2 + ys) * SHARD + half * HALF, 16), HALF), cols]

    def go(cond, zs, ys, cols, send, recv, target, src=None):
        piece = part(zs, ys, c, cols)
        links.go(cond, piece if src is None else src, piece, send, recv, target)

    def arrive(cond, zs, ys, half, cols, recv):
        links.arrive(cond, part(zs, ys, half, cols), recv, twin)

    def spread(cond, sub, zs, ys):
        source = zs * 2 + ys
        if sub == 0:
            go(cond, zs, ys, share, 39 + source, 24 + source, facing)
        go(cond, zs, ys, columns[sub], 47 + sub * 8 + source, 32 + sub * 8 + source, twin)

    def begin(sub, src):
        go(z < 3, z, y, columns[sub], sub * 3, sub * 4 + z, up, src)
        go(z > 0, z, y, columns[sub], 9 + sub * 3, sub * 4 + z, down, src)
        go(None, z, y, columns[sub], 18 + sub * 7, 12 + sub * 4 + z, across, src)

    def along(sub, k):
        below, above = z - k, z + k
        for cond, zs, on, first, target, place_of in (
            (below >= 0, below, z < 3, 0, up, k),
            (above <= 3, above, z > 0, 9, down, 3 + k),
        ):
            arrive(cond, zs, y, c, columns[sub], sub * 4 + zs)
            if k < 3:
                go(cond & on, zs, y, columns[sub], first + sub * 3 + k, sub * 4 + zs, target)
            go(cond, zs, y, columns[sub], 18 + sub * 7 + place_of, 12 + sub * 4 + zs, across)
            spread(cond, sub, zs, y)

    def over(sub, k):
        if k == 0:
            arrive(None, z, 1 - y, c, columns[sub], 12 + sub * 4 + z)
            spread(None, sub, z, 1 - y)
            return
        for cond, zs in ((z - k >= 0, z - k), (z + k <= 3, z + k)):
            arrive(cond, zs, 1 - y, c, columns[sub], 12 + sub * 4 + zs)
            spread(cond, sub, zs, 1 - y)

    half = pl.ds(pl.multiple_of(c * HALF, 16), HALF)
    begin(0, wq.at[half, pl.ds(pl.multiple_of(x * LEFTC, 128), LOW)])
    for fill in fills:
        fill.wait()
    begin(1, None)
    for k in (1, 2, 3):
        for sub in range(2):
            along(sub, k)
            over(sub, k - 1)
        if k == 2:
            begin(2, wp.at[half, :])
    along(2, 1)
    for sub in range(2):
        over(sub, 3)

    def each(what):
        for zs in range(4):
            for ys in range(2):
                what((zs != z) | (ys != y), zs, ys, zs * 2 + ys)

    def gain(other, zs, ys, source):
        arrive(other, zs, ys, c, gained, 24 + source)
        go(other, zs, ys, gained, 71 + source, 56 + source, twin)

    def mostly(other, zs, ys, source):
        for sub in range(2):
            arrive(other, zs, ys, 1 - c, columns[sub], 32 + sub * 8 + source)
        arrive(other, zs, ys, 1 - c, gained, 56 + source)

    def rest(other, zs, ys, source):
        arrive(other, zs, ys, 1 - c, columns[2], 32 + 16 + source)

    each(gain)
    each(mostly)

    def first():
        along(2, 2)
        over(2, 0)

    def second():
        along(2, 3)
        over(2, 1)
        over(2, 2)

    return first, second, lambda: over(2, 3), lambda: each(rest)


def unit(values):
    return lax.rsqrt(jnp.mean(values * values, axis=-1, keepdims=True) + 1e-06)


def heads(rows):
    lane = lax.broadcasted_iota(jnp.int32, rows.shape, 1)
    none = jnp.zeros_like(rows)
    return jnp.concatenate([jnp.where(lane < HEAD, rows, none), jnp.where(lane < HEAD, none, rows)], axis=0)


def beside(blocks):
    return jnp.concatenate([blocks[0:SEQ], blocks[SEQ : 2 * SEQ]], axis=1)


def build_bias(wall, bias):
    table = jnp.concatenate(
        [wall[f * SHARD : f * SHARD + 16, SMALL : SMALL + 128] for f in range(8)], axis=0
    )
    ahead = lax.broadcasted_iota(jnp.int32, (SEQ, SEQ), 0)
    lane = lax.broadcasted_iota(jnp.int32, (SEQ, SEQ), 1)
    turned = jnp.where(ahead + lane == SEQ, 1.0, jnp.where(ahead + lane == 0, 1.0, 0.0)).astype(BF16)
    lines = dot(table, turned, 0, 0)
    for h in range(HEADS):
        line = jnp.broadcast_to(lines[HEAD + h : HEAD + h + 1, :], (SEQ, SEQ))
        rolled = pltpu.roll(line, 0, 1, stride=1, stride_axis=0)
        bias[h * SEQ : (h + 1) * SEQ, 0:SEQ] = jnp.where(ahead >= lane, rolled, NEG)


def pack(gain_attn, gain_moe, router_t, rel, board, wall):
    x, c, z, y = place()
    board[0:SEQ, 0:SEQ] = jnp.zeros((SEQ, SEQ), F32)
    board[0:1, 0:SHARD] = gain_attn[...].astype(F32)
    board[1:2, 0:SHARD] = gain_moe[...].astype(F32)
    board[2 : 2 + EXP, 0:SHARD] = router_t[...].astype(F32)
    turned = jnp.transpose(board[0:SEQ, 0:SEQ])
    board[0:SEQ, 0:SEQ] = turned
    board[0:16, HEAD : HEAD + HEADS] = rel[...].astype(F32)
    own = pl.ds(pl.multiple_of((z * 2 + y) * SHARD, 16), SHARD)
    wall[own, SMALL : SMALL + 128] = board[0:SHARD, 0:SEQ].astype(BF16)


def stand(routes, slots, lines, columns):
    chosen = routes[...]
    lines[...] = jnp.zeros_like(lines)
    lines[0:2, :] = (chosen * CAP + slots[...]).astype(F32)
    lines[2:4, :] = chosen.astype(F32)
    columns[...] = jnp.transpose(lines[...])


def routing(columns, s):
    spots = columns[s * SEQ : (s + 1) * SEQ, :]
    lane = lax.broadcasted_iota(jnp.int32, (SEQ, EXP * CAP), 1).astype(F32)
    return spots[:, 0:1] == lane, spots[:, 1:2] == lane


def named(columns, s):
    spots = columns[s * SEQ : (s + 1) * SEQ, :]
    lane = lax.broadcasted_iota(jnp.int32, (SEQ, 128), 1).astype(F32) - 2.0
    return spots[:, 2:3] == lane, spots[:, 3:4] == lane


def live_column(lengths, s):
    return lax.broadcasted_iota(jnp.int32, (SEQ, 1), 0) < lengths[s]


def attention_forward(
    later, dispatch, x_ref, cot, lengths, columns, wall, rows_t, board, normed, qkv, attended, hidden, normed2, gates,
    out_f, out_g,
):
    rows_t[...] = jnp.transpose(wall[:, SMALL : SMALL + 128].astype(F32))[0:8]
    build_bias(wall, board)
    x = x_ref[...].astype(F32)
    normed[...] = (x * unit(x) * rows_t[0:1, :]).astype(BF16)
    qkv[:, 0:LEFTC] = dot(normed[...], wall[:, 0:LEFTC]).astype(BF16)
    qkv[:, LEFTC : 3 * D] = dot(normed[...], wall[:, HIGH:WALL]).astype(BF16)
    lane = lax.broadcasted_iota(jnp.int32, (2 * SEQ, 128), 1)

    def pair(s, p):
        blocks = pl.ds(pl.multiple_of(p * 2 * SEQ, SEQ), 2 * SEQ)
        rows = slice(s * SEQ, (s + 1) * SEQ)
        q = qkv[rows, pl.ds(pl.multiple_of(p * 128, 128), 128)]
        k = qkv[rows, pl.ds(pl.multiple_of(D + p * 128, 128), 128)]
        v = qkv[rows, pl.ds(pl.multiple_of(2 * D + p * 128, 128), 128)]
        scores = jnp.where(lane < lengths[s], dot(heads(q), k, 1, 1) * SCALE + board[blocks, 0:SEQ], NEG)
        scores = jnp.exp(scores - jnp.max(scores, axis=-1, keepdims=True))
        share = scores * (1.0 / jnp.sum(scores, axis=-1, keepdims=True))
        board[blocks, (1 + s) * SEQ : (2 + s) * SEQ] = share
        attended[rows, pl.ds(pl.multiple_of(p * 128, 128), 128)] = dot(
            beside(share.astype(BF16)), heads(v)
        ).astype(BF16)

    def pairs(s, first, last):
        def step(i, carry):
            pair(s, 2 * i)
            pair(s, 2 * i + 1)
            return carry

        lax.fori_loop(first, last, step, 0)

    def finish(s):
        rows = slice(s * SEQ, (s + 1) * SEQ)
        live = live_column(lengths, s)
        branch = dot(attended[rows, :], wall[:, PROJ:HIGH])
        state = x_ref[rows, :].astype(F32) + jnp.where(live, branch, 0.0)
        hidden[rows, :] = state
        low = (state * unit(state) * rows_t[1:2, :]).astype(BF16)
        normed2[rows, :] = low
        first, second = routing(columns, s)
        first = jnp.where(first & live, 1.0, 0.0).astype(BF16)
        second = jnp.where(second & live, 1.0, 0.0).astype(BF16)
        sent = dot(first + second, low, 0, 0).astype(BF16)
        for e in range(EXP):
            out_f[e, s * CAP : (s + 1) * CAP, :] = sent[e * CAP : (e + 1) * CAP, :]
        dispatch(s)
        logits = dot(low, wall[:, SMALL : SMALL + 128])
        one, two = named(columns, s)
        picked = jnp.where(one, logits, 0.0) - jnp.where(two, logits, 0.0)
        gate = jax.nn.sigmoid(jnp.sum(picked, axis=-1, keepdims=True))
        gates[rows, :] = gate
        grad = jnp.where(live, cot[rows, :].astype(F32), 0.0)
        back = dot(first, (gate * grad).astype(BF16), 0, 0) + dot(
            second, ((1.0 - gate) * grad).astype(BF16), 0, 0
        )
        back = back.astype(BF16)
        for e in range(EXP):
            out_g[e, s * CAP : (s + 1) * CAP, :] = back[e * CAP : (e + 1) * CAP, :]

    for t in range(3):
        later[t]()
        pairs(0, t, t + 1)
    later[3]()
    finish(0)
    pairs(1, 0, 3)
    finish(1)


TILE = 512
Z_ROWS, Y_ROWS, Y_PART, Z_BACK = 80, 88, 96, 104
TWIN_W, FACE_W, TWIN_OUT = 112, 114, 120
RS_TWIN, RS_Y, RS_Z, RS_FACE, RS_OUT = 126, 131, 151, 191, 196
Z_FIRST, Y_FIRST = 206, 214
RS_PART = 216
LINKS = 226


def quarter(zs):
    return pl.ds(pl.multiple_of(zs * 2 * ROWS, 2 * ROWS), 2 * ROWS)


def half_rows(zs, ys):
    return pl.ds(pl.multiple_of((zs * 2 + ys) * ROWS, ROWS), ROWS)


def expert_forward(zs, recv, up, down, act, slope, part):
    rows = quarter(zs)

    def tile(i, carry):
        cols = pl.ds(pl.multiple_of(i * TILE, TILE), TILE)
        before = dot(recv[rows, :], up[:, cols])
        below = 0.5 + 0.5 * lax.erf(before * 0.7071067811865476)
        act[rows, cols] = (before * below).astype(BF16)
        density = jnp.exp(before * before * -0.5) * 0.3989422804014327
        slope[rows, cols] = (below + before * density).astype(BF16)
        return carry

    lax.fori_loop(0, HF // TILE, tile, 0)
    got = dot(act[rows, 0:HF], down[...]).astype(BF16)
    part[zs, 0] = got[0:ROWS]
    part[zs, 1] = got[ROWS : 2 * ROWS]


def expert_backward(zs, recv, up, down, slope, part):
    rows = quarter(zs)

    def tile(i, carry):
        cols = pl.ds(pl.multiple_of(i * TILE, TILE), TILE)
        grad = dot(recv[rows, :], down[cols, :], 1, 1)
        slope[rows, cols] = (grad * slope[rows, cols].astype(F32)).astype(BF16)
        return carry

    lax.fori_loop(0, HF // TILE, tile, 0)
    got = dot(slope[rows, :], up[...], 1, 1).astype(BF16)
    part[zs, 0] = got[0:ROWS]
    part[zs, 1] = got[ROWS : 2 * ROWS]


def one_sequence(zs, ys, s):
    return pl.ds(pl.multiple_of((zs * 2 + ys) * ROWS + s * CAP, CAP), CAP)


def dispatch_forward(links, out, recv, s):
    x, c, z, y = place()
    rows = slice(s * CAP, (s + 1) * CAP)
    there = recv.at[one_sequence(z, y, s), :]
    links.go(None, out.at[z, rows, :], there, Y_FIRST + s, Y_FIRST + s, device(x, c, z, 1 - y))
    for d in (1, 2, 3):
        to = (z + d) % 4
        slot = Z_FIRST + s * 4
        links.go(None, out.at[to, rows, :], there, slot + d, slot + z, device(x, c, to, y))
    recv[one_sequence(z, y, s), :] = out[z, rows, :]


def experts(links, out, recv, up, down, act, slope, part, take, back, w_down, w_up):
    x, c, z, y = place()
    across, facing, twin = device(x, c, z, 1 - y), device(1 - x, c, z, y), device(x, 1 - c, z, y)

    for kind in (1,):
        links.go(None, out[kind].at[z], recv[kind].at[half_rows(z, y), :], Y_ROWS + kind * 4, Y_ROWS + kind * 4 + z, across)
        for d in (1, 2, 3):
            to = (z + d) % 4
            links.go(
                None, out[kind].at[to], recv[kind].at[half_rows(z, y), :], Z_ROWS + kind * 4 + d,
                Z_ROWS + kind * 4 + z, device(x, c, to, y),
            )
        recv[kind][half_rows(z, y), :] = out[kind][z]

    def source(d):
        return (z + 4 - d) % 4

    def reach(kind, d):
        zs = source(d)
        rows = recv[kind].at[half_rows(zs, y), :]
        if kind == 0:
            for s in range(MB):
                links.arrive(None, recv[0].at[one_sequence(zs, y, s), :], Z_FIRST + s * 4 + zs, across)
        else:
            links.arrive(None, rows, Z_ROWS + kind * 4 + zs, across)
        links.go(None, rows, rows, Y_ROWS + kind * 4 + d, Y_ROWS + kind * 4 + zs, across)

    def compute(kind, d):
        zs = source(d)
        if kind == 0 and d == 0:
            for s in range(MB):
                links.arrive(None, recv[0].at[one_sequence(z, 1 - y, s), :], Y_FIRST + s, across)
        else:
            links.arrive(None, recv[kind].at[half_rows(zs, 1 - y), :], Y_ROWS + kind * 4 + zs, across)
        if kind == 0:
            expert_forward(zs, recv[0], up, down, act, slope, part[0])
        else:
            expert_backward(zs, recv[1], up, down, slope, part[1])

    def give_part(kind, d):
        zs = source(d)
        links.go(
            None, part[kind].at[zs, 1 - y], take[kind].at[zs], Y_PART + kind * 4 + d, Y_PART + kind * 4 + zs, across
        )

    def merge(kind, d):
        zs = source(d)
        links.arrive(None, take[kind].at[zs], Y_PART + kind * 4 + zs, across)
        total = (part[kind][zs, y].astype(F32) + take[kind][zs].astype(F32)).astype(BF16)
        if d == 0:
            back[kind][z] = total
        else:
            part[kind][zs, y] = total
            links.go(
                None, part[kind].at[zs, y], back[kind].at[z], Z_BACK + kind * 4 + d, Z_BACK + kind * 4 + z,
                device(x, c, zs, y),
            )

    reach(0, 1)
    compute(0, 0)
    reach(0, 2)
    compute(1, 0)
    reach(0, 3)
    compute(0, 1)
    reach(1, 1)
    give_part(0, 1)
    compute(0, 2)
    reach(1, 2)
    give_part(0, 2)
    compute(1, 1)
    reach(1, 3)
    give_part(1, 1)
    merge(0, 1)
    compute(0, 3)
    give_part(0, 3)
    merge(0, 2)
    compute(1, 2)
    give_part(1, 2)
    compute(1, 3)
    give_part(1, 3)
    give_part(0, 0)
    give_part(1, 0)

    def down_tile(i, part_of, keep):
        cols = pl.ds(pl.multiple_of(part_of * (HF // 2) + i * 256, 128), 256)
        got = dot(act[:, cols], recv[1][...], 0, 0)
        keep[pl.ds(pl.multiple_of(i * 256, 256), 256), :] = got.astype(keep.dtype)

    def up_tile(i, part_of, keep):
        cols = pl.ds(pl.multiple_of(part_of * (D // 2) + i * 128, 128), 128)
        got = dot(recv[0][:, cols], slope[...], 0, 0)
        keep[pl.ds(pl.multiple_of(i * 128, 128), 128), :] = got.astype(keep.dtype)

    def tiles(one, part_of, keep):
        def step(i, carry):
            one(i, part_of, keep)
            return carry

        lax.fori_loop(0, 3, step, 0)

    def spread(i, sent):
        own, give, got, face = (w_down, w_up)[i]
        links.arrive(None, got, TWIN_W + i, twin)
        links.leave(sent)
        count = own.shape[0] // 3
        for m in range(3):
            rows = slice(m * count, (m + 1) * count)
            give[rows, :] = (own[rows, :] + got[rows, :].astype(F32)).astype(BF16)
            links.go(None, give.at[rows, :], face.at[rows, :], FACE_W + i * 3 + m, FACE_W + i * 3 + m, facing)

    tiles(down_tile, 1 - c, w_down[1])
    sent = links.go(None, w_down[1], w_down[2], TWIN_W, TWIN_W, twin)
    merge(1, 1)
    tiles(down_tile, c, w_down[0])
    spread(0, sent)
    merge(0, 3)
    tiles(up_tile, 1 - c, w_up[1])
    sent = links.go(None, w_up[1], w_up[2], TWIN_W + 1, TWIN_W + 1, twin)
    merge(1, 2)
    tiles(up_tile, c, w_up[0])
    spread(1, sent)
    merge(1, 3)
    merge(0, 0)

    def returned(kind):
        if kind == 1:
            merge(1, 0)
        for d in (1, 2, 3):
            zs = source(d)
            links.arrive(None, back[kind].at[zs], Z_BACK + kind * 4 + zs, across)

    return returned


def expert_grad_out(links, piece, w_down, w_up, out_down, out_up, local_sem):
    x, c, z, y = place()
    facing, twin = device(1 - x, c, z, y), device(x, 1 - c, z, y)
    (own, give, got, face), target = ((w_down, out_down), (w_up, out_up))[piece // 3]
    count = own.shape[0] // 3
    rows = slice((piece % 3) * count, (piece % 3 + 1) * count)
    links.arrive(None, face.at[rows, :], FACE_W + piece, facing)
    face[rows, :] = (give[rows, :].astype(F32) + face[rows, :].astype(F32)).astype(BF16)
    there = target.at[pl.ds(pl.multiple_of((c * 3 + piece % 3) * count, 128), count), :]
    links.go(None, face.at[rows, :], there, TWIN_OUT + piece, TWIN_OUT + piece, twin)
    copy = pltpu.make_async_copy(face.at[rows, :], there, local_sem.at[8 + piece])
    copy.start()
    return copy


def expert_grads_arrive(links, out_down, out_up):
    x, c, z, y = place()
    for piece in range(6):
        target = (out_down, out_up)[piece // 3]
        count = target.shape[0] // 6
        there = target.at[pl.ds(pl.multiple_of(((1 - c) * 3 + piece % 3) * count, 128), count), :]
        links.arrive(None, there, TWIN_OUT + piece, device(x, 1 - c, z, y))


SENTC = 2 * D + 128


def combine(returned, cot, lengths, columns, rows_t, hidden, normed2, gates, back_f, back_g, mixed, rb, small_t):
    gain_grad = jnp.zeros((1, D), F32)
    router_grad = jnp.zeros((128, D), F32)
    kept = []
    returned(0)
    for s in range(MB):
        rows = slice(s * SEQ, (s + 1) * SEQ)
        live = live_column(lengths, s)
        first, second = routing(columns, s)
        first = jnp.where(first, 1.0, 0.0).astype(BF16)
        second = jnp.where(second, 1.0, 0.0).astype(BF16)
        given = jnp.concatenate([back_f[e, s * CAP : (s + 1) * CAP, :] for e in range(EXP)], axis=0)
        first_out = dot(first, given)
        second_out = dot(second, given)
        gate = gates[rows, :]
        grad_live = jnp.where(live, cot[rows, :].astype(F32), 0.0)
        moe = gate * first_out + (1.0 - gate) * second_out
        mixed[rows, :] = (hidden[rows, :] + jnp.where(live, moe, 0.0)).astype(BF16)
        tilt = jnp.sum(grad_live * first_out, axis=-1, keepdims=True) - jnp.sum(
            grad_live * second_out, axis=-1, keepdims=True
        )
        tilt = tilt * gate * (1.0 - gate)
        one, two = named(columns, s)
        hot = jnp.where(one, 1.0, 0.0) - jnp.where(two, 1.0, 0.0)
        grad_logits = tilt * hot
        high = grad_logits.astype(BF16)
        low = (grad_logits - high.astype(F32)).astype(BF16)
        router_grad = router_grad + dot(high, normed2[rows, :], 0, 0) + dot(low, normed2[rows, :], 0, 0)
        kept.append((live, first + second, grad_logits))
    returned(1)
    for s in range(MB):
        rows = slice(s * SEQ, (s + 1) * SEQ)
        live, either, grad_logits = kept[s]
        given = jnp.concatenate([back_g[e, s * CAP : (s + 1) * CAP, :] for e in range(EXP)], axis=0)
        grad_low = jnp.where(live, dot(either, given), 0.0)
        for e in range(EXP):
            grad_low = grad_low + grad_logits[:, 2 + e : 3 + e] * rows_t[2 + e : 3 + e, :]
        state = hidden[rows, :]
        factor = unit(state)
        scaled = state * factor
        gain_grad = gain_grad + jnp.sum(grad_low * scaled, axis=0, keepdims=True)
        grad_low = grad_low * rows_t[1:2, :]
        inner = jnp.mean(grad_low * scaled, axis=-1, keepdims=True)
        grad_state = cot[rows, :].astype(F32) + factor * (grad_low - scaled * inner)
        hidden[rows, :] = grad_state
        rb[rows, 3 * D : 4 * D] = jnp.where(live, grad_state, 0.0).astype(BF16)
    small_t[...] = router_grad
    small_t[1:2, :] = gain_grad


def attention_backward(x_ref, wall, rows_t, qkv, board, hidden, grad_att, rb, rel_rows, small_t, grad_tokens, midway, formed):
    grad_att[...] = dot(rb[:, 3 * D : 4 * D], wall[:, PROJ:HIGH], 1, 1).astype(BF16)
    midway()
    lane = lax.broadcasted_iota(jnp.int32, (SEQ, 128), 1)
    ahead = lax.broadcasted_iota(jnp.int32, (SEQ, 128), 0)
    flip = jnp.where(ahead + lane == SEQ - 1, 1.0, 0.0).astype(BF16)
    flip = jnp.concatenate([flip] * MB, axis=1)

    def pair(p, carry):
        blocks = pl.ds(pl.multiple_of(p * 2 * SEQ, SEQ), 2 * SEQ)
        scores = []
        for s in range(MB):
            rows = slice(s * SEQ, (s + 1) * SEQ)
            cols = [pl.ds(pl.multiple_of(i * D + p * 128, 128), 128) for i in range(3)]
            q, k, v = (qkv[rows, cols[i]] for i in range(3))
            grad = heads(grad_att[rows, cols[0]])
            share = board[blocks, (1 + s) * SEQ : (2 + s) * SEQ]
            grad_probs = dot(grad, v, 1, 1)
            inner = jnp.sum(share * grad_probs, axis=-1, keepdims=True)
            grad_scores = (share * (grad_probs - inner)).astype(BF16)
            scores.append(beside(grad_scores))
            rb[rows, cols[0]] = (dot(scores[s], heads(k)) * SCALE).astype(BF16)
            rb[rows, cols[1]] = (dot(grad_scores, heads(q), 0, 0) * SCALE).astype(BF16)
            rb[rows, cols[2]] = dot(share.astype(BF16), grad, 0, 0).astype(BF16)
        flipped = dot(flip, jnp.concatenate(scores, axis=0))
        for j in range(2):
            rolled = pltpu.roll(flipped[:, j * SEQ : (j + 1) * SEQ], 1, 1, stride=1, stride_axis=0)
            rel_rows[pl.ds(2 * p + j, 1), :] = jnp.sum(rolled, axis=0, keepdims=True)
        return carry

    for t in range(3):
        lax.fori_loop(2 * t, 2 * t + 2, pair, 0)
        formed[t]()
    grad_low = dot(rb[:, 0:LEFTC], wall[:, 0:LEFTC], 1, 1) + dot(
        rb[:, LEFTC : 3 * D], wall[:, HIGH:WALL], 1, 1
    )
    state = x_ref[...].astype(F32)
    factor = unit(state)
    scaled = state * factor
    small_t[0:1, :] = jnp.sum(grad_low * scaled, axis=0, keepdims=True)
    grad_low = grad_low * rows_t[0:1, :]
    inner = jnp.mean(grad_low * scaled, axis=-1, keepdims=True)
    grad_tokens[...] = hidden[...] + factor * (grad_low - scaled * inner)

    spot = lax.broadcasted_iota(jnp.int32, (SEQ, D), 0)
    column = lax.broadcasted_iota(jnp.int32, (SEQ, D), 1)
    distance = (SEQ - spot) & (SEQ - 1)
    picks = jnp.where(column == (distance >> 4) * SHARD + (distance & 15), 1.0, 0.0).astype(BF16)
    rest = rel_rows[...]
    spread = jnp.zeros((16, D), F32)
    for _ in range(3):
        high = rest.astype(BF16)
        spread = spread + dot(high, picks)
        rest = rest - high.astype(F32)
    small_t[HEAD : HEAD + 16, :] = spread


HC = D // 2
SMALLS = SENTC - 128
STRAIGHT = (0, 1, 2, 3, 4)


def portions(group):
    if group == 0:
        return 1, 2 * HC, HC, ((0, HC, lambda core: 3 * D + core * HC, lambda core: core * HC),)
    if group == 4:
        return 0, SMALLS, 128, ()
    t = group - 1
    both = (
        (0, 256, lambda core: core * D + 256 * t, lambda core: core * D + 256 * t),
        (256, 128, lambda core: 2 * D + 256 * t + 128 * core, lambda core: 2 * D + 256 * t + 128 * core),
    )
    return 0, (0, HC, 3 * HC)[t], HC, both


class Reduction:
    def __init__(self, links, group, left, rb, small_t, give, take, total, y_take, z_take, face_give, face_take, last):
        self.links, self.group = links, group
        which, first, width, portion = portions(group)
        self.cols = slice(first, first + width)
        self.portion = [(slice(first + at, first + at + wide), wide, rhs, target) for at, wide, rhs, target in portion]
        self.lhs, self.rb, self.small_t = left.at[which], rb, small_t
        self.give, self.take, self.total = give, take, total
        self.y_take, self.z_take, self.face_give, self.face_take, self.last = y_take, z_take, face_give, face_take, last
        x, c, z, y = self.place = place()
        self.across, self.facing, self.twin = device(x, c, z, 1 - y), device(1 - x, c, z, y), device(x, 1 - c, z, y)
        mirror = z // 2
        near = z + mirror * (3 - 2 * z)
        self.order = [o + mirror * (3 - 2 * o) for o in (3, 2, 1 - near, near)]

    def tile(self, core, keep, rows):
        for cols, wide, rhs, target in self.portion:
            right = self.rb[:, pl.ds(pl.multiple_of(rhs(core), 128), wide)]
            keep[rows, cols] = dot(self.lhs[:, rows], right, 0, 0).astype(keep.dtype)

    def form(self):
        x, c, z, y = self.place
        self.sent = []
        for m in range(3):
            self.tile(1 - c, self.give, self.third(m))
            self.to_twin(self.third(m), self.slots()[m])

        def own(m, carry):
            self.tile(c, self.total, pl.ds(pl.multiple_of(m * 256, 256), 256))
            return carry

        lax.fori_loop(0, 3, own, 0)

    def third(self, m):
        return slice(m * 256, (m + 1) * 256)

    def slots(self):
        return RS_TWIN + self.group, RS_PART + self.group * 2, RS_PART + self.group * 2 + 1

    def to_twin(self, rows, slot):
        cols = self.cols
        self.sent.append(self.links.go(None, self.give.at[rows, cols], self.take.at[rows, cols], slot, slot, self.twin))

    def form_small(self):
        small = jnp.transpose(self.small_t[...]).astype(BF16)
        self.give[:, self.cols] = small
        self.sent = []
        for m in range(3):
            self.to_twin(self.third(m), self.slots()[m])
        self.total[:, self.cols] = small.astype(F32)

    def shard(self, zs, ys):
        return pl.ds(pl.multiple_of((zs * 2 + ys) * SHARD, 16), SHARD)

    def halve(self):
        x, c, z, y = self.place
        links, cols = self.links, self.cols
        for m in range(3):
            links.arrive(None, self.take.at[self.third(m), cols], self.slots()[m], self.twin)
        for copy in self.sent:
            links.leave(copy)
        for zs in self.order:
            rows = self.shard(zs, 1 - y)
            self.give[rows, cols] = (self.total[rows, cols] + self.take[rows, cols].astype(F32)).astype(BF16)
            slot = RS_Y + self.group * 4 + zs
            links.go(None, self.give.at[rows, cols], self.y_take.at[zs, :, cols], slot, slot, self.across)
        for zs in self.order:
            rows = self.shard(zs, y)
            self.total[rows, cols] = self.total[rows, cols] + self.take[rows, cols].astype(F32)

    def chain(self, k):
        x, c, z, y = self.place
        links, cols, zs = self.links, self.cols, self.order[k]
        total, z_take = self.total, self.z_take
        rows = self.shard(zs, y)
        links.arrive(None, self.y_take.at[zs, :, cols], RS_Y + self.group * 4 + zs, self.across)
        total[rows, cols] = total[rows, cols] + self.y_take[zs, :, cols].astype(F32)
        if k == 3:
            return
        if self.group in STRAIGHT:
            self.give[rows, cols] = total[rows, cols].astype(BF16)
            base = RS_Z + self.group * 8
            links.go(None, self.give.at[rows, cols], z_take.at[z, :, cols], base + k, base + z, device(x, c, zs, y))
            return
        for cond, more, slot, target in (
            (zs > z, z > 0, zs, device(x, c, z + 1, y)),
            (zs < z, z < 3, 4 + zs, device(x, c, z - 1, y)),
        ):
            self.add_from_z(cond & more, slot, rows)

            @pl.when(cond)
            def _():
                self.give[rows, cols] = total[rows, cols].astype(BF16)

            index = RS_Z + self.group * 8 + slot
            links.go(cond, self.give.at[rows, cols], z_take.at[slot, :, cols], index, index, target)

    def add_from_z(self, cond, slot, rows):
        cols = self.cols

        @pl.when(cond)
        def _():
            part = self.z_take.at[slot, :, cols]
            self.links.arrive(None, part, RS_Z + self.group * 8 + slot, self.across)
            self.total[rows, cols] = self.total[rows, cols] + part[...].astype(F32)

    def face(self):
        x, c, z, y = self.place
        rows, cols = self.shard(z, y), self.cols
        if self.group in STRAIGHT:
            for d in (1, 2, 3):
                zs = (z + d) % 4
                self.links.arrive(None, self.z_take.at[zs, :, cols], RS_Z + self.group * 8 + zs, self.across)
                self.total[rows, cols] = self.total[rows, cols] + self.z_take[zs, :, cols].astype(F32)
        else:
            self.add_from_z(z > 0, z, rows)
            self.add_from_z(z < 3, 4 + z, rows)
        self.face_give[:, cols] = self.total[rows, cols].astype(BF16)
        slot = RS_FACE + self.group
        self.links.go(None, self.face_give.at[:, cols], self.face_take.at[:, cols], slot, slot, self.facing)

    def publish(self, out_qkv, out_proj, out_small, local_sem):
        x, c, z, y = self.place
        cols = self.cols
        self.links.arrive(None, self.face_take.at[:, cols], RS_FACE + self.group, self.facing)
        self.last[:, cols] = self.face_give[:, cols].astype(F32) + self.face_take[:, cols].astype(F32)
        self.out = out_proj if self.group == 0 else out_qkv
        copies = []
        for i, (part, there) in enumerate(self.landing(c)):
            slot = RS_OUT + self.group * 2 + i
            self.links.go(None, part, there, slot, slot, self.twin)
            copies.append(pltpu.make_async_copy(part, there, local_sem.at[16 + self.group * 2 + i]))
        if self.group == 4:
            copies.append(pltpu.make_async_copy(self.last.at[:, cols], out_small, local_sem.at[6]))
        for copy in copies:
            copy.start()
        return copies

    def landing(self, core):
        return [
            (self.last.at[:, cols], self.out.at[:, pl.ds(pl.multiple_of(target(core), 128), wide)])
            for cols, wide, rhs, target in self.portion
        ]

    def landed(self):
        x, c, z, y = self.place
        for i, (part, there) in enumerate(self.landing(1 - c)):
            self.links.arrive(None, there, RS_OUT + self.group * 2 + i, self.twin)


def layer(
    x_in, cot_in, lengths, routes, slots, gain_attn, gain_moe, router_t, rel, wq, wp, w_up, w_down,
    mixed_out, tokens_out, out_qkv, out_proj, out_small, out_up, out_down,
    x_ref, cot, mixed, grad_tokens, board,
    wall, rows_t, lines, columns, left, qkv, hidden, normed2, gates, out_f, out_g, recv_f, recv_g, up, down, act, slope,
    part_f, part_g, take_f, take_g, back_f, back_g, dn_own, dn_give, dn_take, dn_face, up_own, up_give, up_take, up_face,
    rb, rel_rows, small_t, take, total, y_take, z_take, face_give, face_take, last,
    local_sem, send_sem, recv_sem,
):
    inputs = [
        pltpu.make_async_copy(x_in, x_ref, local_sem.at[24]),
        pltpu.make_async_copy(cot_in, cot, local_sem.at[25]),
    ]
    fetch = [
        pltpu.make_async_copy(w_up.at[0], up, local_sem.at[4]),
        pltpu.make_async_copy(w_down.at[0], down, local_sem.at[5]),
    ]
    met = greet()
    links = Links(send_sem, recv_sem)

    def ready():
        pack(gain_attn, gain_moe, router_t, rel, board, wall)
        stand(routes, slots, lines, columns)
        rel_rows[...] = jnp.zeros_like(rel_rows)
        met()

    later = gather_weights(links, wq, wp, wall, local_sem, inputs + fetch, ready)
    for copy in inputs:
        copy.wait()
    normed, attended = left.at[0], left.at[1]
    attention_forward(
        later, functools.partial(dispatch_forward, links, out_f, recv_f), x_ref, cot, lengths, columns, wall, rows_t, board, normed, qkv, attended, hidden, normed2, gates,
        out_f, out_g,
    )
    for copy in fetch:
        copy.wait()
    downs, ups = (dn_own, dn_give, dn_take, dn_face), (up_own, up_give, up_take, up_face)
    returned = experts(
        links, (out_f, out_g), (recv_f, recv_g), up, down, act, slope, (part_f, part_g), (take_f, take_g),
        (back_f, back_g), downs, ups,
    )
    combine(returned, cot, lengths, columns, rows_t, hidden, normed2, gates, back_f, back_g, mixed, rb, small_t)
    pending = []

    def put(src, dst, i):
        copy = pltpu.make_async_copy(src, dst, local_sem.at[i])
        copy.start()
        pending.append(copy)

    put(mixed, mixed_out, 26)
    proj, one, two, three, small = (
        Reduction(
            links, group, left, rb, small_t, act.at[0:D, :], take, total, y_take, z_take, face_give, face_take, last
        )
        for group in range(5)
    )

    def grads(piece):
        pending.append(expert_grad_out(links, piece, downs, ups, out_down, out_up, local_sem))

    def publish(item):
        pending.extend(item.publish(out_qkv, out_proj, out_small, local_sem))

    def early():
        one.form()
        proj.chain(0)

    def middle():
        one.halve()
        two.form()
        proj.chain(1)

    def late():
        two.halve()
        three.form()
        proj.chain(2)
        one.chain(0)
        three.halve()

    proj.form()
    attention_backward(
        x_ref, wall, rows_t, qkv, board, hidden, normed2, rb, rel_rows, small_t, grad_tokens, proj.halve,
        (early, middle, late),
    )
    small.form_small()
    put(grad_tokens, tokens_out, 27)
    proj.chain(3)
    one.chain(1)
    small.halve()
    two.chain(0)
    one.chain(2)
    grads(0)
    proj.face()
    two.chain(1)
    one.chain(3)
    grads(1)
    three.chain(0)
    two.chain(2)
    three.chain(1)
    grads(2)
    one.face()
    three.chain(2)
    small.chain(0)
    two.chain(3)
    small.chain(1)
    small.chain(2)
    grads(3)
    publish(proj)
    two.face()
    grads(4)
    three.chain(3)
    small.chain(3)
    grads(5)
    publish(one)
    three.face()
    small.face()
    publish(two)
    publish(three)
    publish(small)
    for item in (proj, one, two, three):
        item.landed()
    expert_grads_arrive(links, out_down, out_up)
    for copy in pending:
        copy.wait()
    links.finish()


PARTS = 6


def hand_out(
    mixed, tokens, qkv, proj, small, up, down,
    to_mixed, to_tokens, to_qkv, to_proj, to_gain_attn, to_gain_moe, to_router, to_rel, to_up, to_down,
    v_mixed, v_tokens, v_qkv, v_proj, v_small, v_up, v_down,
    v_gain_attn, v_gain_moe, v_router, v_rel, wide_up, wide_down, in_sem, out_sem,
):
    def rows(array, i):
        count = array.shape[0] // PARTS
        return pl.ds(i * count, count)

    def copy(src, dst, sem, i):
        item = pltpu.make_async_copy(src, dst, sem.at[i])
        item.start()
        return item

    halves = [
        (source, held, wide, out, rows(source, i))
        for i in range(PARTS)
        for source, held, wide, out in ((up, v_up, wide_up, to_up), (down, v_down, wide_down, to_down))
    ]
    coming = [copy(source.at[at], held.at[at], in_sem, i) for i, (source, held, _, _, at) in enumerate(halves)]
    plain = ((tokens, v_tokens, to_tokens), (qkv, v_qkv, to_qkv), (mixed, v_mixed, to_mixed), (proj, v_proj, to_proj))
    first = len(halves)
    little = copy(small, v_small, in_sem, first + len(plain))
    others = [copy(source, held, in_sem, first + i) for i, (source, held, _) in enumerate(plain)]
    going = []

    def put(src, dst):
        going.append(copy(src, dst, out_sem, len(going)))

    for item, (source, held, wide, out, at) in zip(coming, halves):
        item.wait()
        wide[at] = held[at].astype(F32)
        put(wide.at[at], out.at[at])
    little.wait()
    turned = jnp.transpose(v_small[...])
    v_gain_attn[...] = turned[0]
    v_gain_moe[...] = turned[1]
    v_router[...] = turned[2 : 2 + EXP]
    v_rel[...] = v_small[0:16, HEAD : HEAD + HEADS]
    put(v_gain_attn, to_gain_attn)
    put(v_gain_moe, to_gain_moe)
    put(v_router, to_router)
    put(v_rel, to_rel)
    for item, (_, held, out) in zip(others, plain):
        item.wait()
        put(held, out)
    for item in going:
        item.wait()


def body_fast(
    tokens, cotangent, lengths, routes, slots, gain_attn, w_qkv, w_proj, rel_table, gain_moe, w_router, w_up, w_down
):
    vm = pl.BlockSpec(memory_space=pltpu.VMEM)
    hbm = pl.BlockSpec(memory_space=pl.ANY)
    sds = jax.ShapeDtypeStruct
    v = pltpu.VMEM
    shapes = (
        sds((TOK, D), BF16), sds((TOK, D), F32), sds((SHARD, 3 * D), F32), sds((SHARD, D), F32),
        sds((SHARD, 128), F32), sds((D, HF), BF16), sds((HF, D), BF16),
    )
    out = pl.pallas_call(
        layer,
        out_shape=shapes,
        in_specs=[hbm, hbm, pl.BlockSpec(memory_space=pltpu.SMEM), vm, vm, vm, vm, vm, vm, hbm, hbm, hbm, hbm],
        out_specs=[hbm, hbm, hbm, hbm, hbm, hbm, hbm],
        scratch_shapes=[
            v((TOK, D), BF16), v((TOK, D), BF16), v((TOK, D), BF16), v((TOK, D), F32), v((HEADS * SEQ, 3 * SEQ), F32),
            v((D, WALL), BF16), v((8, D), F32), v((8, TOK), F32), v((TOK, 8), F32), v((2, TOK, D), BF16),
            v((TOK, 3 * D), BF16), v((TOK, D), F32), v((TOK, D), BF16),
            v((TOK, 1), F32), v((EXP, ROWS, D), BF16), v((EXP, ROWS, D), BF16),
            v((8 * ROWS, D), BF16), v((8 * ROWS, D), BF16), v((D, HF), BF16), v((HF, D), BF16),
            v((8 * ROWS, SENTC), BF16), v((8 * ROWS, HF), BF16),
            v((EXP, 2, ROWS, D), BF16), v((EXP, 2, ROWS, D), BF16), v((EXP, ROWS, D), BF16), v((EXP, ROWS, D), BF16),
            v((EXP, ROWS, D), BF16), v((EXP, ROWS, D), BF16),
            v((HF // 2, D), F32), v((HF // 2, D), BF16), v((HF // 2, D), BF16), v((HF // 2, D), BF16),
            v((D // 2, HF), F32), v((D // 2, HF), BF16), v((D // 2, HF), BF16), v((D // 2, HF), BF16),
            v((TOK, 4 * D), BF16), v((16, SEQ), F32), v((128, D), F32),
            v((D, SENTC), BF16), v((D, SENTC), F32), v((4, SHARD, SENTC), BF16), v((8, SHARD, SENTC), BF16),
            v((SHARD, SENTC), BF16), v((SHARD, SENTC), BF16), v((SHARD, SENTC), F32),
            pltpu.SemaphoreType.DMA((28,)), pltpu.SemaphoreType.DMA((LINKS,)), pltpu.SemaphoreType.DMA((LINKS,)),
        ],
        compiler_params=pltpu.CompilerParams(
            collective_id=0, has_side_effects=True, vmem_limit_bytes=67043328
        ),
        name="layer",
    )(
        tokens, cotangent, lengths, routes.T, slots.T, gain_attn[None], gain_moe[None], w_router.T, rel_table, w_qkv, w_proj,
        w_up, w_down,
    )
    small = (sds((SHARD,), F32), sds((SHARD,), F32), sds((EXP, SHARD), F32), sds((16, HEADS), F32))
    final = shapes[:4] + small + (sds((D, HF), F32), sds((HF, D), F32))
    mixed, grad_tokens, grad_qkv, grad_proj, grad_gain_attn, grad_gain_moe, grad_router, grad_rel, grad_up, grad_down = (
        pl.pallas_call(
            hand_out,
            out_shape=final,
            in_specs=[hbm] * len(shapes),
            out_specs=[hbm] * len(final),
            scratch_shapes=[v(item.shape, item.dtype) for item in shapes + small + final[-2:]]
            + [pltpu.SemaphoreType.DMA((2 * PARTS + 5,)), pltpu.SemaphoreType.DMA((2 * PARTS + 8,))],
            name="hand_out",
        )(*out)
    )
    return (
        mixed,
        grad_tokens,
        grad_gain_attn,
        grad_qkv,
        grad_proj,
        grad_rel,
        grad_gain_moe,
        grad_router.T,
        grad_up[None],
        grad_down[None],
    )


epsilon = 1e-06
exact_precision = lax.Precision.HIGHEST


def rms_norm(values, gain):
    factor = lax.rsqrt(jnp.mean(values * values, axis=-1, keepdims=True) + epsilon)
    return values * factor * gain


def distance_hot():
    places = jnp.arange(SEQ, dtype=jnp.int32)
    distance = jnp.clip(places[:, None] - places[None, :], 0, SEQ - 1).reshape(1, SEQ * SEQ)
    return (distance == places[:, None]).astype(jnp.bfloat16)


def bias_matrix(table, hot):
    flat = jnp.einsum("dh,dp->hp", table, hot, preferred_element_type=jnp.float32)
    return flat.reshape(table.shape[1], SEQ, SEQ)


def exact_gelu(values):
    return jax.nn.gelu(values, approximate=False)


def masked_scores(qkv_rows, bias, allowed, factor):
    raw = jnp.einsum(
        "qhd,khd->hqk", qkv_rows[:, 0], qkv_rows[:, 1], preferred_element_type=jnp.float32
    )
    return jnp.where(allowed[None], raw * factor + bias, -1e30)


def fetch_weights(gain_attn, w_qkv, w_proj, rel_table, gain_moe, w_router):
    rows, experts = w_router.shape
    spread = rel_table.shape[0]
    packed = jnp.concatenate(
        [gain_attn, gain_moe, w_router.reshape(-1), rel_table.reshape(-1)]
    )
    small = lax.all_gather(packed, "fsdp", axis=0, tiled=False)
    groups = small.shape[0]
    edge = 2 * rows + rows * experts
    return (
        small[:, :rows].reshape(-1),
        lax.all_gather(w_qkv, "fsdp", axis=0, tiled=True),
        lax.all_gather(w_proj, "fsdp", axis=0, tiled=True),
        small[:, edge:].reshape(groups * spread, HEADS),
        small[:, rows : 2 * rows].reshape(-1),
        small[:, 2 * rows : edge].reshape(groups * rows, experts),
    )


def body(
    tokens,
    cotangent,
    lengths,
    routes,
    slots,
    gain_attn,
    w_qkv,
    w_proj,
    rel_table,
    gain_moe,
    w_router,
    w_up,
    w_down,
):
    groups = lax.axis_size("fsdp")
    experts = groups // 2
    capacity = 2 * SEQ // experts
    factor = HEAD ** (-0.5)
    up_weight = w_up[0]
    down_weight = w_down[0]
    places = jnp.arange(SEQ, dtype=jnp.int32)
    causal = places[:, None] >= places[None, :]
    expert_ids = jnp.arange(experts, dtype=jnp.int32)
    saved = []
    mixed_parts = []
    weights = fetch_weights(gain_attn, w_qkv, w_proj, rel_table, gain_moe, w_router)
    gain_a = weights[0].astype(jnp.float32)
    gain_m = weights[4].astype(jnp.float32)
    router_float = weights[5].astype(jnp.float32)
    hot = distance_hot()
    bias = bias_matrix(weights[3], hot)
    for batch in range(MB):
        x_float = tokens[batch * SEQ : (batch + 1) * SEQ].astype(jnp.float32)
        live_keys = places < lengths[batch]
        live_col = live_keys.astype(jnp.float32)[:, None]
        allowed = causal & live_keys[None, :]
        normed = rms_norm(x_float, gain_a).astype(jnp.bfloat16)
        qkv_rows = (
            jnp.dot(normed, weights[1], preferred_element_type=jnp.float32)
            .astype(jnp.bfloat16)
            .reshape(SEQ, 3, HEADS, HEAD)
        )
        scores = masked_scores(qkv_rows, bias, allowed, factor)
        row_peak = jnp.max(scores, axis=-1, keepdims=True)
        exp_scores = jnp.exp(scores - row_peak)
        row_total = jnp.sum(exp_scores, axis=-1, keepdims=True)
        log_total = row_peak + jnp.log(row_total)
        probs_low = (exp_scores / row_total).astype(jnp.bfloat16)
        attended = jnp.einsum(
            "hqk,khd->qhd", probs_low, qkv_rows[:, 2], preferred_element_type=jnp.float32
        )
        attended = attended.astype(jnp.bfloat16).reshape(SEQ, D)
        branch = jnp.dot(attended, weights[2], preferred_element_type=jnp.float32)
        hidden = x_float + live_col * branch
        normed2 = rms_norm(hidden, gain_m).astype(jnp.bfloat16)
        logits = jnp.dot(normed2, weights[5], preferred_element_type=jnp.float32)
        route_rows = routes[batch * SEQ : (batch + 1) * SEQ]
        slot_rows = slots[batch * SEQ : (batch + 1) * SEQ]
        hot_first = (route_rows[:, 0:1] == expert_ids[None, :]).astype(jnp.float32)
        hot_second = (route_rows[:, 1:2] == expert_ids[None, :]).astype(jnp.float32)
        gate_first = jax.nn.sigmoid(
            jnp.sum(logits * hot_first, axis=-1) - jnp.sum(logits * hot_second, axis=-1)
        )
        row_place = route_rows * capacity + slot_rows
        target = jnp.where(live_keys[:, None], row_place, experts * capacity)
        outgoing = jnp.zeros((experts * capacity, D), jnp.bfloat16)
        outgoing = (
            outgoing.at[target[:, 0]]
            .set(normed2, mode="drop")
            .at[target[:, 1]]
            .set(normed2, mode="drop")
        )
        outgoing = jnp.repeat(outgoing.reshape(experts, capacity, D), 2, axis=0)
        expert_received = lax.all_to_all(outgoing, "fsdp", split_axis=0, concat_axis=0, tiled=True)
        expert_before = jnp.einsum(
            "scd,df->scf", expert_received, up_weight, preferred_element_type=jnp.float32
        )
        expert_active = exact_gelu(expert_before).astype(jnp.bfloat16)
        partial_value = jnp.einsum(
            "scf,fd->scd", expert_active, down_weight, preferred_element_type=jnp.float32
        ).astype(jnp.bfloat16)
        returned = lax.all_to_all(partial_value, "fsdp", split_axis=0, concat_axis=0, tiled=True)
        results = (returned, expert_received, expert_before)
        combined = (
            results[0]
            .astype(jnp.float32)
            .reshape(experts, 2, capacity, D)
            .sum(axis=1)
            .reshape(experts * capacity, D)
        )
        first_out = combined[row_place[:, 0]]
        second_out = combined[row_place[:, 1]]
        moe = live_col * (
            gate_first[:, None] * first_out + (1.0 - gate_first)[:, None] * second_out
        )
        mixed_parts.append((hidden + moe).astype(jnp.bfloat16))
        saved.append(
            {
                "normed": normed,
                "qkv_rows": qkv_rows,
                "log_total": log_total,
                "attended": attended,
                "hidden": hidden,
                "normed2": normed2,
                "gate_first": gate_first,
                "first_out": first_out,
                "second_out": second_out,
                "results": results,
                "target": target,
                "row_place": row_place,
                "hot_first": hot_first,
                "hot_second": hot_second,
            }
        )
    grad_qkv_w = jnp.zeros((D, 3 * D), jnp.float32)
    grad_proj_w = jnp.zeros((D, D), jnp.float32)
    grad_table = jnp.zeros((SEQ, HEADS), jnp.float32)
    grad_gain_a = jnp.zeros((D,), jnp.float32)
    grad_gain_m = jnp.zeros((D,), jnp.float32)
    grad_router = jnp.zeros((D, experts), jnp.float32)
    grad_up = jnp.zeros((D, FF // 2), jnp.float32)
    grad_down = jnp.zeros((FF // 2, D), jnp.float32)
    grad_parts = [None] * MB
    for batch in reversed(range(MB)):
        kept = saved[batch]
        x_float = tokens[batch * SEQ : (batch + 1) * SEQ].astype(jnp.float32)
        live_keys = places < lengths[batch]
        live_col = live_keys.astype(jnp.float32)[:, None]
        allowed = causal & live_keys[None, :]
        grad_out = cotangent[batch * SEQ : (batch + 1) * SEQ].astype(jnp.float32)
        grad_moe = live_col * grad_out
        gate_first = kept["gate_first"]
        gate_second = 1.0 - gate_first
        grad_gate_first = jnp.sum(grad_moe * kept["first_out"], axis=-1)
        grad_gate_second = jnp.sum(grad_moe * kept["second_out"], axis=-1)
        grad_first = (gate_first[:, None] * grad_moe).astype(jnp.bfloat16)
        grad_second = (gate_second[:, None] * grad_moe).astype(jnp.bfloat16)
        target = kept["target"]
        grad_send = jnp.zeros((experts * capacity, D), jnp.bfloat16)
        grad_send = (
            grad_send.at[target[:, 0]]
            .set(grad_first, mode="drop")
            .at[target[:, 1]]
            .set(grad_second, mode="drop")
        )
        grad_send = jnp.repeat(grad_send.reshape(experts, capacity, D), 2, axis=0)
        grad_recv = lax.all_to_all(grad_send, "fsdp", split_axis=0, concat_axis=0, tiled=True)
        received = kept["results"][1]
        before = kept["results"][2]
        active, gelu_back = jax.vjp(exact_gelu, before)
        active_low = active.astype(jnp.bfloat16)
        grad_active = jnp.einsum(
            "scd,fd->scf", grad_recv, down_weight, preferred_element_type=jnp.float32
        )
        grad_before = gelu_back(grad_active)[0].astype(jnp.bfloat16)
        grad_down = grad_down + jnp.einsum(
            "scf,scd->fd", active_low, grad_recv, preferred_element_type=jnp.float32
        )
        grad_up = grad_up + jnp.einsum(
            "scd,scf->df", received, grad_before, preferred_element_type=jnp.float32
        )
        grad_part = jnp.einsum(
            "scf,df->scd", grad_before, up_weight, preferred_element_type=jnp.float32
        ).astype(jnp.bfloat16)
        grad_back = lax.all_to_all(grad_part, "fsdp", split_axis=0, concat_axis=0, tiled=True)
        grad_rows = (
            grad_back.astype(jnp.float32)
            .reshape(experts, 2, capacity, D)
            .sum(axis=1)
            .reshape(experts * capacity, D)
        )
        row_place = kept["row_place"]
        grad_diff = (grad_gate_first - grad_gate_second) * gate_first * gate_second
        grad_logits = grad_diff[:, None] * (kept["hot_first"] - kept["hot_second"])
        normed2_float = kept["normed2"].astype(jnp.float32)
        grad_router = grad_router + jnp.dot(normed2_float.T, grad_logits, precision=exact_precision)
        grad_normed2 = live_col * (grad_rows[row_place[:, 0]] + grad_rows[row_place[:, 1]])
        grad_normed2 = grad_normed2 + jnp.dot(
            grad_logits, router_float.T, precision=exact_precision
        )
        _, norm_back_moe = jax.vjp(rms_norm, kept["hidden"], gain_m)
        grad_hidden_norm, grad_gain_part = norm_back_moe(grad_normed2)
        grad_gain_m = grad_gain_m + grad_gain_part
        grad_hidden = grad_out + grad_hidden_norm
        grad_branch = (live_col * grad_hidden).astype(jnp.bfloat16)
        grad_proj_w = grad_proj_w + jnp.einsum(
            "sd,se->de", kept["attended"], grad_branch, preferred_element_type=jnp.float32
        )
        grad_attended = jnp.einsum(
            "se,de->sd", grad_branch, weights[2], preferred_element_type=jnp.float32
        )
        grad_attended = grad_attended.astype(jnp.bfloat16).reshape(SEQ, HEADS, HEAD)
        qkv_rows = kept["qkv_rows"]
        scores = masked_scores(qkv_rows, bias, allowed, factor)
        probs = jnp.exp(scores - kept["log_total"])
        probs_low = probs.astype(jnp.bfloat16)
        grad_probs = jnp.einsum(
            "qhd,khd->hqk", grad_attended, qkv_rows[:, 2], preferred_element_type=jnp.float32
        )
        row_dot = jnp.sum(probs * grad_probs, axis=-1, keepdims=True)
        grad_scores = (probs * (grad_probs - row_dot)).astype(jnp.bfloat16)
        grad_table = grad_table + jnp.einsum(
            "dp,hp->dh",
            hot,
            jnp.where(allowed[None], grad_scores, 0).reshape(HEADS, SEQ * SEQ),
            preferred_element_type=jnp.float32,
        )
        grad_queries = (
            jnp.einsum(
                "hqk,khd->qhd", grad_scores, qkv_rows[:, 1], preferred_element_type=jnp.float32
            )
            * factor
        )
        grad_keys = (
            jnp.einsum(
                "hqk,qhd->khd", grad_scores, qkv_rows[:, 0], preferred_element_type=jnp.float32
            )
            * factor
        )
        grad_values = jnp.einsum(
            "hqk,qhd->khd", probs_low, grad_attended, preferred_element_type=jnp.float32
        )
        grad_qkv = (
            jnp.stack([grad_queries, grad_keys, grad_values], axis=1)
            .astype(jnp.bfloat16)
            .reshape(SEQ, 3 * D)
        )
        grad_qkv_w = grad_qkv_w + jnp.einsum(
            "sd,se->de", kept["normed"], grad_qkv, preferred_element_type=jnp.float32
        )
        grad_normed = jnp.einsum(
            "se,de->sd", grad_qkv, weights[1], preferred_element_type=jnp.float32
        )
        _, norm_back_attn = jax.vjp(rms_norm, x_float, gain_a)
        grad_x_norm, grad_gain_piece = norm_back_attn(grad_normed)
        grad_gain_a = grad_gain_a + grad_gain_piece
        grad_parts[batch] = grad_hidden + grad_x_norm
    small = jnp.concatenate(
        [
            grad_gain_a.reshape(groups, -1),
            grad_gain_m.reshape(groups, -1),
            grad_router.reshape(groups, -1),
            grad_table.reshape(groups, -1),
        ],
        axis=1,
    )
    small = lax.psum_scatter(small, "fsdp", scatter_dimension=0, tiled=True)
    shards = (
        small,
        lax.psum_scatter(grad_qkv_w, "fsdp", scatter_dimension=0, tiled=True),
        lax.psum_scatter(grad_proj_w, "fsdp", scatter_dimension=0, tiled=True),
    )
    sums = lax.psum((shards[0], shards[1], shards[2], grad_up[None], grad_down[None]), "replica")
    rows = D // groups
    edge = 2 * rows + rows * experts
    totals = (
        sums[0][0, :rows],
        sums[1],
        sums[2],
        sums[0][0, edge:].reshape(SEQ // groups, HEADS),
        sums[0][0, rows : 2 * rows],
        sums[0][0, 2 * rows : edge].reshape(rows, experts),
        sums[3],
        sums[4],
    )
    mixed = jnp.concatenate(mixed_parts, axis=0)
    grad_tokens = jnp.concatenate(grad_parts, axis=0)
    return (
        mixed,
        grad_tokens,
        totals[0],
        totals[1],
        totals[2],
        totals[3],
        totals[4],
        totals[5],
        totals[6],
        totals[7],
    )


def solution(mesh):
    in_specs = (
        P(("replica", "fsdp"), None),
        P(("replica", "fsdp"), None),
        P(("replica", "fsdp")),
        P(("replica", "fsdp"), None),
        P(("replica", "fsdp"), None),
        P("fsdp"),
        P("fsdp", None),
        P("fsdp", None),
        P("fsdp", None),
        P("fsdp"),
        P("fsdp", None),
        P("fsdp", None, None),
        P("fsdp", None, None),
    )
    out_specs = (
        P(("replica", "fsdp"), None),
        P(("replica", "fsdp"), None),
        P("fsdp"),
        P("fsdp", None),
        P("fsdp", None),
        P("fsdp", None),
        P("fsdp"),
        P("fsdp", None),
        P("fsdp", None, None),
        P("fsdp", None, None),
    )
    fast = dict(mesh.shape) == {"replica": 4, "fsdp": 8}
    return jax.shard_map(body_fast if fast else body, mesh=mesh, in_specs=in_specs, out_specs=out_specs, check_vma=False)
```
